32 devices in a mesh: seq: 8 (over y, x, core), fsdp: 4 (over z).
Axes of the slice: x: 2, y: 2, z: 4, core: 2. Of those that a mesh axis runs over, the one named last changes fastest.
Arguments:
- inputs: bfloat16 [4, 4096, 1280], P('fsdp', 'seq'), may hold values from -6 to 6
- w_query: float32 [1280, 1280], P(('seq', 'fsdp')), may hold values from -0.15625 to 0.15625
- w_key: float32 [1280, 1280], P(('seq', 'fsdp')), may hold values from -0.15625 to 0.15625
- w_value: float32 [1280, 1280], P(('seq', 'fsdp')), may hold values from -0.15625 to 0.15625
- w_proj: float32 [1280, 1280], P(('seq', 'fsdp')), may hold values from -1 to 1
- w_up: float32 [1280, 1280], P(('seq', 'fsdp')), may hold values from -0.15625 to 0.15625
- w_down: float32 [1280, 1280], P(('seq', 'fsdp')), may hold values from -0.3125 to 0.3125
- gain_first: float32 [1280], P(('seq', 'fsdp')), may hold values from 0.25 to 1.75
- gain_second: float32 [1280], P(('seq', 'fsdp')), may hold values from 0.25 to 1.75
- bias_up: float32 [1280], P(('seq', 'fsdp')), may hold values from -3 to 3
- bias_down: float32 [1280], P(('seq', 'fsdp')), may hold values from -3 to 3
- query_scale: float32 [80], replicated, may hold values from 0 to 2
- cotangent: bfloat16 [4, 4096, 1280], P('fsdp', 'seq'), may hold values from -6 to 6
Outputs:
- result: bfloat16 [4, 4096, 1280], P('fsdp', 'seq')
- grad_inputs: bfloat16 [4, 4096, 1280], P('fsdp', 'seq')
- grad_query: float32 [1280, 1280], P(('seq', 'fsdp'))
- grad_key: float32 [1280, 1280], P(('seq', 'fsdp'))
- grad_value: float32 [1280, 1280], P(('seq', 'fsdp'))
- grad_proj: float32 [1280, 1280], P(('seq', 'fsdp'))
- grad_up: float32 [1280, 1280], P(('seq', 'fsdp'))
- grad_down: float32 [1280, 1280], P(('seq', 'fsdp'))
- grad_first: float32 [1280], P(('seq', 'fsdp'))
- grad_second: float32 [1280], P(('seq', 'fsdp'))
- grad_bias_up: float32 [1280], P(('seq', 'fsdp'))
- grad_bias_down: float32 [1280], P(('seq', 'fsdp'))
- grad_scale: float32 [80], replicated
The draws below stay inside these ranges and needn't reach their ends.
All inputs are finite; a program needn't handle non-finite values.
Results may differ from the reference program's by a relative error of at most 0.015.
The reference program's roundings to bfloat16 on the way count: a program that leaves them out, or rounds other values in their place, can miss the bound.
Values may be sent and summed in bfloat16 or wider, within the bound.
A program may use at most 192 MiB of HBM per device.

```python
import math
import jax
import jax.numpy as jnp
from jax import lax

D = 1280
H = 16
HD = 80
FF = 1280
LEN = 4096
SEQS = 4


def levels(stream_key, shape, shards, smallest, high):
    loudness = 1.0
    for dim, shards_of in shards:
        steps = jax.random.uniform(jax.random.fold_in(jax.random.fold_in(stream_key, 6), dim), (shards_of,), jnp.float32, smallest / len(shards), high / len(shards))
        loudness = loudness * jnp.repeat(jnp.exp(steps), shape[dim] // shards_of).reshape((-1,) + (1,) * (len(shape) - 1 - dim))
    return loudness


def centred(own_key, shape, deviation, limit, shards=(), kind=jnp.bfloat16):
    level = levels(own_key, shape, shards, -0.22, 0.18) if shards else 1.0
    drawn = jax.random.normal(own_key, shape, jnp.float32) * deviation * level
    return jnp.minimum(jnp.maximum(drawn, -limit), limit).astype(kind)


def setup_inputs(seed: int = 0) -> dict:
    key_of = jax.random.split(jax.random.key(seed), 14)
    inputs = centred(key_of[0], (SEQS, LEN, D), 1.0, 6.0, ((0, 4), (1, 8)))
    w_query = centred(key_of[1], (D, D), D ** -0.5, 0.15625, ((0, 32),), jnp.float32)
    w_key = centred(key_of[2], (D, D), D ** -0.5, 0.15625, ((0, 32),), jnp.float32)
    w_value = centred(key_of[3], (D, D), D ** -0.5, 0.15625, ((0, 32),), jnp.float32)
    w_proj = centred(key_of[4], (D, D), (D // 32) ** -0.5, 1.0, ((0, 32),), jnp.float32)
    w_up = centred(key_of[5], (D, FF), D ** -0.5, 0.15625, ((0, 32),), jnp.float32)
    w_down = centred(key_of[6], (FF, D), (FF // 4) ** -0.5, 0.3125, ((0, 32),), jnp.float32)
    gain_first = jnp.clip(1.0 + 0.15 * jax.random.normal(key_of[7], (D,), jnp.float32), 0.25, 1.75)
    gain_second = jnp.clip(1.0 + 0.15 * jax.random.normal(key_of[8], (D,), jnp.float32), 0.25, 1.75)
    bias_up = centred(key_of[9], (FF,), 0.5, 3.0, ((0, 32),), jnp.float32)
    bias_down = centred(key_of[10], (D,), 0.5, 3.0, ((0, 32),), jnp.float32)
    query_scale = jnp.clip(jax.random.uniform(key_of[11], (HD,), jnp.float32, 0.0, 2.0), 0.0, 2.0)
    cotangent = centred(key_of[12], (SEQS, LEN, D), 1.0, 6.0, ((0, 4), (1, 8)))
    return dict(inputs=inputs, w_query=w_query, w_key=w_key, w_value=w_value, w_proj=w_proj, w_up=w_up, w_down=w_down, gain_first=gain_first, gain_second=gain_second, bias_up=bias_up, bias_down=bias_down, query_scale=query_scale, cotangent=cotangent)


@jax.custom_vjp
def low(v):
    return lax.optimization_barrier(v.astype(jnp.bfloat16)).astype(jnp.float32)

@jax.custom_vjp
def low_back(v):
    return v

def low_keep(v):
    return (low(v), None)

def low_pass(kept, grad):
    return (grad,)

def back_keep(v):
    return (v, None)

def back_low(kept, grad):
    return (low(grad),)
low.defvjp(low_keep, low_pass)
low_back.defvjp(back_keep, back_low)
eps_norm = 1e-06
log_two_inverse = 1.442695

def rms_scale(values, gain):
    return values * lax.rsqrt(lax.optimization_barrier(jnp.mean(values * values, axis=-1, keepdims=True)) + eps_norm) * gain

def matmul(left, right):
    return jnp.dot(left, right, precision=lax.Precision.HIGHEST, preferred_element_type=jnp.float32)

def attend_series(triple):
    queries, key_rows, value_rows = triple
    rows_block = min(512, LEN)
    block_count = LEN // rows_block
    query_blocks = queries.reshape(block_count, rows_block, H, HD)
    key_heads = key_rows.reshape(LEN, H, HD)
    value_heads = value_rows.reshape(LEN, H, HD)
    key_pos = jnp.arange(LEN, dtype=jnp.int32)

    def one_block(pair):
        query_block, first_row = pair
        scores = jnp.einsum('qhd,khd->hqk', query_block, key_heads, precision=lax.Precision.HIGHEST)
        scores = low_back(scores)
        query_pos = first_row + jnp.arange(rows_block, dtype=jnp.int32)
        allowed = key_pos[None, :] <= query_pos[:, None]
        scores = jnp.where(allowed[None, :, :], scores, -1e+30)
        row_max = lax.optimization_barrier(jnp.max(scores, axis=-1, keepdims=True))
        shifted = jnp.exp(scores - row_max)
        probs = shifted / lax.optimization_barrier(jnp.sum(shifted, axis=-1, keepdims=True))
        return jnp.einsum('hqk,khd->qhd', low(probs), value_heads, precision=lax.Precision.HIGHEST)
    firsts = jnp.arange(block_count, dtype=jnp.int32) * rows_block
    outcome = lax.map(jax.checkpoint(one_block), (query_blocks, firsts))
    return outcome.reshape(LEN, D)

def forward(inputs, w_query, w_key, w_value, w_proj, w_up, w_down, gain_first, gain_second, bias_up, bias_down, query_scale):
    scale_dims = jax.nn.softplus(query_scale) * log_two_inverse / math.sqrt(HD)
    tiled_scale = jnp.tile(scale_dims, H)
    normed = low(rms_scale(inputs, low(gain_first)))
    queries = low_back(matmul(normed, low(w_query)))
    scaled = low_back(low(queries * tiled_scale))
    key_rows = low_back(low(matmul(normed, low(w_key))))
    value_rows = low_back(low(matmul(normed, low(w_value))))
    mixed = lax.map(attend_series, (scaled, key_rows, value_rows))
    mixed = low_back(low(mixed))
    middle = inputs + low_back(matmul(mixed, low(w_proj)))
    second = low(rms_scale(middle, low(gain_second)))
    hidden = low_back(matmul(second, low(w_up))) + low(bias_up)
    active = low(jax.nn.silu(hidden))
    return middle + low_back(matmul(active, low(w_down))) + low(bias_down)

def reference(inputs, w_query, w_key, w_value, w_proj, w_up, w_down, gain_first, gain_second, bias_up, bias_down, query_scale, cotangent):
    result, pullback = jax.vjp(forward, inputs.astype(jnp.float32), w_query, w_key, w_value, w_proj, w_up, w_down, gain_first, gain_second, bias_up, bias_down, query_scale)
    grads = pullback(cotangent.astype(jnp.float32))
    return (result.astype(jnp.bfloat16), grads[0].astype(jnp.bfloat16), grads[1], grads[2], grads[3], grads[4], grads[5], grads[6], grads[7], grads[8], grads[9], grads[10], grads[11])
```

```python
import functools
import math

import jax
import jax.numpy as jnp
from jax import lax
from jax.experimental import pallas as pl
from jax.experimental.pallas import tpu as pltpu
from jax.sharding import PartitionSpec as P

H = 16
HD = 80
eps_norm = 1e-06
log_two_inverse = 1.442695
bf = jnp.bfloat16
f32 = jnp.float32
NEG = -1e30


def rms_scale(values, gain):
    return values * lax.rsqrt(jnp.mean(values * values, axis=-1, keepdims=True) + eps_norm) * gain


def dot(a,b,ca=1,cb=0):
    return lax.dot_general(a,b,(((ca,),(cb,)),((),())),preferred_element_type=f32)

def fwd_kernel(BQ,BK,qt,k,vt,ot,lse):
    nh,hd,L=qt.shape
    i=pl.program_id(0)
    q=[qt[h,:,pl.ds(pl.multiple_of(i*BQ,BQ),BQ)] for h in range(nh)]
    def step(j,carry,diag=None):
        out=[]
        s=[]
        for h in range(nh):
            kk=k[h,pl.ds(pl.multiple_of(j*BK,BK),BK),:]
            s.append(dot(kk,q[h]))
        for h in range(nh):
            m,l,acc=carry[h]
            sh=s[h]
            if diag is not None:
                kp=lax.broadcasted_iota(jnp.int32,sh.shape,0)+diag*BK
                qp=lax.broadcasted_iota(jnp.int32,sh.shape,1)
                sh=jnp.where(kp<=qp,sh,NEG)
            mn=jnp.maximum(m,jnp.max(sh,axis=0,keepdims=True))
            a=jnp.exp(m-mn)
            p=jnp.exp(sh-mn)
            l=l*a+jnp.sum(p,axis=0,keepdims=True)
            vv=vt[h,:,pl.ds(pl.multiple_of(j*BK,BK),BK)]
            acc=acc*a+dot(vv,p.astype(bf))
            out.append((mn,l,acc))
        return tuple(out)
    init=tuple((jnp.full((1,BQ),NEG,f32),jnp.zeros((1,BQ),f32),jnp.zeros((hd,BQ),f32)) for _ in range(nh))
    r=BQ//BK
    c=lax.fori_loop(0,i*r,step,init)
    for d in range(r):
        c=step(i*r+d,c,d)
    for h in range(nh):
        m,l,acc=c[h]
        ot[h,:,:]=(acc/l).astype(bf)
        lse[h,:,:]=m+jnp.log(l)
def flash_fwd(qt,k,vt,BQ=512,BK=512):
    nh,hd,L=qt.shape
    return pl.pallas_call(functools.partial(fwd_kernel,BQ,BK),grid=(L//BQ,),
      in_specs=[pl.BlockSpec((nh,hd,L),lambda i:(0,0,0)),pl.BlockSpec((nh,L,hd),lambda i:(0,0,0)),pl.BlockSpec((nh,hd,L),lambda i:(0,0,0))],
      out_specs=[pl.BlockSpec((nh,hd,BQ),lambda i:(0,0,i)),pl.BlockSpec((nh,1,BQ),lambda i:(0,0,i))],
      out_shape=[jax.ShapeDtypeStruct((nh,hd,L),bf),jax.ShapeDtypeStruct((nh,1,L),f32)],
      compiler_params=pltpu.CompilerParams(vmem_limit_bytes=60<<20),name=f"fwd{BQ}_{BK}")(qt,k,vt)

def bwd_kernel(BQ,BK,qt,q,kt,k,v,dot_,do,lse,delta,dqt,dk,dv,dks,dvs):
    nh,hd,L=qt.shape
    i=pl.program_id(0); nb=L//BQ
    @pl.when(i==0)
    def _():
        dks[...]=jnp.zeros_like(dks); dvs[...]=jnp.zeros_like(dvs)
    qs=pl.ds(pl.multiple_of(i*BQ,BQ),BQ)
    def step(j,carry,diag=None):
        ks=pl.ds(pl.multiple_of(j*BK,BK),BK)
        s=[dot(k[h,ks,:],qt[h,:,qs]) for h in range(nh)]
        dp=[dot(v[h,ks,:],dot_[h,:,qs]) for h in range(nh)]
        out=[]
        for h in range(nh):
            p=jnp.exp(s[h]-lse[h,:,qs])
            if diag is not None:
                kp=lax.broadcasted_iota(jnp.int32,p.shape,0)+diag*BK
                qp=lax.broadcasted_iota(jnp.int32,p.shape,1)
                p=jnp.where(kp<=qp,p,0.0)
            ds=(p*(dp[h]-delta[h,:,qs])).astype(bf)
            dvs[h,ks,:]+=dot(p.astype(bf),do[h,qs,:])
            dks[h,ks,:]+=dot(ds,q[h,qs,:])
            out.append(carry[h]+dot(kt[h,:,ks],ds))
        return tuple(out)
    init=tuple(jnp.zeros((hd,BQ),f32) for _ in range(nh))
    r=BQ//BK
    c=lax.fori_loop(0,i*r,step,init)
    for d in range(r): c=step(i*r+d,c,d)
    for h in range(nh): dqt[h,:,:]=c[h].astype(bf)
    @pl.when(i==nb-1)
    def _():
        dk[...]=dks[...].astype(bf); dv[...]=dvs[...].astype(bf)
def flash_bwd(qt,q,kt,k,v,dot_,do,lse,delta,BQ=512,BK=512):
    nh,hd,L=qt.shape
    full=lambda *s: pl.BlockSpec(s,lambda i:(0,0,0))
    return pl.pallas_call(functools.partial(bwd_kernel,BQ,BK),grid=(L//BQ,),
      in_specs=[full(nh,hd,L),full(nh,L,hd),full(nh,hd,L),full(nh,L,hd),full(nh,L,hd),full(nh,hd,L),full(nh,L,hd),full(nh,1,L),full(nh,1,L)],
      out_specs=[pl.BlockSpec((nh,hd,BQ),lambda i:(0,0,i)),full(nh,L,hd),full(nh,L,hd)],
      out_shape=[jax.ShapeDtypeStruct((nh,hd,L),bf),jax.ShapeDtypeStruct((nh,L,hd),bf),jax.ShapeDtypeStruct((nh,L,hd),bf)],
      scratch_shapes=[pltpu.VMEM((nh,L,hd),f32)]*2,
      compiler_params=pltpu.CompilerParams(vmem_limit_bytes=62<<20),name=f"bwd{BQ}_{BK}")(qt,q,kt,k,v,dot_,do,lse,delta)


def body(
    inputs,
    w_query,
    w_key,
    w_value,
    w_proj,
    w_up,
    w_down,
    gain_first,
    gain_second,
    bias_up,
    bias_down,
    query_scale,
    cotangent,
):
    groups = lax.axis_size("seq")
    rows_of = lax.axis_size("fsdp")
    nh = H // groups
    cols = nh * HD
    both = ("seq", "fsdp")
    tokens, width = inputs.shape[1], inputs.shape[2]
    length = tokens * groups
    shard = w_query.shape[0]
    x_low = inputs.reshape(tokens, width)
    x_all = lax.all_gather(x_low, "seq", axis=0, tiled=True)
    qkv_rows = jnp.stack([w_query, w_key, w_value], 1).astype(bf).reshape(shard, 3, groups, cols)
    qkv_cols = lax.all_to_all(qkv_rows, "seq", split_axis=2, concat_axis=0, tiled=False)
    qkv_cols = lax.all_gather(qkv_cols, "fsdp", axis=1)
    qkv_w = qkv_cols.reshape(width, 3, cols).transpose(1, 0, 2)
    small = jnp.stack([gain_first, gain_second, bias_up, bias_down], 0).astype(bf)
    small = lax.all_gather(small, both, axis=1, tiled=True).astype(f32)
    first_gain, second_gain, upbias, downbias = small[0], small[1], small[2], small[3]
    proj_w = lax.all_gather(w_proj.astype(bf), both, axis=0, tiled=True)
    up_w = lax.all_gather(w_up.astype(bf), both, axis=0, tiled=True)
    down_w = lax.all_gather(w_down.astype(bf), both, axis=0, tiled=True)
    scale_dims = jax.nn.softplus(query_scale) * log_two_inverse / math.sqrt(HD)
    scale_cols = jnp.tile(scale_dims, nh)

    normed = rms_scale(x_all.astype(f32), first_gain).astype(bf)
    query_full = jnp.dot(normed, qkv_w[0], preferred_element_type=f32)
    query_low = (query_full * scale_cols).astype(bf)
    key_low = jnp.dot(normed, qkv_w[1], preferred_element_type=f32).astype(bf)
    value_low = jnp.dot(normed, qkv_w[2], preferred_element_type=f32).astype(bf)

    def by_head(a):
        return a.reshape(length, nh, HD).transpose(1, 0, 2)

    def flip(a):
        return jnp.swapaxes(a, 1, 2)

    q, k, v = by_head(query_low), by_head(key_low), by_head(value_low)
    qt, kt, vt = flip(q), flip(k), flip(v)
    ot, lse = flash_fwd(qt, k, vt, min(1024, length), min(512, length))
    mixed = lax.all_to_all(ot.reshape(cols, length), "seq", split_axis=1, concat_axis=0, tiled=True)
    float_in = x_low.astype(f32)
    middle = float_in + dot(mixed, proj_w, 0, 0)
    second = rms_scale(middle, second_gain).astype(bf)
    hidden = jnp.dot(second, up_w, preferred_element_type=f32) + upbias
    active = jax.nn.silu(hidden).astype(bf)
    result = middle + jnp.dot(active, down_w, preferred_element_type=f32) + downbias

    top_low = cotangent.reshape(tokens, width)
    grad_top = top_low.astype(f32)
    grad_bdown = jnp.sum(grad_top, axis=0)
    grad_wdown = dot(active, top_low, 0, 0)
    grad_active = dot(top_low, down_w, 1, 1)
    gate = 1 / (1 + jnp.exp(-hidden))
    grad_hidden = grad_active * (gate * (1 + hidden * (1 - gate)))
    grad_bup = jnp.sum(grad_hidden, axis=0)
    hidden_low = grad_hidden.astype(bf)
    grad_wup = dot(second, hidden_low, 0, 0)
    grad_second_in = dot(hidden_low, up_w, 1, 1)
    unused_second, second_pull = jax.vjp(rms_scale, middle, second_gain)
    grad_middle, grad_gsecond = second_pull(grad_second_in)
    grad_middle = grad_middle + grad_top
    middle_low = grad_middle.astype(bf)
    grad_wproj = dot(mixed, middle_low, 1, 0)
    grad_mixed = dot(proj_w, middle_low, 1, 1).astype(bf)
    dmt = lax.all_to_all(grad_mixed, "seq", split_axis=0, concat_axis=1, tiled=True)
    dmt = dmt.reshape(nh, HD, length)
    owned = [
        lax.psum_scatter(g.astype(bf), both, scatter_dimension=0, tiled=True).astype(f32)
        for g in (grad_wproj, grad_wup, grad_wdown)
    ]
    delta = jnp.sum(dmt.astype(f32) * ot.astype(f32), axis=1, keepdims=True)
    dqt, dk, dv = flash_bwd(
        qt, q, kt, k, v, dmt, flip(dmt), lse, delta, min(512, length), min(512, length)
    )

    def flat(a):
        return a.transpose(1, 0, 2).reshape(length, cols)

    dqs = flat(flip(dqt)).astype(f32)
    dq = (dqs * scale_cols).astype(bf)
    dk, dv = flat(dk), flat(dv)
    scale_part = jnp.sum(jnp.sum(dqs * query_full, axis=0).reshape(nh, HD), axis=0)
    grad_qkv = jnp.concatenate([dot(normed, g, 0, 0) for g in (dq, dk, dv)], 1)
    back = dot(dq, qkv_w[0], 1, 1) + dot(dk, qkv_w[1], 1, 1) + dot(dv, qkv_w[2], 1, 1)
    back = lax.psum_scatter(back.astype(bf), "seq", scatter_dimension=0, tiled=True).astype(f32)
    grad_qkv = grad_qkv.reshape(groups, rows_of, shard, 3 * cols)
    grad_qkv = lax.psum_scatter(grad_qkv, "fsdp", scatter_dimension=1, tiled=False)
    grad_qkv = lax.all_to_all(grad_qkv, "seq", split_axis=0, concat_axis=0, tiled=False)
    grad_qkv = grad_qkv.reshape(groups, shard, 3, cols).transpose(2, 1, 0, 3).reshape(3, shard, width)
    unused_first, first_pull = jax.vjp(rms_scale, float_in, first_gain)
    grad_below, grad_gfirst = first_pull(back)
    grad_inputs = (grad_middle + grad_below).astype(bf)
    scale_row = jnp.pad(scale_part, (0, width - HD))
    vectors = jnp.stack([grad_gfirst, grad_gsecond, grad_bup, grad_bdown, scale_row], 0)
    vectors = lax.psum(vectors, both)
    at = (lax.axis_index("seq") * rows_of + lax.axis_index("fsdp")) * shard
    mine = lax.dynamic_slice_in_dim(vectors, at, shard, 1)
    grad_scale = vectors[4, :HD] * jax.nn.sigmoid(query_scale) * log_two_inverse / math.sqrt(HD)
    return (
        result.astype(bf).reshape(inputs.shape),
        grad_inputs.reshape(inputs.shape),
        grad_qkv[0],
        grad_qkv[1],
        grad_qkv[2],
        owned[0],
        owned[1],
        owned[2],
        mine[0],
        mine[1],
        mine[2],
        mine[3],
        grad_scale,
    )


def solution(mesh):
    return jax.shard_map(
        body,
        mesh=mesh,
        in_specs=(
            P("fsdp", "seq", None),
            P(("seq", "fsdp"), None),
            P(("seq", "fsdp"), None),
            P(("seq", "fsdp"), None),
            P(("seq", "fsdp"), None),
            P(("seq", "fsdp"), None),
            P(("seq", "fsdp"), None),
            P(("seq", "fsdp")),
            P(("seq", "fsdp")),
            P(("seq", "fsdp")),
            P(("seq", "fsdp")),
            P(),
            P("fsdp", "seq", None),
        ),
        out_specs=(
            P("fsdp", "seq", None),
            P("fsdp", "seq", None),
            P(("seq", "fsdp"), None),
            P(("seq", "fsdp"), None),
            P(("seq", "fsdp"), None),
            P(("seq", "fsdp"), None),
            P(("seq", "fsdp"), None),
            P(("seq", "fsdp"), None),
            P(("seq", "fsdp")),
            P(("seq", "fsdp")),
            P(("seq", "fsdp")),
            P(("seq", "fsdp")),
            P(),
        ),
        check_vma=False,
    )
```

```python
import functools
import math

import jax
import jax.numpy as jnp
from jax import lax
from jax.experimental import pallas as pl
from jax.experimental.pallas import tpu as pltpu
from jax.sharding import PartitionSpec as P

H = 16
HD = 80
eps_norm = 1e-06
log_two_inverse = 1.442695
bf = jnp.bfloat16
f32 = jnp.float32
NEG = -1e30


def rms_scale(values, gain):
    return values * lax.rsqrt(jnp.mean(values * values, axis=-1, keepdims=True) + eps_norm) * gain


def dot(a,b,ca=1,cb=0):
    return lax.dot_general(a,b,(((ca,),(cb,)),((),())),preferred_element_type=f32)

def fwd_kernel(BQ,BK,qt,k,vt,ot,lse):
    nh,hd,L=qt.shape
    i=pl.program_id(0)
    q=[qt[h,:,pl.ds(pl.multiple_of(i*BQ,BQ),BQ)] for h in range(nh)]
    def step(j,carry,diag=None):
        out=[]
        s=[]
        for h in range(nh):
            kk=k[h,pl.ds(pl.multiple_of(j*BK,BK),BK),:]
            s.append(dot(kk,q[h]))
        for h in range(nh):
            m,l,acc=carry[h]
            sh=s[h]
            if diag is not None:
                kp=lax.broadcasted_iota(jnp.int32,sh.shape,0)+diag*BK
                qp=lax.broadcasted_iota(jnp.int32,sh.shape,1)
                sh=jnp.where(kp<=qp,sh,NEG)
            mn=jnp.maximum(m,jnp.max(sh,axis=0,keepdims=True))
            a=jnp.exp(m-mn)
            p=jnp.exp(sh-mn)
            l=l*a+jnp.sum(p,axis=0,keepdims=True)
            vv=vt[h,:,pl.ds(pl.multiple_of(j*BK,BK),BK)]
            acc=acc*a+dot(vv,p.astype(bf))
            out.append((mn,l,acc))
        return tuple(out)
    init=tuple((jnp.full((1,BQ),NEG,f32),jnp.zeros((1,BQ),f32),jnp.zeros((hd,BQ),f32)) for _ in range(nh))
    r=BQ//BK
    c=lax.fori_loop(0,i*r,step,init)
    for d in range(r):
        c=step(i*r+d,c,d)
    for h in range(nh):
        m,l,acc=c[h]
        ot[h,:,:]=(acc/l).astype(bf)
        lse[h,:,:]=m+jnp.log(l)
def flash_fwd(qt,k,vt,BQ=512,BK=512):
    nh,hd,L=qt.shape
    return pl.pallas_call(functools.partial(fwd_kernel,BQ,BK),grid=(L//BQ,),
      in_specs=[pl.BlockSpec((nh,hd,L),lambda i:(0,0,0)),pl.BlockSpec((nh,L,hd),lambda i:(0,0,0)),pl.BlockSpec((nh,hd,L),lambda i:(0,0,0))],
      out_specs=[pl.BlockSpec((nh,hd,BQ),lambda i:(0,0,i)),pl.BlockSpec((nh,1,BQ),lambda i:(0,0,i))],
      out_shape=[jax.ShapeDtypeStruct((nh,hd,L),bf),jax.ShapeDtypeStruct((nh,1,L),f32)],
      compiler_params=pltpu.CompilerParams(vmem_limit_bytes=60<<20),name=f"fwd{BQ}_{BK}")(qt,k,vt)

def bwd_kernel(BQ,BK,qt,q,kt,k,v,dot_,do,lse,delta,dqt,dk,dv,dks,dvs):
    nh,hd,L=qt.shape
    i=pl.program_id(0); nb=L//BQ
    @pl.when(i==0)
    def _():
        dks[...]=jnp.zeros_like(dks); dvs[...]=jnp.zeros_like(dvs)
    qs=pl.ds(pl.multiple_of(i*BQ,BQ),BQ)
    def step(j,carry,diag=None):
        ks=pl.ds(pl.multiple_of(j*BK,BK),BK)
        s=[dot(k[h,ks,:],qt[h,:,qs]) for h in range(nh)]
        dp=[dot(v[h,ks,:],dot_[h,:,qs]) for h in range(nh)]
        out=[]
        for h in range(nh):
            p=jnp.exp(s[h]-lse[h,:,qs])
            if diag is not None:
                kp=lax.broadcasted_iota(jnp.int32,p.shape,0)+diag*BK
                qp=lax.broadcasted_iota(jnp.int32,p.shape,1)
                p=jnp.where(kp<=qp,p,0.0)
            ds=(p*(dp[h]-delta[h,:,qs])).astype(bf)
            dvs[h,ks,:]+=dot(p.astype(bf),do[h,qs,:])
            dks[h,ks,:]+=dot(ds,q[h,qs,:])
            out.append(carry[h]+dot(kt[h,:,ks],ds))
        return tuple(out)
    init=tuple(jnp.zeros((hd,BQ),f32) for _ in range(nh))
    r=BQ//BK
    c=lax.fori_loop(0,i*r,step,init)
    for d in range(r): c=step(i*r+d,c,d)
    for h in range(nh): dqt[h,:,:]=c[h].astype(bf)
    @pl.when(i==nb-1)
    def _():
        dk[...]=dks[...].astype(bf); dv[...]=dvs[...].astype(bf)
def flash_bwd(qt,q,kt,k,v,dot_,do,lse,delta,BQ=512,BK=512):
    nh,hd,L=qt.shape
    full=lambda *s: pl.BlockSpec(s,lambda i:(0,0,0))
    return pl.pallas_call(functools.partial(bwd_kernel,BQ,BK),grid=(L//BQ,),
      in_specs=[full(nh,hd,L),full(nh,L,hd),full(nh,hd,L),full(nh,L,hd),full(nh,L,hd),full(nh,hd,L),full(nh,L,hd),full(nh,1,L),full(nh,1,L)],
      out_specs=[pl.BlockSpec((nh,hd,BQ),lambda i:(0,0,i)),full(nh,L,hd),full(nh,L,hd)],
      out_shape=[jax.ShapeDtypeStruct((nh,hd,L),bf),jax.ShapeDtypeStruct((nh,L,hd),bf),jax.ShapeDtypeStruct((nh,L,hd),bf)],
      scratch_shapes=[pltpu.VMEM((nh,L,hd),f32)]*2,
      compiler_params=pltpu.CompilerParams(vmem_limit_bytes=62<<20),name=f"bwd{BQ}_{BK}")(qt,q,kt,k,v,dot_,do,lse,delta)
MESH = pl.DeviceIdType.MESH


def spots():
    s, f = lax.axis_index("seq"), lax.axis_index("fsdp")
    return s, f, s // 2, lax.rem(s, 2)


def greet(S, F):
    s, f, _, _ = spots()
    barrier = pltpu.get_barrier_semaphore()
    for i in range(1, S):
        pl.semaphore_signal(barrier, inc=1, device_id=(lax.rem(s + i, S), f), device_id_type=MESH)
    for i in range(1, F):
        pl.semaphore_signal(barrier, inc=1, device_id=(s, lax.rem(f + i, F)), device_id_type=MESH)
    pl.semaphore_wait(barrier, S + F - 2)


def remote(src, dst, sends, recvs, n, to):
    return pltpu.make_async_remote_copy(
        src_ref=src,
        dst_ref=dst,
        send_sem=sends.at[n],
        recv_sem=recvs.at[n],
        device_id=to,
        device_id_type=MESH,
    )


def gather_kernel(S, F, x, wq, sm, wm, x_all, wq_all, sm_all, wm_all, xv, qv, sv, mv, local,
                  xs, xr, qs, qr, ss, sr, ms, mr):
    s, f, p, c = spots()
    P_ = S // 2
    other = 1 - c
    loads = [
        pltpu.make_async_copy(sm, sv, local.at[0]),
        pltpu.make_async_copy(wq, qv, local.at[1]),
        pltpu.make_async_copy(x, xv, local.at[2]),
        pltpu.make_async_copy(wm, mv, local.at[3]),
    ]
    for load in loads:
        load.start()
    greet(S, F)
    mate = (p * 2 + other, f)
    todo = []

    def go(copy):
        copy.start()
        todo.append(copy)

    def chip(i):
        return lax.rem(p + i, P_) * 2 + c

    def back(i):
        return lax.rem(p + P_ - i, P_) * 2 + c

    def deep(i):
        return lax.rem(f + i, F)

    def behind(i):
        return lax.rem(f + F - i, F)

    loads[0].wait()
    keep0 = pltpu.make_async_copy(sv, sm_all.at[s, f], local.at[0])
    keep0.start()
    for i in range(1, F):
        go(remote(sv, sm_all.at[s, f], ss, sr, i, (s, deep(i))))
    loads[1].wait()
    keep1 = pltpu.make_async_copy(qv.at[s], wq_all.at[s, f], local.at[1])
    keep1.start()
    for i in range(1, S):
        to = lax.rem(s + i, S)
        go(remote(qv.at[to], wq_all.at[s, f], qs, qr, i, (to, f)))
    loads[2].wait()
    keep2 = pltpu.make_async_copy(xv, x_all.at[s], local.at[2])
    keep2.start()
    for i in range(1, P_):
        go(remote(xv, x_all.at[s], xs, xr, i, (chip(i), f)))
    go(remote(xv, x_all.at[s], xs, xr, 0, mate))
    loads[3].wait()
    keep3 = pltpu.make_async_copy(mv, wm_all.at[:, s, f], local.at[3])
    keep3.start()
    for i in range(1, F):
        go(remote(mv, wm_all.at[:, s, f], ms, mr, i, (s, deep(i))))
    for i in range(1, F):
        g = behind(i)
        remote(sv, sm_all.at[s, g], ss, sr, i, mate).wait_recv()
    keep0.wait()
    for i in range(1, S):
        go(remote(sm_all.at[s], sm_all.at[s], ss, sr, F - 1 + i, (lax.rem(s + i, S), f)))
    for i in range(1, S):
        remote(qv.at[0], wq_all.at[lax.rem(s + S - i, S), f], qs, qr, i, mate).wait_recv()
    keep1.wait()
    for i in range(1, F):
        go(remote(wq_all.at[:, f], wq_all.at[:, f], qs, qr, S - 1 + i, (s, deep(i))))
    for i in range(1, F):
        remote(mv, wm_all.at[:, s, behind(i)], ms, mr, i, mate).wait_recv()
    keep3.wait()
    for i in range(1, P_):
        go(remote(wm_all.at[:, s], wm_all.at[:, s], ms, mr, F - 1 + i, (chip(i), f)))
    go(remote(wm_all.at[:, s], wm_all.at[:, s], ms, mr, 0, mate))
    for i in range(1, P_):
        src = back(i)
        remote(xv, x_all.at[src], xs, xr, i, mate).wait_recv()
        go(remote(x_all.at[src], x_all.at[src], xs, xr, P_ - 1 + i, mate))
    for i in range(1, P_):
        src = back(i)
        remote(wm_all.at[:, s], wm_all.at[:, src], ms, mr, F - 1 + i, mate).wait_recv()
        go(remote(wm_all.at[:, src], wm_all.at[:, src], ms, mr, F + P_ - 2 + i, mate))
    for i in range(1, S):
        src = lax.rem(s + S - i, S)
        remote(sm_all.at[src], sm_all.at[src], ss, sr, F - 1 + i, mate).wait_recv()
    for i in range(1, F):
        g = behind(i)
        remote(wq_all.at[:, g], wq_all.at[:, g], qs, qr, S - 1 + i, mate).wait_recv()
    near = p * 2 + other
    remote(xv, x_all.at[near], xs, xr, 0, mate).wait_recv()
    remote(wm_all.at[:, s], wm_all.at[:, near], ms, mr, 0, mate).wait_recv()
    for i in range(1, P_):
        src = lax.rem(p + P_ - i, P_) * 2 + other
        remote(xv, x_all.at[src], xs, xr, P_ - 1 + i, mate).wait_recv()
        remote(wm_all.at[:, s], wm_all.at[:, src], ms, mr, F + P_ - 2 + i, mate).wait_recv()
    keep2.wait()
    for copy in todo:
        copy.wait_send()


def gather_all(S, F, x, wq, sm, wm):
    any_ = pl.BlockSpec(memory_space=pl.ANY)
    shapes = [
        (S,) + x.shape,
        (S, F) + wq.shape[1:],
        (S, F) + sm.shape,
        (wm.shape[0], S, F) + wm.shape[1:],
    ]
    P_ = S // 2
    dma = pltpu.SemaphoreType.DMA
    counts = [2 * P_ - 1, S + F - 1, F + S - 1, F + 2 * P_ - 2]
    sems = []
    for n in counts:
        sems += [dma((n + 1,)), dma((n + 1,))]
    return pl.pallas_call(
        functools.partial(gather_kernel, S, F),
        out_shape=[
            jax.ShapeDtypeStruct(sh, a.dtype) for sh, a in zip(shapes, (x, wq, sm, wm), strict=True)
        ],
        in_specs=[any_] * 4,
        out_specs=[any_] * 4,
        scratch_shapes=[
            pltpu.VMEM(x.shape, x.dtype),
            pltpu.VMEM(wq.shape, wq.dtype),
            pltpu.VMEM(sm.shape, sm.dtype),
            pltpu.VMEM(wm.shape, wm.dtype),
            dma((4,)),
        ]
        + sems,
        compiler_params=pltpu.CompilerParams(collective_id=1, has_side_effects=True),
        name="gather",
    )(x, wq, sm, wm)


def scatter_kernel(S, F, g, b, q, vec, g_out, b_out, q_out, vec_out,
                   gm, gi, bm, bi, gp, bp, gz, qm, qi, qt_, qo, vi, vz, vp, vo, go_, bo, local,
                   gs, gr, bs, br, qs, qr, vs, vr):
    s, f, p, c = spots()
    P_ = S // 2
    other = 1 - c
    mate = (p * 2 + other, f)
    todo = []

    def go(copy):
        copy.start()
        todo.append(copy)

    def chip(i):
        return lax.rem(p + i, P_)

    def deep(i):
        return lax.rem(f + i, F)

    def behind(i):
        return lax.rem(f + F - i, F)

    lq = pltpu.make_async_copy(q, qm, local.at[0])
    lq.start()
    lv = pltpu.make_async_copy(vec, vi, local.at[1])
    lv.start()
    order = list(range(1, P_)) + [0]
    own = []
    for n, i in enumerate(order):
        t = chip(i)
        own.append(
            (
                pltpu.make_async_copy(g.at[:, t * 2 + c], gm.at[i], local.at[2 + 2 * n]),
                pltpu.make_async_copy(b.at[t * 2 + c], bm.at[i], local.at[3 + 2 * n]),
            )
        )
        own[-1][0].start()
        own[-1][1].start()
    greet(S, F)
    lv.wait()
    for i in range(1, F):
        go(remote(vi, vz.at[i], vs, vr, i, (s, deep(i))))
    for n, i in enumerate(order):
        t = chip(i)
        go(remote(g.at[:, t * 2 + other], gi.at[i], gs, gr, i, mate))
        go(remote(b.at[t * 2 + other], bi.at[i], bs, br, i, mate))
    lq.wait()
    for i in range(1, F):
        go(remote(qm.at[:, deep(i)], qi.at[i], qs, qr, i, (s, deep(i))))

    def add_slabs(n, at_dst, at_parts, kind):
        def one(k, _):
            total = at_parts[0](k)
            for part in at_parts[1:]:
                total = total + part(k)
            at_dst(k, total.astype(kind))
            return 0

        lax.fori_loop(0, n, one, 0)

    NW, R = g.shape[0], g.shape[3]
    T = b.shape[1]
    step = 64 if T % 64 == 0 else T

    def flat_g(k):
        return lax.div(k, F), lax.rem(k, F)

    for n, i in enumerate(order):
        t = chip(i)
        own[n][0].wait()
        remote(g.at[:, s], gi.at[i], gs, gr, i, mate).wait_recv()

        def put(k, v, i=i):
            w, z = flat_g(k)
            gm[i, w, z] = v

        def left(k, i=i):
            w, z = flat_g(k)
            return gm[i, w, z].astype(f32)

        def right(k, i=i):
            w, z = flat_g(k)
            return gi[i, w, z].astype(f32)

        add_slabs(NW * F, put, [left, right], bf)
        if i:
            go(remote(gm.at[i], gp.at[i], gs, gr, P_ + i, (t * 2 + c, f)))
        own[n][1].wait()
        remote(b.at[s], bi.at[i], bs, br, i, mate).wait_recv()

        def putb(k, v, i=i):
            bm[i, pl.ds(k * step, step), :] = v

        def leftb(k, i=i):
            return bm[i, pl.ds(k * step, step), :].astype(f32)

        def rightb(k, i=i):
            return bi[i, pl.ds(k * step, step), :].astype(f32)

        add_slabs(T // step, putb, [leftb, rightb], bf)
        if i:
            go(remote(bm.at[i], bp.at[i], bs, br, P_ + i, (t * 2 + c, f)))
    total = vi[...]
    for i in range(1, F):
        remote(vi, vz.at[i], vs, vr, i, mate).wait_recv()
    for i in range(1, F):
        total = total + vz[i]
    vp[0] = total
    for i in range(1, S):
        go(remote(vp.at[0], vp.at[i], vs, vr, F - 1 + i, (lax.rem(s + i, S), f)))
    for i in range(1, F):
        remote(qm.at[:, f], qi.at[i], qs, qr, i, mate).wait_recv()

    def put_q(k, v):
        qt_[k] = v

    add_slabs(
        S,
        put_q,
        [lambda k: qm[k, f].astype(f32)]
        + [lambda k, i=i: qi[i, k].astype(f32) for i in range(1, F)],
        bf,
    )
    keep = pltpu.make_async_copy(qt_.at[s], qo.at[s], local.at[0])
    keep.start()
    for i in range(1, S):
        to = lax.rem(s + i, S)
        go(remote(qt_.at[to], qo.at[s], qs, qr, F - 1 + i, (to, f)))
    for i in range(1, P_):
        remote(gm.at[0], gp.at[i], gs, gr, P_ + i, mate).wait_recv()

    def put_g(k, v):
        w, z = flat_g(k)
        gp[0, w, z] = v

    def part_g(i):
        def read(k):
            w, z = flat_g(k)
            return (gm if i == 0 else gp)[i, w, z].astype(f32)

        return read

    add_slabs(NW * F, put_g, [part_g(i) for i in range(P_)], bf)
    for i in range(1, F):
        go(remote(gp.at[0, :, deep(i)], gz.at[i], gs, gr, 2 * P_ + i, (s, deep(i))))
    for i in range(1, P_):
        remote(bm.at[0], bp.at[i], bs, br, P_ + i, mate).wait_recv()

    def put_b(k, v):
        bo[pl.ds(k * step, step), :] = v

    def part_b(i):
        def read(k):
            return (bm if i == 0 else bp)[i, pl.ds(k * step, step), :].astype(f32)

        return read

    add_slabs(T // step, put_b, [part_b(i) for i in range(P_)], f32)
    outs = [pltpu.make_async_copy(bo, b_out, local.at[1])]
    outs[0].start()
    total = vp[0]
    for i in range(1, S):
        remote(vp.at[0], vp.at[i], vs, vr, F - 1 + i, mate).wait_recv()
    for i in range(1, S):
        total = total + vp[i]
    vo[...] = total
    outs.append(pltpu.make_async_copy(vo, vec_out, local.at[2]))
    outs[1].start()
    for i in range(1, S):
        src = lax.rem(s + S - i, S)
        remote(qt_.at[0], qo.at[src], qs, qr, F - 1 + i, mate).wait_recv()
    keep.wait()
    outs.append(pltpu.make_async_copy(qo, q_out, local.at[3]))
    outs[2].start()
    for i in range(1, F):
        remote(gp.at[0, :, f], gz.at[i], gs, gr, 2 * P_ + i, mate).wait_recv()
    for w in range(NW):
        total = gp[0, w, f].astype(f32)
        for i in range(1, F):
            total = total + gz[i, w].astype(f32)
        go_[w] = total
    outs.append(pltpu.make_async_copy(go_, g_out, local.at[4]))
    outs[3].start()
    for out in outs:
        out.wait()
    for copy in todo:
        copy.wait_send()


def scatter_all(S, F, g, b, q, vec):
    any_ = pl.BlockSpec(memory_space=pl.ANY)
    P_ = S // 2
    NW, R, D = g.shape[0], g.shape[3], g.shape[4]
    T = b.shape[1]
    C3 = q.shape[3]
    dma = pltpu.SemaphoreType.DMA
    counts = [2 * P_ + F, 2 * P_, F + S, F + S]
    sems = []
    for n in counts:
        sems += [dma((n,)), dma((n,))]
    V = pltpu.VMEM
    return pl.pallas_call(
        functools.partial(scatter_kernel, S, F),
        out_shape=[
            jax.ShapeDtypeStruct((NW, R, D), f32),
            jax.ShapeDtypeStruct((T, D), f32),
            jax.ShapeDtypeStruct((S, R, C3), bf),
            jax.ShapeDtypeStruct(vec.shape, f32),
        ],
        in_specs=[any_] * 4,
        out_specs=[any_] * 4,
        scratch_shapes=[
            V((P_, NW, F, R, D), bf),
            V((P_, NW, F, R, D), bf),
            V((P_, T, D), bf),
            V((P_, T, D), bf),
            V((P_, NW, F, R, D), bf),
            V((P_, T, D), bf),
            V((F, NW, R, D), bf),
            V((S, F, R, C3), bf),
            V((F, S, R, C3), bf),
            V((S, R, C3), bf),
            V((S, R, C3), bf),
            V(vec.shape, f32),
            V((F,) + vec.shape, f32),
            V((S,) + vec.shape, f32),
            V(vec.shape, f32),
            V((NW, R, D), f32),
            V((T, D), f32),
            dma((2 + 2 * P_ + 4,)),
        ]
        + sems,
        compiler_params=pltpu.CompilerParams(
            collective_id=2, has_side_effects=True, vmem_limit_bytes=60 << 20
        ),
        name="scatter",
    )(g, b, q, vec)


def body(
    inputs,
    w_query,
    w_key,
    w_value,
    w_proj,
    w_up,
    w_down,
    gain_first,
    gain_second,
    bias_up,
    bias_down,
    query_scale,
    cotangent,
):
    groups = lax.axis_size("seq")
    rows_of = lax.axis_size("fsdp")
    nh = H // groups
    cols = nh * HD
    both = ("seq", "fsdp")
    tokens, width = inputs.shape[1], inputs.shape[2]
    length = tokens * groups
    shard = w_query.shape[0]
    x_low = inputs.reshape(tokens, width)
    qkv_rows = jnp.stack([w_query, w_key, w_value], 1).astype(bf).reshape(shard, 3, groups, cols)
    qkv_rows = qkv_rows.transpose(2, 0, 1, 3).reshape(groups, shard, 3 * cols)
    small = jnp.stack([gain_first, gain_second, bias_up, bias_down], 0)
    small = jnp.pad(small, ((0, 4), (0, 128 - shard)))
    weights = jnp.stack([w_proj, w_up, w_down], 0).astype(bf)
    x_all, qkv_w, small, weights = gather_all(groups, rows_of, x_low, qkv_rows, small, weights)
    x_all = x_all.reshape(length, width)
    qkv_w = qkv_w.reshape(width, 3, cols).transpose(1, 0, 2)
    small = small[:, :, :4, :shard].transpose(2, 0, 1, 3).reshape(4, width).astype(bf).astype(f32)
    first_gain, second_gain, upbias, downbias = small[0], small[1], small[2], small[3]
    weights = weights.reshape(3, width, width)
    proj_w, up_w, down_w = weights[0], weights[1], weights[2]
    scale_dims = jax.nn.softplus(query_scale) * log_two_inverse / math.sqrt(HD)
    scale_cols = jnp.tile(scale_dims, nh)

    x_wide = x_all.astype(f32)
    hat = x_wide * lax.rsqrt(jnp.mean(x_wide * x_wide, axis=-1, keepdims=True) + eps_norm)
    normed = (hat * first_gain).astype(bf)
    query_full = jnp.dot(normed, qkv_w[0], preferred_element_type=f32)
    query_low = (query_full * scale_cols).astype(bf)
    key_low = jnp.dot(normed, qkv_w[1], preferred_element_type=f32).astype(bf)
    value_low = jnp.dot(normed, qkv_w[2], preferred_element_type=f32).astype(bf)

    def by_head(a):
        return a.reshape(length, nh, HD).transpose(1, 0, 2)

    def flip(a):
        return jnp.swapaxes(a, 1, 2)

    q, k, v = by_head(query_low), by_head(key_low), by_head(value_low)
    qt, kt, vt = flip(q), flip(k), flip(v)
    ot, lse = flash_fwd(qt, k, vt, min(1024, length), min(512, length))
    mixed = lax.all_to_all(ot.reshape(cols, length), "seq", split_axis=1, concat_axis=0, tiled=True)
    float_in = x_low.astype(f32)
    middle = float_in + dot(mixed, proj_w, 0, 0)
    second = rms_scale(middle, second_gain).astype(bf)
    hidden = jnp.dot(second, up_w, preferred_element_type=f32) + upbias
    active = jax.nn.silu(hidden).astype(bf)
    result = middle + jnp.dot(active, down_w, preferred_element_type=f32) + downbias

    top_low = cotangent.reshape(tokens, width)
    grad_top = top_low.astype(f32)
    grad_bdown = jnp.sum(grad_top, axis=0)
    grad_wdown = dot(active, top_low, 0, 0)
    grad_active = dot(top_low, down_w, 1, 1)
    gate = 1 / (1 + jnp.exp(-hidden))
    grad_hidden = grad_active * (gate * (1 + hidden * (1 - gate)))
    grad_bup = jnp.sum(grad_hidden, axis=0)
    hidden_low = grad_hidden.astype(bf)
    grad_wup = dot(second, hidden_low, 0, 0)
    grad_second_in = dot(hidden_low, up_w, 1, 1)
    unused_second, second_pull = jax.vjp(rms_scale, middle, second_gain)
    grad_middle, grad_gsecond = second_pull(grad_second_in)
    grad_middle = grad_middle + grad_top
    middle_low = grad_middle.astype(bf)
    grad_wproj = dot(mixed, middle_low, 1, 0)
    grad_mixed = dot(proj_w, middle_low, 1, 1).astype(bf)
    dmt = lax.all_to_all(grad_mixed, "seq", split_axis=0, concat_axis=1, tiled=True)
    dmt = dmt.reshape(nh, HD, length)
    delta = jnp.sum(dmt.astype(f32) * ot.astype(f32), axis=1, keepdims=True)
    dqt, dk, dv = flash_bwd(
        qt, q, kt, k, v, dmt, flip(dmt), lse, delta, min(512, length), min(512, length)
    )

    def flat(a):
        return a.transpose(1, 0, 2).reshape(length, cols)

    dqs = flat(flip(dqt)).astype(f32)
    dq = (dqs * scale_cols).astype(bf)
    dk, dv = flat(dk), flat(dv)
    scale_part = jnp.sum(jnp.sum(dqs * query_full, axis=0).reshape(nh, HD), axis=0)
    grad_qkv = jnp.concatenate([dot(normed, g, 0, 0) for g in (dq, dk, dv)], 1)
    back = dot(dq, qkv_w[0], 1, 1) + dot(dk, qkv_w[1], 1, 1) + dot(dv, qkv_w[2], 1, 1)
    scale_row = jnp.pad(scale_part, (0, width - HD))
    zeros = jnp.zeros_like(scale_row)
    grad_gfirst = jnp.sum(back * hat, axis=0)
    vectors = jnp.stack([grad_gfirst, grad_gsecond, grad_bup, grad_bdown, scale_row, zeros, zeros, zeros], 0)
    stacked = jnp.stack([grad_wproj.astype(bf), grad_wup.astype(bf), grad_wdown.astype(bf)], 0)
    owned, back, grad_qkv, vectors = scatter_all(
        groups,
        rows_of,
        stacked.reshape(3, groups, rows_of, shard, width),
        back.astype(bf).reshape(groups, tokens, width),
        grad_qkv.astype(bf).reshape(groups, rows_of, shard, 3 * cols),
        vectors,
    )
    grad_qkv = grad_qkv.reshape(groups, shard, 3, cols).transpose(2, 1, 0, 3)
    grad_qkv = grad_qkv.reshape(3, shard, width).astype(f32)
    unused_first, first_pull = jax.vjp(rms_scale, float_in, first_gain)
    grad_below, unused_gain = first_pull(back)
    grad_inputs = (grad_middle + grad_below).astype(bf)
    at = (lax.axis_index("seq") * rows_of + lax.axis_index("fsdp")) * shard
    mine = lax.dynamic_slice_in_dim(vectors, at, shard, 1)
    grad_scale = vectors[4, :HD] * jax.nn.sigmoid(query_scale) * log_two_inverse / math.sqrt(HD)
    return (
        result.astype(bf).reshape(inputs.shape),
        grad_inputs.reshape(inputs.shape),
        grad_qkv[0],
        grad_qkv[1],
        grad_qkv[2],
        owned[0],
        owned[1],
        owned[2],
        mine[0],
        mine[1],
        mine[2],
        mine[3],
        grad_scale,
    )


def solution(mesh):
    return jax.shard_map(
        body,
        mesh=mesh,
        in_specs=(
            P("fsdp", "seq", None),
            P(("seq", "fsdp"), None),
            P(("seq", "fsdp"), None),
            P(("seq", "fsdp"), None),
            P(("seq", "fsdp"), None),
            P(("seq", "fsdp"), None),
            P(("seq", "fsdp"), None),
            P(("seq", "fsdp")),
            P(("seq", "fsdp")),
            P(("seq", "fsdp")),
            P(("seq", "fsdp")),
            P(),
            P("fsdp", "seq", None),
        ),
        out_specs=(
            P("fsdp", "seq", None),
            P("fsdp", "seq", None),
            P(("seq", "fsdp"), None),
            P(("seq", "fsdp"), None),
            P(("seq", "fsdp"), None),
            P(("seq", "fsdp"), None),
            P(("seq", "fsdp"), None),
            P(("seq", "fsdp"), None),
            P(("seq", "fsdp")),
            P(("seq", "fsdp")),
            P(("seq", "fsdp")),
            P(("seq", "fsdp")),
            P(),
        ),
        check_vma=False,
    )
```

```python
import functools
import math

import jax
import jax.numpy as jnp
from jax import lax
from jax.experimental import pallas as pl
from jax.experimental.pallas import tpu as pltpu
from jax.sharding import PartitionSpec as P

H = 16
HD = 80
eps_norm = 1e-06
log_two_inverse = 1.442695
bf = jnp.bfloat16
f32 = jnp.float32
NEG = -1e30


def rms_scale(values, gain):
    return values * lax.rsqrt(jnp.mean(values * values, axis=-1, keepdims=True) + eps_norm) * gain


def dot(a,b,ca=1,cb=0):
    return lax.dot_general(a,b,(((ca,),(cb,)),((),())),preferred_element_type=f32)

def bwd_kernel(BQ,BK,qt,q,kt,k,v,dot_,do,lse,delta,dqt,dk,dv,dks,dvs):
    nh,hd,L=qt.shape
    i=pl.program_id(0); nb=L//BQ
    @pl.when(i==0)
    def _():
        dks[...]=jnp.zeros_like(dks); dvs[...]=jnp.zeros_like(dvs)
    qs=pl.ds(pl.multiple_of(i*BQ,BQ),BQ)
    def step(j,carry,diag=None):
        ks=pl.ds(pl.multiple_of(j*BK,BK),BK)
        s=[dot(k[h,ks,:],qt[h,:,qs]) for h in range(nh)]
        dp=[dot(v[h,ks,:],dot_[h,:,qs]) for h in range(nh)]
        out=[]
        for h in range(nh):
            p=jnp.exp(s[h]-lse[h,:,qs])
            if diag is not None:
                kp=lax.broadcasted_iota(jnp.int32,p.shape,0)+diag*BK
                qp=lax.broadcasted_iota(jnp.int32,p.shape,1)
                p=jnp.where(kp<=qp,p,0.0)
            ds=(p*(dp[h]-delta[h,:,qs])).astype(bf)
            dvs[h,ks,:]+=dot(p.astype(bf),do[h,qs,:])
            dks[h,ks,:]+=dot(ds,q[h,qs,:])
            out.append(carry[h]+dot(kt[h,:,ks],ds))
        return tuple(out)
    init=tuple(jnp.zeros((hd,BQ),f32) for _ in range(nh))
    r=BQ//BK
    c=lax.fori_loop(0,i*r,step,init)
    for d in range(r): c=step(i*r+d,c,d)
    for h in range(nh): dqt[h,:,:]=c[h].astype(bf)
    @pl.when(i==nb-1)
    def _():
        dk[...]=dks[...].astype(bf); dv[...]=dvs[...].astype(bf)
def flash_bwd(qt,q,kt,k,v,dot_,do,lse,delta,BQ=512,BK=512):
    nh,hd,L=qt.shape
    full=lambda *s: pl.BlockSpec(s,lambda i:(0,0,0))
    return pl.pallas_call(functools.partial(bwd_kernel,BQ,BK),grid=(L//BQ,),
      in_specs=[full(nh,hd,L),full(nh,L,hd),full(nh,hd,L),full(nh,L,hd),full(nh,L,hd),full(nh,hd,L),full(nh,L,hd),full(nh,1,L),full(nh,1,L)],
      out_specs=[pl.BlockSpec((nh,hd,BQ),lambda i:(0,0,i)),full(nh,L,hd),full(nh,L,hd)],
      out_shape=[jax.ShapeDtypeStruct((nh,hd,L),bf),jax.ShapeDtypeStruct((nh,L,hd),bf),jax.ShapeDtypeStruct((nh,L,hd),bf)],
      scratch_shapes=[pltpu.VMEM((nh,L,hd),f32)]*2,
      compiler_params=pltpu.CompilerParams(vmem_limit_bytes=62<<20),name=f"bwd{BQ}_{BK}")(qt,q,kt,k,v,dot_,do,lse,delta)
MESH = pl.DeviceIdType.MESH


def spots():
    s, f = lax.axis_index("seq"), lax.axis_index("fsdp")
    return s, f, s // 2, lax.rem(s, 2)


def greet(S, F):
    s, f, _, _ = spots()
    barrier = pltpu.get_barrier_semaphore()
    for i in range(1, S):
        pl.semaphore_signal(barrier, inc=1, device_id=(lax.rem(s + i, S), f), device_id_type=MESH)
    for i in range(1, F):
        pl.semaphore_signal(barrier, inc=1, device_id=(s, lax.rem(f + i, F)), device_id_type=MESH)
    pl.semaphore_wait(barrier, S + F - 2)


def remote(src, dst, sends, recvs, n, to):
    return pltpu.make_async_remote_copy(
        src_ref=src,
        dst_ref=dst,
        send_sem=sends.at[n],
        recv_sem=recvs.at[n],
        device_id=to,
        device_id_type=MESH,
    )


def gather_kernel(S, F, x, wq, sm, wm, x_all, wq_all, sm_all, wm_all, xv, qv, sv, mv, local,
                  xs, xr, qs, qr, ss, sr, ms, mr):
    s, f, p, c = spots()
    P_ = S // 2
    other = 1 - c
    loads = [
        pltpu.make_async_copy(sm, sv, local.at[0]),
        pltpu.make_async_copy(wq, qv, local.at[1]),
        pltpu.make_async_copy(x, xv, local.at[2]),
        pltpu.make_async_copy(wm, mv, local.at[3]),
    ]
    for load in loads:
        load.start()
    greet(S, F)
    mate = (p * 2 + other, f)
    todo = []

    def go(copy):
        copy.start()
        todo.append(copy)

    def chip(i):
        return lax.rem(p + i, P_) * 2 + c

    def back(i):
        return lax.rem(p + P_ - i, P_) * 2 + c

    def deep(i):
        return lax.rem(f + i, F)

    def behind(i):
        return lax.rem(f + F - i, F)

    loads[0].wait()
    keep0 = pltpu.make_async_copy(sv, sm_all.at[s, f], local.at[0])
    keep0.start()
    for i in range(1, F):
        go(remote(sv, sm_all.at[s, f], ss, sr, i, (s, deep(i))))
    loads[1].wait()
    keep1 = pltpu.make_async_copy(qv.at[s], wq_all.at[s, f], local.at[1])
    keep1.start()
    for i in range(1, S):
        to = lax.rem(s + i, S)
        go(remote(qv.at[to], wq_all.at[s, f], qs, qr, i, (to, f)))
    loads[2].wait()
    keep2 = pltpu.make_async_copy(xv, x_all.at[s], local.at[2])
    keep2.start()
    for i in range(1, P_):
        go(remote(xv, x_all.at[s], xs, xr, i, (chip(i), f)))
    go(remote(xv, x_all.at[s], xs, xr, 0, mate))
    loads[3].wait()
    keep3 = pltpu.make_async_copy(mv, wm_all.at[:, f], local.at[3])
    keep3.start()
    for i in range(1, F):
        go(remote(mv, wm_all.at[:, f], ms, mr, i, (s, deep(i))))
    for i in range(1, F):
        g = behind(i)
        remote(sv, sm_all.at[s, g], ss, sr, i, mate).wait_recv()
    keep0.wait()
    for i in range(1, S):
        go(remote(sm_all.at[s], sm_all.at[s], ss, sr, F - 1 + i, (lax.rem(s + i, S), f)))
    for i in range(1, S):
        remote(qv.at[0], wq_all.at[lax.rem(s + S - i, S), f], qs, qr, i, mate).wait_recv()
    keep1.wait()
    for i in range(1, F):
        go(remote(wq_all.at[:, f], wq_all.at[:, f], qs, qr, S - 1 + i, (s, deep(i))))
    for i in range(1, F):
        remote(mv, wm_all.at[:, behind(i)], ms, mr, i, mate).wait_recv()
    keep3.wait()
    for i in range(1, P_):
        src = back(i)
        remote(xv, x_all.at[src], xs, xr, i, mate).wait_recv()
        go(remote(x_all.at[src], x_all.at[src], xs, xr, P_ - 1 + i, mate))
    for i in range(1, S):
        src = lax.rem(s + S - i, S)
        remote(sm_all.at[src], sm_all.at[src], ss, sr, F - 1 + i, mate).wait_recv()
    for i in range(1, F):
        g = behind(i)
        remote(wq_all.at[:, g], wq_all.at[:, g], qs, qr, S - 1 + i, mate).wait_recv()
    near = p * 2 + other
    remote(xv, x_all.at[near], xs, xr, 0, mate).wait_recv()
    for i in range(1, P_):
        src = lax.rem(p + P_ - i, P_) * 2 + other
        remote(xv, x_all.at[src], xs, xr, P_ - 1 + i, mate).wait_recv()
    keep2.wait()
    for copy in todo:
        copy.wait_send()


def gather_all(S, F, x, wq, sm, wm):
    any_ = pl.BlockSpec(memory_space=pl.ANY)
    shapes = [
        (S,) + x.shape,
        (S, F) + wq.shape[1:],
        (S, F) + sm.shape,
        (wm.shape[0], F) + wm.shape[1:],
    ]
    P_ = S // 2
    dma = pltpu.SemaphoreType.DMA
    counts = [2 * P_ - 1, S + F - 1, F + S - 1, F]
    sems = []
    for n in counts:
        sems += [dma((n + 1,)), dma((n + 1,))]
    return pl.pallas_call(
        functools.partial(gather_kernel, S, F),
        out_shape=[
            jax.ShapeDtypeStruct(sh, a.dtype) for sh, a in zip(shapes, (x, wq, sm, wm), strict=True)
        ],
        in_specs=[any_] * 4,
        out_specs=[any_] * 4,
        scratch_shapes=[
            pltpu.VMEM(x.shape, x.dtype),
            pltpu.VMEM(wq.shape, wq.dtype),
            pltpu.VMEM(sm.shape, sm.dtype),
            pltpu.VMEM(wm.shape, wm.dtype),
            dma((4,)),
        ]
        + sems,
        compiler_params=pltpu.CompilerParams(collective_id=1, has_side_effects=True),
        name="gather",
    )(x, wq, sm, wm)


def scatter_kernel(S, F, g, b, q, vec, g_out, b_out, q_out, vec_out,
                   gm, gi, bm, bi, gp, bp, gz, qm, qi, qt_, qo, vi, vz, vp, vo, go_, bo, local,
                   gs, gr, bs, br, qs, qr, vs, vr):
    s, f, p, c = spots()
    P_ = S // 2
    other = 1 - c
    mate = (p * 2 + other, f)
    todo = []

    def go(copy):
        copy.start()
        todo.append(copy)

    def chip(i):
        return lax.rem(p + i, P_)

    def deep(i):
        return lax.rem(f + i, F)

    def behind(i):
        return lax.rem(f + F - i, F)

    lq = pltpu.make_async_copy(q, qm, local.at[0])
    lq.start()
    lv = pltpu.make_async_copy(vec, vi, local.at[1])
    lv.start()
    order = list(range(1, P_)) + [0]
    own = []
    for n, i in enumerate(order):
        t = chip(i)
        own.append(
            (
                pltpu.make_async_copy(g.at[:, t * 2 + c], gm.at[i], local.at[2 + 2 * n]),
                pltpu.make_async_copy(b.at[t * 2 + c], bm.at[i], local.at[3 + 2 * n]),
            )
        )
        own[-1][0].start()
        own[-1][1].start()
    greet(S, F)
    lv.wait()
    for i in range(1, F):
        go(remote(vi, vz.at[i], vs, vr, i, (s, deep(i))))
    for n, i in enumerate(order):
        t = chip(i)
        go(remote(g.at[:, t * 2 + other], gi.at[i], gs, gr, i, mate))
        go(remote(b.at[t * 2 + other], bi.at[i], bs, br, i, mate))
    lq.wait()
    for i in range(1, F):
        go(remote(qm.at[:, deep(i)], qi.at[i], qs, qr, i, (s, deep(i))))

    def add_slabs(n, at_dst, at_parts, kind):
        def one(k, _):
            total = at_parts[0](k)
            for part in at_parts[1:]:
                total = total + part(k)
            at_dst(k, total.astype(kind))
            return 0

        lax.fori_loop(0, n, one, 0)

    NW, R = g.shape[0], g.shape[3]
    T = b.shape[1]
    step = 64 if T % 64 == 0 else T

    def flat_g(k):
        return lax.div(k, F), lax.rem(k, F)

    for n, i in enumerate(order):
        t = chip(i)
        own[n][0].wait()
        remote(g.at[:, s], gi.at[i], gs, gr, i, mate).wait_recv()

        def put(k, v, i=i):
            w, z = flat_g(k)
            gm[i, w, z] = v

        def left(k, i=i):
            w, z = flat_g(k)
            return gm[i, w, z].astype(f32)

        def right(k, i=i):
            w, z = flat_g(k)
            return gi[i, w, z].astype(f32)

        add_slabs(NW * F, put, [left, right], bf)
        if i:
            go(remote(gm.at[i], gp.at[i], gs, gr, P_ + i, (t * 2 + c, f)))
        own[n][1].wait()
        remote(b.at[s], bi.at[i], bs, br, i, mate).wait_recv()

        def putb(k, v, i=i):
            bm[i, pl.ds(k * step, step), :] = v

        def leftb(k, i=i):
            return bm[i, pl.ds(k * step, step), :].astype(f32)

        def rightb(k, i=i):
            return bi[i, pl.ds(k * step, step), :].astype(f32)

        add_slabs(T // step, putb, [leftb, rightb], bf)
        if i:
            go(remote(bm.at[i], bp.at[i], bs, br, P_ + i, (t * 2 + c, f)))
    total = vi[...]
    for i in range(1, F):
        remote(vi, vz.at[i], vs, vr, i, mate).wait_recv()
    for i in range(1, F):
        total = total + vz[i]
    vp[0] = total
    for i in range(1, S):
        go(remote(vp.at[0], vp.at[i], vs, vr, F - 1 + i, (lax.rem(s + i, S), f)))
    for i in range(1, F):
        remote(qm.at[:, f], qi.at[i], qs, qr, i, mate).wait_recv()

    def put_q(k, v):
        qt_[k] = v

    add_slabs(
        S,
        put_q,
        [lambda k: qm[k, f].astype(f32)]
        + [lambda k, i=i: qi[i, k].astype(f32) for i in range(1, F)],
        bf,
    )
    keep = pltpu.make_async_copy(qt_.at[s], qo.at[s], local.at[0])
    keep.start()
    for i in range(1, S):
        to = lax.rem(s + i, S)
        go(remote(qt_.at[to], qo.at[s], qs, qr, F - 1 + i, (to, f)))
    for i in range(1, P_):
        remote(gm.at[0], gp.at[i], gs, gr, P_ + i, mate).wait_recv()

    def put_g(k, v):
        w, z = flat_g(k)
        gp[0, w, z] = v

    def part_g(i):
        def read(k):
            w, z = flat_g(k)
            return (gm if i == 0 else gp)[i, w, z].astype(f32)

        return read

    add_slabs(NW * F, put_g, [part_g(i) for i in range(P_)], bf)
    for i in range(1, F):
        go(remote(gp.at[0, :, deep(i)], gz.at[i], gs, gr, 2 * P_ + i, (s, deep(i))))
    for i in range(1, P_):
        remote(bm.at[0], bp.at[i], bs, br, P_ + i, mate).wait_recv()

    def put_b(k, v):
        bo[pl.ds(k * step, step), :] = v

    def part_b(i):
        def read(k):
            return (bm if i == 0 else bp)[i, pl.ds(k * step, step), :].astype(f32)

        return read

    add_slabs(T // step, put_b, [part_b(i) for i in range(P_)], f32)
    outs = [pltpu.make_async_copy(bo, b_out, local.at[1])]
    outs[0].start()
    total = vp[0]
    for i in range(1, S):
        remote(vp.at[0], vp.at[i], vs, vr, F - 1 + i, mate).wait_recv()
    for i in range(1, S):
        total = total + vp[i]
    vo[...] = total
    outs.append(pltpu.make_async_copy(vo, vec_out, local.at[2]))
    outs[1].start()
    for i in range(1, S):
        src = lax.rem(s + S - i, S)
        remote(qt_.at[0], qo.at[src], qs, qr, F - 1 + i, mate).wait_recv()
    keep.wait()
    outs.append(pltpu.make_async_copy(qo, q_out, local.at[3]))
    outs[2].start()
    for i in range(1, F):
        remote(gp.at[0, :, f], gz.at[i], gs, gr, 2 * P_ + i, mate).wait_recv()
    for w in range(NW):
        total = gp[0, w, f].astype(f32)
        for i in range(1, F):
            total = total + gz[i, w].astype(f32)
        go_[w] = total
    outs.append(pltpu.make_async_copy(go_, g_out, local.at[4]))
    outs[3].start()
    for out in outs:
        out.wait()
    for copy in todo:
        copy.wait_send()


def scatter_all(S, F, g, b, q, vec):
    any_ = pl.BlockSpec(memory_space=pl.ANY)
    P_ = S // 2
    NW, R, D = g.shape[0], g.shape[3], g.shape[4]
    T = b.shape[1]
    C3 = q.shape[3]
    dma = pltpu.SemaphoreType.DMA
    counts = [2 * P_ + F, 2 * P_, F + S, F + S]
    sems = []
    for n in counts:
        sems += [dma((n,)), dma((n,))]
    V = pltpu.VMEM
    return pl.pallas_call(
        functools.partial(scatter_kernel, S, F),
        out_shape=[
            jax.ShapeDtypeStruct((NW, R, D), f32),
            jax.ShapeDtypeStruct((T, D), f32),
            jax.ShapeDtypeStruct((S, R, C3), bf),
            jax.ShapeDtypeStruct(vec.shape, f32),
        ],
        in_specs=[any_] * 4,
        out_specs=[any_] * 4,
        scratch_shapes=[
            V((P_, NW, F, R, D), bf),
            V((P_, NW, F, R, D), bf),
            V((P_, T, D), bf),
            V((P_, T, D), bf),
            V((P_, NW, F, R, D), bf),
            V((P_, T, D), bf),
            V((F, NW, R, D), bf),
            V((S, F, R, C3), bf),
            V((F, S, R, C3), bf),
            V((S, R, C3), bf),
            V((S, R, C3), bf),
            V(vec.shape, f32),
            V((F,) + vec.shape, f32),
            V((S,) + vec.shape, f32),
            V(vec.shape, f32),
            V((NW, R, D), f32),
            V((T, D), f32),
            dma((2 + 2 * P_ + 4,)),
        ]
        + sems,
        compiler_params=pltpu.CompilerParams(
            collective_id=2, has_side_effects=True, vmem_limit_bytes=60 << 20
        ),
        name="scatter",
    )(g, b, q, vec)


def flip_bits(p, i):
    out, bit = p, 1
    while bit <= i:
        if i & bit:
            out = out + bit - 2 * bit * lax.rem(lax.div(p, bit), 2)
        bit *= 2
    return out


def forward_kernel(S, F, nh, x_all, w, g1, sc, wz, n1, qt, kt, vt, ot, lse, mixed, wm,
                   wt, kk, xb, nb, wv, inx, outn, local, osend, orecv, wsend, wrecv):
    s, f, p, c = spots()
    P_ = S // 2
    T, D = x_all.shape[1], x_all.shape[2]
    C = nh * HD
    L = S * T
    BQ = 2 * T
    BK = min(512, BQ)
    other = 1 - c
    mate = (p * 2 + other, f)
    load = pltpu.make_async_copy(wz, wv, local.at[0])
    load.start()

    def fetch(b):
        return pltpu.make_async_copy(x_all.at[b], xb.at[lax.rem(b, 2)], inx.at[lax.rem(b, 2)])

    def store(b):
        return pltpu.make_async_copy(nb.at[lax.rem(b, 2)], n1.at[b], outn.at[lax.rem(b, 2)])

    fetch(0).start()
    greet(S, F)
    load.wait()
    keep = pltpu.make_async_copy(wv, wm.at[:, s], local.at[0])
    keep.start()

    def spread(i):
        return remote(wv, wm.at[:, s], wsend, wrecv, i, (flip_bits(p, i) * 2 + c, f))

    def forward(i):
        src = flip_bits(p, i) * 2 + c
        return remote(wm.at[:, src], wm.at[:, src], wsend, wrecv, P_ + i, mate)

    for i in range(1, P_):
        spread(P_ - i).start()
    near = remote(wv, wm.at[:, s], wsend, wrecv, 0, mate)
    near.start()
    wt[...] = jnp.transpose(w[...])

    rows = 64

    def project(b, _):
        slot = lax.rem(b, 2)
        fetch(b).wait()

        @pl.when(b + 1 < S)
        def _():
            fetch(b + 1).start()

        @pl.when(b >= 2)
        def _():
            store(b - 2).wait()

        def norm(k, _):
            at = pl.ds(pl.multiple_of(k * rows, rows), rows)
            v = xb[slot, at, :].astype(f32)
            r = lax.rsqrt(jnp.mean(v * v, axis=-1, keepdims=True) + eps_norm)
            nb[slot, at, :] = (v * r * g1[...]).astype(bf)
            return 0

        lax.fori_loop(0, T // rows, norm, 0)
        store(b).start()
        cols = pl.ds(pl.multiple_of(b * T, T), T)
        res = dot(wt[...], nb[slot], 1, 1)
        qt[:, cols] = (res[:C] * sc[...]).astype(bf)
        kt[:, cols] = res[C : 2 * C].astype(bf)
        vt[:, cols] = res[2 * C :].astype(bf)
        for h in range(nh):
            kk[h, cols, :] = jnp.transpose(res[C + h * HD : C + (h + 1) * HD]).astype(bf)
        return 0

    lax.fori_loop(0, S, project, 0)
    store(S - 2).wait()
    store(S - 1).wait()

    def attend(t):
        first = pl.multiple_of(t * BQ, BQ)
        q = [qt[h * HD : (h + 1) * HD, pl.ds(first, BQ)] for h in range(nh)]

        def step(j, carry, diag=None):
            at = pl.ds(pl.multiple_of(j * BK, BK), BK)
            scores = [dot(kk[h, at, :], q[h]) for h in range(nh)]
            out = []
            for h in range(nh):
                m, l, acc = carry[h]
                sh = scores[h]
                if diag is not None:
                    kp = lax.broadcasted_iota(jnp.int32, sh.shape, 0) + diag * BK
                    qp = lax.broadcasted_iota(jnp.int32, sh.shape, 1)
                    sh = jnp.where(kp <= qp, sh, NEG)
                mn = jnp.maximum(m, jnp.max(sh, axis=0, keepdims=True))
                a = jnp.exp(m - mn)
                e = jnp.exp(sh - mn)
                l = l * a + jnp.sum(e, axis=0, keepdims=True)
                acc = acc * a + dot(vt[h * HD : (h + 1) * HD, at], e.astype(bf))
                out.append((mn, l, acc))
            return tuple(out)

        carry = tuple(
            (jnp.full((1, BQ), NEG, f32), jnp.zeros((1, BQ), f32), jnp.zeros((HD, BQ), f32))
            for _ in range(nh)
        )
        r = BQ // BK
        carry = lax.fori_loop(0, t * r, step, carry)
        for d in range(r):
            carry = step(t * r + d, carry, d)
        for h in range(nh):
            m, l, acc = carry[h]
            ot[h * HD : (h + 1) * HD, pl.ds(first, BQ)] = (acc / l).astype(bf)
            lse[h : h + 1, pl.ds(first, BQ)] = m + jnp.log(l)

    def to_owner(src, n, to):
        return pltpu.make_async_remote_copy(
            src_ref=src,
            dst_ref=mixed.at[s],
            send_sem=osend.at[n],
            recv_sem=orecv.at[n - n % 2 + c],
            device_id=to,
            device_id_type=MESH,
        )

    def send(i, half):
        t = flip_bits(p, i)
        src = ot.at[:, pl.ds(pl.multiple_of(t * BQ + half * T, T), T)]
        return to_owner(src, 2 * i + half, (t * 2 + half, f))

    for i in range(1, P_):
        attend(flip_bits(p, P_ - i))
        send(P_ - i, 0).start()
        send(P_ - i, 1).start()
        spread(P_ - i).wait_recv()
        forward(P_ - i).start()
    attend(p)
    mine = ot.at[:, pl.ds(pl.multiple_of(s * T, T), T)]
    theirs = ot.at[:, pl.ds(pl.multiple_of((p * 2 + other) * T, T), T)]
    last = to_owner(theirs, 0, mate)
    last.start()
    own = pltpu.make_async_copy(mine, mixed.at[s], local.at[1])
    own.start()
    def from_source(i, core):
        return pltpu.make_async_remote_copy(
            src_ref=mine,
            dst_ref=mixed.at[flip_bits(p, i) * 2 + core],
            send_sem=osend.at[0],
            recv_sem=orecv.at[2 * i + core],
            device_id=mate,
            device_id_type=MESH,
        )

    for i in range(1, P_):
        for core in range(2):
            from_source(i, core).wait_recv()
    from_source(0, other).wait_recv()
    last.wait_send()
    own.wait()
    keep.wait()
    near.wait()
    for i in range(1, P_):
        forward(i).wait()
        spread(i).wait_send()
        send(i, 0).wait_send()
        send(i, 1).wait_send()


def forward_all(S, F, nh, x_all, w, g1, sc, wz):
    T, D = x_all.shape[1], x_all.shape[2]
    C = nh * HD
    L = S * T
    P_ = S // 2
    any_ = pl.BlockSpec(memory_space=pl.ANY)
    vm = pl.BlockSpec(memory_space=pltpu.VMEM)
    dma = pltpu.SemaphoreType.DMA
    shape = jax.ShapeDtypeStruct
    NW, R = wz.shape[0], wz.shape[2]
    V = pltpu.VMEM
    return pl.pallas_call(
        functools.partial(forward_kernel, S, F, nh),
        out_shape=[
            shape((S, T, D), bf),
            shape((C, L), bf),
            shape((C, L), bf),
            shape((C, L), bf),
            shape((C, L), bf),
            shape((nh, L), f32),
            shape((S, C, T), bf),
            shape((NW, S, F, R, D), bf),
        ],
        in_specs=[any_, vm, vm, vm, any_],
        out_specs=[any_, vm, vm, vm, vm, vm, any_, any_],
        scratch_shapes=[
            V((3 * C, D), bf),
            V((nh, L, HD), bf),
            V((2, T, D), bf),
            V((2, T, D), bf),
            V((NW, F, R, D), bf),
            dma((2,)),
            dma((2,)),
            dma((2,)),
            dma((2 * P_,)),
            dma((2 * P_,)),
            dma((2 * P_,)),
            dma((2 * P_,)),
        ],
        compiler_params=pltpu.CompilerParams(
            collective_id=3, has_side_effects=True, vmem_limit_bytes=60 << 20
        ),
        name="forward",
    )(x_all, w, g1, sc, wz)


def body(
    inputs,
    w_query,
    w_key,
    w_value,
    w_proj,
    w_up,
    w_down,
    gain_first,
    gain_second,
    bias_up,
    bias_down,
    query_scale,
    cotangent,
):
    groups = lax.axis_size("seq")
    rows_of = lax.axis_size("fsdp")
    nh = H // groups
    cols = nh * HD
    both = ("seq", "fsdp")
    tokens, width = inputs.shape[1], inputs.shape[2]
    length = tokens * groups
    shard = w_query.shape[0]
    x_low = inputs.reshape(tokens, width)
    qkv_rows = jnp.stack([w_query, w_key, w_value], 1).astype(bf).reshape(shard, 3, groups, cols)
    qkv_rows = qkv_rows.transpose(2, 0, 1, 3).reshape(groups, shard, 3 * cols)
    small = jnp.stack([gain_first, gain_second, bias_up, bias_down], 0)
    small = jnp.pad(small.astype(bf), ((0, 12), (0, 128 - shard)))
    weights = jnp.stack([w_proj, w_up, w_down], 0).astype(bf)
    x_all, qkv_w, small, weights = gather_all(groups, rows_of, x_low, qkv_rows, small, weights)
    qkv_w = qkv_w.reshape(width, 3 * cols)
    small = small[:, :, :4, :shard].transpose(2, 0, 1, 3).reshape(4, width).astype(f32)
    first_gain, second_gain, upbias, downbias = small[0], small[1], small[2], small[3]
    scale_dims = jax.nn.softplus(query_scale) * log_two_inverse / math.sqrt(HD)
    scale_cols = jnp.tile(scale_dims, nh)
    normed, qt, kt, vt, ot, lse, mixed, weights = forward_all(
        groups, rows_of, nh, x_all, qkv_w, small[:1], scale_cols[:, None], weights
    )
    weights = weights.reshape(3, width, width)
    proj_w, up_w, down_w = weights[0], weights[1], weights[2]
    mixed = mixed.reshape(width, tokens)
    normed = normed.reshape(length, width)
    qkv_w = qkv_w.reshape(width, 3, cols).transpose(1, 0, 2)
    x_all = x_all.reshape(length, width)

    def by_head(a):
        return a.reshape(nh, HD, length)

    def flip(a):
        return jnp.swapaxes(a, 1, 2)

    qt, kt, vt, ot = by_head(qt), by_head(kt), by_head(vt), by_head(ot)
    q, k, v = flip(qt), flip(kt), flip(vt)
    lse = lse.reshape(nh, 1, length)
    query_full = qt.reshape(cols, length).T.astype(f32) / scale_cols
    float_in = x_low.astype(f32)
    middle = float_in + dot(mixed, proj_w, 0, 0)
    second = rms_scale(middle, second_gain).astype(bf)
    hidden = jnp.dot(second, up_w, preferred_element_type=f32) + upbias
    active = jax.nn.silu(hidden).astype(bf)
    result = middle + jnp.dot(active, down_w, preferred_element_type=f32) + downbias

    top_low = cotangent.reshape(tokens, width)
    grad_top = top_low.astype(f32)
    grad_bdown = jnp.sum(grad_top, axis=0)
    grad_wdown = dot(active, top_low, 0, 0)
    grad_active = dot(top_low, down_w, 1, 1)
    gate = 1 / (1 + jnp.exp(-hidden))
    grad_hidden = grad_active * (gate * (1 + hidden * (1 - gate)))
    grad_bup = jnp.sum(grad_hidden, axis=0)
    hidden_low = grad_hidden.astype(bf)
    grad_wup = dot(second, hidden_low, 0, 0)
    grad_second_in = dot(hidden_low, up_w, 1, 1)
    unused_second, second_pull = jax.vjp(rms_scale, middle, second_gain)
    grad_middle, grad_gsecond = second_pull(grad_second_in)
    grad_middle = grad_middle + grad_top
    middle_low = grad_middle.astype(bf)
    grad_wproj = dot(mixed, middle_low, 1, 0)
    grad_mixed = dot(proj_w, middle_low, 1, 1).astype(bf)
    dmt = lax.all_to_all(grad_mixed, "seq", split_axis=0, concat_axis=1, tiled=True)
    dmt = dmt.reshape(nh, HD, length)
    delta = jnp.sum(dmt.astype(f32) * ot.astype(f32), axis=1, keepdims=True)
    dqt, dk, dv = flash_bwd(
        qt, q, kt, k, v, dmt, flip(dmt), lse, delta, min(512, length), min(512, length)
    )

    def flat(a):
        return a.transpose(1, 0, 2).reshape(length, cols)

    dqs = flat(flip(dqt)).astype(f32)
    dq = (dqs * scale_cols).astype(bf)
    dk, dv = flat(dk), flat(dv)
    scale_part = jnp.sum(jnp.sum(dqs * query_full, axis=0).reshape(nh, HD), axis=0)
    grad_qkv = jnp.concatenate([dot(normed, g, 0, 0) for g in (dq, dk, dv)], 1)
    back = dot(dq, qkv_w[0], 1, 1) + dot(dk, qkv_w[1], 1, 1) + dot(dv, qkv_w[2], 1, 1)
    scale_row = jnp.pad(scale_part, (0, width - HD))
    zeros = jnp.zeros_like(scale_row)
    wide = x_all.astype(f32)
    hat = wide * lax.rsqrt(jnp.mean(wide * wide, axis=-1, keepdims=True) + eps_norm)
    grad_gfirst = jnp.sum(back * hat, axis=0)
    vectors = jnp.stack([grad_gfirst, grad_gsecond, grad_bup, grad_bdown, scale_row, zeros, zeros, zeros], 0)
    stacked = jnp.stack([grad_wproj.astype(bf), grad_wup.astype(bf), grad_wdown.astype(bf)], 0)
    owned, back, grad_qkv, vectors = scatter_all(
        groups,
        rows_of,
        stacked.reshape(3, groups, rows_of, shard, width),
        back.astype(bf).reshape(groups, tokens, width),
        grad_qkv.astype(bf).reshape(groups, rows_of, shard, 3 * cols),
        vectors,
    )
    grad_qkv = grad_qkv.reshape(groups, shard, 3, cols).transpose(2, 1, 0, 3)
    grad_qkv = grad_qkv.reshape(3, shard, width).astype(f32)
    unused_first, first_pull = jax.vjp(rms_scale, float_in, first_gain)
    grad_below, unused_gain = first_pull(back)
    grad_inputs = (grad_middle + grad_below).astype(bf)
    at = (lax.axis_index("seq") * rows_of + lax.axis_index("fsdp")) * shard
    mine = lax.dynamic_slice_in_dim(vectors, at, shard, 1)
    grad_scale = vectors[4, :HD] * jax.nn.sigmoid(query_scale) * log_two_inverse / math.sqrt(HD)
    return (
        result.astype(bf).reshape(inputs.shape),
        grad_inputs.reshape(inputs.shape),
        grad_qkv[0],
        grad_qkv[1],
        grad_qkv[2],
        owned[0],
        owned[1],
        owned[2],
        mine[0],
        mine[1],
        mine[2],
        mine[3],
        grad_scale,
    )


def solution(mesh):
    return jax.shard_map(
        body,
        mesh=mesh,
        in_specs=(
            P("fsdp", "seq", None),
            P(("seq", "fsdp"), None),
            P(("seq", "fsdp"), None),
            P(("seq", "fsdp"), None),
            P(("seq", "fsdp"), None),
            P(("seq", "fsdp"), None),
            P(("seq", "fsdp"), None),
            P(("seq", "fsdp")),
            P(("seq", "fsdp")),
            P(("seq", "fsdp")),
            P(("seq", "fsdp")),
            P(),
            P("fsdp", "seq", None),
        ),
        out_specs=(
            P("fsdp", "seq", None),
            P("fsdp", "seq", None),
            P(("seq", "fsdp"), None),
            P(("seq", "fsdp"), None),
            P(("seq", "fsdp"), None),
            P(("seq", "fsdp"), None),
            P(("seq", "fsdp"), None),
            P(("seq", "fsdp"), None),
            P(("seq", "fsdp")),
            P(("seq", "fsdp")),
            P(("seq", "fsdp")),
            P(("seq", "fsdp")),
            P(),
        ),
        check_vma=False,
    )
```

```python
import functools
import math

import jax
import jax.numpy as jnp
from jax import lax
from jax.experimental import pallas as pl
from jax.experimental.pallas import tpu as pltpu
from jax.sharding import PartitionSpec as P

H = 16
HD = 80
eps_norm = 1e-06
log_two_inverse = 1.442695
bf = jnp.bfloat16
f32 = jnp.float32
NEG = -1e30


def rms_scale(values, gain):
    return values * lax.rsqrt(jnp.mean(values * values, axis=-1, keepdims=True) + eps_norm) * gain


def dot(a,b,ca=1,cb=0):
    return lax.dot_general(a,b,(((ca,),(cb,)),((),())),preferred_element_type=f32)


MESH = pl.DeviceIdType.MESH


def spots():
    s, f = lax.axis_index("seq"), lax.axis_index("fsdp")
    return s, f, s // 2, lax.rem(s, 2)


def greet(S, F):
    s, f, _, _ = spots()
    barrier = pltpu.get_barrier_semaphore()
    for i in range(1, S):
        pl.semaphore_signal(barrier, inc=1, device_id=(lax.rem(s + i, S), f), device_id_type=MESH)
    for i in range(1, F):
        pl.semaphore_signal(barrier, inc=1, device_id=(s, lax.rem(f + i, F)), device_id_type=MESH)
    pl.semaphore_wait(barrier, S + F - 2)


def remote(src, dst, sends, recvs, n, to):
    return pltpu.make_async_remote_copy(
        src_ref=src,
        dst_ref=dst,
        send_sem=sends.at[n],
        recv_sem=recvs.at[n],
        device_id=to,
        device_id_type=MESH,
    )


def gather_kernel(S, F, x, wq, sm, wm, x_all, wq_all, sm_all, wm_all, xv, qv, sv, mv, local,
                  xs, xr, qs, qr, ss, sr, ms, mr):
    s, f, p, c = spots()
    P_ = S // 2
    other = 1 - c
    loads = [
        pltpu.make_async_copy(sm, sv, local.at[0]),
        pltpu.make_async_copy(wq, qv, local.at[1]),
        pltpu.make_async_copy(x, xv, local.at[2]),
        pltpu.make_async_copy(wm, mv, local.at[3]),
    ]
    for load in loads:
        load.start()
    greet(S, F)
    mate = (p * 2 + other, f)
    todo = []

    def go(copy):
        copy.start()
        todo.append(copy)

    def chip(i):
        return lax.rem(p + i, P_) * 2 + c

    def back(i):
        return lax.rem(p + P_ - i, P_) * 2 + c

    def deep(i):
        return lax.rem(f + i, F)

    def behind(i):
        return lax.rem(f + F - i, F)

    loads[0].wait()
    keep0 = pltpu.make_async_copy(sv, sm_all.at[s, f], local.at[0])
    keep0.start()
    for i in range(1, F):
        go(remote(sv, sm_all.at[s, f], ss, sr, i, (s, deep(i))))
    loads[1].wait()
    keep1 = pltpu.make_async_copy(qv.at[s], wq_all.at[s, f], local.at[1])
    keep1.start()
    for i in range(1, S):
        to = lax.rem(s + i, S)
        go(remote(qv.at[to], wq_all.at[s, f], qs, qr, i, (to, f)))
    loads[2].wait()
    keep2 = pltpu.make_async_copy(xv, x_all.at[s], local.at[2])
    keep2.start()
    for i in range(1, P_):
        go(remote(xv, x_all.at[s], xs, xr, i, (chip(i), f)))
    go(remote(xv, x_all.at[s], xs, xr, 0, mate))
    loads[3].wait()
    keep3 = pltpu.make_async_copy(mv, wm_all.at[:, f], local.at[3])
    keep3.start()
    for i in range(1, F):
        go(remote(mv, wm_all.at[:, f], ms, mr, i, (s, deep(i))))
    for i in range(1, F):
        g = behind(i)
        remote(sv, sm_all.at[s, g], ss, sr, i, mate).wait_recv()
    keep0.wait()
    for i in range(1, S):
        go(remote(sm_all.at[s], sm_all.at[s], ss, sr, F - 1 + i, (lax.rem(s + i, S), f)))
    for i in range(1, S):
        remote(qv.at[0], wq_all.at[lax.rem(s + S - i, S), f], qs, qr, i, mate).wait_recv()
    keep1.wait()
    for i in range(1, F):
        go(remote(wq_all.at[:, f], wq_all.at[:, f], qs, qr, S - 1 + i, (s, deep(i))))
    for i in range(1, F):
        remote(mv, wm_all.at[:, behind(i)], ms, mr, i, mate).wait_recv()
    keep3.wait()
    for i in range(1, P_):
        src = back(i)
        remote(xv, x_all.at[src], xs, xr, i, mate).wait_recv()
        go(remote(x_all.at[src], x_all.at[src], xs, xr, P_ - 1 + i, mate))
    for i in range(1, S):
        src = lax.rem(s + S - i, S)
        remote(sm_all.at[src], sm_all.at[src], ss, sr, F - 1 + i, mate).wait_recv()
    for i in range(1, F):
        g = behind(i)
        remote(wq_all.at[:, g], wq_all.at[:, g], qs, qr, S - 1 + i, mate).wait_recv()
    near = p * 2 + other
    remote(xv, x_all.at[near], xs, xr, 0, mate).wait_recv()
    for i in range(1, P_):
        src = lax.rem(p + P_ - i, P_) * 2 + other
        remote(xv, x_all.at[src], xs, xr, P_ - 1 + i, mate).wait_recv()
    keep2.wait()
    for copy in todo:
        copy.wait_send()


def gather_all(S, F, x, wq, sm, wm):
    any_ = pl.BlockSpec(memory_space=pl.ANY)
    shapes = [
        (S,) + x.shape,
        (S, F) + wq.shape[1:],
        (S, F) + sm.shape,
        (wm.shape[0], F) + wm.shape[1:],
    ]
    P_ = S // 2
    dma = pltpu.SemaphoreType.DMA
    counts = [2 * P_ - 1, S + F - 1, F + S - 1, F]
    sems = []
    for n in counts:
        sems += [dma((n + 1,)), dma((n + 1,))]
    return pl.pallas_call(
        functools.partial(gather_kernel, S, F),
        out_shape=[
            jax.ShapeDtypeStruct(sh, a.dtype) for sh, a in zip(shapes, (x, wq, sm, wm), strict=True)
        ],
        in_specs=[any_] * 4,
        out_specs=[any_] * 4,
        scratch_shapes=[
            pltpu.VMEM(x.shape, x.dtype),
            pltpu.VMEM(wq.shape, wq.dtype),
            pltpu.VMEM(sm.shape, sm.dtype),
            pltpu.VMEM(wm.shape, wm.dtype),
            dma((4,)),
        ]
        + sems,
        compiler_params=pltpu.CompilerParams(collective_id=1, has_side_effects=True),
        name="gather",
    )(x, wq, sm, wm)


def flip_bits(p, i):
    out, bit = p, 1
    while bit <= i:
        if i & bit:
            out = out + bit - 2 * bit * lax.rem(lax.div(p, bit), 2)
        bit *= 2
    return out


def forward_kernel(S, F, nh, x_all, w, g1, sc, wz, n1, qt, kt, vt, ot, lse, mixed, wm,
                   wt, kk, xb, nb, wv, inx, outn, local, osend, orecv, wsend, wrecv):
    s, f, p, c = spots()
    P_ = S // 2
    T, D = x_all.shape[1], x_all.shape[2]
    C = nh * HD
    L = S * T
    BQ = 2 * T
    BK = min(512, BQ)
    other = 1 - c
    mate = (p * 2 + other, f)
    load = pltpu.make_async_copy(wz, wv, local.at[0])
    load.start()

    def fetch(b):
        return pltpu.make_async_copy(x_all.at[b], xb.at[lax.rem(b, 2)], inx.at[lax.rem(b, 2)])

    def store(b):
        return pltpu.make_async_copy(nb.at[lax.rem(b, 2)], n1.at[b], outn.at[lax.rem(b, 2)])

    fetch(0).start()
    greet(S, F)
    load.wait()
    keep = pltpu.make_async_copy(wv, wm.at[:, s], local.at[0])
    keep.start()

    def spread(i):
        return remote(wv, wm.at[:, s], wsend, wrecv, i, (flip_bits(p, i) * 2 + c, f))

    def forward(i):
        src = flip_bits(p, i) * 2 + c
        return remote(wm.at[:, src], wm.at[:, src], wsend, wrecv, P_ + i, mate)

    for i in range(1, P_):
        spread(P_ - i).start()
    near = remote(wv, wm.at[:, s], wsend, wrecv, 0, mate)
    near.start()
    wt[...] = jnp.transpose(w[...])

    rows = 64

    def project(b, _):
        slot = lax.rem(b, 2)
        fetch(b).wait()

        @pl.when(b + 1 < S)
        def _():
            fetch(b + 1).start()

        @pl.when(b >= 2)
        def _():
            store(b - 2).wait()

        def norm(k, _):
            at = pl.ds(pl.multiple_of(k * rows, rows), rows)
            v = xb[slot, at, :].astype(f32)
            r = lax.rsqrt(jnp.mean(v * v, axis=-1, keepdims=True) + eps_norm)
            nb[slot, at, :] = (v * r * g1[...]).astype(bf)
            return 0

        lax.fori_loop(0, T // rows, norm, 0)
        store(b).start()
        cols = pl.ds(pl.multiple_of(b * T, T), T)
        res = dot(wt[...], nb[slot], 1, 1)
        qt[:, cols] = (res[:C] * sc[...]).astype(bf)
        kt[:, cols] = res[C : 2 * C].astype(bf)
        vt[:, cols] = res[2 * C :].astype(bf)
        for h in range(nh):
            kk[h, cols, :] = jnp.transpose(res[C + h * HD : C + (h + 1) * HD]).astype(bf)
        return 0

    lax.fori_loop(0, S, project, 0)
    store(S - 2).wait()
    store(S - 1).wait()

    def attend(t):
        first = pl.multiple_of(t * BQ, BQ)
        q = [qt[h * HD : (h + 1) * HD, pl.ds(first, BQ)] for h in range(nh)]

        def step(j, carry, diag=None):
            at = pl.ds(pl.multiple_of(j * BK, BK), BK)
            scores = [dot(kk[h, at, :], q[h]) for h in range(nh)]
            out = []
            for h in range(nh):
                m, l, acc = carry[h]
                sh = scores[h]
                if diag is not None:
                    kp = lax.broadcasted_iota(jnp.int32, sh.shape, 0) + diag * BK
                    qp = lax.broadcasted_iota(jnp.int32, sh.shape, 1)
                    sh = jnp.where(kp <= qp, sh, NEG)
                mn = jnp.maximum(m, jnp.max(sh, axis=0, keepdims=True))
                a = jnp.exp(m - mn)
                e = jnp.exp(sh - mn)
                l = l * a + jnp.sum(e, axis=0, keepdims=True)
                acc = acc * a + dot(vt[h * HD : (h + 1) * HD, at], e.astype(bf))
                out.append((mn, l, acc))
            return tuple(out)

        carry = tuple(
            (jnp.full((1, BQ), NEG, f32), jnp.zeros((1, BQ), f32), jnp.zeros((HD, BQ), f32))
            for _ in range(nh)
        )
        r = BQ // BK
        carry = lax.fori_loop(0, t * r, step, carry)
        for d in range(r):
            carry = step(t * r + d, carry, d)
        for h in range(nh):
            m, l, acc = carry[h]
            ot[h * HD : (h + 1) * HD, pl.ds(first, BQ)] = (acc / l).astype(bf)
            lse[h : h + 1, pl.ds(first, BQ)] = m + jnp.log(l)

    def to_owner(src, n, to):
        return pltpu.make_async_remote_copy(
            src_ref=src,
            dst_ref=mixed.at[s],
            send_sem=osend.at[n],
            recv_sem=orecv.at[n - n % 2 + c],
            device_id=to,
            device_id_type=MESH,
        )

    def send(i, half):
        t = flip_bits(p, i)
        src = ot.at[:, pl.ds(pl.multiple_of(t * BQ + half * T, T), T)]
        return to_owner(src, 2 * i + half, (t * 2 + half, f))

    for i in range(1, P_):
        attend(flip_bits(p, P_ - i))
        send(P_ - i, 0).start()
        send(P_ - i, 1).start()
        spread(P_ - i).wait_recv()
        forward(P_ - i).start()
    attend(p)
    mine = ot.at[:, pl.ds(pl.multiple_of(s * T, T), T)]
    theirs = ot.at[:, pl.ds(pl.multiple_of((p * 2 + other) * T, T), T)]
    last = to_owner(theirs, 0, mate)
    last.start()
    own = pltpu.make_async_copy(mine, mixed.at[s], local.at[1])
    own.start()
    def from_source(i, core):
        return pltpu.make_async_remote_copy(
            src_ref=mine,
            dst_ref=mixed.at[flip_bits(p, i) * 2 + core],
            send_sem=osend.at[0],
            recv_sem=orecv.at[2 * i + core],
            device_id=mate,
            device_id_type=MESH,
        )

    for i in range(1, P_):
        for core in range(2):
            from_source(i, core).wait_recv()
    from_source(0, other).wait_recv()
    last.wait_send()
    own.wait()
    keep.wait()
    near.wait()
    for i in range(1, P_):
        forward(i).wait()
        spread(i).wait_send()
        send(i, 0).wait_send()
        send(i, 1).wait_send()


def forward_all(S, F, nh, x_all, w, g1, sc, wz):
    T, D = x_all.shape[1], x_all.shape[2]
    C = nh * HD
    L = S * T
    P_ = S // 2
    any_ = pl.BlockSpec(memory_space=pl.ANY)
    vm = pl.BlockSpec(memory_space=pltpu.VMEM)
    dma = pltpu.SemaphoreType.DMA
    shape = jax.ShapeDtypeStruct
    NW, R = wz.shape[0], wz.shape[2]
    V = pltpu.VMEM
    return pl.pallas_call(
        functools.partial(forward_kernel, S, F, nh),
        out_shape=[
            shape((S, T, D), bf),
            shape((C, L), bf),
            shape((C, L), bf),
            shape((C, L), bf),
            shape((C, L), bf),
            shape((nh, L), f32),
            shape((S, C, T), bf),
            shape((NW, S, F, R, D), bf),
        ],
        in_specs=[any_, vm, vm, vm, any_],
        out_specs=[any_, vm, vm, vm, vm, vm, any_, any_],
        scratch_shapes=[
            V((3 * C, D), bf),
            V((nh, L, HD), bf),
            V((2, T, D), bf),
            V((2, T, D), bf),
            V((NW, F, R, D), bf),
            dma((2,)),
            dma((2,)),
            dma((2,)),
            dma((2 * P_,)),
            dma((2 * P_,)),
            dma((2 * P_,)),
            dma((2 * P_,)),
        ],
        compiler_params=pltpu.CompilerParams(
            collective_id=3, has_side_effects=True, vmem_limit_bytes=60 << 20
        ),
        name="forward",
    )(x_all, w, g1, sc, wz)


def xor(a, b, n):
    out, bit = 0, 1
    while bit < n:
        both = lax.rem(lax.div(a, bit), 2) + lax.rem(lax.div(b, bit), 2)
        out = out + bit * lax.rem(both, 2)
        bit *= 2
    return out


def backward_kernel(S, F, nh, dm, qt, kt, vt, ot, lse, n1, x_all, w, sc, g1, g, vec, dx2,
                    g_out, in_out, q_out, vec_out, gi, gp,
                    dmt, wt, dwt, ab, fm, tm, nx, xx, rr, mb, own, bi, bp, ga, gb, gz, qi, qo,
                    vi, vz, vp, gf, gs_, local, nsem, bload,
                    gsend, grecv, bsend, brecv, qsend, qrecv, vsend, vrecv):
    s, f, p, c = spots()
    P_ = S // 2
    T, D = x_all.shape[1], x_all.shape[2]
    C = nh * HD
    L = S * T
    BQ = 2 * T
    BK = min(512, BQ)
    NW, R = g.shape[0], g.shape[3]
    other = 1 - c
    mate = (p * 2 + other, f)
    todo = []

    def go(copy):
        copy.start()
        todo.append(copy)

    def chip(i):
        return flip_bits(p, i)

    def deep(i):
        return lax.rem(f + i, F)

    def head(ref, h, at):
        return ref[h * HD : (h + 1) * HD, at]

    loads = [
        pltpu.make_async_copy(dm.at[b], dmt.at[:, b * T : (b + 1) * T], bload.at[b])
        for b in range(S)
    ]
    for load in loads:
        load.start()
    greet(S, F)

    def swap(i):
        t = chip(i)
        return remote(g.at[:, t * 2 + other], gi.at[i], gsend, grecv, i, mate)

    order = list(range(P_ - 1, -1, -1))
    for i in order:
        swap(i).start()
    wt[...] = jnp.transpose(w[...])
    dwt[...] = jnp.zeros_like(dwt)
    gf[...] = jnp.zeros_like(gf)
    gs_[...] = jnp.zeros_like(gs_)
    for load in loads:
        load.wait()

    def slabs(body):
        def one(n, _):
            body(lax.div(n, F), lax.rem(n, F))
            return 0

        lax.fori_loop(0, NW * F, one, 0)

    def out_g(i):
        return remote(gi.at[i], gp.at[i], gsend, grecv, P_ + i, (chip(i) * 2 + c, f))

    def sum_pairs():
        for i in order:
            la = pltpu.make_async_copy(g.at[:, chip(i) * 2 + c], ga, local.at[1])
            la.start()
            swap(i).wait_recv()
            lb = pltpu.make_async_copy(gi.at[i], gb, local.at[2])
            lb.start()
            la.wait()
            lb.wait()

            def add(a, z):
                ga[a, z] = (ga[a, z].astype(f32) + gb[a, z].astype(f32)).astype(bf)

            slabs(add)
            st = pltpu.make_async_copy(ga, gi.at[i], local.at[1])
            st.start()
            st.wait()
            if i:
                out_g(i).start()

    rows = 64
    wide = 256 if D % 256 == 0 else D

    def over(i):
        return remote(mb, bi.at[i], bsend, brecv, i, mate)

    def out_b(i, t):
        return pltpu.make_async_remote_copy(
            src_ref=bi.at[i],
            dst_ref=bp.at[i - 1],
            send_sem=bsend.at[P_ + i],
            recv_sem=brecv.at[P_ + i],
            device_id=(t * 2 + c, f),
            device_id_type=MESH,
        )

    def attention(q, k, v, do, delta, dqt, dk, dv):
        dqt[...] = jnp.zeros_like(dqt)
        dk[...] = jnp.zeros_like(dk)
        dv[...] = jnp.zeros_like(dv)

        def turn(b, _):
            at = pl.ds(pl.multiple_of(b * T, T), T)
            va = pltpu.make_async_copy(vt.at[:, at], ab.at[0], nsem.at[0])
            oa = pltpu.make_async_copy(ot.at[:, at], ab.at[1], nsem.at[1])
            va.start()
            oa.start()
            for h in range(nh):
                q[h, at, :] = jnp.transpose(head(qt, h, at))
                k[h, at, :] = jnp.transpose(head(kt, h, at))
                do[h, at, :] = jnp.transpose(head(dmt, h, at))
            va.wait()
            oa.wait()
            for h in range(nh):
                v[h, at, :] = jnp.transpose(ab[0, h * HD : (h + 1) * HD, :])
                old = ab[1, h * HD : (h + 1) * HD, :].astype(f32)
                prod = head(dmt, h, at).astype(f32) * old
                delta[h : h + 1, at] = jnp.sum(prod, axis=0, keepdims=True)
            return 0

        lax.fori_loop(0, S, turn, 0)

        sum_pairs()

        def tile(q0, k0, masked):
            qa = pl.ds(q0, BK)
            ka = pl.ds(k0, BK)
            scores = [dot(k[h, ka, :], head(qt, h, qa)) for h in range(nh)]
            dps = [dot(v[h, ka, :], head(dmt, h, qa)) for h in range(nh)]
            for h in range(nh):
                e = jnp.exp(scores[h] - lse[h : h + 1, qa])
                if masked:
                    kp = lax.broadcasted_iota(jnp.int32, e.shape, 0)
                    qp = lax.broadcasted_iota(jnp.int32, e.shape, 1)
                    e = jnp.where(kp <= qp, e, 0.0)
                ds = (e * (dps[h] - delta[h : h + 1, qa])).astype(bf)
                dv[h, ka, :] += dot(e.astype(bf), do[h, qa, :])
                dk[h, ka, :] += dot(ds, q[h, qa, :])
                dqt[h * HD : (h + 1) * HD, qa] += dot(head(kt, h, ka), ds)

        r = BQ // BK

        def rect(qb, kb):
            def one(n, _):
                q0 = pl.multiple_of(qb * BQ + lax.div(n, r) * BK, BK)
                k0 = pl.multiple_of(kb * BQ + lax.rem(n, r) * BK, BK)
                tile(q0, k0, False)
                return 0

            lax.fori_loop(0, r * r, one, 0)

        def triangle(t):
            def one(n, _):
                at = pl.multiple_of(t * BQ + n * BK, BK)
                tile(at, at, True)

                def below(j, _):
                    tile(at, pl.multiple_of(t * BQ + j * BK, BK), False)
                    return 0

                lax.fori_loop(0, n, below, 0)
                return 0

            lax.fori_loop(0, r, one, 0)

        def fetch(t, half):
            b = t * 2 + half
            return (
                pltpu.make_async_copy(n1.at[b], nx, nsem.at[0]),
                pltpu.make_async_copy(x_all.at[b], xx, nsem.at[1]),
            )

        def finish(t, half, dst):
            for copy in fetch(t, half):
                copy.start()
            at = pl.ds(pl.multiple_of((t * 2 + half) * T, T), T)
            dqs = dqt[:, at].astype(bf)
            dqf = dqs.astype(f32)
            gs_[...] += jnp.sum(dqf * qt[:, at].astype(f32), axis=1, keepdims=True)
            fm[:C, :] = (dqf * sc[...]).astype(bf)
            for h in range(nh):
                fm[C + h * HD : C + (h + 1) * HD, :] = jnp.transpose(dk[h, at, :]).astype(bf)
                fm[2 * C + h * HD : 2 * C + (h + 1) * HD, :] = jnp.transpose(dv[h, at, :]).astype(bf)
            tm[...] = jnp.transpose(fm[...])
            for copy in fetch(t, half):
                copy.wait()

            def inverse(n, _):
                a = pl.ds(pl.multiple_of(n * rows, rows), rows)
                z = xx[a, :].astype(f32)
                rr[a, :] = lax.rsqrt(jnp.mean(z * z, axis=-1, keepdims=True) + eps_norm)
                return 0

            lax.fori_loop(0, T // rows, inverse, 0)

            def column(n, _):
                a = pl.ds(pl.multiple_of(n * wide, wide), wide)
                back = dot(tm[...], wt[:, a])
                dst[:, a] = back.astype(bf)
                hat = xx[:, a].astype(f32) * rr[...]
                gf[:, a] += jnp.sum(back * hat, axis=0, keepdims=True)
                dwt[:, a] += dot(fm[...], nx[:, a])
                return 0

            lax.fori_loop(0, D // wide, column, 0)

        def combine(i):
            def one(n, _):
                a = pl.ds(pl.multiple_of(n * rows, rows), rows)
                bi[i, a, :] = (bi[i, a, :].astype(f32) + own[a, :].astype(f32)).astype(bf)
                return 0

            lax.fori_loop(0, T // rows, one, 0)

        def advance(i, t, last):
            def pair(m, _):
                u = xor(p, m, P_)
                rect(jnp.maximum(t, u), jnp.minimum(t, u))
                return 0

            lax.fori_loop(0, i, pair, 0)
            triangle(t)
            if not last:

                @pl.when(i < P_ - 1)
                def _():
                    over(i + 1).wait_send()

            else:
                over(1).wait_send()
            finish(t, other, mb)
            over(i).start()
            finish(t, c, own)
            over(i).wait_recv()
            combine(i)
            if not last:
                out_b(i, t).start()

        def stage(n, _):
            i = P_ - 1 - n
            advance(i, xor(p, i, P_), False)
            return 0

        lax.fori_loop(0, P_ - 1, stage, 0)
        advance(0, p, True)


    V = pltpu.VMEM
    pl.run_scoped(
        attention,
        V((nh, L, HD), bf),
        V((nh, L, HD), bf),
        V((nh, L, HD), bf),
        V((nh, L, HD), bf),
        V((nh, L), f32),
        V((C, L), f32),
        V((nh, L, HD), f32),
        V((nh, L, HD), f32),
    )

    def closing(dw, up, qm, qs_, go_, vo):
        up_load = pltpu.make_async_copy(dx2, up, local.at[0])
        up_load.start()
        x_load = pltpu.make_async_copy(x_all.at[s], xx, nsem.at[1])
        x_load.start()
        vi[...] = vec[...]
        vi[0:1, :] = gf[...]
        turned = jnp.transpose(jnp.broadcast_to(gs_[...], (C, 128)))
        vi[4:5, 0:C] = turned[0:1, :]
        for i in range(1, F):
            go(remote(vi, vz.at[i], vsend, vrecv, i, (s, deep(i))))
        dw[...] = jnp.transpose(dwt[...])

        bunch = 8 // math.gcd(R, 8)

        def piece(n, _):
            part = dw[pl.ds(pl.multiple_of(n * (bunch * R), 8), bunch * R), :]
            for j in range(bunch):
                to = n * bunch + j
                qm[lax.div(to, F), lax.rem(to, F)] = part[j * R : (j + 1) * R].astype(bf)
            return 0

        lax.fori_loop(0, S * F // bunch, piece, 0)
        for i in range(1, F):
            go(remote(qm.at[:, deep(i)], qi.at[i], qsend, qrecv, i, (s, deep(i))))
        la = pltpu.make_async_copy(gi.at[0], ga, local.at[1])
        la.start()
        la.wait()
        for i in order[:-1]:
            out_g(i).wait_recv()
            lb = pltpu.make_async_copy(gp.at[i], gb, local.at[2])
            lb.start()
            lb.wait()

            def more(a, z):
                ga[a, z] = (ga[a, z].astype(f32) + gb[a, z].astype(f32)).astype(bf)

            slabs(more)
        for i in range(1, F):
            go(remote(ga.at[:, deep(i)], gz.at[i], gsend, grecv, 2 * P_ + i, (s, deep(i))))
        total = vi[...]
        for i in range(1, F):
            remote(vi, vz.at[i], vsend, vrecv, i, mate).wait_recv()
            total = total + vz[i]
        vp[0] = total
        for i in range(1, S):
            go(remote(vp.at[0], vp.at[i], vsend, vrecv, F - 1 + i, (lax.rem(s + i, S), f)))
        for i in range(1, F):
            remote(qm.at[:, f], qi.at[i], qsend, qrecv, i, mate).wait_recv()

        def sum_q(n, _):
            part = qm[n, f].astype(f32)
            for i in range(1, F):
                part = part + qi[i, n].astype(f32)
            qs_[n] = part.astype(bf)
            return 0

        lax.fori_loop(0, S, sum_q, 0)
        keep = pltpu.make_async_copy(qs_.at[s], qo.at[s], local.at[1])
        keep.start()
        for i in range(1, S):
            to = lax.rem(s + i, S)
            go(remote(qs_.at[to], qo.at[s], qsend, qrecv, F - 1 + i, (to, f)))
        up_load.wait()
        x_load.wait()
        over(0).wait_send()
        for i in order[:-1]:
            out_b(i, chip(i)).wait_recv()

        def below(n, _):
            a = pl.ds(pl.multiple_of(n * rows, rows), rows)
            back = bi[0, a, :].astype(f32)
            for i in range(1, P_):
                back = back + bp[i - 1, a, :].astype(f32)
            z = xx[a, :].astype(f32)
            r1 = lax.rsqrt(jnp.mean(z * z, axis=-1, keepdims=True) + eps_norm)
            e1 = back * g1[...]
            tilt = jnp.mean(e1 * z, axis=-1, keepdims=True)
            mb[a, :] = (up[a, :] + r1 * e1 - z * (r1 * r1 * r1 * tilt)).astype(bf)
            return 0

        lax.fori_loop(0, T // rows, below, 0)
        outs = [pltpu.make_async_copy(mb, in_out, local.at[0])]
        outs[0].start()
        for i in range(1, F):
            remote(ga.at[:, f], gz.at[i], gsend, grecv, 2 * P_ + i, mate).wait_recv()
        for a in range(NW):
            part = ga[a, f].astype(f32)
            for i in range(1, F):
                part = part + gz[i, a].astype(f32)
            go_[a] = part
        outs.append(pltpu.make_async_copy(go_, g_out, local.at[2]))
        outs[1].start()
        total = vp[0]
        for i in range(1, S):
            remote(vp.at[0], vp.at[i], vsend, vrecv, F - 1 + i, mate).wait_recv()
            total = total + vp[i]
        vo[...] = total
        outs.append(pltpu.make_async_copy(vo, vec_out, nsem.at[0]))
        outs[2].start()
        for i in range(1, S):
            src = lax.rem(s + S - i, S)
            remote(qs_.at[0], qo.at[src], qsend, qrecv, F - 1 + i, mate).wait_recv()
        keep.wait()
        outs.append(pltpu.make_async_copy(qo, q_out, local.at[1]))
        outs[3].start()
        for out in outs:
            out.wait()
        for copy in todo:
            copy.wait_send()
        for i in range(P_):
            swap(i).wait_send()
        for i in range(1, P_):
            out_g(i).wait_send()
            out_b(i, chip(i)).wait_send()

    pl.run_scoped(
        closing,
        V((D, 3 * C), f32),
        V((T, D), f32),
        V((S, F, R, 3 * C), bf),
        V((S, R, 3 * C), bf),
        V((NW, R, D), f32),
        V(vec.shape, f32),
    )


def backward_all(S, F, nh, dm, qt, kt, vt, ot, lse, n1, x_all, w, sc, g1, g, vec, dx2):
    T, D = x_all.shape[1], x_all.shape[2]
    C = nh * HD
    L = S * T
    P_ = S // 2
    NW, R = g.shape[0], g.shape[3]
    any_ = pl.BlockSpec(memory_space=pl.ANY)
    vm = pl.BlockSpec(memory_space=pltpu.VMEM)
    dma = pltpu.SemaphoreType.DMA
    shape = jax.ShapeDtypeStruct
    V = pltpu.VMEM
    return pl.pallas_call(
        functools.partial(backward_kernel, S, F, nh),
        out_shape=[
            shape((NW, R, D), f32),
            shape((T, D), bf),
            shape((S, R, 3 * C), bf),
            shape(vec.shape, f32),
            shape((P_, NW, F, R, D), bf),
            shape((P_, NW, F, R, D), bf),
        ],
        in_specs=[any_, vm, vm, any_, any_, vm, any_, any_, vm, vm, vm, any_, vm, any_],
        out_specs=[any_] * 6,
        scratch_shapes=[
            V((C, L), bf),
            V((3 * C, D), bf),
            V((3 * C, D), f32),
            V((2, C, T), bf),
            V((3 * C, T), bf),
            V((T, 3 * C), bf),
            V((T, D), bf),
            V((T, D), bf),
            V((T, 1), f32),
            V((T, D), bf),
            V((T, D), bf),
            V((P_, T, D), bf),
            V((P_ - 1, T, D), bf),
            V((NW, F, R, D), bf),
            V((NW, F, R, D), bf),
            V((F, NW, R, D), bf),
            V((F, S, R, 3 * C), bf),
            V((S, R, 3 * C), bf),
            V(vec.shape, f32),
            V((F,) + vec.shape, f32),
            V((S,) + vec.shape, f32),
            V((1, D), f32),
            V((C, 1), f32),
            dma((3,)),
            dma((2,)),
            dma((S,)),
            dma((2 * P_ + F,)),
            dma((2 * P_ + F,)),
            dma((2 * P_,)),
            dma((2 * P_,)),
            dma((S + F,)),
            dma((S + F,)),
            dma((S + F,)),
            dma((S + F,)),
        ],
        compiler_params=pltpu.CompilerParams(
            collective_id=4, has_side_effects=True, vmem_limit_bytes=66_000_000
        ),
        name="backward",
    )(dm, qt, kt, vt, ot, lse, n1, x_all, w, sc, g1, g, vec, dx2)


def body(
    inputs,
    w_query,
    w_key,
    w_value,
    w_proj,
    w_up,
    w_down,
    gain_first,
    gain_second,
    bias_up,
    bias_down,
    query_scale,
    cotangent,
):
    groups = lax.axis_size("seq")
    rows_of = lax.axis_size("fsdp")
    nh = H // groups
    cols = nh * HD
    both = ("seq", "fsdp")
    tokens, width = inputs.shape[1], inputs.shape[2]
    length = tokens * groups
    shard = w_query.shape[0]
    x_low = inputs.reshape(tokens, width)
    qkv_rows = jnp.stack([w_query, w_key, w_value], 1).astype(bf).reshape(shard, 3, groups, cols)
    qkv_rows = qkv_rows.transpose(2, 0, 1, 3).reshape(groups, shard, 3 * cols)
    small = jnp.stack([gain_first, gain_second, bias_up, bias_down], 0)
    small = jnp.pad(small.astype(bf), ((0, 12), (0, 128 - shard)))
    weights = jnp.stack([w_proj, w_up, w_down], 0).astype(bf)
    x_all, qkv_w, small, weights = gather_all(groups, rows_of, x_low, qkv_rows, small, weights)
    qkv_w = qkv_w.reshape(width, 3 * cols)
    small = small[:, :, :4, :shard].transpose(2, 0, 1, 3).reshape(4, width).astype(f32)
    first_gain, second_gain, upbias, downbias = small[0], small[1], small[2], small[3]
    scale_dims = jax.nn.softplus(query_scale) * log_two_inverse / math.sqrt(HD)
    scale_cols = jnp.tile(scale_dims, nh)
    normed, qt, kt, vt, ot, lse, mixed, weights = forward_all(
        groups, rows_of, nh, x_all, qkv_w, small[:1], scale_cols[:, None], weights
    )
    weights = weights.reshape(3, width, width)
    proj_w, up_w, down_w = weights[0], weights[1], weights[2]
    mixed = mixed.reshape(width, tokens)
    float_in = x_low.astype(f32)
    middle = float_in + dot(mixed, proj_w, 0, 0)
    second = rms_scale(middle, second_gain).astype(bf)
    hidden = jnp.dot(second, up_w, preferred_element_type=f32) + upbias
    active = jax.nn.silu(hidden).astype(bf)
    result = middle + jnp.dot(active, down_w, preferred_element_type=f32) + downbias

    top_low = cotangent.reshape(tokens, width)
    grad_top = top_low.astype(f32)
    grad_bdown = jnp.sum(grad_top, axis=0)
    grad_wdown = dot(active, top_low, 0, 0)
    grad_active = dot(top_low, down_w, 1, 1)
    gate = 1 / (1 + jnp.exp(-hidden))
    grad_hidden = grad_active * (gate * (1 + hidden * (1 - gate)))
    grad_bup = jnp.sum(grad_hidden, axis=0)
    hidden_low = grad_hidden.astype(bf)
    grad_wup = dot(second, hidden_low, 0, 0)
    grad_second_in = dot(hidden_low, up_w, 1, 1)
    unused_second, second_pull = jax.vjp(rms_scale, middle, second_gain)
    grad_middle, grad_gsecond = second_pull(grad_second_in)
    grad_middle = grad_middle + grad_top
    middle_low = grad_middle.astype(bf)
    grad_wproj = dot(mixed, middle_low, 1, 0)
    grad_mixed = dot(proj_w, middle_low, 1, 1).astype(bf)
    dm = lax.all_to_all(grad_mixed.reshape(groups, cols, tokens), "seq", 0, 0)
    zeros = jnp.zeros((width,), f32)
    vectors = jnp.stack([zeros, grad_gsecond, grad_bup, grad_bdown] + [zeros] * 4, 0)
    stacked = jnp.stack([grad_wproj.astype(bf), grad_wup.astype(bf), grad_wdown.astype(bf)], 0)
    owned, grad_inputs, grad_qkv, vectors, unused_pair, unused_plane = backward_all(
        groups,
        rows_of,
        nh,
        dm,
        qt,
        kt,
        vt,
        ot,
        lse,
        normed,
        x_all,
        qkv_w,
        scale_cols[:, None],
        small[:1],
        stacked.reshape(3, groups, rows_of, shard, width),
        vectors,
        grad_middle,
    )
    grad_qkv = grad_qkv.reshape(groups, shard, 3, cols).transpose(2, 1, 0, 3)
    grad_qkv = grad_qkv.reshape(3, shard, width).astype(f32)
    at = (lax.axis_index("seq") * rows_of + lax.axis_index("fsdp")) * shard
    mine = lax.dynamic_slice_in_dim(vectors, at, shard, 1)
    scale_total = jnp.sum(vectors[4, :cols].reshape(nh, HD), axis=0) / scale_dims
    grad_scale = scale_total * jax.nn.sigmoid(query_scale) * log_two_inverse / math.sqrt(HD)
    return (
        result.astype(bf).reshape(inputs.shape),
        grad_inputs.reshape(inputs.shape),
        grad_qkv[0],
        grad_qkv[1],
        grad_qkv[2],
        owned[0],
        owned[1],
        owned[2],
        mine[0],
        mine[1],
        mine[2],
        mine[3],
        grad_scale,
    )


def solution(mesh):
    return jax.shard_map(
        body,
        mesh=mesh,
        in_specs=(
            P("fsdp", "seq", None),
            P(("seq", "fsdp"), None),
            P(("seq", "fsdp"), None),
            P(("seq", "fsdp"), None),
            P(("seq", "fsdp"), None),
            P(("seq", "fsdp"), None),
            P(("seq", "fsdp"), None),
            P(("seq", "fsdp")),
            P(("seq", "fsdp")),
            P(("seq", "fsdp")),
            P(("seq", "fsdp")),
            P(),
            P("fsdp", "seq", None),
        ),
        out_specs=(
            P("fsdp", "seq", None),
            P("fsdp", "seq", None),
            P(("seq", "fsdp"), None),
            P(("seq", "fsdp"), None),
            P(("seq", "fsdp"), None),
            P(("seq", "fsdp"), None),
            P(("seq", "fsdp"), None),
            P(("seq", "fsdp"), None),
            P(("seq", "fsdp")),
            P(("seq", "fsdp")),
            P(("seq", "fsdp")),
            P(("seq", "fsdp")),
            P(),
        ),
        check_vma=False,
    )
```

```python
import functools
import math

import jax
import jax.numpy as jnp
from jax import lax
from jax.experimental import pallas as pl
from jax.experimental.pallas import tpu as pltpu
from jax.sharding import PartitionSpec as P

H = 16
HD = 80
eps_norm = 1e-06
log_two_inverse = 1.442695
bf = jnp.bfloat16
f32 = jnp.float32
NEG = -1e30


def rms_scale(values, gain):
    return values * lax.rsqrt(jnp.mean(values * values, axis=-1, keepdims=True) + eps_norm) * gain


def dot(a,b,ca=1,cb=0):
    return lax.dot_general(a,b,(((ca,),(cb,)),((),())),preferred_element_type=f32)


MESH = pl.DeviceIdType.MESH


def spots():
    s, f = lax.axis_index("seq"), lax.axis_index("fsdp")
    return s, f, s // 2, lax.rem(s, 2)


def greet(S, F):
    s, f, _, _ = spots()
    barrier = pltpu.get_barrier_semaphore()
    for i in range(1, S):
        pl.semaphore_signal(barrier, inc=1, device_id=(lax.rem(s + i, S), f), device_id_type=MESH)
    for i in range(1, F):
        pl.semaphore_signal(barrier, inc=1, device_id=(s, lax.rem(f + i, F)), device_id_type=MESH)
    pl.semaphore_wait(barrier, S + F - 2)


def remote(src, dst, sends, recvs, n, to):
    return pltpu.make_async_remote_copy(
        src_ref=src,
        dst_ref=dst,
        send_sem=sends.at[n],
        recv_sem=recvs.at[n],
        device_id=to,
        device_id_type=MESH,
    )


def gather_kernel(S, F, x, wq, sm, wm, x_all, wq_all, sm_all, wm_all, xv, qv, sv, mv, local,
                  xs, xr, qs, qr, ss, sr, ms, mr):
    s, f, p, c = spots()
    P_ = S // 2
    other = 1 - c
    loads = [
        pltpu.make_async_copy(sm, sv, local.at[0]),
        pltpu.make_async_copy(wq, qv, local.at[1]),
        pltpu.make_async_copy(x, xv, local.at[2]),
        pltpu.make_async_copy(wm, mv, local.at[3]),
    ]
    for load in loads:
        load.start()
    greet(S, F)
    mate = (p * 2 + other, f)
    todo = []

    def go(copy):
        copy.start()
        todo.append(copy)

    def chip(i):
        return lax.rem(p + i, P_) * 2 + c

    def back(i):
        return lax.rem(p + P_ - i, P_) * 2 + c

    def near_chip(i):
        return flip_bits(p, i) * 2 + c

    H_ = x.shape[0] // 2

    def deep(i):
        return lax.rem(f + i, F)

    def behind(i):
        return lax.rem(f + F - i, F)

    loads[0].wait()
    keep0 = pltpu.make_async_copy(sv, sm_all.at[s, f], local.at[0])
    keep0.start()
    for i in range(1, F):
        go(remote(sv, sm_all.at[s, f], ss, sr, i, (s, deep(i))))
    loads[1].wait()
    keep1 = pltpu.make_async_copy(qv.at[s], wq_all.at[s, f], local.at[1])
    keep1.start()
    for i in range(1, S):
        to = lax.rem(s + i, S)
        go(remote(qv.at[to], wq_all.at[s, f], qs, qr, i, (to, f)))
    loads[2].wait()
    keep2 = pltpu.make_async_copy(xv, x_all.at[s], local.at[2])
    keep2.start()
    if P_ == 4:
        for first in range(2):
            for i in (1, 2):
                half = first if i == 1 else 1 - first
                part = pl.ds(half * H_, H_)
                go(remote(xv.at[part], x_all.at[s, part], xs, xr, 2 * i + half, (near_chip(i), f)))
    else:
        for i in range(1, P_):
            go(remote(xv, x_all.at[s], xs, xr, i, (chip(i), f)))
    go(remote(xv, x_all.at[s], xs, xr, 0, mate))
    loads[3].wait()
    keep3 = pltpu.make_async_copy(mv, wm_all.at[:, f], local.at[3])
    keep3.start()
    for i in range(1, F):
        go(remote(mv, wm_all.at[:, f], ms, mr, i, (s, deep(i))))
    for i in range(1, F):
        g = behind(i)
        remote(sv, sm_all.at[s, g], ss, sr, i, mate).wait_recv()
    keep0.wait()
    for i in range(1, S):
        go(remote(sm_all.at[s], sm_all.at[s], ss, sr, F - 1 + i, (lax.rem(s + i, S), f)))
    for i in range(1, S):
        remote(qv.at[0], wq_all.at[lax.rem(s + S - i, S), f], qs, qr, i, mate).wait_recv()
    keep1.wait()
    for i in range(1, F):
        go(remote(wq_all.at[:, f], wq_all.at[:, f], qs, qr, S - 1 + i, (s, deep(i))))
    for i in range(1, F):
        remote(mv, wm_all.at[:, behind(i)], ms, mr, i, mate).wait_recv()
    keep3.wait()
    if P_ == 4:
        for i in (1, 2):
            half = i - 1
            part = pl.ds(half * H_, H_)
            src = near_chip(i)
            remote(xv.at[part], x_all.at[src, part], xs, xr, 2 * i + half, mate).wait_recv()
            blk = x_all.at[src, part]
            go(remote(blk, blk, xs, xr, 6 + half, (near_chip(3 - i), f)))
        for i in (1, 2):
            half = 2 - i
            part = pl.ds(half * H_, H_)
            src = near_chip(i)
            remote(xv.at[part], x_all.at[src, part], xs, xr, 2 * i + half, mate).wait_recv()
            go(remote(x_all.at[src], x_all.at[src], xs, xr, 8 + i, mate))
    for i in range(1, P_ if P_ != 4 else 1):
        src = back(i)
        remote(xv, x_all.at[src], xs, xr, i, mate).wait_recv()
        go(remote(x_all.at[src], x_all.at[src], xs, xr, P_ - 1 + i, mate))
    for i in range(1, S):
        src = lax.rem(s + S - i, S)
        remote(sm_all.at[src], sm_all.at[src], ss, sr, F - 1 + i, mate).wait_recv()
    for i in range(1, F):
        g = behind(i)
        remote(wq_all.at[:, g], wq_all.at[:, g], qs, qr, S - 1 + i, mate).wait_recv()
    near = p * 2 + other
    remote(xv, x_all.at[near], xs, xr, 0, mate).wait_recv()
    if P_ == 4:
        for half in range(2):
            part = pl.ds(half * H_, H_)
            blk = x_all.at[near_chip(3), part]
            remote(blk, blk, xs, xr, 6 + half, mate).wait_recv()
            go(remote(blk, blk, xs, xr, 11 + half, mate))
        for i in (1, 2):
            blk = x_all.at[flip_bits(p, i) * 2 + other]
            remote(blk, blk, xs, xr, 8 + i, mate).wait_recv()
        for half in range(2):
            blk = x_all.at[flip_bits(p, 3) * 2 + other, pl.ds(half * H_, H_)]
            remote(blk, blk, xs, xr, 11 + half, mate).wait_recv()
    else:
        for i in range(1, P_):
            src = lax.rem(p + P_ - i, P_) * 2 + other
            remote(xv, x_all.at[src], xs, xr, P_ - 1 + i, mate).wait_recv()
    keep2.wait()
    for copy in todo:
        copy.wait_send()


def gather_all(S, F, x, wq, sm, wm):
    any_ = pl.BlockSpec(memory_space=pl.ANY)
    shapes = [
        (S,) + x.shape,
        (S, F) + wq.shape[1:],
        (S, F) + sm.shape,
        (wm.shape[0], F) + wm.shape[1:],
    ]
    P_ = S // 2
    dma = pltpu.SemaphoreType.DMA
    counts = [max(2 * P_ - 1, 12), S + F - 1, F + S - 1, F]
    sems = []
    for n in counts:
        sems += [dma((n + 1,)), dma((n + 1,))]
    return pl.pallas_call(
        functools.partial(gather_kernel, S, F),
        out_shape=[
            jax.ShapeDtypeStruct(sh, a.dtype) for sh, a in zip(shapes, (x, wq, sm, wm), strict=True)
        ],
        in_specs=[any_] * 4,
        out_specs=[any_] * 4,
        scratch_shapes=[
            pltpu.VMEM(x.shape, x.dtype),
            pltpu.VMEM(wq.shape, wq.dtype),
            pltpu.VMEM(sm.shape, sm.dtype),
            pltpu.VMEM(wm.shape, wm.dtype),
            dma((4,)),
        ]
        + sems,
        compiler_params=pltpu.CompilerParams(collective_id=1, has_side_effects=True),
        name="gather",
    )(x, wq, sm, wm)


def flip_bits(p, i):
    out, bit = p, 1
    while bit <= i:
        if i & bit:
            out = out + bit - 2 * bit * lax.rem(lax.div(p, bit), 2)
        bit *= 2
    return out


def forward_kernel(S, F, nh, x_all, w, g1, sc, wz, n1, qt, kt, vt, ot, lse, mixed, wm,
                   wt, kk, xb, nb, wv, inx, outn, local, osend, orecv, wsend, wrecv):
    s, f, p, c = spots()
    P_ = S // 2
    T, D = x_all.shape[1], x_all.shape[2]
    C = nh * HD
    L = S * T
    BQ = 2 * T
    BK = min(512, BQ)
    other = 1 - c
    mate = (p * 2 + other, f)
    load = pltpu.make_async_copy(wz, wv, local.at[0])
    load.start()

    def fetch(b):
        return pltpu.make_async_copy(x_all.at[b], xb.at[lax.rem(b, 2)], inx.at[lax.rem(b, 2)])

    def store(b):
        return pltpu.make_async_copy(nb.at[lax.rem(b, 2)], n1.at[b], outn.at[lax.rem(b, 2)])

    fetch(0).start()
    greet(S, F)
    load.wait()
    keep = pltpu.make_async_copy(wv, wm.at[:, s], local.at[0])
    keep.start()

    def spread(i):
        return remote(wv, wm.at[:, s], wsend, wrecv, i, (flip_bits(p, i) * 2 + c, f))

    def forward(i):
        src = flip_bits(p, i) * 2 + c
        return remote(wm.at[:, src], wm.at[:, src], wsend, wrecv, (7 if P_ == 4 else P_) + i, mate)

    def part_of(src, half):
        return wm.at[:, src, pl.ds(half * (F // 2), F // 2)]

    def direct(i, half):
        src = wv.at[:, pl.ds(half * (F // 2), F // 2)]
        to = (flip_bits(p, i) * 2 + c, f)
        return remote(src, part_of(s, half), wsend, wrecv, 2 * i + half, to)

    def arrived(i, half):
        blk = part_of(flip_bits(p, i) * 2 + c, half)
        remote(blk, blk, wsend, wrecv, 2 * i + half, mate).wait_recv()

    def relay(i):
        blk = part_of(flip_bits(p, i) * 2 + c, i - 1)
        return remote(blk, blk, wsend, wrecv, 5 + i, (flip_bits(p, 3 - i) * 2 + c, f))

    def relayed(half):
        blk = part_of(flip_bits(p, 3) * 2 + c, half)
        return remote(blk, blk, wsend, wrecv, 6 + half, mate)

    def corner(half, core):
        blk = part_of(flip_bits(p, 3) * 2 + core, half)
        return remote(blk, blk, wsend, wrecv, 10 + half, mate)

    square = P_ == 4
    if square:
        for first in range(2):
            for i in (1, 2):
                direct(i, first if i == 1 else 1 - first).start()
    else:
        for i in range(1, P_):
            spread(P_ - i).start()
    near = remote(wv, wm.at[:, s], wsend, wrecv, 0, mate)
    near.start()
    wt[...] = jnp.transpose(w[...])

    rows = 64

    def project(b, _):
        slot = lax.rem(b, 2)
        fetch(b).wait()

        @pl.when(b + 1 < S)
        def _():
            fetch(b + 1).start()

        @pl.when(b >= 2)
        def _():
            store(b - 2).wait()

        def norm(k, _):
            at = pl.ds(pl.multiple_of(k * rows, rows), rows)
            v = xb[slot, at, :].astype(f32)
            r = lax.rsqrt(jnp.mean(v * v, axis=-1, keepdims=True) + eps_norm)
            nb[slot, at, :] = (v * r * g1[...]).astype(bf)
            return 0

        lax.fori_loop(0, T // rows, norm, 0)
        store(b).start()
        cols = pl.ds(pl.multiple_of(b * T, T), T)
        res = dot(wt[...], nb[slot], 1, 1)
        qt[:, cols] = (res[:C] * sc[...]).astype(bf)
        kt[:, cols] = res[C : 2 * C].astype(bf)
        vt[:, cols] = res[2 * C :].astype(bf)
        for h in range(nh):
            kk[h, cols, :] = jnp.transpose(res[C + h * HD : C + (h + 1) * HD]).astype(bf)
        return 0

    lax.fori_loop(0, S, project, 0)
    if square:
        for i in (1, 2):
            arrived(i, i - 1)
            relay(i).start()
    store(S - 2).wait()
    store(S - 1).wait()

    def attend(t):
        first = pl.multiple_of(t * BQ, BQ)
        q = [qt[h * HD : (h + 1) * HD, pl.ds(first, BQ)] for h in range(nh)]

        def step(j, carry, diag=None):
            at = pl.ds(pl.multiple_of(j * BK, BK), BK)
            scores = [dot(kk[h, at, :], q[h]) for h in range(nh)]
            out = []
            for h in range(nh):
                m, l, acc = carry[h]
                sh = scores[h]
                if diag is not None:
                    kp = lax.broadcasted_iota(jnp.int32, sh.shape, 0) + diag * BK
                    qp = lax.broadcasted_iota(jnp.int32, sh.shape, 1)
                    sh = jnp.where(kp <= qp, sh, NEG)
                mn = jnp.maximum(m, jnp.max(sh, axis=0, keepdims=True))
                a = jnp.exp(m - mn)
                e = jnp.exp(sh - mn)
                l = l * a + jnp.sum(e, axis=0, keepdims=True)
                acc = acc * a + dot(vt[h * HD : (h + 1) * HD, at], e.astype(bf))
                out.append((mn, l, acc))
            return tuple(out)

        carry = tuple(
            (jnp.full((1, BQ), NEG, f32), jnp.zeros((1, BQ), f32), jnp.zeros((HD, BQ), f32))
            for _ in range(nh)
        )
        r = BQ // BK
        carry = lax.fori_loop(0, t * r, step, carry)
        for d in range(r):
            carry = step(t * r + d, carry, d)
        for h in range(nh):
            m, l, acc = carry[h]
            ot[h * HD : (h + 1) * HD, pl.ds(first, BQ)] = (acc / l).astype(bf)
            lse[h : h + 1, pl.ds(first, BQ)] = m + jnp.log(l)

    def to_owner(src, n, to):
        return pltpu.make_async_remote_copy(
            src_ref=src,
            dst_ref=mixed.at[s],
            send_sem=osend.at[n],
            recv_sem=orecv.at[n - n % 2 + c],
            device_id=to,
            device_id_type=MESH,
        )

    def send(i, half):
        t = flip_bits(p, i)
        src = ot.at[:, pl.ds(pl.multiple_of(t * BQ + half * T, T), T)]
        return to_owner(src, 2 * i + half, (t * 2 + half, f))

    for i in range(1, P_):
        attend(flip_bits(p, P_ - i))
        send(P_ - i, 0).start()
        send(P_ - i, 1).start()
        if not square:
            spread(P_ - i).wait_recv()
            forward(P_ - i).start()
        elif i < 3:
            arrived(3 - i, i - 1)
            forward(3 - i).start()
        else:
            for half in range(2):
                relayed(half).wait_recv()
                corner(half, c).start()
    attend(p)
    mine = ot.at[:, pl.ds(pl.multiple_of(s * T, T), T)]
    theirs = ot.at[:, pl.ds(pl.multiple_of((p * 2 + other) * T, T), T)]
    last = to_owner(theirs, 0, mate)
    last.start()
    own = pltpu.make_async_copy(mine, mixed.at[s], local.at[1])
    own.start()
    def from_source(i, core):
        return pltpu.make_async_remote_copy(
            src_ref=mine,
            dst_ref=mixed.at[flip_bits(p, i) * 2 + core],
            send_sem=osend.at[0],
            recv_sem=orecv.at[2 * i + core],
            device_id=mate,
            device_id_type=MESH,
        )

    for i in range(1, P_):
        for core in range(2):
            from_source(i, core).wait_recv()
    from_source(0, other).wait_recv()
    last.wait_send()
    own.wait()
    keep.wait()
    near.wait()
    if square:
        for i in (1, 2):
            forward(i).wait()
            relay(i).wait_send()
            for half in range(2):
                direct(i, half).wait_send()
        for half in range(2):
            corner(half, c).wait_send()
            corner(half, other).wait_recv()
    for i in range(1, P_):
        if not square:
            forward(i).wait()
            spread(i).wait_send()
        send(i, 0).wait_send()
        send(i, 1).wait_send()


def forward_all(S, F, nh, x_all, w, g1, sc, wz):
    T, D = x_all.shape[1], x_all.shape[2]
    C = nh * HD
    L = S * T
    P_ = S // 2
    any_ = pl.BlockSpec(memory_space=pl.ANY)
    vm = pl.BlockSpec(memory_space=pltpu.VMEM)
    dma = pltpu.SemaphoreType.DMA
    shape = jax.ShapeDtypeStruct
    NW, R = wz.shape[0], wz.shape[2]
    V = pltpu.VMEM
    return pl.pallas_call(
        functools.partial(forward_kernel, S, F, nh),
        out_shape=[
            shape((S, T, D), bf),
            shape((C, L), bf),
            shape((C, L), bf),
            shape((C, L), bf),
            shape((C, L), bf),
            shape((nh, L), f32),
            shape((S, C, T), bf),
            shape((NW, S, F, R, D), bf),
        ],
        in_specs=[any_, vm, vm, vm, any_],
        out_specs=[any_, vm, vm, vm, vm, vm, any_, any_],
        scratch_shapes=[
            V((3 * C, D), bf),
            V((nh, L, HD), bf),
            V((2, T, D), bf),
            V((2, T, D), bf),
            V((NW, F, R, D), bf),
            dma((2,)),
            dma((2,)),
            dma((2,)),
            dma((2 * P_,)),
            dma((2 * P_,)),
            dma((max(2 * P_, 12),)),
            dma((max(2 * P_, 12),)),
        ],
        compiler_params=pltpu.CompilerParams(
            collective_id=3, has_side_effects=True, vmem_limit_bytes=60 << 20
        ),
        name="forward",
    )(x_all, w, g1, sc, wz)


def xor(a, b, n):
    out, bit = 0, 1
    while bit < n:
        both = lax.rem(lax.div(a, bit), 2) + lax.rem(lax.div(b, bit), 2)
        out = out + bit * lax.rem(both, 2)
        bit *= 2
    return out


def backward_kernel(S, F, nh, dm, qt, kt, vt, ot, lse, n1, x_all, w, sc, g1, g, vec, dx2,
                    g_out, in_out, q_out, vec_out, gi, gp,
                    dmt, wt, dwt, ab, fm, tm, nx, xx, rr, mb, own, bi, bp, ga, gb, gz, qi, qo,
                    vi, vz, vp, gf, gs_, local, nsem, bload,
                    gsend, grecv, bsend, brecv, qsend, qrecv, vsend, vrecv):
    s, f, p, c = spots()
    P_ = S // 2
    T, D = x_all.shape[1], x_all.shape[2]
    C = nh * HD
    L = S * T
    BQ = 2 * T
    BK = min(512, BQ)
    NW, R = g.shape[0], g.shape[3]
    other = 1 - c
    mate = (p * 2 + other, f)
    todo = []

    def go(copy):
        copy.start()
        todo.append(copy)

    def chip(i):
        return flip_bits(p, i)

    def deep(i):
        return lax.rem(f + i, F)

    def head(ref, h, at):
        return ref[h * HD : (h + 1) * HD, at]

    loads = [
        pltpu.make_async_copy(dm.at[b], dmt.at[:, b * T : (b + 1) * T], bload.at[b])
        for b in range(S)
    ]
    for load in loads:
        load.start()
    greet(S, F)

    def swap(i):
        t = chip(i)
        return remote(g.at[:, t * 2 + other], gi.at[i], gsend, grecv, i, mate)

    order = list(range(P_ - 1, -1, -1))
    for i in order:
        swap(i).start()
    wt[...] = jnp.transpose(w[...])
    dwt[...] = jnp.zeros_like(dwt)
    gf[...] = jnp.zeros_like(gf)
    gs_[...] = jnp.zeros_like(gs_)
    for load in loads:
        load.wait()

    def slabs(body):
        def one(n, _):
            body(lax.div(n, F), lax.rem(n, F))
            return 0

        lax.fori_loop(0, NW * F, one, 0)

    def out_g(i):
        return remote(gi.at[i], gp.at[i], gsend, grecv, P_ + i, (chip(i) * 2 + c, f))

    def sum_pairs():
        for i in order:
            la = pltpu.make_async_copy(g.at[:, chip(i) * 2 + c], ga, local.at[1])
            la.start()
            swap(i).wait_recv()
            lb = pltpu.make_async_copy(gi.at[i], gb, local.at[2])
            lb.start()
            la.wait()
            lb.wait()

            def add(a, z):
                ga[a, z] = (ga[a, z].astype(f32) + gb[a, z].astype(f32)).astype(bf)

            slabs(add)
            st = pltpu.make_async_copy(ga, gi.at[i], local.at[1])
            st.start()
            st.wait()
            if i:
                out_g(i).start()

    rows = 64
    wide = 256 if D % 256 == 0 else D

    def over(i):
        return remote(mb, bi.at[i], bsend, brecv, i, mate)

    def out_b(i, t):
        return pltpu.make_async_remote_copy(
            src_ref=bi.at[i],
            dst_ref=bp.at[i - 1],
            send_sem=bsend.at[P_ + i],
            recv_sem=brecv.at[P_ + i],
            device_id=(t * 2 + c, f),
            device_id_type=MESH,
        )

    def attention(q, k, v, do, delta, dqt, dk, dv):
        dqt[...] = jnp.zeros_like(dqt)
        dk[...] = jnp.zeros_like(dk)
        dv[...] = jnp.zeros_like(dv)

        def turn(b, _):
            at = pl.ds(pl.multiple_of(b * T, T), T)
            va = pltpu.make_async_copy(vt.at[:, at], ab.at[0], nsem.at[0])
            oa = pltpu.make_async_copy(ot.at[:, at], ab.at[1], nsem.at[1])
            va.start()
            oa.start()
            for h in range(nh):
                q[h, at, :] = jnp.transpose(head(qt, h, at))
                k[h, at, :] = jnp.transpose(head(kt, h, at))
                do[h, at, :] = jnp.transpose(head(dmt, h, at))
            va.wait()
            oa.wait()
            for h in range(nh):
                v[h, at, :] = jnp.transpose(ab[0, h * HD : (h + 1) * HD, :])
                old = ab[1, h * HD : (h + 1) * HD, :].astype(f32)
                prod = head(dmt, h, at).astype(f32) * old
                delta[h : h + 1, at] = jnp.sum(prod, axis=0, keepdims=True)
            return 0

        lax.fori_loop(0, S, turn, 0)

        sum_pairs()

        def tile(q0, k0, masked):
            qa = pl.ds(q0, BK)
            ka = pl.ds(k0, BK)
            scores = [dot(k[h, ka, :], head(qt, h, qa)) for h in range(nh)]
            dps = [dot(v[h, ka, :], head(dmt, h, qa)) for h in range(nh)]
            for h in range(nh):
                e = jnp.exp(scores[h] - lse[h : h + 1, qa])
                if masked:
                    kp = lax.broadcasted_iota(jnp.int32, e.shape, 0)
                    qp = lax.broadcasted_iota(jnp.int32, e.shape, 1)
                    e = jnp.where(kp <= qp, e, 0.0)
                ds = (e * (dps[h] - delta[h : h + 1, qa])).astype(bf)
                dv[h, ka, :] += dot(e.astype(bf), do[h, qa, :])
                dk[h, ka, :] += dot(ds, q[h, qa, :])
                dqt[h * HD : (h + 1) * HD, qa] += dot(head(kt, h, ka), ds)

        r = BQ // BK

        def rect(qb, kb):
            def one(n, _):
                q0 = pl.multiple_of(qb * BQ + lax.div(n, r) * BK, BK)
                k0 = pl.multiple_of(kb * BQ + lax.rem(n, r) * BK, BK)
                tile(q0, k0, False)
                return 0

            lax.fori_loop(0, r * r, one, 0)

        def triangle(t):
            def one(n, _):
                at = pl.multiple_of(t * BQ + n * BK, BK)
                tile(at, at, True)

                def below(j, _):
                    tile(at, pl.multiple_of(t * BQ + j * BK, BK), False)
                    return 0

                lax.fori_loop(0, n, below, 0)
                return 0

            lax.fori_loop(0, r, one, 0)

        def fetch(t, half):
            b = t * 2 + half
            return (
                pltpu.make_async_copy(n1.at[b], nx, nsem.at[0]),
                pltpu.make_async_copy(x_all.at[b], xx, nsem.at[1]),
            )

        def finish(t, half, dst):
            for copy in fetch(t, half):
                copy.start()
            at = pl.ds(pl.multiple_of((t * 2 + half) * T, T), T)
            dqs = dqt[:, at].astype(bf)
            dqf = dqs.astype(f32)
            gs_[...] += jnp.sum(dqf * qt[:, at].astype(f32), axis=1, keepdims=True)
            fm[:C, :] = (dqf * sc[...]).astype(bf)
            for h in range(nh):
                fm[C + h * HD : C + (h + 1) * HD, :] = jnp.transpose(dk[h, at, :]).astype(bf)
                fm[2 * C + h * HD : 2 * C + (h + 1) * HD, :] = jnp.transpose(dv[h, at, :]).astype(bf)
            tm[...] = jnp.transpose(fm[...])
            for copy in fetch(t, half):
                copy.wait()

            def inverse(n, _):
                a = pl.ds(pl.multiple_of(n * rows, rows), rows)
                z = xx[a, :].astype(f32)
                rr[a, :] = lax.rsqrt(jnp.mean(z * z, axis=-1, keepdims=True) + eps_norm)
                return 0

            lax.fori_loop(0, T // rows, inverse, 0)

            def column(n, _):
                a = pl.ds(pl.multiple_of(n * wide, wide), wide)
                back = dot(tm[...], wt[:, a])
                dst[:, a] = back.astype(bf)
                hat = xx[:, a].astype(f32) * rr[...]
                gf[:, a] += jnp.sum(back * hat, axis=0, keepdims=True)
                dwt[:, a] += dot(fm[...], nx[:, a])
                return 0

            lax.fori_loop(0, D // wide, column, 0)

        def combine(i):
            def one(n, _):
                a = pl.ds(pl.multiple_of(n * rows, rows), rows)
                bi[i, a, :] = (bi[i, a, :].astype(f32) + own[a, :].astype(f32)).astype(bf)
                return 0

            lax.fori_loop(0, T // rows, one, 0)

        def advance(i, t, last):
            def pair(m, _):
                u = xor(p, m, P_)
                rect(jnp.maximum(t, u), jnp.minimum(t, u))
                return 0

            lax.fori_loop(0, i, pair, 0)
            triangle(t)
            if not last:

                @pl.when(i < P_ - 1)
                def _():
                    over(i + 1).wait_send()

            else:
                over(1).wait_send()
            finish(t, other, mb)
            over(i).start()
            finish(t, c, own)
            over(i).wait_recv()
            combine(i)
            if not last:
                out_b(i, t).start()

        def stage(n, _):
            i = P_ - 1 - n
            advance(i, xor(p, i, P_), False)
            return 0

        lax.fori_loop(0, P_ - 1, stage, 0)
        advance(0, p, True)


    V = pltpu.VMEM
    pl.run_scoped(
        attention,
        V((nh, L, HD), bf),
        V((nh, L, HD), bf),
        V((nh, L, HD), bf),
        V((nh, L, HD), bf),
        V((nh, L), f32),
        V((C, L), f32),
        V((nh, L, HD), f32),
        V((nh, L, HD), f32),
    )

    def closing(dw, up, qm, qs_, go_, vo):
        up_load = pltpu.make_async_copy(dx2, up, local.at[0])
        up_load.start()
        x_load = pltpu.make_async_copy(x_all.at[s], xx, nsem.at[1])
        x_load.start()
        vi[...] = vec[...]
        vi[0:1, :] = gf[...]
        turned = jnp.transpose(jnp.broadcast_to(gs_[...], (C, 128)))
        vi[4:5, 0:C] = turned[0:1, :]
        for i in range(1, F):
            go(remote(vi, vz.at[i], vsend, vrecv, i, (s, deep(i))))
        dw[...] = jnp.transpose(dwt[...])

        bunch = 8 // math.gcd(R, 8)

        def piece(n, _):
            part = dw[pl.ds(pl.multiple_of(n * (bunch * R), 8), bunch * R), :]
            for j in range(bunch):
                to = n * bunch + j
                qm[lax.div(to, F), lax.rem(to, F)] = part[j * R : (j + 1) * R].astype(bf)
            return 0

        lax.fori_loop(0, S * F // bunch, piece, 0)
        for i in range(1, F):
            go(remote(qm.at[:, deep(i)], qi.at[i], qsend, qrecv, i, (s, deep(i))))
        la = pltpu.make_async_copy(gi.at[0], ga, local.at[1])
        la.start()
        la.wait()
        for i in order[:-1]:
            out_g(i).wait_recv()
            lb = pltpu.make_async_copy(gp.at[i], gb, local.at[2])
            lb.start()
            lb.wait()

            def more(a, z):
                ga[a, z] = (ga[a, z].astype(f32) + gb[a, z].astype(f32)).astype(bf)

            slabs(more)
        for i in range(1, F):
            go(remote(ga.at[:, deep(i)], gz.at[i], gsend, grecv, 2 * P_ + i, (s, deep(i))))
        total = vi[...]
        for i in range(1, F):
            remote(vi, vz.at[i], vsend, vrecv, i, mate).wait_recv()
            total = total + vz[i]
        vp[0] = total
        for i in range(1, S):
            go(remote(vp.at[0], vp.at[i], vsend, vrecv, F - 1 + i, (lax.rem(s + i, S), f)))
        for i in range(1, F):
            remote(qm.at[:, f], qi.at[i], qsend, qrecv, i, mate).wait_recv()

        def sum_q(n, _):
            part = qm[n, f].astype(f32)
            for i in range(1, F):
                part = part + qi[i, n].astype(f32)
            qs_[n] = part.astype(bf)
            return 0

        lax.fori_loop(0, S, sum_q, 0)
        keep = pltpu.make_async_copy(qs_.at[s], qo.at[s], local.at[1])
        keep.start()
        for i in range(1, S):
            to = lax.rem(s + i, S)
            go(remote(qs_.at[to], qo.at[s], qsend, qrecv, F - 1 + i, (to, f)))
        up_load.wait()
        x_load.wait()
        over(0).wait_send()
        for i in order[:-1]:
            out_b(i, chip(i)).wait_recv()

        def below(n, _):
            a = pl.ds(pl.multiple_of(n * rows, rows), rows)
            back = bi[0, a, :].astype(f32)
            for i in range(1, P_):
                back = back + bp[i - 1, a, :].astype(f32)
            z = xx[a, :].astype(f32)
            r1 = lax.rsqrt(jnp.mean(z * z, axis=-1, keepdims=True) + eps_norm)
            e1 = back * g1[...]
            tilt = jnp.mean(e1 * z, axis=-1, keepdims=True)
            mb[a, :] = (up[a, :] + r1 * e1 - z * (r1 * r1 * r1 * tilt)).astype(bf)
            return 0

        lax.fori_loop(0, T // rows, below, 0)
        outs = [pltpu.make_async_copy(mb, in_out, local.at[0])]
        outs[0].start()
        for i in range(1, F):
            remote(ga.at[:, f], gz.at[i], gsend, grecv, 2 * P_ + i, mate).wait_recv()
        for a in range(NW):
            part = ga[a, f].astype(f32)
            for i in range(1, F):
                part = part + gz[i, a].astype(f32)
            go_[a] = part
        outs.append(pltpu.make_async_copy(go_, g_out, local.at[2]))
        outs[1].start()
        total = vp[0]
        for i in range(1, S):
            remote(vp.at[0], vp.at[i], vsend, vrecv, F - 1 + i, mate).wait_recv()
            total = total + vp[i]
        vo[...] = total
        outs.append(pltpu.make_async_copy(vo, vec_out, nsem.at[0]))
        outs[2].start()
        for i in range(1, S):
            src = lax.rem(s + S - i, S)
            remote(qs_.at[0], qo.at[src], qsend, qrecv, F - 1 + i, mate).wait_recv()
        keep.wait()
        outs.append(pltpu.make_async_copy(qo, q_out, local.at[1]))
        outs[3].start()
        for out in outs:
            out.wait()
        for copy in todo:
            copy.wait_send()
        for i in range(P_):
            swap(i).wait_send()
        for i in range(1, P_):
            out_g(i).wait_send()
            out_b(i, chip(i)).wait_send()

    pl.run_scoped(
        closing,
        V((D, 3 * C), f32),
        V((T, D), f32),
        V((S, F, R, 3 * C), bf),
        V((S, R, 3 * C), bf),
        V((NW, R, D), f32),
        V(vec.shape, f32),
    )


def backward_all(S, F, nh, dm, qt, kt, vt, ot, lse, n1, x_all, w, sc, g1, g, vec, dx2):
    T, D = x_all.shape[1], x_all.shape[2]
    C = nh * HD
    L = S * T
    P_ = S // 2
    NW, R = g.shape[0], g.shape[3]
    any_ = pl.BlockSpec(memory_space=pl.ANY)
    vm = pl.BlockSpec(memory_space=pltpu.VMEM)
    dma = pltpu.SemaphoreType.DMA
    shape = jax.ShapeDtypeStruct
    V = pltpu.VMEM
    return pl.pallas_call(
        functools.partial(backward_kernel, S, F, nh),
        out_shape=[
            shape((NW, R, D), f32),
            shape((T, D), bf),
            shape((S, R, 3 * C), bf),
            shape(vec.shape, f32),
            shape((P_, NW, F, R, D), bf),
            shape((P_, NW, F, R, D), bf),
        ],
        in_specs=[any_, vm, vm, any_, any_, vm, any_, any_, vm, vm, vm, any_, vm, any_],
        out_specs=[any_] * 6,
        scratch_shapes=[
            V((C, L), bf),
            V((3 * C, D), bf),
            V((3 * C, D), f32),
            V((2, C, T), bf),
            V((3 * C, T), bf),
            V((T, 3 * C), bf),
            V((T, D), bf),
            V((T, D), bf),
            V((T, 1), f32),
            V((T, D), bf),
            V((T, D), bf),
            V((P_, T, D), bf),
            V((P_ - 1, T, D), bf),
            V((NW, F, R, D), bf),
            V((NW, F, R, D), bf),
            V((F, NW, R, D), bf),
            V((F, S, R, 3 * C), bf),
            V((S, R, 3 * C), bf),
            V(vec.shape, f32),
            V((F,) + vec.shape, f32),
            V((S,) + vec.shape, f32),
            V((1, D), f32),
            V((C, 1), f32),
            dma((3,)),
            dma((2,)),
            dma((S,)),
            dma((2 * P_ + F,)),
            dma((2 * P_ + F,)),
            dma((2 * P_,)),
            dma((2 * P_,)),
            dma((S + F,)),
            dma((S + F,)),
            dma((S + F,)),
            dma((S + F,)),
        ],
        compiler_params=pltpu.CompilerParams(
            collective_id=4, has_side_effects=True, vmem_limit_bytes=66_000_000
        ),
        name="backward",
    )(dm, qt, kt, vt, ot, lse, n1, x_all, w, sc, g1, g, vec, dx2)


def body(
    inputs,
    w_query,
    w_key,
    w_value,
    w_proj,
    w_up,
    w_down,
    gain_first,
    gain_second,
    bias_up,
    bias_down,
    query_scale,
    cotangent,
):
    groups = lax.axis_size("seq")
    rows_of = lax.axis_size("fsdp")
    nh = H // groups
    cols = nh * HD
    both = ("seq", "fsdp")
    tokens, width = inputs.shape[1], inputs.shape[2]
    length = tokens * groups
    shard = w_query.shape[0]
    x_low = inputs.reshape(tokens, width)
    qkv_rows = jnp.stack([w_query, w_key, w_value], 1).astype(bf).reshape(shard, 3, groups, cols)
    qkv_rows = qkv_rows.transpose(2, 0, 1, 3).reshape(groups, shard, 3 * cols)
    small = jnp.stack([gain_first, gain_second, bias_up, bias_down], 0)
    small = jnp.pad(small.astype(bf), ((0, 12), (0, 128 - shard)))
    weights = jnp.stack([w_proj, w_up, w_down], 0).astype(bf)
    x_all, qkv_w, small, weights = gather_all(groups, rows_of, x_low, qkv_rows, small, weights)
    qkv_w = qkv_w.reshape(width, 3 * cols)
    small = small[:, :, :4, :shard].transpose(2, 0, 1, 3).reshape(4, width).astype(f32)
    first_gain, second_gain, upbias, downbias = small[0], small[1], small[2], small[3]
    scale_dims = jax.nn.softplus(query_scale) * log_two_inverse / math.sqrt(HD)
    scale_cols = jnp.tile(scale_dims, nh)
    normed, qt, kt, vt, ot, lse, mixed, weights = forward_all(
        groups, rows_of, nh, x_all, qkv_w, small[:1], scale_cols[:, None], weights
    )
    weights = weights.reshape(3, width, width)
    proj_w, up_w, down_w = weights[0], weights[1], weights[2]
    mixed = mixed.reshape(width, tokens)
    float_in = x_low.astype(f32)
    middle = float_in + dot(mixed, proj_w, 0, 0)
    second = rms_scale(middle, second_gain).astype(bf)
    hidden = jnp.dot(second, up_w, preferred_element_type=f32) + upbias
    active = jax.nn.silu(hidden).astype(bf)
    result = middle + jnp.dot(active, down_w, preferred_element_type=f32) + downbias

    top_low = cotangent.reshape(tokens, width)
    grad_top = top_low.astype(f32)
    grad_bdown = jnp.sum(grad_top, axis=0)
    grad_wdown = dot(active, top_low, 0, 0)
    grad_active = dot(top_low, down_w, 1, 1)
    gate = 1 / (1 + jnp.exp(-hidden))
    grad_hidden = grad_active * (gate * (1 + hidden * (1 - gate)))
    grad_bup = jnp.sum(grad_hidden, axis=0)
    hidden_low = grad_hidden.astype(bf)
    grad_wup = dot(second, hidden_low, 0, 0)
    grad_second_in = dot(hidden_low, up_w, 1, 1)
    unused_second, second_pull = jax.vjp(rms_scale, middle, second_gain)
    grad_middle, grad_gsecond = second_pull(grad_second_in)
    grad_middle = grad_middle + grad_top
    middle_low = grad_middle.astype(bf)
    grad_wproj = dot(mixed, middle_low, 1, 0)
    grad_mixed = dot(proj_w, middle_low, 1, 1).astype(bf)
    dm = lax.all_to_all(grad_mixed.reshape(groups, cols, tokens), "seq", 0, 0)
    zeros = jnp.zeros((width,), f32)
    vectors = jnp.stack([zeros, grad_gsecond, grad_bup, grad_bdown] + [zeros] * 4, 0)
    stacked = jnp.stack([grad_wproj.astype(bf), grad_wup.astype(bf), grad_wdown.astype(bf)], 0)
    owned, grad_inputs, grad_qkv, vectors, unused_pair, unused_plane = backward_all(
        groups,
        rows_of,
        nh,
        dm,
        qt,
        kt,
        vt,
        ot,
        lse,
        normed,
        x_all,
        qkv_w,
        scale_cols[:, None],
        small[:1],
        stacked.reshape(3, groups, rows_of, shard, width),
        vectors,
        grad_middle,
    )
    grad_qkv = grad_qkv.reshape(groups, shard, 3, cols).transpose(2, 1, 0, 3)
    grad_qkv = grad_qkv.reshape(3, shard, width).astype(f32)
    at = (lax.axis_index("seq") * rows_of + lax.axis_index("fsdp")) * shard
    mine = lax.dynamic_slice_in_dim(vectors, at, shard, 1)
    scale_total = jnp.sum(vectors[4, :cols].reshape(nh, HD), axis=0) / scale_dims
    grad_scale = scale_total * jax.nn.sigmoid(query_scale) * log_two_inverse / math.sqrt(HD)
    return (
        result.astype(bf).reshape(inputs.shape),
        grad_inputs.reshape(inputs.shape),
        grad_qkv[0],
        grad_qkv[1],
        grad_qkv[2],
        owned[0],
        owned[1],
        owned[2],
        mine[0],
        mine[1],
        mine[2],
        mine[3],
        grad_scale,
    )


def solution(mesh):
    return jax.shard_map(
        body,
        mesh=mesh,
        in_specs=(
            P("fsdp", "seq", None),
            P(("seq", "fsdp"), None),
            P(("seq", "fsdp"), None),
            P(("seq", "fsdp"), None),
            P(("seq", "fsdp"), None),
            P(("seq", "fsdp"), None),
            P(("seq", "fsdp"), None),
            P(("seq", "fsdp")),
            P(("seq", "fsdp")),
            P(("seq", "fsdp")),
            P(("seq", "fsdp")),
            P(),
            P("fsdp", "seq", None),
        ),
        out_specs=(
            P("fsdp", "seq", None),
            P("fsdp", "seq", None),
            P(("seq", "fsdp"), None),
            P(("seq", "fsdp"), None),
            P(("seq", "fsdp"), None),
            P(("seq", "fsdp"), None),
            P(("seq", "fsdp"), None),
            P(("seq", "fsdp"), None),
            P(("seq", "fsdp")),
            P(("seq", "fsdp")),
            P(("seq", "fsdp")),
            P(("seq", "fsdp")),
            P(),
        ),
        check_vma=False,
    )
```

```python
import functools
import math

import jax
import jax.numpy as jnp
from jax import lax
from jax.experimental import pallas as pl
from jax.experimental.pallas import tpu as pltpu
from jax.sharding import PartitionSpec as P

H = 16
HD = 80
eps_norm = 1e-06
log_two_inverse = 1.442695
bf = jnp.bfloat16
f32 = jnp.float32
NEG = -1e30


def dot(a,b,ca=1,cb=0):
    return lax.dot_general(a,b,(((ca,),(cb,)),((),())),preferred_element_type=f32)


MESH = pl.DeviceIdType.MESH


def spots():
    s, f = lax.axis_index("seq"), lax.axis_index("fsdp")
    return s, f, s // 2, lax.rem(s, 2)


def greet(S, F):
    s, f, _, _ = spots()
    barrier = pltpu.get_barrier_semaphore()
    for i in range(1, S):
        pl.semaphore_signal(barrier, inc=1, device_id=(lax.rem(s + i, S), f), device_id_type=MESH)
    for i in range(1, F):
        pl.semaphore_signal(barrier, inc=1, device_id=(s, lax.rem(f + i, F)), device_id_type=MESH)
    pl.semaphore_wait(barrier, S + F - 2)


def remote(src, dst, sends, recvs, n, to):
    return pltpu.make_async_remote_copy(
        src_ref=src,
        dst_ref=dst,
        send_sem=sends.at[n],
        recv_sem=recvs.at[n],
        device_id=to,
        device_id_type=MESH,
    )


def gather_kernel(S, F, x, wq, sm, wm, x_all, wq_all, sm_all, wm_all, xv, qv, sv, mv, local,
                  xs, xr, qs, qr, ss, sr, ms, mr):
    s, f, p, c = spots()
    P_ = S // 2
    other = 1 - c
    loads = [
        pltpu.make_async_copy(sm, sv, local.at[0]),
        pltpu.make_async_copy(wq, qv, local.at[1]),
        pltpu.make_async_copy(x, xv, local.at[2]),
        pltpu.make_async_copy(wm, mv, local.at[3]),
    ]
    for load in loads:
        load.start()
    greet(S, F)
    mate = (p * 2 + other, f)
    todo = []

    def go(copy):
        copy.start()
        todo.append(copy)

    def chip(i):
        return lax.rem(p + i, P_) * 2 + c

    def back(i):
        return lax.rem(p + P_ - i, P_) * 2 + c

    def near_chip(i):
        return flip_bits(p, i) * 2 + c

    H_ = x.shape[0] // 2

    def deep(i):
        return lax.rem(f + i, F)

    def behind(i):
        return lax.rem(f + F - i, F)

    loads[0].wait()
    keep0 = pltpu.make_async_copy(sv, sm_all.at[s, f], local.at[0])
    keep0.start()
    for i in range(1, F):
        go(remote(sv, sm_all.at[s, f], ss, sr, i, (s, deep(i))))
    loads[1].wait()
    keep1 = pltpu.make_async_copy(qv.at[s], wq_all.at[s, f], local.at[1])
    keep1.start()
    for i in range(1, S):
        to = lax.rem(s + i, S)
        go(remote(qv.at[to], wq_all.at[s, f], qs, qr, i, (to, f)))
    loads[2].wait()
    keep2 = pltpu.make_async_copy(xv, x_all.at[s], local.at[2])
    keep2.start()
    if P_ == 4:
        for first in range(2):
            for i in (1, 2):
                half = first if i == 1 else 1 - first
                part = pl.ds(half * H_, H_)
                go(remote(xv.at[part], x_all.at[s, part], xs, xr, 2 * i + half, (near_chip(i), f)))
    else:
        for i in range(1, P_):
            go(remote(xv, x_all.at[s], xs, xr, i, (chip(i), f)))
    go(remote(xv, x_all.at[s], xs, xr, 0, mate))
    loads[3].wait()
    keep3 = pltpu.make_async_copy(mv, wm_all.at[:, f], local.at[3])
    keep3.start()
    for i in range(1, F):
        go(remote(mv, wm_all.at[:, f], ms, mr, i, (s, deep(i))))
    for i in range(1, F):
        g = behind(i)
        remote(sv, sm_all.at[s, g], ss, sr, i, mate).wait_recv()
    keep0.wait()
    for i in range(1, S):
        go(remote(sm_all.at[s], sm_all.at[s], ss, sr, F - 1 + i, (lax.rem(s + i, S), f)))
    for i in range(1, S):
        remote(qv.at[0], wq_all.at[lax.rem(s + S - i, S), f], qs, qr, i, mate).wait_recv()
    keep1.wait()
    for i in range(1, F):
        go(remote(wq_all.at[:, f], wq_all.at[:, f], qs, qr, S - 1 + i, (s, deep(i))))
    for i in range(1, F):
        remote(mv, wm_all.at[:, behind(i)], ms, mr, i, mate).wait_recv()
    keep3.wait()
    if P_ == 4:
        for i in (1, 2):
            half = i - 1
            part = pl.ds(half * H_, H_)
            src = near_chip(i)
            remote(xv.at[part], x_all.at[src, part], xs, xr, 2 * i + half, mate).wait_recv()
            blk = x_all.at[src, part]
            go(remote(blk, blk, xs, xr, 6 + half, (near_chip(3 - i), f)))
        for i in (1, 2):
            half = 2 - i
            part = pl.ds(half * H_, H_)
            src = near_chip(i)
            remote(xv.at[part], x_all.at[src, part], xs, xr, 2 * i + half, mate).wait_recv()
            go(remote(x_all.at[src], x_all.at[src], xs, xr, 8 + i, mate))
    for i in range(1, P_ if P_ != 4 else 1):
        src = back(i)
        remote(xv, x_all.at[src], xs, xr, i, mate).wait_recv()
        go(remote(x_all.at[src], x_all.at[src], xs, xr, P_ - 1 + i, mate))
    for i in range(1, S):
        src = lax.rem(s + S - i, S)
        remote(sm_all.at[src], sm_all.at[src], ss, sr, F - 1 + i, mate).wait_recv()
    for i in range(1, F):
        g = behind(i)
        remote(wq_all.at[:, g], wq_all.at[:, g], qs, qr, S - 1 + i, mate).wait_recv()
    near = p * 2 + other
    remote(xv, x_all.at[near], xs, xr, 0, mate).wait_recv()
    if P_ == 4:
        for half in range(2):
            part = pl.ds(half * H_, H_)
            blk = x_all.at[near_chip(3), part]
            remote(blk, blk, xs, xr, 6 + half, mate).wait_recv()
            go(remote(blk, blk, xs, xr, 11 + half, mate))
        for i in (1, 2):
            blk = x_all.at[flip_bits(p, i) * 2 + other]
            remote(blk, blk, xs, xr, 8 + i, mate).wait_recv()
        for half in range(2):
            blk = x_all.at[flip_bits(p, 3) * 2 + other, pl.ds(half * H_, H_)]
            remote(blk, blk, xs, xr, 11 + half, mate).wait_recv()
    else:
        for i in range(1, P_):
            src = lax.rem(p + P_ - i, P_) * 2 + other
            remote(xv, x_all.at[src], xs, xr, P_ - 1 + i, mate).wait_recv()
    keep2.wait()
    for copy in todo:
        copy.wait_send()


def gather_all(S, F, x, wq, sm, wm):
    any_ = pl.BlockSpec(memory_space=pl.ANY)
    shapes = [
        (S,) + x.shape,
        (S, F) + wq.shape[1:],
        (S, F) + sm.shape,
        (wm.shape[0], F) + wm.shape[1:],
    ]
    P_ = S // 2
    dma = pltpu.SemaphoreType.DMA
    counts = [max(2 * P_ - 1, 12), S + F - 1, F + S - 1, F]
    sems = []
    for n in counts:
        sems += [dma((n + 1,)), dma((n + 1,))]
    return pl.pallas_call(
        functools.partial(gather_kernel, S, F),
        out_shape=[
            jax.ShapeDtypeStruct(sh, a.dtype) for sh, a in zip(shapes, (x, wq, sm, wm), strict=True)
        ],
        in_specs=[any_] * 4,
        out_specs=[any_] * 4,
        scratch_shapes=[
            pltpu.VMEM(x.shape, x.dtype),
            pltpu.VMEM(wq.shape, wq.dtype),
            pltpu.VMEM(sm.shape, sm.dtype),
            pltpu.VMEM(wm.shape, wm.dtype),
            dma((4,)),
        ]
        + sems,
        compiler_params=pltpu.CompilerParams(collective_id=1, has_side_effects=True),
        name="gather",
    )(x, wq, sm, wm)


def flip_bits(p, i):
    out, bit = p, 1
    while bit <= i:
        if i & bit:
            out = out + bit - 2 * bit * lax.rem(lax.div(p, bit), 2)
        bit *= 2
    return out


def forward_kernel(S, F, nh, x_all, w, g1, sc, wz, n1, qt, kt, qn, kk, vn, ot, lse, mixed, wm,
                   wt, vt, xb, nb, wv, inx, outn, local, osend, orecv, wsend, wrecv):
    s, f, p, c = spots()
    P_ = S // 2
    T, D = x_all.shape[1], x_all.shape[2]
    C = nh * HD
    L = S * T
    BQ = 2 * T
    BK = min(512, BQ)
    other = 1 - c
    mate = (p * 2 + other, f)
    load = pltpu.make_async_copy(wz, wv, local.at[0])
    load.start()

    def fetch(b):
        return pltpu.make_async_copy(x_all.at[b], xb.at[lax.rem(b, 2)], inx.at[lax.rem(b, 2)])

    def store(b):
        return pltpu.make_async_copy(nb.at[lax.rem(b, 2)], n1.at[b], outn.at[lax.rem(b, 2)])

    fetch(0).start()
    greet(S, F)
    load.wait()
    keep = pltpu.make_async_copy(wv, wm.at[:, s], local.at[0])
    keep.start()

    def spread(i):
        return remote(wv, wm.at[:, s], wsend, wrecv, i, (flip_bits(p, i) * 2 + c, f))

    def forward(i):
        src = flip_bits(p, i) * 2 + c
        return remote(wm.at[:, src], wm.at[:, src], wsend, wrecv, (7 if P_ == 4 else P_) + i, mate)

    def part_of(src, half):
        return wm.at[:, src, pl.ds(half * (F // 2), F // 2)]

    def direct(i, half):
        src = wv.at[:, pl.ds(half * (F // 2), F // 2)]
        to = (flip_bits(p, i) * 2 + c, f)
        return remote(src, part_of(s, half), wsend, wrecv, 2 * i + half, to)

    def arrived(i, half):
        blk = part_of(flip_bits(p, i) * 2 + c, half)
        remote(blk, blk, wsend, wrecv, 2 * i + half, mate).wait_recv()

    def relay(i):
        blk = part_of(flip_bits(p, i) * 2 + c, i - 1)
        return remote(blk, blk, wsend, wrecv, 5 + i, (flip_bits(p, 3 - i) * 2 + c, f))

    def relayed(half):
        blk = part_of(flip_bits(p, 3) * 2 + c, half)
        return remote(blk, blk, wsend, wrecv, 6 + half, mate)

    def corner(half, core):
        blk = part_of(flip_bits(p, 3) * 2 + core, half)
        return remote(blk, blk, wsend, wrecv, 10 + half, mate)

    square = P_ == 4
    if square:
        for first in range(2):
            for i in (1, 2):
                direct(i, first if i == 1 else 1 - first).start()
    else:
        for i in range(1, P_):
            spread(P_ - i).start()
    near = remote(wv, wm.at[:, s], wsend, wrecv, 0, mate)
    near.start()
    wt[...] = jnp.transpose(w[...])

    rows = 64

    def project(b, _):
        slot = lax.rem(b, 2)
        fetch(b).wait()

        @pl.when(b + 1 < S)
        def _():
            fetch(b + 1).start()

        @pl.when(b >= 2)
        def _():
            store(b - 2).wait()

        def norm(k, _):
            at = pl.ds(pl.multiple_of(k * rows, rows), rows)
            v = xb[slot, at, :].astype(f32)
            r = lax.rsqrt(jnp.mean(v * v, axis=-1, keepdims=True) + eps_norm)
            nb[slot, at, :] = (v * r * g1[...]).astype(bf)
            return 0

        lax.fori_loop(0, T // rows, norm, 0)
        store(b).start()
        cols = pl.ds(pl.multiple_of(b * T, T), T)
        res = dot(wt[...], nb[slot], 1, 1)
        qt[:, cols] = (res[:C] * sc[...]).astype(bf)
        kt[:, cols] = res[C : 2 * C].astype(bf)
        vt[:, cols] = res[2 * C :].astype(bf)
        for h in range(nh):
            part = slice(h * HD, (h + 1) * HD)
            qn[h, cols, :] = jnp.transpose(res[:C][part] * sc[part]).astype(bf)
            kk[h, cols, :] = jnp.transpose(res[C : 2 * C][part]).astype(bf)
            vn[h, cols, :] = jnp.transpose(res[2 * C :][part]).astype(bf)
        return 0

    lax.fori_loop(0, S, project, 0)
    if square:
        for i in (1, 2):
            arrived(i, i - 1)
            relay(i).start()
    store(S - 2).wait()
    store(S - 1).wait()

    def attend(t):
        first = pl.multiple_of(t * BQ, BQ)
        q = [qt[h * HD : (h + 1) * HD, pl.ds(first, BQ)] for h in range(nh)]

        def step(j, carry, diag=None):
            at = pl.ds(pl.multiple_of(j * BK, BK), BK)
            scores = [dot(kk[h, at, :], q[h]) for h in range(nh)]
            out = []
            for h in range(nh):
                m, l, acc = carry[h]
                sh = scores[h]
                if diag is not None:
                    kp = lax.broadcasted_iota(jnp.int32, sh.shape, 0) + diag * BK
                    qp = lax.broadcasted_iota(jnp.int32, sh.shape, 1)
                    sh = jnp.where(kp <= qp, sh, NEG)
                mn = jnp.maximum(m, jnp.max(sh, axis=0, keepdims=True))
                a = jnp.exp(m - mn)
                e = jnp.exp(sh - mn)
                l = l * a + jnp.sum(e, axis=0, keepdims=True)
                acc = acc * a + dot(vt[h * HD : (h + 1) * HD, at], e.astype(bf))
                out.append((mn, l, acc))
            return tuple(out)

        carry = tuple(
            (jnp.full((1, BQ), NEG, f32), jnp.zeros((1, BQ), f32), jnp.zeros((HD, BQ), f32))
            for _ in range(nh)
        )
        r = BQ // BK
        carry = lax.fori_loop(0, t * r, step, carry)
        for d in range(r):
            carry = step(t * r + d, carry, d)
        for h in range(nh):
            m, l, acc = carry[h]
            ot[h * HD : (h + 1) * HD, pl.ds(first, BQ)] = (acc / l).astype(bf)
            lse[h : h + 1, pl.ds(first, BQ)] = m + jnp.log(l)

    def to_owner(src, n, to):
        return pltpu.make_async_remote_copy(
            src_ref=src,
            dst_ref=mixed.at[s],
            send_sem=osend.at[n],
            recv_sem=orecv.at[n - n % 2 + c],
            device_id=to,
            device_id_type=MESH,
        )

    def send(i, half):
        t = flip_bits(p, i)
        src = ot.at[:, pl.ds(pl.multiple_of(t * BQ + half * T, T), T)]
        return to_owner(src, 2 * i + half, (t * 2 + half, f))

    for i in range(1, P_):
        attend(flip_bits(p, P_ - i))
        send(P_ - i, 0).start()
        send(P_ - i, 1).start()
        if not square:
            spread(P_ - i).wait_recv()
            forward(P_ - i).start()
        elif i < 3:
            arrived(3 - i, i - 1)
            forward(3 - i).start()
        else:
            for half in range(2):
                relayed(half).wait_recv()
                corner(half, c).start()
    attend(p)
    mine = ot.at[:, pl.ds(pl.multiple_of(s * T, T), T)]
    theirs = ot.at[:, pl.ds(pl.multiple_of((p * 2 + other) * T, T), T)]
    last = to_owner(theirs, 0, mate)
    last.start()
    own = pltpu.make_async_copy(mine, mixed.at[s], local.at[1])
    own.start()
    def from_source(i, core):
        return pltpu.make_async_remote_copy(
            src_ref=mine,
            dst_ref=mixed.at[flip_bits(p, i) * 2 + core],
            send_sem=osend.at[0],
            recv_sem=orecv.at[2 * i + core],
            device_id=mate,
            device_id_type=MESH,
        )

    for i in range(1, P_):
        for core in range(2):
            from_source(i, core).wait_recv()
    from_source(0, other).wait_recv()
    last.wait_send()
    own.wait()
    keep.wait()
    near.wait()
    if square:
        for i in (1, 2):
            forward(i).wait()
            relay(i).wait_send()
            for half in range(2):
                direct(i, half).wait_send()
        for half in range(2):
            corner(half, c).wait_send()
            corner(half, other).wait_recv()
    for i in range(1, P_):
        if not square:
            forward(i).wait()
            spread(i).wait_send()
        send(i, 0).wait_send()
        send(i, 1).wait_send()


def forward_all(S, F, nh, x_all, w, g1, sc, wz):
    T, D = x_all.shape[1], x_all.shape[2]
    C = nh * HD
    L = S * T
    P_ = S // 2
    any_ = pl.BlockSpec(memory_space=pl.ANY)
    vm = pl.BlockSpec(memory_space=pltpu.VMEM)
    dma = pltpu.SemaphoreType.DMA
    shape = jax.ShapeDtypeStruct
    NW, R = wz.shape[0], wz.shape[2]
    V = pltpu.VMEM
    return pl.pallas_call(
        functools.partial(forward_kernel, S, F, nh),
        out_shape=[
            shape((S, T, D), bf),
            shape((C, L), bf),
            shape((C, L), bf),
            shape((nh, L, HD), bf),
            shape((nh, L, HD), bf),
            shape((nh, L, HD), bf),
            shape((C, L), bf),
            shape((nh, L), f32),
            shape((S, C, T), bf),
            shape((NW, S, F, R, D), bf),
        ],
        in_specs=[any_, vm, vm, vm, any_],
        out_specs=[any_] + [vm] * 7 + [any_, any_],
        scratch_shapes=[
            V((3 * C, D), bf),
            V((C, L), bf),
            V((2, T, D), bf),
            V((2, T, D), bf),
            V((NW, F, R, D), bf),
            dma((2,)),
            dma((2,)),
            dma((2,)),
            dma((2 * P_,)),
            dma((2 * P_,)),
            dma((max(2 * P_, 12),)),
            dma((max(2 * P_, 12),)),
        ],
        compiler_params=pltpu.CompilerParams(
            collective_id=3, has_side_effects=True, vmem_limit_bytes=60 << 20
        ),
        name="forward",
    )(x_all, w, g1, sc, wz)


def middle_kernel(S, F, nh, mixed, x, ct, wm, small, out, dx2, dm, gi, vec,
                  mx, lt, xv, cv, wv, x2, n2, dn, ab, ub, eb, r2, sb, rb, ob, dov, rv, local, wsem,
                  dsend, drecv, gsend, grecv):
    s, f, p, c = spots()
    P_ = S // 2
    T, D = x.shape
    C = nh * HD
    NW = wm.shape[0]
    G = D // S
    other = 1 - c
    mate = (p * 2 + other, f)
    wide = 256 if D % 256 == 0 else D
    rows = 64
    loads = [
        pltpu.make_async_copy(mixed, mx, local.at[0]),
        pltpu.make_async_copy(x, xv, local.at[1]),
        pltpu.make_async_copy(ct, cv, local.at[2]),
    ]
    loads += [pltpu.make_async_copy(wm.at[n], wv.at[n], wsem.at[n]) for n in range(NW)]
    for load in loads:
        load.start()
    greet(S, F)
    g2, b1, b2 = small[1:2, :], small[2:3, :], small[3:4, :]

    def by_core(n, tall):
        for t in range(P_):
            for core in range(2):
                at = (t * 2 + core) * G
                lt[n, core, t * G : (t + 1) * G, :] = tall[at : at + G]

    def chunk(n):
        return pl.ds(pl.multiple_of(n * wide, wide), wide)

    def over(n, body):
        def one(k, _):
            body(k)
            return 0

        lax.fori_loop(0, n, one, 0)

    def lines(n):
        return pl.ds(pl.multiple_of(n * rows, rows), rows)

    loads[0].wait()
    tall = mx[...].reshape(D, T)
    by_core(0, tall)
    ub[...] = jnp.transpose(tall)
    loads[1].wait()
    loads[2].wait()
    loads[3].wait()

    def attend_out(n):
        at = chunk(n)
        x2[:, at] = xv[:, at].astype(f32) + dot(ub[...], wv[0, :, at])

    over(D // wide, attend_out)

    def norm(n):
        at = lines(n)
        z = x2[at, :]
        r = lax.rsqrt(jnp.mean(z * z, axis=-1, keepdims=True) + eps_norm)
        r2[at, :] = r
        n2[at, :] = (z * r * g2).astype(bf)

    over(T // rows, norm)
    loads[4].wait()
    loads[5].wait()
    rv[...] = jnp.zeros_like(rv)

    def hidden(n):
        at = chunk(n)
        u = dot(n2[...], wv[1, :, at]) + small[2:3, at]
        gate = 1 / (1 + jnp.exp(-u))
        ab[:, at] = (u * gate).astype(bf)
        ga = dot(cv[...], wv[2, at, :], 1, 1)
        du = ga * (gate * (1 + u * (1 - gate)))
        rv[2:3, at] = jnp.sum(du, axis=0, keepdims=True)
        ub[:, at] = du.astype(bf)
        rv[3:4, at] = jnp.sum(cv[:, at].astype(f32), axis=0, keepdims=True)

    over(D // wide, hidden)

    def up_back(n):
        at = chunk(n)
        dn[:, at] = dot(ub[...], wv[1, at, :], 1, 1)

    over(D // wide, up_back)

    def second(n):
        at = lines(n)
        z, r, d = x2[at, :], r2[at, :], dn[at, :]
        e = d * g2
        tilt = jnp.mean(e * z, axis=-1, keepdims=True)
        v = cv[at, :].astype(f32) + r * e - z * (r * r * r * tilt)
        rv[1:2, :] += jnp.sum(d * z * r, axis=0, keepdims=True)
        dn[at, :] = v
        eb[at, :] = v.astype(bf)

    over(T // rows, second)
    keep = pltpu.make_async_copy(dn, dx2, local.at[0])
    keep.start()

    def head_out(i, to):
        return remote(dov.at[i], dm.at[s], dsend, drecv, i, (to, f))

    def heads(i, _):
        to = lax.rem(s + i, S)
        rows_of = pl.ds(pl.multiple_of(to * C, C), C)
        dov[i] = dot(wv[0, rows_of, :], eb[...], 1, 1).astype(bf)

        head_out(i, to).start()
        return 0

    lax.fori_loop(1, S, heads, 0)
    mine = pl.ds(pl.multiple_of(s * C, C), C)
    dov[0] = dot(wv[0, mine, :], eb[...], 1, 1).astype(bf)
    home = pltpu.make_async_copy(dov.at[0], dm.at[s], local.at[1])
    home.start()

    by_core(1, jnp.transpose(n2[...]))
    by_core(2, jnp.transpose(ab[...]))
    right = [eb, ub, cv]

    def pass_on(n):
        return remote(sb.at[n], rb.at[n], gsend, grecv, n, mate)

    for n in range(NW):

        def send_side(k, n=n):
            at = chunk(k)
            sb[n, :, at] = dot(lt[n, other], right[n][:, at]).astype(bf)

        over(D // wide, send_side)
        pass_on(n).start()

    def top(n):
        at = chunk(n)
        y = x2[:, at] + dot(ab[...], wv[2, :, at]) + small[3:4, at]
        xv[:, at] = y.astype(bf)

    over(D // wide, top)
    done = pltpu.make_async_copy(xv, out, local.at[2])
    done.start()
    for n in range(NW):
        pass_on(n).wait_recv()

        def keep_side(k, n=n):
            at = chunk(k)
            both = dot(lt[n, c], right[n][:, at]) + rb[n, :, at].astype(f32)
            ob[n, :, at] = both.astype(bf)

        over(D // wide, keep_side)
    stores = []
    for i in range(P_):
        here = pl.ds(pl.multiple_of(flip_bits(p, i) * G, G), G)
        stores.append(pltpu.make_async_copy(ob.at[:, here], gi.at[i], wsem.at[i]))
        stores[-1].start()
    vec[...] = rv[...]
    for i in range(1, S):
        remote(dov.at[0], dm.at[lax.rem(s + S - i, S)], dsend, drecv, i, mate).wait_recv()
    for store in stores:
        store.wait()
    keep.wait()
    home.wait()
    done.wait()
    for i in range(1, S):
        head_out(i, lax.rem(s + i, S)).wait_send()
    for n in range(NW):
        pass_on(n).wait_send()


def middle_all(S, F, nh, mixed, x, ct, wm, small):
    T, D = x.shape
    C = nh * HD
    P_ = S // 2
    NW = wm.shape[0]
    G = D // S
    any_ = pl.BlockSpec(memory_space=pl.ANY)
    vm = pl.BlockSpec(memory_space=pltpu.VMEM)
    dma = pltpu.SemaphoreType.DMA
    shape = jax.ShapeDtypeStruct
    V = pltpu.VMEM
    return pl.pallas_call(
        functools.partial(middle_kernel, S, F, nh),
        out_shape=[
            shape((T, D), bf),
            shape((T, D), f32),
            shape((S, C, T), bf),
            shape((P_, NW, G, D), bf),
            shape((8, D), f32),
        ],
        in_specs=[any_, any_, any_, any_, vm],
        out_specs=[any_, any_, any_, any_, vm],
        scratch_shapes=[
            V((S, C, T), bf),
            V((NW, 2, P_ * G, T), bf),
            V((T, D), bf),
            V((T, D), bf),
            V((NW, D, D), bf),
            V((T, D), f32),
            V((T, D), bf),
            V((T, D), f32),
            V((T, D), bf),
            V((T, D), bf),
            V((T, D), bf),
            V((T, 1), f32),
            V((NW, P_ * G, D), bf),
            V((NW, P_ * G, D), bf),
            V((NW, P_ * G, D), bf),
            V((S, C, T), bf),
            V((8, D), f32),
            dma((3,)),
            dma((max(NW, P_),)),
            dma((S,)),
            dma((S,)),
            dma((NW,)),
            dma((NW,)),
        ],
        compiler_params=pltpu.CompilerParams(
            collective_id=5, has_side_effects=True, vmem_limit_bytes=64_000_000
        ),
        name="middle",
    )(mixed, x, ct, wm, small)


def xor(a, b, n):
    out, bit = 0, 1
    while bit < n:
        both = lax.rem(lax.div(a, bit), 2) + lax.rem(lax.div(b, bit), 2)
        out = out + bit * lax.rem(both, 2)
        bit *= 2
    return out


def backward_kernel(S, F, nh, dm, qt, kt, q, k, v, ot, lse, n1, x_all, w, sc, g1, gi, vec, dx2,
                    g_out, in_out, q_out, vec_out, gp, gr_, gj,
                    dmt, wt, dwt, fm, tm, nx, xx, rr, mb, own, bi, bp, rl, ga, gb, gz, qi, qo,
                    vi, vz, vp, gf, gs_, local, nsem, bload,
                    gsend, grecv, bsend, brecv, qsend, qrecv, vsend, vrecv):
    s, f, p, c = spots()
    P_ = S // 2
    T, D = x_all.shape[1], x_all.shape[2]
    C = nh * HD
    L = S * T
    BQ = 2 * T
    BK = min(512, BQ)
    NW, R = gi.shape[1], gi.shape[3]
    other = 1 - c
    mate = (p * 2 + other, f)
    todo = []

    def go(copy):
        copy.start()
        todo.append(copy)

    chips = [flip_bits(p, i) for i in range(P_)]
    zero = s - s

    def num(n):
        return zero + n

    def chip(i):
        return chips[i]

    deeps = [lax.rem(f + i, F) for i in range(F)]

    def deep(i):
        return deeps[i]

    def head(ref, h, at):
        return ref[h * HD : (h + 1) * HD, at]

    loads = [
        pltpu.make_async_copy(dm.at[b], dmt.at[:, b * T : (b + 1) * T], bload.at[b])
        for b in range(S)
    ]
    for load in loads:
        load.start()
    greet(S, F)

    order = list(range(P_ - 1, -1, -1))
    wt[...] = jnp.transpose(w[...])
    dwt[...] = jnp.zeros_like(dwt)
    gf[...] = jnp.zeros_like(gf)
    gs_[...] = jnp.zeros_like(gs_)
    for load in loads:
        load.wait()

    def slabs(body):
        def one(n, _):
            body(lax.div(n, F), lax.rem(n, F))
            return 0

        lax.fori_loop(0, NW * F, one, 0)

    square = P_ == 4
    ZG = 10 if square else 2 * P_
    FH, H_ = F // 2, T // 2

    def half_g(ref, half):
        return ref.at[:, pl.ds(num(half * FH), FH)]

    def direct_g(i, half):
        src, dst = half_g(gi.at[num(i)], half), half_g(gp.at[num(i)], half)
        if half == 2 - i:
            src = gj.at[num(half)]
        return remote(src, dst, gsend, grecv, num(2 + 2 * i + half), (chip(i) * 2 + c, f))

    def relay_g(i):
        src = half_g(gi.at[num(3)], i - 1)
        return remote(src, gr_.at[num(i - 1)], gsend, grecv, num(7 + i), (chip(i) * 2 + c, f))

    def join_g(i):
        half = 2 - i
        la = pltpu.make_async_copy(half_g(gi.at[num(i)], half), half_g(ga, 0), local.at[num(1)])
        la.start()
        relay_g(3 - i).wait_recv()
        lb = pltpu.make_async_copy(gr_.at[num(half)], half_g(gb, 0), local.at[num(2)])
        lb.start()
        la.wait()
        lb.wait()

        def add(z, _):
            for a in range(NW):
                w_ = num(a)
                ga[w_, z] = (ga[w_, z].astype(f32) + gb[w_, z].astype(f32)).astype(bf)
            return 0

        lax.fori_loop(0, FH, add, 0)
        st = pltpu.make_async_copy(half_g(ga, 0), gj.at[num(half)], local.at[num(1)])
        st.start()
        st.wait()
        direct_g(i, half).start()

    def out_g(i):
        return remote(gi.at[i], gp.at[i], gsend, grecv, P_ + i, (chip(i) * 2 + c, f))

    if square:
        relay_g(1).start()
        relay_g(2).start()
        direct_g(2, 1).start()
        direct_g(1, 0).start()
    else:
        for i in order[:-1]:
            out_g(i).start()

    rows = 64
    wide = 256 if D % 256 == 0 else D

    def over(i):
        return remote(mb, bi.at[i], bsend, brecv, i, mate)

    def direct_b(i, half):
        part = pl.ds(pl.multiple_of(num(half * H_), H_), H_)
        src, dst = bi.at[num(i), part], bp.at[num(i - 1), part]
        return remote(src, dst, bsend, brecv, num(2 + 2 * i + half), (chip(i) * 2 + c, f))

    def relay_b(i):
        part = pl.ds(pl.multiple_of(num((i - 1) * H_), H_), H_)
        src = bi.at[num(3), part]
        return remote(src, rl.at[num(i - 1)], bsend, brecv, num(7 + i), (chip(i) * 2 + c, f))

    def join_b(i):
        half = 2 - i
        direct_b(i, 1 - half).start()
        relay_b(3 - i).wait_recv()
        few = min(rows, H_)

        def add(n, _):
            here = pl.ds(pl.multiple_of(half * H_ + n * few, few), few)
            there = pl.ds(pl.multiple_of(n * few, few), few)
            both = bi[num(i), here, :].astype(f32) + rl[num(half), there, :].astype(f32)
            bi[num(i), here, :] = both.astype(bf)
            return 0

        lax.fori_loop(0, H_ // few, add, 0)
        direct_b(i, half).start()

    def out_b(i, t):
        return pltpu.make_async_remote_copy(
            src_ref=bi.at[i],
            dst_ref=bp.at[i - 1],
            send_sem=bsend.at[P_ + i],
            recv_sem=brecv.at[P_ + i],
            device_id=(t * 2 + c, f),
            device_id_type=MESH,
        )

    def deep_g(i):
        src = ga.at[:, deep(i)]
        return remote(src, gz.at[i], gsend, grecv, ZG + i, (s, deep(i)))

    def plane_sums():
        la = pltpu.make_async_copy(gi.at[0], ga, local.at[1])
        la.start()
        la.wait()
        for i in order[1:-1] if square else order[:-1]:
            if square:
                direct_g(i, 0).wait_recv()
                direct_g(i, 1).wait_recv()
            else:
                out_g(i).wait_recv()
            lb = pltpu.make_async_copy(gp.at[i], gb, local.at[2])
            lb.start()
            lb.wait()

            def more(a, z):
                ga[a, z] = (ga[a, z].astype(f32) + gb[a, z].astype(f32)).astype(bf)

            slabs(more)
        for i in range(1, F):
            deep_g(i).start()

    def attention(do, delta, dqt, dk, dv):
        dqt[...] = jnp.zeros_like(dqt)
        dk[...] = jnp.zeros_like(dk)
        dv[...] = jnp.zeros_like(dv)

        def turn(b, _):
            at = pl.ds(pl.multiple_of(b * T, T), T)
            for h in range(nh):
                do[h, at, :] = jnp.transpose(head(dmt, h, at))
                prod = head(dmt, h, at).astype(f32) * head(ot, h, at).astype(f32)
                delta[h : h + 1, at] = jnp.sum(prod, axis=0, keepdims=True)
            return 0

        lax.fori_loop(0, S, turn, 0)

        def tile(q0, k0, masked):
            qa = pl.ds(q0, BK)
            ka = pl.ds(k0, BK)
            scores = [dot(k[h, ka, :], head(qt, h, qa)) for h in range(nh)]
            dps = [dot(v[h, ka, :], head(dmt, h, qa)) for h in range(nh)]
            for h in range(nh):
                e = jnp.exp(scores[h] - lse[h : h + 1, qa])
                if masked:
                    kp = lax.broadcasted_iota(jnp.int32, e.shape, 0)
                    qp = lax.broadcasted_iota(jnp.int32, e.shape, 1)
                    e = jnp.where(kp <= qp, e, 0.0)
                ds = (e * (dps[h] - delta[h : h + 1, qa])).astype(bf)
                dv[h, ka, :] += dot(e.astype(bf), do[h, qa, :])
                dk[h, ka, :] += dot(ds, q[h, qa, :])
                dqt[h * HD : (h + 1) * HD, qa] += dot(head(kt, h, ka), ds)

        r = BQ // BK

        def rect(qb, kb):
            def one(n, _):
                q0 = pl.multiple_of(qb * BQ + lax.div(n, r) * BK, BK)
                k0 = pl.multiple_of(kb * BQ + lax.rem(n, r) * BK, BK)
                tile(q0, k0, False)
                return 0

            lax.fori_loop(0, r * r, one, 0)

        def triangle(t):
            def one(n, _):
                at = pl.multiple_of(t * BQ + n * BK, BK)
                tile(at, at, True)

                def below(j, _):
                    tile(at, pl.multiple_of(t * BQ + j * BK, BK), False)
                    return 0

                lax.fori_loop(0, n, below, 0)
                return 0

            lax.fori_loop(0, r, one, 0)

        def fetch(t, half):
            b = t * 2 + half
            return (
                pltpu.make_async_copy(n1.at[b], nx, nsem.at[0]),
                pltpu.make_async_copy(x_all.at[b], xx, nsem.at[1]),
            )

        def finish(t, half, dst):
            for copy in fetch(t, half):
                copy.start()
            at = pl.ds(pl.multiple_of((t * 2 + half) * T, T), T)
            dqs = dqt[:, at].astype(bf)
            dqf = dqs.astype(f32)
            gs_[...] += jnp.sum(dqf * qt[:, at].astype(f32), axis=1, keepdims=True)
            fm[:C, :] = (dqf * sc[...]).astype(bf)
            for h in range(nh):
                fm[C + h * HD : C + (h + 1) * HD, :] = jnp.transpose(dk[h, at, :]).astype(bf)
                fm[2 * C + h * HD : 2 * C + (h + 1) * HD, :] = jnp.transpose(dv[h, at, :]).astype(bf)
            tm[...] = jnp.transpose(fm[...])
            for copy in fetch(t, half):
                copy.wait()

            def inverse(n, _):
                a = pl.ds(pl.multiple_of(n * rows, rows), rows)
                z = xx[a, :].astype(f32)
                rr[a, :] = lax.rsqrt(jnp.mean(z * z, axis=-1, keepdims=True) + eps_norm)
                return 0

            lax.fori_loop(0, T // rows, inverse, 0)

            def column(n, _):
                a = pl.ds(pl.multiple_of(n * wide, wide), wide)
                back = dot(tm[...], wt[:, a])
                dst[:, a] = back.astype(bf)
                hat = xx[:, a].astype(f32) * rr[...]
                gf[:, a] += jnp.sum(back * hat, axis=0, keepdims=True)
                dwt[:, a] += dot(fm[...], nx[:, a])
                return 0

            lax.fori_loop(0, D // wide, column, 0)

        def combine(i):
            def one(n, _):
                a = pl.ds(pl.multiple_of(n * rows, rows), rows)
                bi[i, a, :] = (bi[i, a, :].astype(f32) + own[a, :].astype(f32)).astype(bf)
                return 0

            lax.fori_loop(0, T // rows, one, 0)

        def advance(i, t, last):
            def pair(m, _):
                u = xor(p, m, P_)
                rect(jnp.maximum(t, u), jnp.minimum(t, u))
                return 0

            lax.fori_loop(0, i, pair, 0)
            triangle(t)
            if not last:

                @pl.when(i < P_ - 1)
                def _():
                    over(i + 1).wait_send()

            else:
                over(1).wait_send()
            finish(t, other, mb)
            over(i).start()
            finish(t, c, own)
            over(i).wait_recv()
            combine(i)
            if last:
                return
            if not square:
                out_b(i, t).start()
                return

            @pl.when(i == 3)
            def _():
                relay_b(1).start()
                relay_b(2).start()
                join_g(2)
                join_g(1)

            @pl.when(i == 2)
            def _():
                join_b(2)

            @pl.when(i == 1)
            def _():
                join_b(1)

        def stage(n, _):
            i = P_ - 1 - n
            advance(i, xor(p, i, P_), False)
            return 0

        lax.fori_loop(0, P_ - 1, stage, 0)
        plane_sums()
        advance(0, p, True)


    V = pltpu.VMEM
    pl.run_scoped(
        attention,
        V((nh, L, HD), bf),
        V((nh, L), f32),
        V((C, L), f32),
        V((nh, L, HD), f32),
        V((nh, L, HD), f32),
    )

    def closing(dw, up, qm, qs_, go_, vo):
        up_load = pltpu.make_async_copy(dx2, up, local.at[0])
        up_load.start()
        x_load = pltpu.make_async_copy(x_all.at[s], xx, nsem.at[1])
        x_load.start()
        vi[...] = vec[...]
        vi[0:1, :] = gf[...]
        turned = jnp.transpose(jnp.broadcast_to(gs_[...], (C, 128)))
        vi[4:5, 0:C] = turned[0:1, :]
        for i in range(1, F):
            go(remote(vi, vz.at[i], vsend, vrecv, i, (s, deep(i))))
        dw[...] = jnp.transpose(dwt[...])

        bunch = 8 // math.gcd(R, 8)

        def piece(n, _):
            part = dw[pl.ds(pl.multiple_of(n * (bunch * R), 8), bunch * R), :]
            for j in range(bunch):
                to = n * bunch + j
                qm[lax.div(to, F), lax.rem(to, F)] = part[j * R : (j + 1) * R].astype(bf)
            return 0

        lax.fori_loop(0, S * F // bunch, piece, 0)
        for i in range(1, F):
            go(remote(qm.at[:, deep(i)], qi.at[i], qsend, qrecv, i, (s, deep(i))))
        total = vi[...]
        for i in range(1, F):
            remote(vi, vz.at[i], vsend, vrecv, i, mate).wait_recv()
            total = total + vz[i]
        vp[0] = total
        for i in range(1, S):
            go(remote(vp.at[0], vp.at[i], vsend, vrecv, F - 1 + i, (lax.rem(s + i, S), f)))
        for i in range(1, F):
            remote(qm.at[:, f], qi.at[i], qsend, qrecv, i, mate).wait_recv()

        def sum_q(n, _):
            part = qm[n, f].astype(f32)
            for i in range(1, F):
                part = part + qi[i, n].astype(f32)
            qs_[n] = part.astype(bf)
            return 0

        lax.fori_loop(0, S, sum_q, 0)
        keep = pltpu.make_async_copy(qs_.at[s], qo.at[s], local.at[1])
        keep.start()
        for i in range(1, S):
            to = lax.rem(s + i, S)
            go(remote(qs_.at[to], qo.at[s], qsend, qrecv, F - 1 + i, (to, f)))
        up_load.wait()
        x_load.wait()
        over(0).wait_send()
        used = (1, 2) if square else range(1, P_)
        for i in used:
            if square:
                direct_b(i, 0).wait_recv()
                direct_b(i, 1).wait_recv()
            else:
                out_b(i, chip(i)).wait_recv()

        def below(n, _):
            a = pl.ds(pl.multiple_of(n * rows, rows), rows)
            back = bi[0, a, :].astype(f32)
            for i in used:
                back = back + bp[i - 1, a, :].astype(f32)
            z = xx[a, :].astype(f32)
            r1 = lax.rsqrt(jnp.mean(z * z, axis=-1, keepdims=True) + eps_norm)
            e1 = back * g1[...]
            tilt = jnp.mean(e1 * z, axis=-1, keepdims=True)
            mb[a, :] = (up[a, :] + r1 * e1 - z * (r1 * r1 * r1 * tilt)).astype(bf)
            return 0

        lax.fori_loop(0, T // rows, below, 0)
        outs = [pltpu.make_async_copy(mb, in_out, local.at[0])]
        outs[0].start()
        for i in range(1, F):
            remote(ga.at[:, f], gz.at[i], gsend, grecv, ZG + i, mate).wait_recv()
        for a in range(NW):
            part = ga[a, f].astype(f32)
            for i in range(1, F):
                part = part + gz[i, a].astype(f32)
            go_[a] = part
        outs.append(pltpu.make_async_copy(go_, g_out, local.at[2]))
        outs[1].start()
        total = vp[0]
        for i in range(1, S):
            remote(vp.at[0], vp.at[i], vsend, vrecv, F - 1 + i, mate).wait_recv()
            total = total + vp[i]
        vo[...] = total
        outs.append(pltpu.make_async_copy(vo, vec_out, nsem.at[0]))
        outs[2].start()
        for i in range(1, S):
            src = lax.rem(s + S - i, S)
            remote(qs_.at[0], qo.at[src], qsend, qrecv, F - 1 + i, mate).wait_recv()
        keep.wait()
        outs.append(pltpu.make_async_copy(qo, q_out, local.at[1]))
        outs[3].start()
        for out in outs:
            out.wait()
        for copy in todo:
            copy.wait_send()
        for i in range(1, F):
            deep_g(i).wait_send()
        for i in used:
            if square:
                relay_g(i).wait_send()
                relay_b(i).wait_send()
                for half in range(2):
                    direct_g(i, half).wait_send()
                    direct_b(i, half).wait_send()
            else:
                out_g(i).wait_send()
                out_b(i, chip(i)).wait_send()

    pl.run_scoped(
        closing,
        V((D, 3 * C), f32),
        V((T, D), f32),
        V((S, F, R, 3 * C), bf),
        V((S, R, 3 * C), bf),
        V((NW, R, D), f32),
        V(vec.shape, f32),
    )


def backward_all(S, F, nh, dm, qt, kt, q, k, v, ot, lse, n1, x_all, w, sc, g1, gi, vec, dx2):
    T, D = x_all.shape[1], x_all.shape[2]
    C = nh * HD
    L = S * T
    P_ = S // 2
    NW, R = gi.shape[1], gi.shape[3]
    any_ = pl.BlockSpec(memory_space=pl.ANY)
    vm = pl.BlockSpec(memory_space=pltpu.VMEM)
    dma = pltpu.SemaphoreType.DMA
    shape = jax.ShapeDtypeStruct
    V = pltpu.VMEM
    return pl.pallas_call(
        functools.partial(backward_kernel, S, F, nh),
        out_shape=[
            shape((NW, R, D), f32),
            shape((T, D), bf),
            shape((S, R, 3 * C), bf),
            shape(vec.shape, f32),
            shape((P_, NW, F, R, D), bf),
            shape((2, NW, F // 2, R, D), bf),
            shape((2, NW, F // 2, R, D), bf),
        ],
        in_specs=[any_] + [vm] * 7 + [any_, any_, vm, vm, vm, any_, vm, any_],
        out_specs=[any_] * 7,
        scratch_shapes=[
            V((C, L), bf),
            V((3 * C, D), bf),
            V((3 * C, D), f32),
            V((3 * C, T), bf),
            V((T, 3 * C), bf),
            V((T, D), bf),
            V((T, D), bf),
            V((T, 1), f32),
            V((T, D), bf),
            V((T, D), bf),
            V((P_, T, D), bf),
            V((2 if P_ == 4 else P_ - 1, T, D), bf),
            V((2, T // 2, D), bf),
            V((NW, F, R, D), bf),
            V((NW, F, R, D), bf),
            V((F, NW, R, D), bf),
            V((F, S, R, 3 * C), bf),
            V((S, R, 3 * C), bf),
            V(vec.shape, f32),
            V((F,) + vec.shape, f32),
            V((S,) + vec.shape, f32),
            V((1, D), f32),
            V((C, 1), f32),
            dma((3,)),
            dma((2,)),
            dma((S,)),
            dma((10 + 2 * P_ + F,)),
            dma((10 + 2 * P_ + F,)),
            dma((max(2 * P_, 10),)),
            dma((max(2 * P_, 10),)),
            dma((S + F,)),
            dma((S + F,)),
            dma((S + F,)),
            dma((S + F,)),
        ],
        compiler_params=pltpu.CompilerParams(
            collective_id=4, has_side_effects=True, vmem_limit_bytes=66_000_000
        ),
        name="backward",
    )(dm, qt, kt, q, k, v, ot, lse, n1, x_all, w, sc, g1, gi, vec, dx2)


def body(
    inputs,
    w_query,
    w_key,
    w_value,
    w_proj,
    w_up,
    w_down,
    gain_first,
    gain_second,
    bias_up,
    bias_down,
    query_scale,
    cotangent,
):
    groups = lax.axis_size("seq")
    rows_of = lax.axis_size("fsdp")
    nh = H // groups
    cols = nh * HD
    both = ("seq", "fsdp")
    tokens, width = inputs.shape[1], inputs.shape[2]
    length = tokens * groups
    shard = w_query.shape[0]
    x_low = inputs.reshape(tokens, width)
    qkv_rows = jnp.stack([w_query, w_key, w_value], 1).astype(bf).reshape(shard, 3, groups, cols)
    qkv_rows = qkv_rows.transpose(2, 0, 1, 3).reshape(groups, shard, 3 * cols)
    small = jnp.stack([gain_first, gain_second, bias_up, bias_down], 0)
    small = jnp.pad(small.astype(bf), ((0, 12), (0, 128 - shard)))
    weights = jnp.stack([w_proj, w_up, w_down], 0).astype(bf)
    x_all, qkv_w, small, weights = gather_all(groups, rows_of, x_low, qkv_rows, small, weights)
    qkv_w = qkv_w.reshape(width, 3 * cols)
    small = small[:, :, :4, :shard].transpose(2, 0, 1, 3).reshape(4, width).astype(f32)
    scale_dims = jax.nn.softplus(query_scale) * log_two_inverse / math.sqrt(HD)
    scale_cols = jnp.tile(scale_dims, nh)
    normed, qt, kt, q, k, v, ot, lse, mixed, weights = forward_all(
        groups, rows_of, nh, x_all, qkv_w, small[:1], scale_cols[:, None], weights
    )
    result, grad_middle, dm, pairs, vectors = middle_all(
        groups,
        rows_of,
        nh,
        mixed,
        x_low,
        cotangent.reshape(tokens, width),
        weights.reshape(3, width, width),
        small,
    )
    owned, grad_inputs, grad_qkv, vectors, *unused = backward_all(
        groups,
        rows_of,
        nh,
        dm,
        qt,
        kt,
        q,
        k,
        v,
        ot,
        lse,
        normed,
        x_all,
        qkv_w,
        scale_cols[:, None],
        small[:1],
        pairs.reshape(groups // 2, 3, rows_of, shard, width),
        vectors,
        grad_middle,
    )
    grad_qkv = grad_qkv.reshape(groups, shard, 3, cols).transpose(2, 1, 0, 3)
    grad_qkv = grad_qkv.reshape(3, shard, width).astype(f32)
    at = (lax.axis_index("seq") * rows_of + lax.axis_index("fsdp")) * shard
    mine = lax.dynamic_slice_in_dim(vectors, at, shard, 1)
    scale_total = jnp.sum(vectors[4, :cols].reshape(nh, HD), axis=0) / scale_dims
    grad_scale = scale_total * jax.nn.sigmoid(query_scale) * log_two_inverse / math.sqrt(HD)
    return (
        result.reshape(inputs.shape),
        grad_inputs.reshape(inputs.shape),
        grad_qkv[0],
        grad_qkv[1],
        grad_qkv[2],
        owned[0],
        owned[1],
        owned[2],
        mine[0],
        mine[1],
        mine[2],
        mine[3],
        grad_scale,
    )


def solution(mesh):
    return jax.shard_map(
        body,
        mesh=mesh,
        in_specs=(
            P("fsdp", "seq", None),
            P(("seq", "fsdp"), None),
            P(("seq", "fsdp"), None),
            P(("seq", "fsdp"), None),
            P(("seq", "fsdp"), None),
            P(("seq", "fsdp"), None),
            P(("seq", "fsdp"), None),
            P(("seq", "fsdp")),
            P(("seq", "fsdp")),
            P(("seq", "fsdp")),
            P(("seq", "fsdp")),
            P(),
            P("fsdp", "seq", None),
        ),
        out_specs=(
            P("fsdp", "seq", None),
            P("fsdp", "seq", None),
            P(("seq", "fsdp"), None),
            P(("seq", "fsdp"), None),
            P(("seq", "fsdp"), None),
            P(("seq", "fsdp"), None),
            P(("seq", "fsdp"), None),
            P(("seq", "fsdp"), None),
            P(("seq", "fsdp")),
            P(("seq", "fsdp")),
            P(("seq", "fsdp")),
            P(("seq", "fsdp")),
            P(),
        ),
        check_vma=False,
    )
```

```python
import functools
import math

import jax
import jax.numpy as jnp
from jax import lax
from jax.experimental import pallas as pl
from jax.experimental.pallas import tpu as pltpu
from jax.sharding import PartitionSpec as P

H = 16
HD = 80
eps_norm = 1e-06
log_two_inverse = 1.442695
bf = jnp.bfloat16
f32 = jnp.float32
NEG = -1e30


def dot(a,b,ca=1,cb=0):
    return lax.dot_general(a,b,(((ca,),(cb,)),((),())),preferred_element_type=f32)


MESH = pl.DeviceIdType.MESH


def spots():
    s, f = lax.axis_index("seq"), lax.axis_index("fsdp")
    return s, f, s // 2, lax.rem(s, 2)


def greet(S, F):
    s, f, _, _ = spots()
    barrier = pltpu.get_barrier_semaphore()
    for i in range(1, S):
        pl.semaphore_signal(barrier, inc=1, device_id=(lax.rem(s + i, S), f), device_id_type=MESH)
    for i in range(1, F):
        pl.semaphore_signal(barrier, inc=1, device_id=(s, lax.rem(f + i, F)), device_id_type=MESH)
    pl.semaphore_wait(barrier, S + F - 2)


def remote(src, dst, sends, recvs, n, to):
    return pltpu.make_async_remote_copy(
        src_ref=src,
        dst_ref=dst,
        send_sem=sends.at[n],
        recv_sem=recvs.at[n],
        device_id=to,
        device_id_type=MESH,
    )


def gather_kernel(S, F, x, wq, sm, wm, x_all, wq_all, sm_all, wm_all, xv, qv, sv, mv, local,
                  xs, xr, qs, qr, ss, sr, ms, mr):
    s, f, p, c = spots()
    P_ = S // 2
    other = 1 - c
    loads = [
        pltpu.make_async_copy(sm, sv, local.at[0]),
        pltpu.make_async_copy(wq, qv, local.at[1]),
        pltpu.make_async_copy(x, xv, local.at[2]),
        pltpu.make_async_copy(wm, mv, local.at[3]),
    ]
    for load in loads:
        load.start()
    greet(S, F)
    mate = (p * 2 + other, f)
    todo = []

    def go(copy):
        copy.start()
        todo.append(copy)

    def chip(i):
        return lax.rem(p + i, P_) * 2 + c

    def back(i):
        return lax.rem(p + P_ - i, P_) * 2 + c

    def near_chip(i):
        return flip_bits(p, i) * 2 + c

    H_ = x.shape[0] // 2

    def deep(i):
        return lax.rem(f + i, F)

    def behind(i):
        return lax.rem(f + F - i, F)

    loads[0].wait()
    keep0 = pltpu.make_async_copy(sv, sm_all.at[s, f], local.at[0])
    keep0.start()
    for i in range(1, F):
        go(remote(sv, sm_all.at[s, f], ss, sr, i, (s, deep(i))))
    loads[1].wait()
    keep1 = pltpu.make_async_copy(qv.at[s], wq_all.at[s, f], local.at[1])
    keep1.start()
    for i in range(1, S):
        to = lax.rem(s + i, S)
        go(remote(qv.at[to], wq_all.at[s, f], qs, qr, i, (to, f)))
    loads[2].wait()
    keep2 = pltpu.make_async_copy(xv, x_all.at[s], local.at[2])
    keep2.start()
    if P_ == 4:
        for first in range(2):
            for i in (1, 2):
                half = first if i == 1 else 1 - first
                part = pl.ds(half * H_, H_)
                go(remote(xv.at[part], x_all.at[s, part], xs, xr, 2 * i + half, (near_chip(i), f)))
    else:
        for i in range(1, P_):
            go(remote(xv, x_all.at[s], xs, xr, i, (chip(i), f)))
    go(remote(xv, x_all.at[s], xs, xr, 0, mate))
    loads[3].wait()
    keep3 = pltpu.make_async_copy(mv, wm_all.at[:, f], local.at[3])
    keep3.start()
    for i in range(1, F):
        go(remote(mv, wm_all.at[:, f], ms, mr, i, (s, deep(i))))
    for i in range(1, F):
        g = behind(i)
        remote(sv, sm_all.at[s, g], ss, sr, i, mate).wait_recv()
    keep0.wait()
    for i in range(1, S):
        go(remote(sm_all.at[s], sm_all.at[s], ss, sr, F - 1 + i, (lax.rem(s + i, S), f)))
    for i in range(1, S):
        remote(qv.at[0], wq_all.at[lax.rem(s + S - i, S), f], qs, qr, i, mate).wait_recv()
    keep1.wait()
    for i in range(1, F):
        go(remote(wq_all.at[:, f], wq_all.at[:, f], qs, qr, S - 1 + i, (s, deep(i))))
    for i in range(1, F):
        remote(mv, wm_all.at[:, behind(i)], ms, mr, i, mate).wait_recv()
    keep3.wait()
    if P_ == 4:
        for i in (1, 2):
            half = i - 1
            part = pl.ds(half * H_, H_)
            src = near_chip(i)
            remote(xv.at[part], x_all.at[src, part], xs, xr, 2 * i + half, mate).wait_recv()
            blk = x_all.at[src, part]
            go(remote(blk, blk, xs, xr, 6 + half, (near_chip(3 - i), f)))
        for i in (1, 2):
            half = 2 - i
            part = pl.ds(half * H_, H_)
            src = near_chip(i)
            remote(xv.at[part], x_all.at[src, part], xs, xr, 2 * i + half, mate).wait_recv()
            go(remote(x_all.at[src], x_all.at[src], xs, xr, 8 + i, mate))
    for i in range(1, P_ if P_ != 4 else 1):
        src = back(i)
        remote(xv, x_all.at[src], xs, xr, i, mate).wait_recv()
        go(remote(x_all.at[src], x_all.at[src], xs, xr, P_ - 1 + i, mate))
    for i in range(1, S):
        src = lax.rem(s + S - i, S)
        remote(sm_all.at[src], sm_all.at[src], ss, sr, F - 1 + i, mate).wait_recv()
    for i in range(1, F):
        g = behind(i)
        remote(wq_all.at[:, g], wq_all.at[:, g], qs, qr, S - 1 + i, mate).wait_recv()
    near = p * 2 + other
    remote(xv, x_all.at[near], xs, xr, 0, mate).wait_recv()
    if P_ == 4:
        for half in range(2):
            part = pl.ds(half * H_, H_)
            blk = x_all.at[near_chip(3), part]
            remote(blk, blk, xs, xr, 6 + half, mate).wait_recv()
            go(remote(blk, blk, xs, xr, 11 + half, mate))
        for i in (1, 2):
            blk = x_all.at[flip_bits(p, i) * 2 + other]
            remote(blk, blk, xs, xr, 8 + i, mate).wait_recv()
        for half in range(2):
            blk = x_all.at[flip_bits(p, 3) * 2 + other, pl.ds(half * H_, H_)]
            remote(blk, blk, xs, xr, 11 + half, mate).wait_recv()
    else:
        for i in range(1, P_):
            src = lax.rem(p + P_ - i, P_) * 2 + other
            remote(xv, x_all.at[src], xs, xr, P_ - 1 + i, mate).wait_recv()
    keep2.wait()
    for copy in todo:
        copy.wait_send()


def gather_all(S, F, x, wq, sm, wm):
    any_ = pl.BlockSpec(memory_space=pl.ANY)
    shapes = [
        (S,) + x.shape,
        (S, F) + wq.shape[1:],
        (S, F) + sm.shape,
        (wm.shape[0], F) + wm.shape[1:],
    ]
    P_ = S // 2
    dma = pltpu.SemaphoreType.DMA
    counts = [max(2 * P_ - 1, 12), S + F - 1, F + S - 1, F]
    sems = []
    for n in counts:
        sems += [dma((n + 1,)), dma((n + 1,))]
    return pl.pallas_call(
        functools.partial(gather_kernel, S, F),
        out_shape=[
            jax.ShapeDtypeStruct(sh, a.dtype) for sh, a in zip(shapes, (x, wq, sm, wm), strict=True)
        ],
        in_specs=[any_] * 4,
        out_specs=[any_] * 4,
        scratch_shapes=[
            pltpu.VMEM(x.shape, x.dtype),
            pltpu.VMEM(wq.shape, wq.dtype),
            pltpu.VMEM(sm.shape, sm.dtype),
            pltpu.VMEM(wm.shape, wm.dtype),
            dma((4,)),
        ]
        + sems,
        compiler_params=pltpu.CompilerParams(collective_id=1, has_side_effects=True),
        name="gather",
    )(x, wq, sm, wm)


def xor(a, b, n):
    out, bit = 0, 1
    while bit < n:
        both = lax.rem(lax.div(a, bit), 2) + lax.rem(lax.div(b, bit), 2)
        out = out + bit * lax.rem(both, 2)
        bit *= 2
    return out


def flip_bits(p, i):
    out, bit = p, 1
    while bit <= i:
        if i & bit:
            out = out + bit - 2 * bit * lax.rem(lax.div(p, bit), 2)
        bit *= 2
    return out


def forward_kernel(S, F, nh, x_all, w, g1, sc, wz, n1, qt, kt, qn, kk, vn, ot, lse, mixed, wm,
                   wt, vt, xb, nb, wv, inx, outn, local, osend, orecv, wsend, wrecv):
    s, f, p, c = spots()
    P_ = S // 2
    T, D = x_all.shape[1], x_all.shape[2]
    C = nh * HD
    L = S * T
    BQ = 2 * T
    BK = min(512, BQ)
    other = 1 - c
    mate = (p * 2 + other, f)
    load = pltpu.make_async_copy(wz, wv, local.at[0])
    load.start()

    def fetch(b):
        return pltpu.make_async_copy(x_all.at[b], xb.at[lax.rem(b, 2)], inx.at[lax.rem(b, 2)])

    def store(b):
        return pltpu.make_async_copy(nb.at[lax.rem(b, 2)], n1.at[b], outn.at[lax.rem(b, 2)])

    fetch(0).start()
    greet(S, F)
    load.wait()
    keep = pltpu.make_async_copy(wv, wm.at[:, s], local.at[0])
    keep.start()

    zero = s - s
    chips = [flip_bits(p, i) for i in range(P_)]

    def num(n):
        return zero + n

    def spread(i):
        return remote(wv, wm.at[:, s], wsend, wrecv, i, (xor(p, i, P_) * 2 + c, f))

    def forward(i):
        src = xor(p, i, P_) * 2 + c
        n = (7 if P_ == 4 else P_) + i
        return remote(wm.at[:, src], wm.at[:, src], wsend, wrecv, n, mate)

    def part_of(src, half):
        return wm.at[:, src, pl.ds(num(half * (F // 2)), F // 2)]

    def direct(i, half):
        src = wv.at[:, pl.ds(half * (F // 2), F // 2)]
        to = (flip_bits(p, i) * 2 + c, f)
        return remote(src, part_of(s, half), wsend, wrecv, 2 * i + half, to)

    def arrived(i, half):
        blk = part_of(chips[i] * 2 + c, half)
        remote(blk, blk, wsend, wrecv, num(2 * i + half), mate).wait_recv()

    def relay(i):
        blk = part_of(flip_bits(p, i) * 2 + c, i - 1)
        return remote(blk, blk, wsend, wrecv, 5 + i, (flip_bits(p, 3 - i) * 2 + c, f))

    def relayed(half):
        blk = part_of(chips[3] * 2 + c, half)
        return remote(blk, blk, wsend, wrecv, num(6 + half), mate)

    def corner(half, core):
        blk = part_of(chips[3] * 2 + core, half)
        return remote(blk, blk, wsend, wrecv, num(10 + half), mate)

    square = P_ == 4
    if square:
        for first in range(2):
            for i in (1, 2):
                direct(i, first if i == 1 else 1 - first).start()
    else:
        for i in range(1, P_):
            spread(P_ - i).start()
    near = remote(wv, wm.at[:, s], wsend, wrecv, 0, mate)
    near.start()
    wt[...] = jnp.transpose(w[...])

    rows = 64

    def project(b, _):
        slot = lax.rem(b, 2)
        fetch(b).wait()

        @pl.when(b + 1 < S)
        def _():
            fetch(b + 1).start()

        @pl.when(b >= 2)
        def _():
            store(b - 2).wait()

        def norm(k, _):
            at = pl.ds(pl.multiple_of(k * rows, rows), rows)
            v = xb[slot, at, :].astype(f32)
            r = lax.rsqrt(jnp.mean(v * v, axis=-1, keepdims=True) + eps_norm)
            nb[slot, at, :] = (v * r * g1[...]).astype(bf)
            return 0

        lax.fori_loop(0, T // rows, norm, 0)
        store(b).start()
        cols = pl.ds(pl.multiple_of(b * T, T), T)
        res = dot(wt[...], nb[slot], 1, 1)
        qt[:, cols] = (res[:C] * sc[...]).astype(bf)
        kt[:, cols] = res[C : 2 * C].astype(bf)
        vt[:, cols] = res[2 * C :].astype(bf)
        for h in range(nh):
            part = slice(h * HD, (h + 1) * HD)
            qn[h, cols, :] = jnp.transpose(res[:C][part] * sc[part]).astype(bf)
            kk[h, cols, :] = jnp.transpose(res[C : 2 * C][part]).astype(bf)
            vn[h, cols, :] = jnp.transpose(res[2 * C :][part]).astype(bf)
        return 0

    lax.fori_loop(0, S, project, 0)
    if square:
        for i in (1, 2):
            arrived(i, i - 1)
            relay(i).start()
    store(S - 2).wait()
    store(S - 1).wait()

    r = BQ // BK

    def attend(t):
        first = pl.multiple_of(t * BQ, BQ)
        q = [qt[h * HD : (h + 1) * HD, pl.ds(first, BQ)] for h in range(nh)]

        def step(j, carry, diag=None):
            at = pl.ds(pl.multiple_of(j * BK, BK), BK)
            scores = [dot(kk[h, at, :], q[h]) for h in range(nh)]
            out = []
            for h in range(nh):
                m, l, acc = carry[h]
                sh = scores[h]
                if diag is not None:
                    kp = lax.broadcasted_iota(jnp.int32, sh.shape, 0) + diag * BK
                    qp = lax.broadcasted_iota(jnp.int32, sh.shape, 1)
                    sh = jnp.where(kp <= qp, sh, NEG)
                mn = jnp.maximum(m, jnp.max(sh, axis=0, keepdims=True))
                a = jnp.exp(m - mn)
                e = jnp.exp(sh - mn)
                l = l * a + jnp.sum(e, axis=0, keepdims=True)
                acc = acc * a + dot(vt[h * HD : (h + 1) * HD, at], e.astype(bf))
                out.append((mn, l, acc))
            return tuple(out)

        carry = tuple(
            (jnp.full((1, BQ), NEG, f32), jnp.zeros((1, BQ), f32), jnp.zeros((HD, BQ), f32))
            for _ in range(nh)
        )
        carry = lax.fori_loop(0, t * r, step, carry)
        for d in range(r):
            carry = step(t * r + d, carry, d)
        for h in range(nh):
            m, l, acc = carry[h]
            ot[h * HD : (h + 1) * HD, pl.ds(first, BQ)] = (acc / l).astype(bf)
            lse[h : h + 1, pl.ds(first, BQ)] = m + jnp.log(l)

    def to_owner(src, n, i, to):
        return pltpu.make_async_remote_copy(
            src_ref=src,
            dst_ref=mixed.at[s],
            send_sem=osend.at[n],
            recv_sem=orecv.at[2 * i + c],
            device_id=to,
            device_id_type=MESH,
        )

    def send(i, half):
        t = xor(p, i, P_)
        src = ot.at[:, pl.ds(pl.multiple_of(t * BQ + half * T, T), T)]
        return to_owner(src, 2 * i + half, i, (t * 2 + half, f))

    def turn(n, _):
        i = P_ - 1 - n
        attend(xor(p, i, P_))
        send(i, 0).start()
        send(i, 1).start()
        if not square:
            spread(i).wait_recv()
            forward(i).start()
            return 0

        @pl.when(i == 3)
        def _():
            arrived(2, 0)
            forward(num(2)).start()

        @pl.when(i == 2)
        def _():
            arrived(1, 1)
            forward(num(1)).start()

        @pl.when(i == 1)
        def _():
            for half in range(2):
                relayed(half).wait_recv()
                corner(half, c).start()

        return 0

    lax.fori_loop(0, P_ - 1, turn, 0)
    attend(p)
    mine = ot.at[:, pl.ds(pl.multiple_of(s * T, T), T)]
    theirs = ot.at[:, pl.ds(pl.multiple_of((p * 2 + other) * T, T), T)]
    last = to_owner(theirs, 0, 0, mate)
    last.start()
    own = pltpu.make_async_copy(mine, mixed.at[s], local.at[1])
    own.start()
    def from_source(i, core):
        return pltpu.make_async_remote_copy(
            src_ref=mine,
            dst_ref=mixed.at[flip_bits(p, i) * 2 + core],
            send_sem=osend.at[0],
            recv_sem=orecv.at[2 * i + core],
            device_id=mate,
            device_id_type=MESH,
        )

    for i in range(1, P_):
        for core in range(2):
            from_source(i, core).wait_recv()
    from_source(0, other).wait_recv()
    last.wait_send()
    own.wait()
    keep.wait()
    near.wait()
    if square:
        for i in (1, 2):
            forward(i).wait()
            relay(i).wait_send()
            for half in range(2):
                direct(i, half).wait_send()
        for half in range(2):
            corner(half, c).wait_send()
            corner(half, other).wait_recv()
    for i in range(1, P_):
        if not square:
            forward(i).wait()
            spread(i).wait_send()
        send(i, 0).wait_send()
        send(i, 1).wait_send()


def forward_all(S, F, nh, x_all, w, g1, sc, wz):
    T, D = x_all.shape[1], x_all.shape[2]
    C = nh * HD
    L = S * T
    P_ = S // 2
    any_ = pl.BlockSpec(memory_space=pl.ANY)
    vm = pl.BlockSpec(memory_space=pltpu.VMEM)
    dma = pltpu.SemaphoreType.DMA
    shape = jax.ShapeDtypeStruct
    NW, R = wz.shape[0], wz.shape[2]
    V = pltpu.VMEM
    return pl.pallas_call(
        functools.partial(forward_kernel, S, F, nh),
        out_shape=[
            shape((S, T, D), bf),
            shape((C, L), bf),
            shape((C, L), bf),
            shape((nh, L, HD), bf),
            shape((nh, L, HD), bf),
            shape((nh, L, HD), bf),
            shape((C, L), bf),
            shape((nh, L), f32),
            shape((S, C, T), bf),
            shape((NW, S, F, R, D), bf),
        ],
        in_specs=[any_, vm, vm, vm, any_],
        out_specs=[any_] + [vm] * 7 + [any_, any_],
        scratch_shapes=[
            V((3 * C, D), bf),
            V((C, L), bf),
            V((2, T, D), bf),
            V((2, T, D), bf),
            V((NW, F, R, D), bf),
            dma((2,)),
            dma((2,)),
            dma((2,)),
            dma((2 * P_,)),
            dma((2 * P_,)),
            dma((max(2 * P_, 12),)),
            dma((max(2 * P_, 12),)),
        ],
        compiler_params=pltpu.CompilerParams(
            collective_id=3, has_side_effects=True, vmem_limit_bytes=60 << 20
        ),
        name="forward",
    )(x_all, w, g1, sc, wz)


def middle_kernel(S, F, nh, mixed, x, ct, wm, small, out, dx2, dm, gi, vec,
                  mx, lt, xv, cv, wv, x2, n2, dn, ab, ub, eb, r2, sb, rb, ob, dov, rv, local, wsem,
                  dsend, drecv, gsend, grecv):
    s, f, p, c = spots()
    P_ = S // 2
    T, D = x.shape
    C = nh * HD
    NW = wm.shape[0]
    G = D // S
    other = 1 - c
    mate = (p * 2 + other, f)
    wide = 256 if D % 256 == 0 else D
    rows = 64
    loads = [
        pltpu.make_async_copy(mixed, mx, local.at[0]),
        pltpu.make_async_copy(x, xv, local.at[1]),
        pltpu.make_async_copy(ct, cv, local.at[2]),
    ]
    loads += [pltpu.make_async_copy(wm.at[n], wv.at[n], wsem.at[n]) for n in range(NW)]
    for load in loads:
        load.start()
    greet(S, F)
    g2, b1, b2 = small[1:2, :], small[2:3, :], small[3:4, :]

    def by_core(n, tall):
        for t in range(P_):
            for core in range(2):
                at = (t * 2 + core) * G
                lt[n, core, t * G : (t + 1) * G, :] = tall[at : at + G]

    def chunk(n):
        return pl.ds(pl.multiple_of(n * wide, wide), wide)

    def over(n, body):
        def one(k, _):
            body(k)
            return 0

        lax.fori_loop(0, n, one, 0)

    def lines(n):
        return pl.ds(pl.multiple_of(n * rows, rows), rows)

    loads[0].wait()
    tall = mx[...].reshape(D, T)
    by_core(0, tall)
    ub[...] = jnp.transpose(tall)
    loads[1].wait()
    loads[2].wait()
    loads[3].wait()

    def attend_out(n):
        at = chunk(n)
        x2[:, at] = xv[:, at].astype(f32) + dot(ub[...], wv[0, :, at])

    over(D // wide, attend_out)

    def norm(n):
        at = lines(n)
        z = x2[at, :]
        r = lax.rsqrt(jnp.mean(z * z, axis=-1, keepdims=True) + eps_norm)
        r2[at, :] = r
        n2[at, :] = (z * r * g2).astype(bf)

    over(T // rows, norm)
    loads[4].wait()
    loads[5].wait()
    rv[...] = jnp.zeros_like(rv)

    def hidden(n):
        at = chunk(n)
        u = dot(n2[...], wv[1, :, at]) + small[2:3, at]
        gate = 1 / (1 + jnp.exp(-u))
        ab[:, at] = (u * gate).astype(bf)
        ga = dot(cv[...], wv[2, at, :], 1, 1)
        du = ga * (gate * (1 + u * (1 - gate)))
        rv[2:3, at] = jnp.sum(du, axis=0, keepdims=True)
        ub[:, at] = du.astype(bf)
        rv[3:4, at] = jnp.sum(cv[:, at].astype(f32), axis=0, keepdims=True)

    over(D // wide, hidden)

    def up_back(n):
        at = chunk(n)
        dn[:, at] = dot(ub[...], wv[1, at, :], 1, 1)

    over(D // wide, up_back)

    def second(n):
        at = lines(n)
        z, r, d = x2[at, :], r2[at, :], dn[at, :]
        e = d * g2
        tilt = jnp.mean(e * z, axis=-1, keepdims=True)
        v = cv[at, :].astype(f32) + r * e - z * (r * r * r * tilt)
        rv[1:2, :] += jnp.sum(d * z * r, axis=0, keepdims=True)
        dn[at, :] = v
        eb[at, :] = v.astype(bf)

    over(T // rows, second)
    keep = pltpu.make_async_copy(dn, dx2, local.at[0])
    keep.start()

    def head_out(i, to):
        return remote(dov.at[i], dm.at[s], dsend, drecv, i, (to, f))

    def heads(i, _):
        to = lax.rem(s + i, S)
        rows_of = pl.ds(pl.multiple_of(to * C, C), C)
        dov[i] = dot(wv[0, rows_of, :], eb[...], 1, 1).astype(bf)

        head_out(i, to).start()
        return 0

    lax.fori_loop(1, S, heads, 0)
    mine = pl.ds(pl.multiple_of(s * C, C), C)
    dov[0] = dot(wv[0, mine, :], eb[...], 1, 1).astype(bf)
    home = pltpu.make_async_copy(dov.at[0], dm.at[s], local.at[1])
    home.start()

    by_core(1, jnp.transpose(n2[...]))
    by_core(2, jnp.transpose(ab[...]))
    right = [eb, ub, cv]

    def pass_on(n):
        return remote(sb.at[n], rb.at[n], gsend, grecv, n, mate)

    for n in range(NW):

        def send_side(k, n=n):
            at = chunk(k)
            sb[n, :, at] = dot(lt[n, other], right[n][:, at]).astype(bf)

        over(D // wide, send_side)
        pass_on(n).start()

    def top(n):
        at = chunk(n)
        y = x2[:, at] + dot(ab[...], wv[2, :, at]) + small[3:4, at]
        xv[:, at] = y.astype(bf)

    over(D // wide, top)
    done = pltpu.make_async_copy(xv, out, local.at[2])
    done.start()
    for n in range(NW):
        pass_on(n).wait_recv()

        def keep_side(k, n=n):
            at = chunk(k)
            both = dot(lt[n, c], right[n][:, at]) + rb[n, :, at].astype(f32)
            ob[n, :, at] = both.astype(bf)

        over(D // wide, keep_side)
    stores = []
    for i in range(P_):
        here = pl.ds(pl.multiple_of(flip_bits(p, i) * G, G), G)
        stores.append(pltpu.make_async_copy(ob.at[:, here], gi.at[i], wsem.at[i]))
        stores[-1].start()
    vec[...] = rv[...]
    for i in range(1, S):
        remote(dov.at[0], dm.at[lax.rem(s + S - i, S)], dsend, drecv, i, mate).wait_recv()
    for store in stores:
        store.wait()
    keep.wait()
    home.wait()
    done.wait()
    for i in range(1, S):
        head_out(i, lax.rem(s + i, S)).wait_send()
    for n in range(NW):
        pass_on(n).wait_send()


def middle_all(S, F, nh, mixed, x, ct, wm, small):
    T, D = x.shape
    C = nh * HD
    P_ = S // 2
    NW = wm.shape[0]
    G = D // S
    any_ = pl.BlockSpec(memory_space=pl.ANY)
    vm = pl.BlockSpec(memory_space=pltpu.VMEM)
    dma = pltpu.SemaphoreType.DMA
    shape = jax.ShapeDtypeStruct
    V = pltpu.VMEM
    return pl.pallas_call(
        functools.partial(middle_kernel, S, F, nh),
        out_shape=[
            shape((T, D), bf),
            shape((T, D), f32),
            shape((S, C, T), bf),
            shape((P_, NW, G, D), bf),
            shape((8, D), f32),
        ],
        in_specs=[any_, any_, any_, any_, vm],
        out_specs=[any_, any_, any_, any_, vm],
        scratch_shapes=[
            V((S, C, T), bf),
            V((NW, 2, P_ * G, T), bf),
            V((T, D), bf),
            V((T, D), bf),
            V((NW, D, D), bf),
            V((T, D), f32),
            V((T, D), bf),
            V((T, D), f32),
            V((T, D), bf),
            V((T, D), bf),
            V((T, D), bf),
            V((T, 1), f32),
            V((NW, P_ * G, D), bf),
            V((NW, P_ * G, D), bf),
            V((NW, P_ * G, D), bf),
            V((S, C, T), bf),
            V((8, D), f32),
            dma((3,)),
            dma((max(NW, P_),)),
            dma((S,)),
            dma((S,)),
            dma((NW,)),
            dma((NW,)),
        ],
        compiler_params=pltpu.CompilerParams(
            collective_id=5, has_side_effects=True, vmem_limit_bytes=64_000_000
        ),
        name="middle",
    )(mixed, x, ct, wm, small)


def backward_kernel(S, F, nh, dm, qt, kt, q, k, v, ot, lse, n1, x_all, w, sc, g1, gi, vec, dx2,
                    g_out, in_out, q_out, vec_out, gp, gr_, gj,
                    dmt, wt, dwt, fm, tm, nx, xx, rr, mb, own, bi, bp, rl, ga, gb, gz, qi, qo,
                    vi, vz, vp, gf, gs_, local, nsem, bload,
                    gsend, grecv, bsend, brecv, qsend, qrecv, vsend, vrecv):
    s, f, p, c = spots()
    P_ = S // 2
    T, D = x_all.shape[1], x_all.shape[2]
    C = nh * HD
    L = S * T
    BQ = 2 * T
    BK = min(512, BQ)
    NW, R = gi.shape[1], gi.shape[3]
    other = 1 - c
    mate = (p * 2 + other, f)
    todo = []

    def go(copy):
        copy.start()
        todo.append(copy)

    chips = [flip_bits(p, i) for i in range(P_)]
    zero = s - s

    def num(n):
        return zero + n

    def chip(i):
        return chips[i]

    deeps = [lax.rem(f + i, F) for i in range(F)]

    def deep(i):
        return deeps[i]

    def head(ref, h, at):
        return ref[h * HD : (h + 1) * HD, at]

    loads = [
        pltpu.make_async_copy(dm.at[b], dmt.at[:, b * T : (b + 1) * T], bload.at[b])
        for b in range(S)
    ]
    for load in loads:
        load.start()
    greet(S, F)

    order = list(range(P_ - 1, -1, -1))
    wt[...] = jnp.transpose(w[...])
    dwt[...] = jnp.zeros_like(dwt)
    gf[...] = jnp.zeros_like(gf)
    gs_[...] = jnp.zeros_like(gs_)
    for load in loads:
        load.wait()

    def slabs(body):
        def one(n, _):
            body(lax.div(n, F), lax.rem(n, F))
            return 0

        lax.fori_loop(0, NW * F, one, 0)

    square = P_ == 4
    ZG = 10 if square else 2 * P_
    FH, H_ = F // 2, T // 2

    def half_g(ref, half):
        return ref.at[:, pl.ds(num(half * FH), FH)]

    def direct_g(i, half):
        src, dst = half_g(gi.at[num(i)], half), half_g(gp.at[num(i)], half)
        if half == 2 - i:
            src = gj.at[num(half)]
        return remote(src, dst, gsend, grecv, num(2 + 2 * i + half), (chip(i) * 2 + c, f))

    def relay_g(i):
        src = half_g(gi.at[num(3)], i - 1)
        return remote(src, gr_.at[num(i - 1)], gsend, grecv, num(7 + i), (chip(i) * 2 + c, f))

    def join_g(i):
        half = 2 - i
        la = pltpu.make_async_copy(half_g(gi.at[num(i)], half), half_g(ga, 0), local.at[num(1)])
        la.start()
        relay_g(3 - i).wait_recv()
        lb = pltpu.make_async_copy(gr_.at[num(half)], half_g(gb, 0), local.at[num(2)])
        lb.start()
        la.wait()
        lb.wait()

        def add(z, _):
            for a in range(NW):
                w_ = num(a)
                ga[w_, z] = (ga[w_, z].astype(f32) + gb[w_, z].astype(f32)).astype(bf)
            return 0

        lax.fori_loop(0, FH, add, 0)
        st = pltpu.make_async_copy(half_g(ga, 0), gj.at[num(half)], local.at[num(1)])
        st.start()
        st.wait()
        direct_g(i, half).start()

    def out_g(i):
        return remote(gi.at[i], gp.at[i], gsend, grecv, P_ + i, (chip(i) * 2 + c, f))

    if square:
        relay_g(1).start()
        relay_g(2).start()
        direct_g(2, 1).start()
        direct_g(1, 0).start()
    else:
        for i in order[:-1]:
            out_g(i).start()

    rows = 64
    wide = 256 if D % 256 == 0 else D

    def over(i):
        return remote(mb, bi.at[i], bsend, brecv, i, mate)

    def direct_b(i, half):
        part = pl.ds(pl.multiple_of(num(half * H_), H_), H_)
        src, dst = bi.at[num(i), part], bp.at[num(i - 1), part]
        return remote(src, dst, bsend, brecv, num(2 + 2 * i + half), (chip(i) * 2 + c, f))

    def relay_b(i):
        part = pl.ds(pl.multiple_of(num((i - 1) * H_), H_), H_)
        src = bi.at[num(3), part]
        return remote(src, rl.at[num(i - 1)], bsend, brecv, num(7 + i), (chip(i) * 2 + c, f))

    def join_b(i):
        half = 2 - i
        direct_b(i, 1 - half).start()
        relay_b(3 - i).wait_recv()
        few = min(rows, H_)

        def add(n, _):
            here = pl.ds(pl.multiple_of(half * H_ + n * few, few), few)
            there = pl.ds(pl.multiple_of(n * few, few), few)
            both = bi[num(i), here, :].astype(f32) + rl[num(half), there, :].astype(f32)
            bi[num(i), here, :] = both.astype(bf)
            return 0

        lax.fori_loop(0, H_ // few, add, 0)
        direct_b(i, half).start()

    def out_b(i, t):
        return pltpu.make_async_remote_copy(
            src_ref=bi.at[i],
            dst_ref=bp.at[i - 1],
            send_sem=bsend.at[P_ + i],
            recv_sem=brecv.at[P_ + i],
            device_id=(t * 2 + c, f),
            device_id_type=MESH,
        )

    def deep_g(i):
        src = ga.at[:, deep(i)]
        return remote(src, gz.at[i], gsend, grecv, ZG + i, (s, deep(i)))

    def plane_sums():
        la = pltpu.make_async_copy(gi.at[0], ga, local.at[1])
        la.start()
        la.wait()
        for i in order[1:-1] if square else order[:-1]:
            if square:
                direct_g(i, 0).wait_recv()
                direct_g(i, 1).wait_recv()
            else:
                out_g(i).wait_recv()
            lb = pltpu.make_async_copy(gp.at[i], gb, local.at[2])
            lb.start()
            lb.wait()

            def more(a, z):
                ga[a, z] = (ga[a, z].astype(f32) + gb[a, z].astype(f32)).astype(bf)

            slabs(more)
        for i in range(1, F):
            deep_g(i).start()

    def attention(do, delta, dqt, dk, dv):
        dqt[...] = jnp.zeros_like(dqt)
        dk[...] = jnp.zeros_like(dk)
        dv[...] = jnp.zeros_like(dv)

        def turn(b, _):
            at = pl.ds(pl.multiple_of(b * T, T), T)
            for h in range(nh):
                do[h, at, :] = jnp.transpose(head(dmt, h, at))
                prod = head(dmt, h, at).astype(f32) * head(ot, h, at).astype(f32)
                delta[h : h + 1, at] = jnp.sum(prod, axis=0, keepdims=True)
            return 0

        lax.fori_loop(0, S, turn, 0)

        def tile(q0, k0, masked):
            qa = pl.ds(q0, BK)
            ka = pl.ds(k0, BK)
            scores = [dot(k[h, ka, :], head(qt, h, qa)) for h in range(nh)]
            dps = [dot(v[h, ka, :], head(dmt, h, qa)) for h in range(nh)]
            for h in range(nh):
                e = jnp.exp(scores[h] - lse[h : h + 1, qa])
                if masked:
                    kp = lax.broadcasted_iota(jnp.int32, e.shape, 0)
                    qp = lax.broadcasted_iota(jnp.int32, e.shape, 1)
                    e = jnp.where(kp <= qp, e, 0.0)
                ds = (e * (dps[h] - delta[h : h + 1, qa])).astype(bf)
                dv[h, ka, :] += dot(e.astype(bf), do[h, qa, :])
                dk[h, ka, :] += dot(ds, q[h, qa, :])
                dqt[h * HD : (h + 1) * HD, qa] += dot(head(kt, h, ka), ds)

        r = BQ // BK

        def rect(qb, kb):
            def one(n, _):
                q0 = pl.multiple_of(qb * BQ + lax.div(n, r) * BK, BK)
                k0 = pl.multiple_of(kb * BQ + lax.rem(n, r) * BK, BK)
                tile(q0, k0, False)
                return 0

            lax.fori_loop(0, r * r, one, 0)

        def triangle(t):
            def one(n, _):
                at = pl.multiple_of(t * BQ + n * BK, BK)
                tile(at, at, True)

                def below(j, _):
                    tile(at, pl.multiple_of(t * BQ + j * BK, BK), False)
                    return 0

                lax.fori_loop(0, n, below, 0)
                return 0

            lax.fori_loop(0, r, one, 0)

        def fetch(t, half):
            b = t * 2 + half
            return (
                pltpu.make_async_copy(n1.at[b], nx, nsem.at[0]),
                pltpu.make_async_copy(x_all.at[b], xx, nsem.at[1]),
            )

        def finish(t, half, dst):
            for copy in fetch(t, half):
                copy.start()
            at = pl.ds(pl.multiple_of((t * 2 + half) * T, T), T)
            dqs = dqt[:, at].astype(bf)
            dqf = dqs.astype(f32)
            gs_[...] += jnp.sum(dqf * qt[:, at].astype(f32), axis=1, keepdims=True)
            fm[:C, :] = (dqf * sc[...]).astype(bf)
            for h in range(nh):
                fm[C + h * HD : C + (h + 1) * HD, :] = jnp.transpose(dk[h, at, :]).astype(bf)
                fm[2 * C + h * HD : 2 * C + (h + 1) * HD, :] = jnp.transpose(dv[h, at, :]).astype(bf)
            tm[...] = jnp.transpose(fm[...])
            for copy in fetch(t, half):
                copy.wait()

            def inverse(n, _):
                a = pl.ds(pl.multiple_of(n * rows, rows), rows)
                z = xx[a, :].astype(f32)
                rr[a, :] = lax.rsqrt(jnp.mean(z * z, axis=-1, keepdims=True) + eps_norm)
                return 0

            lax.fori_loop(0, T // rows, inverse, 0)

            def column(n, _):
                a = pl.ds(pl.multiple_of(n * wide, wide), wide)
                back = dot(tm[...], wt[:, a])
                dst[:, a] = back.astype(bf)
                hat = xx[:, a].astype(f32) * rr[...]
                gf[:, a] += jnp.sum(back * hat, axis=0, keepdims=True)
                dwt[:, a] += dot(fm[...], nx[:, a])
                return 0

            lax.fori_loop(0, D // wide, column, 0)

        def combine(i):
            def one(n, _):
                a = pl.ds(pl.multiple_of(n * rows, rows), rows)
                bi[i, a, :] = (bi[i, a, :].astype(f32) + own[a, :].astype(f32)).astype(bf)
                return 0

            lax.fori_loop(0, T // rows, one, 0)

        def advance(i, t, last):
            def pair(m, _):
                u = xor(p, m, P_)
                rect(jnp.maximum(t, u), jnp.minimum(t, u))
                return 0

            lax.fori_loop(0, i, pair, 0)
            triangle(t)
            if not last:

                @pl.when(i < P_ - 1)
                def _():
                    over(i + 1).wait_send()

            else:
                over(1).wait_send()
            finish(t, other, mb)
            over(i).start()
            finish(t, c, own)
            over(i).wait_recv()
            combine(i)
            if last:
                return
            if not square:
                out_b(i, t).start()
                return

            @pl.when(i == 3)
            def _():
                relay_b(1).start()
                relay_b(2).start()
                join_g(2)
                join_g(1)

            @pl.when(i == 2)
            def _():
                join_b(2)

            @pl.when(i == 1)
            def _():
                join_b(1)

        def stage(n, _):
            i = P_ - 1 - n
            advance(i, xor(p, i, P_), False)
            return 0

        lax.fori_loop(0, P_ - 1, stage, 0)
        plane_sums()
        advance(0, p, True)


    V = pltpu.VMEM
    pl.run_scoped(
        attention,
        V((nh, L, HD), bf),
        V((nh, L), f32),
        V((C, L), f32),
        V((nh, L, HD), f32),
        V((nh, L, HD), f32),
    )

    def closing(dw, up, qm, qs_, go_, vo):
        up_load = pltpu.make_async_copy(dx2, up, local.at[0])
        up_load.start()
        x_load = pltpu.make_async_copy(x_all.at[s], xx, nsem.at[1])
        x_load.start()
        vi[...] = vec[...]
        vi[0:1, :] = gf[...]
        turned = jnp.transpose(jnp.broadcast_to(gs_[...], (C, 128)))
        vi[4:5, 0:C] = turned[0:1, :]
        for i in range(1, F):
            go(remote(vi, vz.at[i], vsend, vrecv, i, (s, deep(i))))
        dw[...] = jnp.transpose(dwt[...])

        bunch = 8 // math.gcd(R, 8)

        def piece(n, _):
            part = dw[pl.ds(pl.multiple_of(n * (bunch * R), 8), bunch * R), :]
            for j in range(bunch):
                to = n * bunch + j
                qm[lax.div(to, F), lax.rem(to, F)] = part[j * R : (j + 1) * R].astype(bf)
            return 0

        lax.fori_loop(0, S * F // bunch, piece, 0)
        for i in range(1, F):
            go(remote(qm.at[:, deep(i)], qi.at[i], qsend, qrecv, i, (s, deep(i))))
        total = vi[...]
        for i in range(1, F):
            remote(vi, vz.at[i], vsend, vrecv, i, mate).wait_recv()
            total = total + vz[i]
        vp[0] = total
        for i in range(1, S):
            go(remote(vp.at[0], vp.at[i], vsend, vrecv, F - 1 + i, (lax.rem(s + i, S), f)))
        for i in range(1, F):
            remote(qm.at[:, f], qi.at[i], qsend, qrecv, i, mate).wait_recv()

        def sum_q(n, _):
            part = qm[n, f].astype(f32)
            for i in range(1, F):
                part = part + qi[i, n].astype(f32)
            qs_[n] = part.astype(bf)
            return 0

        lax.fori_loop(0, S, sum_q, 0)
        keep = pltpu.make_async_copy(qs_.at[s], qo.at[s], local.at[1])
        keep.start()
        for i in range(1, S):
            to = lax.rem(s + i, S)
            go(remote(qs_.at[to], qo.at[s], qsend, qrecv, F - 1 + i, (to, f)))
        up_load.wait()
        x_load.wait()
        over(0).wait_send()
        used = (1, 2) if square else range(1, P_)
        for i in used:
            if square:
                direct_b(i, 0).wait_recv()
                direct_b(i, 1).wait_recv()
            else:
                out_b(i, chip(i)).wait_recv()

        def below(n, _):
            a = pl.ds(pl.multiple_of(n * rows, rows), rows)
            back = bi[0, a, :].astype(f32)
            for i in used:
                back = back + bp[i - 1, a, :].astype(f32)
            z = xx[a, :].astype(f32)
            r1 = lax.rsqrt(jnp.mean(z * z, axis=-1, keepdims=True) + eps_norm)
            e1 = back * g1[...]
            tilt = jnp.mean(e1 * z, axis=-1, keepdims=True)
            mb[a, :] = (up[a, :] + r1 * e1 - z * (r1 * r1 * r1 * tilt)).astype(bf)
            return 0

        lax.fori_loop(0, T // rows, below, 0)
        outs = [pltpu.make_async_copy(mb, in_out, local.at[0])]
        outs[0].start()
        for i in range(1, F):
            remote(ga.at[:, f], gz.at[i], gsend, grecv, ZG + i, mate).wait_recv()
        for a in range(NW):
            part = ga[a, f].astype(f32)
            for i in range(1, F):
                part = part + gz[i, a].astype(f32)
            go_[a] = part
        outs.append(pltpu.make_async_copy(go_, g_out, local.at[2]))
        outs[1].start()
        total = vp[0]
        for i in range(1, S):
            remote(vp.at[0], vp.at[i], vsend, vrecv, F - 1 + i, mate).wait_recv()
            total = total + vp[i]
        vo[...] = total
        outs.append(pltpu.make_async_copy(vo, vec_out, nsem.at[0]))
        outs[2].start()
        for i in range(1, S):
            src = lax.rem(s + S - i, S)
            remote(qs_.at[0], qo.at[src], qsend, qrecv, F - 1 + i, mate).wait_recv()
        keep.wait()
        outs.append(pltpu.make_async_copy(qo, q_out, local.at[1]))
        outs[3].start()
        for out in outs:
            out.wait()
        for copy in todo:
            copy.wait_send()
        for i in range(1, F):
            deep_g(i).wait_send()
        for i in used:
            if square:
                relay_g(i).wait_send()
                relay_b(i).wait_send()
                for half in range(2):
                    direct_g(i, half).wait_send()
                    direct_b(i, half).wait_send()
            else:
                out_g(i).wait_send()
                out_b(i, chip(i)).wait_send()

    pl.run_scoped(
        closing,
        V((D, 3 * C), f32),
        V((T, D), f32),
        V((S, F, R, 3 * C), bf),
        V((S, R, 3 * C), bf),
        V((NW, R, D), f32),
        V(vec.shape, f32),
    )


def backward_all(S, F, nh, dm, qt, kt, q, k, v, ot, lse, n1, x_all, w, sc, g1, gi, vec, dx2):
    T, D = x_all.shape[1], x_all.shape[2]
    C = nh * HD
    L = S * T
    P_ = S // 2
    NW, R = gi.shape[1], gi.shape[3]
    any_ = pl.BlockSpec(memory_space=pl.ANY)
    vm = pl.BlockSpec(memory_space=pltpu.VMEM)
    dma = pltpu.SemaphoreType.DMA
    shape = jax.ShapeDtypeStruct
    V = pltpu.VMEM
    return pl.pallas_call(
        functools.partial(backward_kernel, S, F, nh),
        out_shape=[
            shape((NW, R, D), f32),
            shape((T, D), bf),
            shape((S, R, 3 * C), bf),
            shape(vec.shape, f32),
            shape((P_, NW, F, R, D), bf),
            shape((2, NW, F // 2, R, D), bf),
            shape((2, NW, F // 2, R, D), bf),
        ],
        in_specs=[any_] + [vm] * 7 + [any_, any_, vm, vm, vm, any_, vm, any_],
        out_specs=[any_] * 7,
        scratch_shapes=[
            V((C, L), bf),
            V((3 * C, D), bf),
            V((3 * C, D), f32),
            V((3 * C, T), bf),
            V((T, 3 * C), bf),
            V((T, D), bf),
            V((T, D), bf),
            V((T, 1), f32),
            V((T, D), bf),
            V((T, D), bf),
            V((P_, T, D), bf),
            V((2 if P_ == 4 else P_ - 1, T, D), bf),
            V((2, T // 2, D), bf),
            V((NW, F, R, D), bf),
            V((NW, F, R, D), bf),
            V((F, NW, R, D), bf),
            V((F, S, R, 3 * C), bf),
            V((S, R, 3 * C), bf),
            V(vec.shape, f32),
            V((F,) + vec.shape, f32),
            V((S,) + vec.shape, f32),
            V((1, D), f32),
            V((C, 1), f32),
            dma((3,)),
            dma((2,)),
            dma((S,)),
            dma((10 + 2 * P_ + F,)),
            dma((10 + 2 * P_ + F,)),
            dma((max(2 * P_, 10),)),
            dma((max(2 * P_, 10),)),
            dma((S + F,)),
            dma((S + F,)),
            dma((S + F,)),
            dma((S + F,)),
        ],
        compiler_params=pltpu.CompilerParams(
            collective_id=4, has_side_effects=True, vmem_limit_bytes=66_000_000
        ),
        name="backward",
    )(dm, qt, kt, q, k, v, ot, lse, n1, x_all, w, sc, g1, gi, vec, dx2)


def body(
    inputs,
    w_query,
    w_key,
    w_value,
    w_proj,
    w_up,
    w_down,
    gain_first,
    gain_second,
    bias_up,
    bias_down,
    query_scale,
    cotangent,
):
    groups = lax.axis_size("seq")
    rows_of = lax.axis_size("fsdp")
    nh = H // groups
    cols = nh * HD
    both = ("seq", "fsdp")
    tokens, width = inputs.shape[1], inputs.shape[2]
    length = tokens * groups
    shard = w_query.shape[0]
    x_low = inputs.reshape(tokens, width)
    qkv_rows = jnp.stack([w_query, w_key, w_value], 1).astype(bf).reshape(shard, 3, groups, cols)
    qkv_rows = qkv_rows.transpose(2, 0, 1, 3).reshape(groups, shard, 3 * cols)
    small = jnp.stack([gain_first, gain_second, bias_up, bias_down], 0)
    small = jnp.pad(small.astype(bf), ((0, 12), (0, 128 - shard)))
    weights = jnp.stack([w_proj, w_up, w_down], 0).astype(bf)
    x_all, qkv_w, small, weights = gather_all(groups, rows_of, x_low, qkv_rows, small, weights)
    qkv_w = qkv_w.reshape(width, 3 * cols)
    small = small[:, :, :4, :shard].transpose(2, 0, 1, 3).reshape(4, width).astype(f32)
    scale_dims = jax.nn.softplus(query_scale) * log_two_inverse / math.sqrt(HD)
    scale_cols = jnp.tile(scale_dims, nh)
    normed, qt, kt, q, k, v, ot, lse, mixed, weights = forward_all(
        groups, rows_of, nh, x_all, qkv_w, small[:1], scale_cols[:, None], weights
    )
    result, grad_middle, dm, pairs, vectors = middle_all(
        groups,
        rows_of,
        nh,
        mixed,
        x_low,
        cotangent.reshape(tokens, width),
        weights.reshape(3, width, width),
        small,
    )
    owned, grad_inputs, grad_qkv, vectors, *unused = backward_all(
        groups,
        rows_of,
        nh,
        dm,
        qt,
        kt,
        q,
        k,
        v,
        ot,
        lse,
        normed,
        x_all,
        qkv_w,
        scale_cols[:, None],
        small[:1],
        pairs.reshape(groups // 2, 3, rows_of, shard, width),
        vectors,
        grad_middle,
    )
    grad_qkv = grad_qkv.reshape(groups, shard, 3, cols).transpose(2, 1, 0, 3)
    grad_qkv = grad_qkv.reshape(3, shard, width).astype(f32)
    at = (lax.axis_index("seq") * rows_of + lax.axis_index("fsdp")) * shard
    mine = lax.dynamic_slice_in_dim(vectors, at, shard, 1)
    scale_total = jnp.sum(vectors[4, :cols].reshape(nh, HD), axis=0) / scale_dims
    grad_scale = scale_total * jax.nn.sigmoid(query_scale) * log_two_inverse / math.sqrt(HD)
    return (
        result.reshape(inputs.shape),
        grad_inputs.reshape(inputs.shape),
        grad_qkv[0],
        grad_qkv[1],
        grad_qkv[2],
        owned[0],
        owned[1],
        owned[2],
        mine[0],
        mine[1],
        mine[2],
        mine[3],
        grad_scale,
    )


def solution(mesh):
    return jax.shard_map(
        body,
        mesh=mesh,
        in_specs=(
            P("fsdp", "seq", None),
            P(("seq", "fsdp"), None),
            P(("seq", "fsdp"), None),
            P(("seq", "fsdp"), None),
            P(("seq", "fsdp"), None),
            P(("seq", "fsdp"), None),
            P(("seq", "fsdp"), None),
            P(("seq", "fsdp")),
            P(("seq", "fsdp")),
            P(("seq", "fsdp")),
            P(("seq", "fsdp")),
            P(),
            P("fsdp", "seq", None),
        ),
        out_specs=(
            P("fsdp", "seq", None),
            P("fsdp", "seq", None),
            P(("seq", "fsdp"), None),
            P(("seq", "fsdp"), None),
            P(("seq", "fsdp"), None),
            P(("seq", "fsdp"), None),
            P(("seq", "fsdp"), None),
            P(("seq", "fsdp"), None),
            P(("seq", "fsdp")),
            P(("seq", "fsdp")),
            P(("seq", "fsdp")),
            P(("seq", "fsdp")),
            P(),
        ),
        check_vma=False,
    )
```

```python
import functools
import math

import jax
import jax.numpy as jnp
from jax import lax
from jax.experimental import pallas as pl
from jax.experimental.pallas import tpu as pltpu
from jax.sharding import PartitionSpec as P

H = 16
HD = 80
eps_norm = 1e-06
log_two_inverse = 1.442695
bf = jnp.bfloat16
f32 = jnp.float32
NEG = -1e30


def dot(a,b,ca=1,cb=0):
    return lax.dot_general(a,b,(((ca,),(cb,)),((),())),preferred_element_type=f32)


MESH = pl.DeviceIdType.MESH


def spots():
    s, f = lax.axis_index("seq"), lax.axis_index("fsdp")
    return s, f, s // 2, lax.rem(s, 2)


def greet(S, F):
    s, f, _, _ = spots()
    barrier = pltpu.get_barrier_semaphore()
    for i in range(1, S):
        pl.semaphore_signal(barrier, inc=1, device_id=(lax.rem(s + i, S), f), device_id_type=MESH)
    for i in range(1, F):
        pl.semaphore_signal(barrier, inc=1, device_id=(s, lax.rem(f + i, F)), device_id_type=MESH)
    pl.semaphore_wait(barrier, S + F - 2)


def remote(src, dst, sends, recvs, n, to):
    return pltpu.make_async_remote_copy(
        src_ref=src,
        dst_ref=dst,
        send_sem=sends.at[n],
        recv_sem=recvs.at[n],
        device_id=to,
        device_id_type=MESH,
    )


def gather_kernel(S, F, x, wq, sm, wm, x_all, wq_all, sm_all, wm_all, xv, qv, sv, mv, local,
                  xs, xr, qs, qr, ss, sr, ms, mr):
    s, f, p, c = spots()
    P_ = S // 2
    other = 1 - c
    loads = [
        pltpu.make_async_copy(sm, sv, local.at[0]),
        pltpu.make_async_copy(wq, qv, local.at[1]),
        pltpu.make_async_copy(x, xv, local.at[2]),
        pltpu.make_async_copy(wm, mv, local.at[3]),
    ]
    for load in loads:
        load.start()
    greet(S, F)
    mate = (p * 2 + other, f)
    todo = []

    def go(copy):
        copy.start()
        todo.append(copy)

    def chip(i):
        return lax.rem(p + i, P_) * 2 + c

    def back(i):
        return lax.rem(p + P_ - i, P_) * 2 + c

    def near_chip(i):
        return flip_bits(p, i) * 2 + c

    H_ = x.shape[0] // 2

    def deep(i):
        return lax.rem(f + i, F)

    def behind(i):
        return lax.rem(f + F - i, F)

    loads[0].wait()
    keep0 = pltpu.make_async_copy(sv, sm_all.at[s, f], local.at[0])
    keep0.start()
    for i in range(1, F):
        go(remote(sv, sm_all.at[s, f], ss, sr, i, (s, deep(i))))
    loads[1].wait()
    keep1 = pltpu.make_async_copy(qv.at[s], wq_all.at[s, f], local.at[1])
    keep1.start()
    for i in range(1, S):
        to = lax.rem(s + i, S)
        go(remote(qv.at[to], wq_all.at[s, f], qs, qr, i, (to, f)))
    loads[2].wait()
    keep2 = pltpu.make_async_copy(xv, x_all.at[s], local.at[2])
    keep2.start()
    if P_ == 4:
        for first in range(2):
            for i in (1, 2):
                half = first if i == 1 else 1 - first
                part = pl.ds(half * H_, H_)
                go(remote(xv.at[part], x_all.at[s, part], xs, xr, 2 * i + half, (near_chip(i), f)))
    else:
        for i in range(1, P_):
            go(remote(xv, x_all.at[s], xs, xr, i, (chip(i), f)))
    go(remote(xv, x_all.at[s], xs, xr, 0, mate))
    loads[3].wait()
    keep3 = pltpu.make_async_copy(mv, wm_all.at[:, f], local.at[3])
    keep3.start()
    for i in range(1, F):
        go(remote(mv, wm_all.at[:, f], ms, mr, i, (s, deep(i))))
    for i in range(1, F):
        g = behind(i)
        remote(sv, sm_all.at[s, g], ss, sr, i, mate).wait_recv()
    keep0.wait()
    for i in range(1, S):
        go(remote(sm_all.at[s], sm_all.at[s], ss, sr, F - 1 + i, (lax.rem(s + i, S), f)))
    for i in range(1, S):
        remote(qv.at[0], wq_all.at[lax.rem(s + S - i, S), f], qs, qr, i, mate).wait_recv()
    keep1.wait()
    for i in range(1, F):
        go(remote(wq_all.at[:, f], wq_all.at[:, f], qs, qr, S - 1 + i, (s, deep(i))))
    for i in range(1, F):
        remote(mv, wm_all.at[:, behind(i)], ms, mr, i, mate).wait_recv()
    keep3.wait()
    if P_ == 4:
        for i in (1, 2):
            half = i - 1
            part = pl.ds(half * H_, H_)
            src = near_chip(i)
            remote(xv.at[part], x_all.at[src, part], xs, xr, 2 * i + half, mate).wait_recv()
            blk = x_all.at[src, part]
            go(remote(blk, blk, xs, xr, 6 + half, (near_chip(3 - i), f)))
        for i in (1, 2):
            half = 2 - i
            part = pl.ds(half * H_, H_)
            src = near_chip(i)
            remote(xv.at[part], x_all.at[src, part], xs, xr, 2 * i + half, mate).wait_recv()
            go(remote(x_all.at[src], x_all.at[src], xs, xr, 8 + i, mate))
    for i in range(1, P_ if P_ != 4 else 1):
        src = back(i)
        remote(xv, x_all.at[src], xs, xr, i, mate).wait_recv()
        go(remote(x_all.at[src], x_all.at[src], xs, xr, P_ - 1 + i, mate))
    for i in range(1, S):
        src = lax.rem(s + S - i, S)
        remote(sm_all.at[src], sm_all.at[src], ss, sr, F - 1 + i, mate).wait_recv()
    for i in range(1, F):
        g = behind(i)
        remote(wq_all.at[:, g], wq_all.at[:, g], qs, qr, S - 1 + i, mate).wait_recv()
    near = p * 2 + other
    remote(xv, x_all.at[near], xs, xr, 0, mate).wait_recv()
    if P_ == 4:
        for half in range(2):
            part = pl.ds(half * H_, H_)
            blk = x_all.at[near_chip(3), part]
            remote(blk, blk, xs, xr, 6 + half, mate).wait_recv()
            go(remote(blk, blk, xs, xr, 11 + half, mate))
        for i in (1, 2):
            blk = x_all.at[flip_bits(p, i) * 2 + other]
            remote(blk, blk, xs, xr, 8 + i, mate).wait_recv()
        for half in range(2):
            blk = x_all.at[flip_bits(p, 3) * 2 + other, pl.ds(half * H_, H_)]
            remote(blk, blk, xs, xr, 11 + half, mate).wait_recv()
    else:
        for i in range(1, P_):
            src = lax.rem(p + P_ - i, P_) * 2 + other
            remote(xv, x_all.at[src], xs, xr, P_ - 1 + i, mate).wait_recv()
    keep2.wait()
    for copy in todo:
        copy.wait_send()


def gather_all(S, F, x, wq, sm, wm):
    any_ = pl.BlockSpec(memory_space=pl.ANY)
    shapes = [
        (S,) + x.shape,
        (S, F) + wq.shape[1:],
        (S, F) + sm.shape,
        (wm.shape[0], F) + wm.shape[1:],
    ]
    P_ = S // 2
    dma = pltpu.SemaphoreType.DMA
    counts = [max(2 * P_ - 1, 12), S + F - 1, F + S - 1, F]
    sems = []
    for n in counts:
        sems += [dma((n + 1,)), dma((n + 1,))]
    return pl.pallas_call(
        functools.partial(gather_kernel, S, F),
        out_shape=[
            jax.ShapeDtypeStruct(sh, a.dtype) for sh, a in zip(shapes, (x, wq, sm, wm), strict=True)
        ],
        in_specs=[any_] * 4,
        out_specs=[any_] * 4,
        scratch_shapes=[
            pltpu.VMEM(x.shape, x.dtype),
            pltpu.VMEM(wq.shape, wq.dtype),
            pltpu.VMEM(sm.shape, sm.dtype),
            pltpu.VMEM(wm.shape, wm.dtype),
            dma((4,)),
        ]
        + sems,
        compiler_params=pltpu.CompilerParams(collective_id=1, has_side_effects=True),
        name="gather",
    )(x, wq, sm, wm)


def xor(a, b, n):
    out, bit = 0, 1
    while bit < n:
        both = lax.rem(lax.div(a, bit), 2) + lax.rem(lax.div(b, bit), 2)
        out = out + bit * lax.rem(both, 2)
        bit *= 2
    return out


def flip_bits(p, i):
    out, bit = p, 1
    while bit <= i:
        if i & bit:
            out = out + bit - 2 * bit * lax.rem(lax.div(p, bit), 2)
        bit *= 2
    return out


def forward_kernel(S, F, nh, x_all, w, g1, sc, wz, n1, qt, kt, qn, kk, vn, ot, lse, mixed, wm,
                   wt, vt, xb, nb, wv, inx, outn, local, osend, orecv, wsend, wrecv):
    s, f, p, c = spots()
    P_ = S // 2
    T, D = x_all.shape[1], x_all.shape[2]
    C = nh * HD
    L = S * T
    BQ = 2 * T
    BK = min(512, BQ)
    other = 1 - c
    mate = (p * 2 + other, f)
    load = pltpu.make_async_copy(wz, wv, local.at[0])
    load.start()

    def fetch(b):
        return pltpu.make_async_copy(x_all.at[b], xb.at[lax.rem(b, 2)], inx.at[lax.rem(b, 2)])

    def store(b):
        return pltpu.make_async_copy(nb.at[lax.rem(b, 2)], n1.at[b], outn.at[lax.rem(b, 2)])

    fetch(0).start()
    greet(S, F)
    load.wait()
    keep = pltpu.make_async_copy(wv, wm.at[:, s], local.at[0])
    keep.start()

    zero = s - s
    chips = [flip_bits(p, i) for i in range(P_)]

    def num(n):
        return zero + n

    def spread(i):
        return remote(wv, wm.at[:, s], wsend, wrecv, i, (xor(p, i, P_) * 2 + c, f))

    def forward(i):
        src = xor(p, i, P_) * 2 + c
        n = (7 if P_ == 4 else P_) + i
        return remote(wm.at[:, src], wm.at[:, src], wsend, wrecv, n, mate)

    def part_of(src, half):
        return wm.at[:, src, pl.ds(num(half * (F // 2)), F // 2)]

    def direct(i, half):
        src = wv.at[:, pl.ds(half * (F // 2), F // 2)]
        to = (flip_bits(p, i) * 2 + c, f)
        return remote(src, part_of(s, half), wsend, wrecv, 2 * i + half, to)

    def arrived(i, half):
        blk = part_of(chips[i] * 2 + c, half)
        remote(blk, blk, wsend, wrecv, num(2 * i + half), mate).wait_recv()

    def relay(i):
        blk = part_of(flip_bits(p, i) * 2 + c, i - 1)
        return remote(blk, blk, wsend, wrecv, 5 + i, (flip_bits(p, 3 - i) * 2 + c, f))

    def relayed(half):
        blk = part_of(chips[3] * 2 + c, half)
        return remote(blk, blk, wsend, wrecv, num(6 + half), mate)

    def corner(half, core):
        blk = part_of(chips[3] * 2 + core, half)
        return remote(blk, blk, wsend, wrecv, num(10 + half), mate)

    square = P_ == 4
    if square:
        for first in range(2):
            for i in (1, 2):
                direct(i, first if i == 1 else 1 - first).start()
    else:
        for i in range(1, P_):
            spread(P_ - i).start()
    near = remote(wv, wm.at[:, s], wsend, wrecv, 0, mate)
    near.start()
    wt[...] = jnp.transpose(w[...])

    rows = 64

    def project(b, _):
        slot = lax.rem(b, 2)
        fetch(b).wait()

        @pl.when(b + 1 < S)
        def _():
            fetch(b + 1).start()

        @pl.when(b >= 2)
        def _():
            store(b - 2).wait()

        def norm(k, _):
            at = pl.ds(pl.multiple_of(k * rows, rows), rows)
            v = xb[slot, at, :].astype(f32)
            r = lax.rsqrt(jnp.mean(v * v, axis=-1, keepdims=True) + eps_norm)
            nb[slot, at, :] = (v * r * g1[...]).astype(bf)
            return 0

        lax.fori_loop(0, T // rows, norm, 0)
        store(b).start()
        cols = pl.ds(pl.multiple_of(b * T, T), T)
        res = dot(wt[...], nb[slot], 1, 1)
        qt[:, cols] = (res[:C] * sc[...]).astype(bf)
        kt[:, cols] = res[C : 2 * C].astype(bf)
        vt[:, cols] = res[2 * C :].astype(bf)
        for h in range(nh):
            part = slice(h * HD, (h + 1) * HD)
            qn[h, cols, :] = jnp.transpose(res[:C][part] * sc[part]).astype(bf)
            kk[h, cols, :] = jnp.transpose(res[C : 2 * C][part]).astype(bf)
            vn[h, cols, :] = jnp.transpose(res[2 * C :][part]).astype(bf)
        return 0

    lax.fori_loop(0, S, project, 0)
    if square:
        for i in (1, 2):
            arrived(i, i - 1)
            relay(i).start()
    store(S - 2).wait()
    store(S - 1).wait()

    r = BQ // BK

    def attend(t):
        first = pl.multiple_of(t * BQ, BQ)
        q = [qt[h * HD : (h + 1) * HD, pl.ds(first, BQ)] for h in range(nh)]

        def step(j, carry, diag=None):
            at = pl.ds(pl.multiple_of(j * BK, BK), BK)
            scores = [dot(kk[h, at, :], q[h]) for h in range(nh)]
            out = []
            for h in range(nh):
                m, l, acc = carry[h]
                sh = scores[h]
                if diag is not None:
                    kp = lax.broadcasted_iota(jnp.int32, sh.shape, 0) + diag * BK
                    qp = lax.broadcasted_iota(jnp.int32, sh.shape, 1)
                    sh = jnp.where(kp <= qp, sh, NEG)
                mn = jnp.maximum(m, jnp.max(sh, axis=0, keepdims=True))
                a = jnp.exp(m - mn)
                e = jnp.exp(sh - mn)
                l = l * a + jnp.sum(e, axis=0, keepdims=True)
                acc = acc * a + dot(vt[h * HD : (h + 1) * HD, at], e.astype(bf))
                out.append((mn, l, acc))
            return tuple(out)

        carry = tuple(
            (jnp.full((1, BQ), NEG, f32), jnp.zeros((1, BQ), f32), jnp.zeros((HD, BQ), f32))
            for _ in range(nh)
        )
        carry = lax.fori_loop(0, t * r, step, carry)
        for d in range(r):
            carry = step(t * r + d, carry, d)
        for h in range(nh):
            m, l, acc = carry[h]
            ot[h * HD : (h + 1) * HD, pl.ds(first, BQ)] = (acc / l).astype(bf)
            lse[h : h + 1, pl.ds(first, BQ)] = m + jnp.log(l)

    def to_owner(src, n, i, to):
        return pltpu.make_async_remote_copy(
            src_ref=src,
            dst_ref=mixed.at[s],
            send_sem=osend.at[n],
            recv_sem=orecv.at[2 * i + c],
            device_id=to,
            device_id_type=MESH,
        )

    def send(i, half):
        t = xor(p, i, P_)
        src = ot.at[:, pl.ds(pl.multiple_of(t * BQ + half * T, T), T)]
        return to_owner(src, 2 * i + half, i, (t * 2 + half, f))

    def turn(n, _):
        i = P_ - 1 - n
        attend(xor(p, i, P_))
        send(i, 0).start()
        send(i, 1).start()
        if not square:
            spread(i).wait_recv()
            forward(i).start()
            return 0

        @pl.when(i == 3)
        def _():
            arrived(2, 0)
            forward(num(2)).start()

        @pl.when(i == 2)
        def _():
            arrived(1, 1)
            forward(num(1)).start()

        @pl.when(i == 1)
        def _():
            for half in range(2):
                relayed(half).wait_recv()
                corner(half, c).start()

        return 0

    lax.fori_loop(0, P_ - 1, turn, 0)
    attend(p)
    mine = ot.at[:, pl.ds(pl.multiple_of(s * T, T), T)]
    theirs = ot.at[:, pl.ds(pl.multiple_of((p * 2 + other) * T, T), T)]
    last = to_owner(theirs, 0, 0, mate)
    last.start()
    own = pltpu.make_async_copy(mine, mixed.at[s], local.at[1])
    own.start()
    def from_source(i, core):
        return pltpu.make_async_remote_copy(
            src_ref=mine,
            dst_ref=mixed.at[flip_bits(p, i) * 2 + core],
            send_sem=osend.at[0],
            recv_sem=orecv.at[2 * i + core],
            device_id=mate,
            device_id_type=MESH,
        )

    for i in range(1, P_):
        for core in range(2):
            from_source(i, core).wait_recv()
    from_source(0, other).wait_recv()
    last.wait_send()
    own.wait()
    keep.wait()
    near.wait()
    if square:
        for i in (1, 2):
            forward(i).wait()
            relay(i).wait_send()
            for half in range(2):
                direct(i, half).wait_send()
        for half in range(2):
            corner(half, c).wait_send()
            corner(half, other).wait_recv()
    for i in range(1, P_):
        if not square:
            forward(i).wait()
            spread(i).wait_send()
        send(i, 0).wait_send()
        send(i, 1).wait_send()


def forward_all(S, F, nh, x_all, w, g1, sc, wz):
    T, D = x_all.shape[1], x_all.shape[2]
    C = nh * HD
    L = S * T
    P_ = S // 2
    any_ = pl.BlockSpec(memory_space=pl.ANY)
    vm = pl.BlockSpec(memory_space=pltpu.VMEM)
    dma = pltpu.SemaphoreType.DMA
    shape = jax.ShapeDtypeStruct
    NW, R = wz.shape[0], wz.shape[2]
    V = pltpu.VMEM
    return pl.pallas_call(
        functools.partial(forward_kernel, S, F, nh),
        out_shape=[
            shape((S, T, D), bf),
            shape((C, L), bf),
            shape((C, L), bf),
            shape((nh, L, HD), bf),
            shape((nh, L, HD), bf),
            shape((nh, L, HD), bf),
            shape((C, L), bf),
            shape((nh, L), f32),
            shape((S, C, T), bf),
            shape((NW, S, F, R, D), bf),
        ],
        in_specs=[any_, vm, vm, vm, any_],
        out_specs=[any_] + [vm] * 7 + [any_, any_],
        scratch_shapes=[
            V((3 * C, D), bf),
            V((C, L), bf),
            V((2, T, D), bf),
            V((2, T, D), bf),
            V((NW, F, R, D), bf),
            dma((2,)),
            dma((2,)),
            dma((2,)),
            dma((2 * P_,)),
            dma((2 * P_,)),
            dma((max(2 * P_, 12),)),
            dma((max(2 * P_, 12),)),
        ],
        compiler_params=pltpu.CompilerParams(
            collective_id=3, has_side_effects=True, vmem_limit_bytes=60 << 20
        ),
        name="forward",
    )(x_all, w, g1, sc, wz)


def middle_kernel(S, F, nh, mixed, x, ct, wm, small, out, dx2, dm, gi, vec,
                  mx, lt, xv, cv, wv, x2, n2, dn, ab, ub, eb, r2, sb, rb, ob, dov, rv, vz, vp, local, wsem,
                  dsend, drecv, gsend, grecv, vsend, vrecv):
    s, f, p, c = spots()
    P_ = S // 2
    T, D = x.shape
    C = nh * HD
    NW = wm.shape[0]
    G = D // S
    other = 1 - c
    mate = (p * 2 + other, f)
    wide = 256 if D % 256 == 0 else D
    rows = 64
    loads = [
        pltpu.make_async_copy(mixed, mx, local.at[0]),
        pltpu.make_async_copy(x, xv, local.at[1]),
        pltpu.make_async_copy(ct, cv, local.at[2]),
    ]
    loads += [pltpu.make_async_copy(wm.at[n], wv.at[n], wsem.at[n]) for n in range(NW)]
    for load in loads:
        load.start()
    greet(S, F)
    g2, b1, b2 = small[1:2, :], small[2:3, :], small[3:4, :]

    def by_core(n, tall):
        for t in range(P_):
            for core in range(2):
                at = (t * 2 + core) * G
                lt[n, core, t * G : (t + 1) * G, :] = tall[at : at + G]

    def chunk(n):
        return pl.ds(pl.multiple_of(n * wide, wide), wide)

    def over(n, body):
        def one(k, _):
            body(k)
            return 0

        lax.fori_loop(0, n, one, 0)

    def lines(n):
        return pl.ds(pl.multiple_of(n * rows, rows), rows)

    loads[0].wait()
    tall = mx[...].reshape(D, T)
    by_core(0, tall)
    ub[...] = jnp.transpose(tall)
    loads[1].wait()
    loads[2].wait()
    loads[3].wait()

    def attend_out(n):
        at = chunk(n)
        x2[:, at] = xv[:, at].astype(f32) + dot(ub[...], wv[0, :, at])

    over(D // wide, attend_out)

    def norm(n):
        at = lines(n)
        z = x2[at, :]
        r = lax.rsqrt(jnp.mean(z * z, axis=-1, keepdims=True) + eps_norm)
        r2[at, :] = r
        n2[at, :] = (z * r * g2).astype(bf)

    over(T // rows, norm)
    loads[4].wait()
    loads[5].wait()
    rv[...] = jnp.zeros_like(rv)

    def hidden(n):
        at = chunk(n)
        u = dot(n2[...], wv[1, :, at]) + small[2:3, at]
        gate = 1 / (1 + jnp.exp(-u))
        ab[:, at] = (u * gate).astype(bf)
        ga = dot(cv[...], wv[2, at, :], 1, 1)
        du = ga * (gate * (1 + u * (1 - gate)))
        rv[2:3, at] = jnp.sum(du, axis=0, keepdims=True)
        ub[:, at] = du.astype(bf)
        rv[3:4, at] = jnp.sum(cv[:, at].astype(f32), axis=0, keepdims=True)

    over(D // wide, hidden)

    def up_back(n):
        at = chunk(n)
        dn[:, at] = dot(ub[...], wv[1, at, :], 1, 1)

    over(D // wide, up_back)

    def second(n):
        at = lines(n)
        z, r, d = x2[at, :], r2[at, :], dn[at, :]
        e = d * g2
        tilt = jnp.mean(e * z, axis=-1, keepdims=True)
        v = cv[at, :].astype(f32) + r * e - z * (r * r * r * tilt)
        rv[1:2, :] += jnp.sum(d * z * r, axis=0, keepdims=True)
        dn[at, :] = v
        eb[at, :] = v.astype(bf)

    over(T // rows, second)
    keep = pltpu.make_async_copy(dn, dx2, local.at[0])
    keep.start()

    def vec_z(i):
        return remote(rv, vz.at[i], vsend, vrecv, i, (s, lax.rem(f + i, F)))

    def vec_s(i):
        return remote(vp.at[0], vp.at[i], vsend, vrecv, F - 1 + i, (lax.rem(s + i, S), f))

    for i in range(1, F):
        vec_z(i).start()

    def head_out(i, to):
        return remote(dov.at[i], dm.at[s], dsend, drecv, i, (to, f))

    def heads(i, _):
        to = lax.rem(s + i, S)
        rows_of = pl.ds(pl.multiple_of(to * C, C), C)
        dov[i] = dot(wv[0, rows_of, :], eb[...], 1, 1).astype(bf)

        head_out(i, to).start()
        return 0

    lax.fori_loop(1, S, heads, 0)
    mine = pl.ds(pl.multiple_of(s * C, C), C)
    dov[0] = dot(wv[0, mine, :], eb[...], 1, 1).astype(bf)
    home = pltpu.make_async_copy(dov.at[0], dm.at[s], local.at[1])
    home.start()

    by_core(1, jnp.transpose(n2[...]))
    by_core(2, jnp.transpose(ab[...]))
    right = [eb, ub, cv]

    def pass_on(n):
        return remote(sb.at[n], rb.at[n], gsend, grecv, n, mate)

    for n in range(NW):

        def send_side(k, n=n):
            at = chunk(k)
            sb[n, :, at] = dot(lt[n, other], right[n][:, at]).astype(bf)

        over(D // wide, send_side)
        pass_on(n).start()

    part = rv[...]
    for i in range(1, F):
        vec_z(i).wait_recv()
        part = part + vz[i]
    vp[0] = part
    for i in range(1, S):
        vec_s(i).start()

    def top(n):
        at = chunk(n)
        y = x2[:, at] + dot(ab[...], wv[2, :, at]) + small[3:4, at]
        xv[:, at] = y.astype(bf)

    over(D // wide, top)
    done = pltpu.make_async_copy(xv, out, local.at[2])
    done.start()
    for n in range(NW):
        pass_on(n).wait_recv()

        def keep_side(k, n=n):
            at = chunk(k)
            both = dot(lt[n, c], right[n][:, at]) + rb[n, :, at].astype(f32)
            ob[n, :, at] = both.astype(bf)

        over(D // wide, keep_side)
    stores = []
    for i in range(P_):
        here = pl.ds(pl.multiple_of(flip_bits(p, i) * G, G), G)
        stores.append(pltpu.make_async_copy(ob.at[:, here], gi.at[i], wsem.at[i]))
        stores[-1].start()
    part = vp[0]
    for i in range(1, S):
        vec_s(i).wait_recv()
        part = part + vp[i]
    vec[...] = part
    for i in range(1, F):
        vec_z(i).wait_send()
    for i in range(1, S):
        vec_s(i).wait_send()
    for i in range(1, S):
        remote(dov.at[0], dm.at[lax.rem(s + S - i, S)], dsend, drecv, i, mate).wait_recv()
    for store in stores:
        store.wait()
    keep.wait()
    home.wait()
    done.wait()
    for i in range(1, S):
        head_out(i, lax.rem(s + i, S)).wait_send()
    for n in range(NW):
        pass_on(n).wait_send()


def middle_all(S, F, nh, mixed, x, ct, wm, small):
    T, D = x.shape
    C = nh * HD
    P_ = S // 2
    NW = wm.shape[0]
    G = D // S
    any_ = pl.BlockSpec(memory_space=pl.ANY)
    vm = pl.BlockSpec(memory_space=pltpu.VMEM)
    dma = pltpu.SemaphoreType.DMA
    shape = jax.ShapeDtypeStruct
    V = pltpu.VMEM
    return pl.pallas_call(
        functools.partial(middle_kernel, S, F, nh),
        out_shape=[
            shape((T, D), bf),
            shape((T, D), f32),
            shape((S, C, T), bf),
            shape((P_, NW, G, D), bf),
            shape((8, D), f32),
        ],
        in_specs=[any_, any_, any_, any_, vm],
        out_specs=[any_, any_, any_, any_, vm],
        scratch_shapes=[
            V((S, C, T), bf),
            V((NW, 2, P_ * G, T), bf),
            V((T, D), bf),
            V((T, D), bf),
            V((NW, D, D), bf),
            V((T, D), f32),
            V((T, D), bf),
            V((T, D), f32),
            V((T, D), bf),
            V((T, D), bf),
            V((T, D), bf),
            V((T, 1), f32),
            V((NW, P_ * G, D), bf),
            V((NW, P_ * G, D), bf),
            V((NW, P_ * G, D), bf),
            V((S, C, T), bf),
            V((8, D), f32),
            V((F, 8, D), f32),
            V((S, 8, D), f32),
            dma((3,)),
            dma((max(NW, P_),)),
            dma((S,)),
            dma((S,)),
            dma((NW,)),
            dma((NW,)),
            dma((S + F,)),
            dma((S + F,)),
        ],
        compiler_params=pltpu.CompilerParams(
            collective_id=5, has_side_effects=True, vmem_limit_bytes=64_000_000
        ),
        name="middle",
    )(mixed, x, ct, wm, small)


def backward_kernel(S, F, nh, dm, qt, kt, q, k, v, ot, lse, n1, x_all, w, sc, g1, gi, dx2,
                    o_proj, o_up, o_down, in_out, o_q, o_k, o_v, vec_out, gp, gr_, gj,
                    dmt, wt, dwt, fm, tm, nx, xx, rr, mb, own, bi, bp, rl, ga, gb, gz, qi, qo,
                    vi, vz, vp, gf, gs_, local, nsem, bload,
                    gsend, grecv, bsend, brecv, qsend, qrecv, vsend, vrecv):
    s, f, p, c = spots()
    P_ = S // 2
    T, D = x_all.shape[1], x_all.shape[2]
    C = nh * HD
    L = S * T
    BQ = 2 * T
    BK = min(512, BQ)
    NW, R = gi.shape[1], gi.shape[3]
    other = 1 - c
    mate = (p * 2 + other, f)
    todo = []

    def go(copy):
        copy.start()
        todo.append(copy)

    chips = [flip_bits(p, i) for i in range(P_)]
    zero = s - s

    def num(n):
        return zero + n

    def chip(i):
        return chips[i]

    deeps = [lax.rem(f + i, F) for i in range(F)]

    def deep(i):
        return deeps[i]

    def head(ref, h, at):
        return ref[h * HD : (h + 1) * HD, at]

    loads = [
        pltpu.make_async_copy(dm.at[b], dmt.at[:, b * T : (b + 1) * T], bload.at[b])
        for b in range(S)
    ]
    for load in loads:
        load.start()
    greet(S, F)

    order = list(range(P_ - 1, -1, -1))
    wt[...] = jnp.transpose(w[...])
    dwt[...] = jnp.zeros_like(dwt)
    gf[...] = jnp.zeros_like(gf)
    gs_[...] = jnp.zeros_like(gs_)
    for load in loads:
        load.wait()

    def slabs(body):
        def one(n, _):
            body(lax.div(n, F), lax.rem(n, F))
            return 0

        lax.fori_loop(0, NW * F, one, 0)

    square = P_ == 4
    ZG = 10 if square else 2 * P_
    FH, H_ = F // 2, T // 2

    def half_g(ref, half):
        return ref.at[:, pl.ds(num(half * FH), FH)]

    def direct_g(i, half):
        src, dst = half_g(gi.at[num(i)], half), half_g(gp.at[num(i)], half)
        if half == 2 - i:
            src = gj.at[num(half)]
        return remote(src, dst, gsend, grecv, num(2 + 2 * i + half), (chip(i) * 2 + c, f))

    def relay_g(i):
        src = half_g(gi.at[num(3)], i - 1)
        return remote(src, gr_.at[num(i - 1)], gsend, grecv, num(7 + i), (chip(i) * 2 + c, f))

    def join_g(i):
        half = 2 - i
        la = pltpu.make_async_copy(half_g(gi.at[num(i)], half), half_g(ga, 0), local.at[num(1)])
        la.start()
        relay_g(3 - i).wait_recv()
        lb = pltpu.make_async_copy(gr_.at[num(half)], half_g(gb, 0), local.at[num(2)])
        lb.start()
        la.wait()
        lb.wait()

        def add(z, _):
            for a in range(NW):
                w_ = num(a)
                ga[w_, z] = (ga[w_, z].astype(f32) + gb[w_, z].astype(f32)).astype(bf)
            return 0

        lax.fori_loop(0, FH, add, 0)
        st = pltpu.make_async_copy(half_g(ga, 0), gj.at[num(half)], local.at[num(1)])
        st.start()
        st.wait()
        direct_g(i, half).start()

    def out_g(i):
        return remote(gi.at[num(i)], gp.at[num(i)], gsend, grecv, num(P_ + i), (chip(i) * 2 + c, f))

    if square:
        relay_g(1).start()
        relay_g(2).start()
        direct_g(2, 1).start()
        direct_g(1, 0).start()
    else:
        for i in order[:-1]:
            out_g(i).start()

    rows = 64
    wide = 256 if D % 256 == 0 else D

    def over(i):
        return remote(mb, bi.at[i], bsend, brecv, i, mate)

    def inverse(slot):
        def one(n, _):
            a = pl.ds(pl.multiple_of(n * rows, rows), rows)
            z = xx[slot, a, :].astype(f32)
            rr[a, :] = lax.rsqrt(jnp.mean(z * z, axis=-1, keepdims=True) + eps_norm)
            return 0

        lax.fori_loop(0, T // rows, one, 0)

    def back_part(slot, a, dst):
        back = dot(tm[slot], wt[:, a])
        dst[:, a] = back.astype(bf)
        hat = xx[slot, :, a].astype(f32) * rr[...]
        gf[:, a] += jnp.sum(back * hat, axis=0, keepdims=True)

    def finish_back(slot, dst):
        inverse(slot)

        def column(n, _):
            back_part(slot, pl.ds(pl.multiple_of(n * wide, wide), wide), dst)
            return 0

        lax.fori_loop(0, D // wide, column, 0)

    def combine(i):
        def one(n, _):
            a = pl.ds(pl.multiple_of(n * rows, rows), rows)
            bi[i, a, :] = (bi[i, a, :].astype(f32) + own[a, :].astype(f32)).astype(bf)
            return 0

        lax.fori_loop(0, T // rows, one, 0)

    def direct_b(i, half):
        part = pl.ds(pl.multiple_of(num(half * H_), H_), H_)
        src, dst = bi.at[num(i), part], bp.at[num(i - 1), part]
        return remote(src, dst, bsend, brecv, num(2 + 2 * i + half), (chip(i) * 2 + c, f))

    def relay_b(i):
        part = pl.ds(pl.multiple_of(num((i - 1) * H_), H_), H_)
        src = bi.at[num(3), part]
        return remote(src, rl.at[num(i - 1)], bsend, brecv, num(7 + i), (chip(i) * 2 + c, f))

    def join_b(i):
        half = 2 - i
        direct_b(i, 1 - half).start()
        relay_b(3 - i).wait_recv()
        few = min(rows, H_)

        def add(n, _):
            here = pl.ds(pl.multiple_of(half * H_ + n * few, few), few)
            there = pl.ds(pl.multiple_of(n * few, few), few)
            both = bi[num(i), here, :].astype(f32) + rl[num(half), there, :].astype(f32)
            bi[num(i), here, :] = both.astype(bf)
            return 0

        lax.fori_loop(0, H_ // few, add, 0)
        direct_b(i, half).start()

    def out_b(i, t):
        return pltpu.make_async_remote_copy(
            src_ref=bi.at[i],
            dst_ref=bp.at[i - 1],
            send_sem=bsend.at[P_ + i],
            recv_sem=brecv.at[P_ + i],
            device_id=(t * 2 + c, f),
            device_id_type=MESH,
        )

    def deep_g(i):
        src = ga.at[:, deep(i)]
        return remote(src, gz.at[num(i)], gsend, grecv, num(ZG + i), (s, deep(i)))

    def plane_sums():
        la = pltpu.make_async_copy(gi.at[num(0)], ga, local.at[num(1)])
        la.start()
        la.wait()
        for i in order[1:-1] if square else order[:-1]:
            if square:
                direct_g(i, 0).wait_recv()
                direct_g(i, 1).wait_recv()
            else:
                out_g(i).wait_recv()
            lb = pltpu.make_async_copy(gp.at[num(i)], gb, local.at[num(2)])
            lb.start()
            lb.wait()

            def more(z, _):
                for a in range(NW):
                    w_ = num(a)
                    ga[w_, z] = (ga[w_, z].astype(f32) + gb[w_, z].astype(f32)).astype(bf)
                return 0

            lax.fori_loop(0, F, more, 0)
        for i in range(1, F):
            deep_g(i).start()

    def attention(do, delta, dqt, dk, dv):
        dqt[...] = jnp.zeros_like(dqt)
        dk[...] = jnp.zeros_like(dk)
        dv[...] = jnp.zeros_like(dv)

        def turn(b, _):
            at = pl.ds(pl.multiple_of(b * T, T), T)
            for h in range(nh):
                do[h, at, :] = jnp.transpose(head(dmt, h, at))
                prod = head(dmt, h, at).astype(f32) * head(ot, h, at).astype(f32)
                delta[h : h + 1, at] = jnp.sum(prod, axis=0, keepdims=True)
            return 0

        lax.fori_loop(0, S, turn, 0)

        def tile(q0, k0, masked):
            qa = pl.ds(q0, BK)
            ka = pl.ds(k0, BK)
            scores = [dot(k[h, ka, :], head(qt, h, qa)) for h in range(nh)]
            dps = [dot(v[h, ka, :], head(dmt, h, qa)) for h in range(nh)]
            for h in range(nh):
                e = jnp.exp(scores[h] - lse[h : h + 1, qa])
                if masked:
                    kp = lax.broadcasted_iota(jnp.int32, e.shape, 0)
                    qp = lax.broadcasted_iota(jnp.int32, e.shape, 1)
                    e = jnp.where(kp <= qp, e, 0.0)
                ds = (e * (dps[h] - delta[h : h + 1, qa])).astype(bf)
                dv[h, ka, :] += dot(e.astype(bf), do[h, qa, :])
                dk[h, ka, :] += dot(ds, q[h, qa, :])
                dqt[h * HD : (h + 1) * HD, qa] += dot(head(kt, h, ka), ds)

        r = BQ // BK

        def rect(qb, kb):
            def one(n, _):
                q0 = pl.multiple_of(qb * BQ + lax.div(n, r) * BK, BK)
                k0 = pl.multiple_of(kb * BQ + lax.rem(n, r) * BK, BK)
                tile(q0, k0, False)
                return 0

            lax.fori_loop(0, r * r, one, 0)

        def triangle(t):
            def one(n, _):
                at = pl.multiple_of(t * BQ + n * BK, BK)
                tile(at, at, True)

                def below(j, _):
                    tile(at, pl.multiple_of(t * BQ + j * BK, BK), False)
                    return 0

                lax.fori_loop(0, n, below, 0)
                return 0

            lax.fori_loop(0, r, one, 0)

        def fetch(t, slot):
            b = t * 2 + ((other, c)[slot])
            return (
                pltpu.make_async_copy(n1.at[b], nx.at[slot], nsem.at[2 * slot]),
                pltpu.make_async_copy(x_all.at[b], xx.at[slot], nsem.at[2 * slot + 1]),
            )

        def fetch_both(t):
            for slot in range(2):
                for copy in fetch(t, slot):
                    copy.start()

        def prepare(t, slot):
            half = (other, c)[slot]
            at = pl.ds(pl.multiple_of((t * 2 + half) * T, T), T)
            dqs = dqt[:, at].astype(bf)
            dqf = dqs.astype(f32)
            gs_[...] += jnp.sum(dqf * qt[:, at].astype(f32), axis=1, keepdims=True)
            fm[:C, :] = (dqf * sc[...]).astype(bf)
            for h in range(nh):
                fm[C + h * HD : C + (h + 1) * HD, :] = jnp.transpose(dk[h, at, :]).astype(bf)
                fm[2 * C + h * HD : 2 * C + (h + 1) * HD, :] = jnp.transpose(dv[h, at, :]).astype(bf)
            tm[slot] = jnp.transpose(fm[...])
            for copy in fetch(t, slot):
                copy.wait()

        def weight_part(slot, a):
            dwt[:, a] += dot(fm[...], nx[slot, :, a])

        def finish(t, slot, dst):
            prepare(t, slot)
            inverse(slot)

            def column(n, _):
                a = pl.ds(pl.multiple_of(n * wide, wide), wide)
                back_part(slot, a, dst)
                weight_part(slot, a)
                return 0

            lax.fori_loop(0, D // wide, column, 0)

        def finish_weights(t, slot):
            prepare(t, slot)

            def column(n, _):
                weight_part(slot, pl.ds(pl.multiple_of(n * wide, wide), wide))
                return 0

            lax.fori_loop(0, D // wide, column, 0)

        def flash(i, t):
            fetch_both(t)

            def pair(m, _):
                u = xor(p, m, P_)
                rect(jnp.maximum(t, u), jnp.minimum(t, u))
                return 0

            lax.fori_loop(0, i, pair, 0)
            triangle(t)

        def advance(i, t):
            @pl.when(i == 1)
            def _():
                plane_sums()

            flash(i, t)
            if square:

                @pl.when(i == 3)
                def _():
                    join_g(2)
                    join_g(1)

            @pl.when(i < P_ - 1)
            def _():
                over(i + 1).wait_send()

            finish(t, 0, mb)
            over(i).start()
            finish(t, 1, own)
            over(i).wait_recv()
            combine(i)
            if not square:
                out_b(i, t).start()
                return

            @pl.when(i == 3)
            def _():
                relay_b(1).start()
                relay_b(2).start()

            @pl.when(i == 2)
            def _():
                join_b(2)

            @pl.when(i == 1)
            def _():
                join_b(1)

        def stage(n, _):
            i = P_ - 1 - n
            advance(i, xor(p, i, P_))
            return 0

        lax.fori_loop(0, P_ - 1, stage, 0)
        flash(0, p)
        finish_weights(p, 0)
        finish_weights(p, 1)


    V = pltpu.VMEM
    pl.run_scoped(
        attention,
        V((nh, L, HD), bf),
        V((nh, L), f32),
        V((C, L), f32),
        V((nh, L, HD), f32),
        V((nh, L, HD), f32),
    )

    def closing(dw, up, qm, qs_, go_, vo):
        dw[...] = jnp.transpose(dwt[...])

        bunch = 8 // math.gcd(R, 8)

        def piece(n, _):
            part = dw[pl.ds(pl.multiple_of(n * (bunch * R), 8), bunch * R), :]
            for j in range(bunch):
                to = n * bunch + j
                qm[lax.div(to, F), lax.rem(to, F)] = part[j * R : (j + 1) * R].astype(bf)
            return 0

        lax.fori_loop(0, S * F // bunch, piece, 0)
        for i in range(1, F):
            go(remote(qm.at[:, deep(i)], qi.at[i], qsend, qrecv, i, (s, deep(i))))
        up_load = pltpu.make_async_copy(dx2, up, local.at[0])
        up_load.start()
        over(1).wait_send()
        finish_back(0, mb)
        over(0).start()
        finish_back(1, own)
        vi[0:1, :] = gf[...]
        vi[1:2, :] = jnp.zeros_like(gf)
        turned = jnp.transpose(jnp.broadcast_to(gs_[...], (C, 128)))
        vi[1:2, 0:C] = turned[0:1, :]
        for i in range(1, F):
            go(remote(vi, vz.at[i], vsend, vrecv, i, (s, deep(i))))
        x_load = pltpu.make_async_copy(x_all.at[s], xx.at[0], nsem.at[1])
        x_load.start()
        over(0).wait_recv()
        combine(0)
        total = vi[...]
        for i in range(1, F):
            remote(vi, vz.at[i], vsend, vrecv, i, mate).wait_recv()
            total = total + vz[i]
        vp[0] = total
        for i in range(1, S):
            go(remote(vp.at[0], vp.at[i], vsend, vrecv, F - 1 + i, (lax.rem(s + i, S), f)))
        for i in range(1, F):
            remote(qm.at[:, f], qi.at[i], qsend, qrecv, i, mate).wait_recv()

        def sum_q(n, _):
            part = qm[n, f].astype(f32)
            for i in range(1, F):
                part = part + qi[i, n].astype(f32)
            qs_[n] = part.astype(bf)
            return 0

        lax.fori_loop(0, S, sum_q, 0)
        keep = pltpu.make_async_copy(qs_.at[s], qo.at[s], local.at[1])
        keep.start()
        for i in range(1, S):
            to = lax.rem(s + i, S)
            go(remote(qs_.at[to], qo.at[s], qsend, qrecv, F - 1 + i, (to, f)))
        up_load.wait()
        x_load.wait()
        over(0).wait_send()
        used = (1, 2) if square else range(1, P_)
        for i in used:
            if square:
                direct_b(i, 0).wait_recv()
                direct_b(i, 1).wait_recv()
            else:
                out_b(i, chip(i)).wait_recv()

        def below(n, _):
            a = pl.ds(pl.multiple_of(n * rows, rows), rows)
            back = bi[0, a, :].astype(f32)
            for i in used:
                back = back + bp[i - 1, a, :].astype(f32)
            z = xx[0, a, :].astype(f32)
            r1 = lax.rsqrt(jnp.mean(z * z, axis=-1, keepdims=True) + eps_norm)
            e1 = back * g1[...]
            tilt = jnp.mean(e1 * z, axis=-1, keepdims=True)
            mb[a, :] = (up[a, :] + r1 * e1 - z * (r1 * r1 * r1 * tilt)).astype(bf)
            return 0

        lax.fori_loop(0, T // rows, below, 0)
        outs = [pltpu.make_async_copy(mb, in_out, local.at[0])]
        outs[0].start()
        for i in range(1, F):
            remote(ga.at[:, f], gz.at[i], gsend, grecv, ZG + i, mate).wait_recv()
        for a in range(NW):
            part = ga[a, f].astype(f32)
            for i in range(1, F):
                part = part + gz[i, a].astype(f32)
            go_[a] = part
        for a, ref in enumerate((o_proj, o_up, o_down)):
            outs.append(pltpu.make_async_copy(go_.at[a], ref, bload.at[a]))
            outs[-1].start()
        total = vp[0]
        for i in range(1, S):
            remote(vp.at[0], vp.at[i], vsend, vrecv, F - 1 + i, mate).wait_recv()
            total = total + vp[i]
        vo[...] = total
        outs.append(pltpu.make_async_copy(vo, vec_out, nsem.at[0]))
        outs[-1].start()
        for i in range(1, S):
            src = lax.rem(s + S - i, S)
            remote(qs_.at[0], qo.at[src], qsend, qrecv, F - 1 + i, mate).wait_recv()
        keep.wait()
        for a, ref in enumerate((o_q, o_k, o_v)):
            for src in range(S):
                part = qo[src, :, a * C : (a + 1) * C].astype(f32)
                go_[NW + a, :, src * C : (src + 1) * C] = part
            outs.append(pltpu.make_async_copy(go_.at[NW + a], ref, bload.at[NW + a]))
            outs[-1].start()
        for out in outs:
            out.wait()
        for copy in todo:
            copy.wait_send()
        for i in range(1, F):
            deep_g(i).wait_send()
        for i in used:
            if square:
                relay_g(i).wait_send()
                relay_b(i).wait_send()
                for half in range(2):
                    direct_g(i, half).wait_send()
                    direct_b(i, half).wait_send()
            else:
                out_g(i).wait_send()
                out_b(i, chip(i)).wait_send()

    pl.run_scoped(
        closing,
        V((D, 3 * C), f32),
        V((T, D), f32),
        V((S, F, R, 3 * C), bf),
        V((S, R, 3 * C), bf),
        V((NW + 3, R, D), f32),
        V((2, D), f32),
    )


def backward_all(S, F, nh, dm, qt, kt, q, k, v, ot, lse, n1, x_all, w, sc, g1, gi, dx2):
    T, D = x_all.shape[1], x_all.shape[2]
    C = nh * HD
    L = S * T
    P_ = S // 2
    NW, R = gi.shape[1], gi.shape[3]
    any_ = pl.BlockSpec(memory_space=pl.ANY)
    vm = pl.BlockSpec(memory_space=pltpu.VMEM)
    dma = pltpu.SemaphoreType.DMA
    shape = jax.ShapeDtypeStruct
    V = pltpu.VMEM
    return pl.pallas_call(
        functools.partial(backward_kernel, S, F, nh),
        out_shape=[
            shape((R, D), f32),
            shape((R, D), f32),
            shape((R, D), f32),
            shape((T, D), bf),
            shape((R, D), f32),
            shape((R, D), f32),
            shape((R, D), f32),
            shape((2, D), f32),
            shape((P_, NW, F, R, D), bf),
            shape((2, NW, F // 2, R, D), bf),
            shape((2, NW, F // 2, R, D), bf),
        ],
        in_specs=[any_] + [vm] * 7 + [any_, any_, vm, vm, vm, any_, any_],
        out_specs=[any_] * 11,
        scratch_shapes=[
            V((C, L), bf),
            V((3 * C, D), bf),
            V((3 * C, D), f32),
            V((3 * C, T), bf),
            V((2, T, 3 * C), bf),
            V((2, T, D), bf),
            V((2, T, D), bf),
            V((T, 1), f32),
            V((T, D), bf),
            V((T, D), bf),
            V((P_, T, D), bf),
            V((2 if P_ == 4 else P_ - 1, T, D), bf),
            V((2, T // 2, D), bf),
            V((NW, F, R, D), bf),
            V((NW, F, R, D), bf),
            V((F, NW, R, D), bf),
            V((F, S, R, 3 * C), bf),
            V((S, R, 3 * C), bf),
            V((2, D), f32),
            V((F, 2, D), f32),
            V((S, 2, D), f32),
            V((1, D), f32),
            V((C, 1), f32),
            dma((3,)),
            dma((4,)),
            dma((S,)),
            dma((10 + 2 * P_ + F,)),
            dma((10 + 2 * P_ + F,)),
            dma((max(2 * P_, 10),)),
            dma((max(2 * P_, 10),)),
            dma((S + F,)),
            dma((S + F,)),
            dma((S + F,)),
            dma((S + F,)),
        ],
        compiler_params=pltpu.CompilerParams(
            collective_id=4, has_side_effects=True, vmem_limit_bytes=66_000_000
        ),
        name="backward",
    )(dm, qt, kt, q, k, v, ot, lse, n1, x_all, w, sc, g1, gi, dx2)


def body(
    inputs,
    w_query,
    w_key,
    w_value,
    w_proj,
    w_up,
    w_down,
    gain_first,
    gain_second,
    bias_up,
    bias_down,
    query_scale,
    cotangent,
):
    groups = lax.axis_size("seq")
    rows_of = lax.axis_size("fsdp")
    nh = H // groups
    cols = nh * HD
    both = ("seq", "fsdp")
    tokens, width = inputs.shape[1], inputs.shape[2]
    length = tokens * groups
    shard = w_query.shape[0]
    x_low = inputs.reshape(tokens, width)
    qkv_rows = jnp.stack([w_query, w_key, w_value], 1).astype(bf).reshape(shard, 3, groups, cols)
    qkv_rows = qkv_rows.transpose(2, 0, 1, 3).reshape(groups, shard, 3 * cols)
    small = jnp.stack([gain_first, gain_second, bias_up, bias_down], 0)
    small = jnp.pad(small.astype(bf), ((0, 12), (0, 128 - shard)))
    weights = jnp.stack([w_proj, w_up, w_down], 0).astype(bf)
    x_all, qkv_w, small, weights = gather_all(groups, rows_of, x_low, qkv_rows, small, weights)
    qkv_w = qkv_w.reshape(width, 3 * cols)
    small = small[:, :, :4, :shard].transpose(2, 0, 1, 3).reshape(4, width).astype(f32)
    scale_dims = jax.nn.softplus(query_scale) * log_two_inverse / math.sqrt(HD)
    scale_cols = jnp.tile(scale_dims, nh)
    normed, qt, kt, q, k, v, ot, lse, mixed, weights = forward_all(
        groups, rows_of, nh, x_all, qkv_w, small[:1], scale_cols[:, None], weights
    )
    result, grad_middle, dm, pairs, vectors = middle_all(
        groups,
        rows_of,
        nh,
        mixed,
        x_low,
        cotangent.reshape(tokens, width),
        weights.reshape(3, width, width),
        small,
    )
    (
        grad_proj,
        grad_up,
        grad_down,
        grad_inputs,
        grad_query,
        grad_key,
        grad_value,
        late,
        *unused,
    ) = backward_all(
        groups,
        rows_of,
        nh,
        dm,
        qt,
        kt,
        q,
        k,
        v,
        ot,
        lse,
        normed,
        x_all,
        qkv_w,
        scale_cols[:, None],
        small[:1],
        pairs.reshape(groups // 2, 3, rows_of, shard, width),
        grad_middle,
    )
    at = (lax.axis_index("seq") * rows_of + lax.axis_index("fsdp")) * shard
    vectors = jnp.concatenate([late[:1], vectors[1:4]], 0)
    mine = lax.dynamic_slice_in_dim(vectors, at, shard, 1)
    scale_total = jnp.sum(late[1, :cols].reshape(nh, HD), axis=0) / scale_dims
    grad_scale = scale_total * jax.nn.sigmoid(query_scale) * log_two_inverse / math.sqrt(HD)
    return (
        result.reshape(inputs.shape),
        grad_inputs.reshape(inputs.shape),
        grad_query,
        grad_key,
        grad_value,
        grad_proj,
        grad_up,
        grad_down,
        mine[0],
        mine[1],
        mine[2],
        mine[3],
        grad_scale,
    )


def solution(mesh):
    return jax.shard_map(
        body,
        mesh=mesh,
        in_specs=(
            P("fsdp", "seq", None),
            P(("seq", "fsdp"), None),
            P(("seq", "fsdp"), None),
            P(("seq", "fsdp"), None),
            P(("seq", "fsdp"), None),
            P(("seq", "fsdp"), None),
            P(("seq", "fsdp"), None),
            P(("seq", "fsdp")),
            P(("seq", "fsdp")),
            P(("seq", "fsdp")),
            P(("seq", "fsdp")),
            P(),
            P("fsdp", "seq", None),
        ),
        out_specs=(
            P("fsdp", "seq", None),
            P("fsdp", "seq", None),
            P(("seq", "fsdp"), None),
            P(("seq", "fsdp"), None),
            P(("seq", "fsdp"), None),
            P(("seq", "fsdp"), None),
            P(("seq", "fsdp"), None),
            P(("seq", "fsdp"), None),
            P(("seq", "fsdp")),
            P(("seq", "fsdp")),
            P(("seq", "fsdp")),
            P(("seq", "fsdp")),
            P(),
        ),
        check_vma=False,
    )
```

```python
import functools
import math

import jax
import jax.numpy as jnp
from jax import lax
from jax.experimental import pallas as pl
from jax.experimental.pallas import tpu as pltpu
from jax.sharding import PartitionSpec as P

H = 16
HD = 80
eps_norm = 1e-06
log_two_inverse = 1.442695
bf = jnp.bfloat16
f32 = jnp.float32
NEG = -1e30


def dot(a,b,ca=1,cb=0):
    return lax.dot_general(a,b,(((ca,),(cb,)),((),())),preferred_element_type=f32)


MESH = pl.DeviceIdType.MESH


def spots():
    s, f = lax.axis_index("seq"), lax.axis_index("fsdp")
    return s, f, s // 2, lax.rem(s, 2)


def greet(S, F):
    s, f, _, _ = spots()
    barrier = pltpu.get_barrier_semaphore()
    for i in range(1, S):
        pl.semaphore_signal(barrier, inc=1, device_id=(lax.rem(s + i, S), f), device_id_type=MESH)
    for i in range(1, F):
        pl.semaphore_signal(barrier, inc=1, device_id=(s, lax.rem(f + i, F)), device_id_type=MESH)
    pl.semaphore_wait(barrier, S + F - 2)


def remote(src, dst, sends, recvs, n, to):
    return pltpu.make_async_remote_copy(
        src_ref=src,
        dst_ref=dst,
        send_sem=sends.at[n],
        recv_sem=recvs.at[n],
        device_id=to,
        device_id_type=MESH,
    )


def gather_kernel(S, F, x, sm, w_q, w_k, w_v, w_o, w_1, w_2, x_all, wq_all, sm_all, wm_all, xv, qv, sv, mv, local,
                  xs, xr, qs, qr, ss, sr, ms, mr):
    s, f, p, c = spots()
    P_ = S // 2
    other = 1 - c
    loads = [
        pltpu.make_async_copy(sm, sv, local.at[0]),
        pltpu.make_async_copy(x, xv, local.at[2]),
    ]
    for load in loads:
        load.start()
    greet(S, F)
    mate = (p * 2 + other, f)
    todo = []

    def go(copy):
        copy.start()
        todo.append(copy)

    def chip(i):
        return lax.rem(p + i, P_) * 2 + c

    def back(i):
        return lax.rem(p + P_ - i, P_) * 2 + c

    def near_chip(i):
        return flip_bits(p, i) * 2 + c

    H_ = x.shape[0] // 2

    def deep(i):
        return lax.rem(f + i, F)

    def behind(i):
        return lax.rem(f + F - i, F)

    loads[0].wait()
    keep0 = pltpu.make_async_copy(sv, sm_all.at[s, f], local.at[0])
    keep0.start()
    for i in range(1, F):
        go(remote(sv, sm_all.at[s, f], ss, sr, i, (s, deep(i))))
    C = qv.shape[2] // 3
    for n, w in enumerate((w_q, w_k, w_v)):
        for to in range(S):
            qv[to, :, n * C : (n + 1) * C] = w[:, to * C : (to + 1) * C].astype(bf)
    keep1 = pltpu.make_async_copy(qv.at[s], wq_all.at[s, f], local.at[1])
    keep1.start()
    for i in range(1, S):
        to = lax.rem(s + i, S)
        go(remote(qv.at[to], wq_all.at[s, f], qs, qr, i, (to, f)))
    loads[1].wait()
    keep2 = pltpu.make_async_copy(xv, x_all.at[s], local.at[2])
    keep2.start()
    if P_ == 4:
        for first in range(2):
            for i in (1, 2):
                half = first if i == 1 else 1 - first
                part = pl.ds(half * H_, H_)
                go(remote(xv.at[part], x_all.at[s, part], xs, xr, 2 * i + half, (near_chip(i), f)))
    else:
        for i in range(1, P_):
            go(remote(xv, x_all.at[s], xs, xr, i, (chip(i), f)))
    go(remote(xv, x_all.at[s], xs, xr, 0, mate))
    for n, w in enumerate((w_o, w_1, w_2)):
        mv[n] = w[...].astype(bf)
    keep3 = pltpu.make_async_copy(mv, wm_all.at[:, f], local.at[3])
    keep3.start()
    for i in range(1, F):
        go(remote(mv, wm_all.at[:, f], ms, mr, i, (s, deep(i))))
    for i in range(1, F):
        g = behind(i)
        remote(sv, sm_all.at[s, g], ss, sr, i, mate).wait_recv()
    keep0.wait()
    for i in range(1, S):
        go(remote(sm_all.at[s], sm_all.at[s], ss, sr, F - 1 + i, (lax.rem(s + i, S), f)))
    for i in range(1, S):
        remote(qv.at[0], wq_all.at[lax.rem(s + S - i, S), f], qs, qr, i, mate).wait_recv()
    keep1.wait()
    for i in range(1, F):
        go(remote(wq_all.at[:, f], wq_all.at[:, f], qs, qr, S - 1 + i, (s, deep(i))))
    for i in range(1, F):
        remote(mv, wm_all.at[:, behind(i)], ms, mr, i, mate).wait_recv()
    keep3.wait()
    if P_ == 4:
        for i in (1, 2):
            half = i - 1
            part = pl.ds(half * H_, H_)
            src = near_chip(i)
            remote(xv.at[part], x_all.at[src, part], xs, xr, 2 * i + half, mate).wait_recv()
            blk = x_all.at[src, part]
            go(remote(blk, blk, xs, xr, 6 + half, (near_chip(3 - i), f)))
        for i in (1, 2):
            half = 2 - i
            part = pl.ds(half * H_, H_)
            src = near_chip(i)
            remote(xv.at[part], x_all.at[src, part], xs, xr, 2 * i + half, mate).wait_recv()
            go(remote(x_all.at[src], x_all.at[src], xs, xr, 8 + i, mate))
    for i in range(1, P_ if P_ != 4 else 1):
        src = back(i)
        remote(xv, x_all.at[src], xs, xr, i, mate).wait_recv()
        go(remote(x_all.at[src], x_all.at[src], xs, xr, P_ - 1 + i, mate))
    for i in range(1, S):
        src = lax.rem(s + S - i, S)
        remote(sm_all.at[src], sm_all.at[src], ss, sr, F - 1 + i, mate).wait_recv()
    for i in range(1, F):
        g = behind(i)
        remote(wq_all.at[:, g], wq_all.at[:, g], qs, qr, S - 1 + i, mate).wait_recv()
    near = p * 2 + other
    remote(xv, x_all.at[near], xs, xr, 0, mate).wait_recv()
    if P_ == 4:
        for half in range(2):
            part = pl.ds(half * H_, H_)
            blk = x_all.at[near_chip(3), part]
            remote(blk, blk, xs, xr, 6 + half, mate).wait_recv()
            go(remote(blk, blk, xs, xr, 11 + half, mate))
        for i in (1, 2):
            blk = x_all.at[flip_bits(p, i) * 2 + other]
            remote(blk, blk, xs, xr, 8 + i, mate).wait_recv()
        for half in range(2):
            blk = x_all.at[flip_bits(p, 3) * 2 + other, pl.ds(half * H_, H_)]
            remote(blk, blk, xs, xr, 11 + half, mate).wait_recv()
    else:
        for i in range(1, P_):
            src = lax.rem(p + P_ - i, P_) * 2 + other
            remote(xv, x_all.at[src], xs, xr, P_ - 1 + i, mate).wait_recv()
    keep2.wait()
    for copy in todo:
        copy.wait_send()


def gather_all(S, F, x, sm, *weights):
    R, D = weights[0].shape
    C3 = 3 * D // S
    vm = pl.BlockSpec(memory_space=pltpu.VMEM)
    any_ = pl.BlockSpec(memory_space=pl.ANY)
    shapes = [
        (S,) + x.shape,
        (S, F, R, C3),
        (S, F) + sm.shape,
        (3, F, R, D),
    ]
    P_ = S // 2
    dma = pltpu.SemaphoreType.DMA
    counts = [max(2 * P_ - 1, 12), S + F - 1, F + S - 1, F]
    sems = []
    for n in counts:
        sems += [dma((n + 1,)), dma((n + 1,))]
    return pl.pallas_call(
        functools.partial(gather_kernel, S, F),
        out_shape=[
            jax.ShapeDtypeStruct(sh, bf) for sh in shapes
        ],
        in_specs=[any_] * 2 + [vm] * 6,
        out_specs=[any_] * 4,
        scratch_shapes=[
            pltpu.VMEM(x.shape, x.dtype),
            pltpu.VMEM((S, R, C3), bf),
            pltpu.VMEM(sm.shape, sm.dtype),
            pltpu.VMEM((3, R, D), bf),
            dma((4,)),
        ]
        + sems,
        compiler_params=pltpu.CompilerParams(collective_id=1, has_side_effects=True),
        name="gather",
    )(x, sm, *weights)


def xor(a, b, n):
    out, bit = 0, 1
    while bit < n:
        both = lax.rem(lax.div(a, bit), 2) + lax.rem(lax.div(b, bit), 2)
        out = out + bit * lax.rem(both, 2)
        bit *= 2
    return out


def flip_bits(p, i):
    out, bit = p, 1
    while bit <= i:
        if i & bit:
            out = out + bit - 2 * bit * lax.rem(lax.div(p, bit), 2)
        bit *= 2
    return out


def forward_kernel(S, F, nh, x_all, w, g1, sc, wz, n1, qt, kt, qn, kk, vn, ot, lse, mixed, wm,
                   wt, vt, xb, nb, wv, inx, outn, local, osend, orecv, wsend, wrecv):
    s, f, p, c = spots()
    P_ = S // 2
    T, D = x_all.shape[1], x_all.shape[2]
    C = nh * HD
    L = S * T
    BQ = 2 * T
    BK = min(512, BQ)
    other = 1 - c
    mate = (p * 2 + other, f)
    load = pltpu.make_async_copy(wz, wv, local.at[0])
    load.start()

    def fetch(b):
        return pltpu.make_async_copy(x_all.at[b], xb.at[lax.rem(b, 2)], inx.at[lax.rem(b, 2)])

    def store(b):
        return pltpu.make_async_copy(nb.at[lax.rem(b, 2)], n1.at[b], outn.at[lax.rem(b, 2)])

    fetch(0).start()
    greet(S, F)
    load.wait()
    keep = pltpu.make_async_copy(wv, wm.at[:, s], local.at[0])
    keep.start()

    zero = s - s
    chips = [flip_bits(p, i) for i in range(P_)]

    def num(n):
        return zero + n

    def spread(i):
        return remote(wv, wm.at[:, s], wsend, wrecv, i, (xor(p, i, P_) * 2 + c, f))

    def forward(i):
        src = xor(p, i, P_) * 2 + c
        n = (7 if P_ == 4 else P_) + i
        return remote(wm.at[:, src], wm.at[:, src], wsend, wrecv, n, mate)

    def part_of(src, half):
        return wm.at[:, src, pl.ds(num(half * (F // 2)), F // 2)]

    def direct(i, half):
        src = wv.at[:, pl.ds(half * (F // 2), F // 2)]
        to = (flip_bits(p, i) * 2 + c, f)
        return remote(src, part_of(s, half), wsend, wrecv, 2 * i + half, to)

    def arrived(i, half):
        blk = part_of(chips[i] * 2 + c, half)
        remote(blk, blk, wsend, wrecv, num(2 * i + half), mate).wait_recv()

    def relay(i):
        blk = part_of(flip_bits(p, i) * 2 + c, i - 1)
        return remote(blk, blk, wsend, wrecv, 5 + i, (flip_bits(p, 3 - i) * 2 + c, f))

    def relayed(half):
        blk = part_of(chips[3] * 2 + c, half)
        return remote(blk, blk, wsend, wrecv, num(6 + half), mate)

    def corner(half, core):
        blk = part_of(chips[3] * 2 + core, half)
        return remote(blk, blk, wsend, wrecv, num(10 + half), mate)

    square = P_ == 4
    if square:
        for first in range(2):
            for i in (1, 2):
                direct(i, first if i == 1 else 1 - first).start()
    else:
        for i in range(1, P_):
            spread(P_ - i).start()
    near = remote(wv, wm.at[:, s], wsend, wrecv, 0, mate)
    near.start()
    wt[...] = jnp.transpose(w[...])

    rows = 64

    def project(b, _):
        slot = lax.rem(b, 2)
        fetch(b).wait()

        @pl.when(b + 1 < S)
        def _():
            fetch(b + 1).start()

        @pl.when(b >= 2)
        def _():
            store(b - 2).wait()

        def norm(k, _):
            at = pl.ds(pl.multiple_of(k * rows, rows), rows)
            v = xb[slot, at, :].astype(f32)
            r = lax.rsqrt(jnp.mean(v * v, axis=-1, keepdims=True) + eps_norm)
            nb[slot, at, :] = (v * r * g1[...]).astype(bf)
            return 0

        lax.fori_loop(0, T // rows, norm, 0)
        store(b).start()
        cols = pl.ds(pl.multiple_of(b * T, T), T)
        res = dot(wt[...], nb[slot], 1, 1)
        qt[:, cols] = (res[:C] * sc[...]).astype(bf)
        kt[:, cols] = res[C : 2 * C].astype(bf)
        vt[:, cols] = res[2 * C :].astype(bf)
        for h in range(nh):
            part = slice(h * HD, (h + 1) * HD)
            qn[h, cols, :] = jnp.transpose(res[:C][part] * sc[part]).astype(bf)
            kk[h, cols, :] = jnp.transpose(res[C : 2 * C][part]).astype(bf)
            vn[h, cols, :] = jnp.transpose(res[2 * C :][part]).astype(bf)
        return 0

    lax.fori_loop(0, S, project, 0)
    if square:
        for i in (1, 2):
            arrived(i, i - 1)
            relay(i).start()
    store(S - 2).wait()
    store(S - 1).wait()

    r = BQ // BK

    def attend(t):
        first = pl.multiple_of(t * BQ, BQ)
        q = [qt[h * HD : (h + 1) * HD, pl.ds(first, BQ)] for h in range(nh)]

        def step(j, carry, diag=None):
            at = pl.ds(pl.multiple_of(j * BK, BK), BK)
            scores = [dot(kk[h, at, :], q[h]) for h in range(nh)]
            out = []
            for h in range(nh):
                m, l, acc = carry[h]
                sh = scores[h]
                if diag is not None:
                    kp = lax.broadcasted_iota(jnp.int32, sh.shape, 0) + diag * BK
                    qp = lax.broadcasted_iota(jnp.int32, sh.shape, 1)
                    sh = jnp.where(kp <= qp, sh, NEG)
                mn = jnp.maximum(m, jnp.max(sh, axis=0, keepdims=True))
                a = jnp.exp(m - mn)
                e = jnp.exp(sh - mn)
                l = l * a + jnp.sum(e, axis=0, keepdims=True)
                acc = acc * a + dot(vt[h * HD : (h + 1) * HD, at], e.astype(bf))
                out.append((mn, l, acc))
            return tuple(out)

        carry = tuple(
            (jnp.full((1, BQ), NEG, f32), jnp.zeros((1, BQ), f32), jnp.zeros((HD, BQ), f32))
            for _ in range(nh)
        )
        carry = lax.fori_loop(0, t * r, step, carry)
        for d in range(r):
            carry = step(t * r + d, carry, d)
        for h in range(nh):
            m, l, acc = carry[h]
            ot[h * HD : (h + 1) * HD, pl.ds(first, BQ)] = (acc / l).astype(bf)
            lse[h : h + 1, pl.ds(first, BQ)] = m + jnp.log(l)

    def to_owner(src, n, i, to):
        return pltpu.make_async_remote_copy(
            src_ref=src,
            dst_ref=mixed.at[s],
            send_sem=osend.at[n],
            recv_sem=orecv.at[2 * i + c],
            device_id=to,
            device_id_type=MESH,
        )

    def send(i, half):
        t = xor(p, i, P_)
        src = ot.at[:, pl.ds(pl.multiple_of(t * BQ + half * T, T), T)]
        return to_owner(src, 2 * i + half, i, (t * 2 + half, f))

    def turn(n, _):
        i = P_ - 1 - n
        attend(xor(p, i, P_))
        send(i, 0).start()
        send(i, 1).start()
        if not square:
            spread(i).wait_recv()
            forward(i).start()
            return 0

        @pl.when(i == 3)
        def _():
            arrived(2, 0)
            forward(num(2)).start()

        @pl.when(i == 2)
        def _():
            arrived(1, 1)
            forward(num(1)).start()

        @pl.when(i == 1)
        def _():
            for half in range(2):
                relayed(half).wait_recv()
                corner(half, c).start()

        return 0

    lax.fori_loop(0, P_ - 1, turn, 0)
    attend(p)
    mine = ot.at[:, pl.ds(pl.multiple_of(s * T, T), T)]
    theirs = ot.at[:, pl.ds(pl.multiple_of((p * 2 + other) * T, T), T)]
    last = to_owner(theirs, 0, 0, mate)
    last.start()
    own = pltpu.make_async_copy(mine, mixed.at[s], local.at[1])
    own.start()
    def from_source(i, core):
        return pltpu.make_async_remote_copy(
            src_ref=mine,
            dst_ref=mixed.at[flip_bits(p, i) * 2 + core],
            send_sem=osend.at[0],
            recv_sem=orecv.at[2 * i + core],
            device_id=mate,
            device_id_type=MESH,
        )

    for i in range(1, P_):
        for core in range(2):
            from_source(i, core).wait_recv()
    from_source(0, other).wait_recv()
    last.wait_send()
    own.wait()
    keep.wait()
    near.wait()
    if square:
        for i in (1, 2):
            forward(i).wait()
            relay(i).wait_send()
            for half in range(2):
                direct(i, half).wait_send()
        for half in range(2):
            corner(half, c).wait_send()
            corner(half, other).wait_recv()
    for i in range(1, P_):
        if not square:
            forward(i).wait()
            spread(i).wait_send()
        send(i, 0).wait_send()
        send(i, 1).wait_send()


def forward_all(S, F, nh, x_all, w, g1, sc, wz):
    T, D = x_all.shape[1], x_all.shape[2]
    C = nh * HD
    L = S * T
    P_ = S // 2
    any_ = pl.BlockSpec(memory_space=pl.ANY)
    vm = pl.BlockSpec(memory_space=pltpu.VMEM)
    dma = pltpu.SemaphoreType.DMA
    shape = jax.ShapeDtypeStruct
    NW, R = wz.shape[0], wz.shape[2]
    V = pltpu.VMEM
    return pl.pallas_call(
        functools.partial(forward_kernel, S, F, nh),
        out_shape=[
            shape((S, T, D), bf),
            shape((C, L), bf),
            shape((C, L), bf),
            shape((nh, L, HD), bf),
            shape((nh, L, HD), bf),
            shape((nh, L, HD), bf),
            shape((C, L), bf),
            shape((nh, L), f32),
            shape((S, C, T), bf),
            shape((NW, S, F, R, D), bf),
        ],
        in_specs=[any_, vm, vm, vm, any_],
        out_specs=[any_] + [vm] * 7 + [any_, any_],
        scratch_shapes=[
            V((3 * C, D), bf),
            V((C, L), bf),
            V((2, T, D), bf),
            V((2, T, D), bf),
            V((NW, F, R, D), bf),
            dma((2,)),
            dma((2,)),
            dma((2,)),
            dma((2 * P_,)),
            dma((2 * P_,)),
            dma((max(2 * P_, 12),)),
            dma((max(2 * P_, 12),)),
        ],
        compiler_params=pltpu.CompilerParams(
            collective_id=3, has_side_effects=True, vmem_limit_bytes=60 << 20
        ),
        name="forward",
    )(x_all, w, g1, sc, wz)


def middle_kernel(S, F, nh, mixed, x, ct, wm, small, out, dx2, dm, gi, vec,
                  mx, lt, xv, cv, wv, x2, n2, dn, ab, ub, eb, r2, sb, rb, ob, dov, rv, vz, vp, local, wsem,
                  dsend, drecv, gsend, grecv, vsend, vrecv):
    s, f, p, c = spots()
    P_ = S // 2
    T, D = x.shape
    C = nh * HD
    NW = wm.shape[0]
    G = D // S
    other = 1 - c
    mate = (p * 2 + other, f)
    wide = 256 if D % 256 == 0 else D
    rows = 64
    loads = [
        pltpu.make_async_copy(mixed, mx, local.at[0]),
        pltpu.make_async_copy(x, xv, local.at[1]),
        pltpu.make_async_copy(ct, cv, local.at[2]),
    ]
    loads += [pltpu.make_async_copy(wm.at[n], wv.at[n], wsem.at[n]) for n in range(NW)]
    for load in loads:
        load.start()
    greet(S, F)
    g2, b1, b2 = small[1:2, :], small[2:3, :], small[3:4, :]

    def by_core(n, tall):
        for t in range(P_):
            for core in range(2):
                at = (t * 2 + core) * G
                lt[n, core, t * G : (t + 1) * G, :] = tall[at : at + G]

    def chunk(n):
        return pl.ds(pl.multiple_of(n * wide, wide), wide)

    def over(n, body):
        def one(k, _):
            body(k)
            return 0

        lax.fori_loop(0, n, one, 0)

    def lines(n):
        return pl.ds(pl.multiple_of(n * rows, rows), rows)

    loads[0].wait()
    tall = mx[...].reshape(D, T)
    by_core(0, tall)
    ub[...] = jnp.transpose(tall)
    loads[1].wait()
    loads[2].wait()
    loads[3].wait()

    def attend_out(n):
        at = chunk(n)
        x2[:, at] = xv[:, at].astype(f32) + dot(ub[...], wv[0, :, at])

    over(D // wide, attend_out)

    def norm(n):
        at = lines(n)
        z = x2[at, :]
        r = lax.rsqrt(jnp.mean(z * z, axis=-1, keepdims=True) + eps_norm)
        r2[at, :] = r
        n2[at, :] = (z * r * g2).astype(bf)

    over(T // rows, norm)
    loads[4].wait()
    loads[5].wait()
    rv[...] = jnp.zeros_like(rv)

    def hidden(n):
        at = chunk(n)
        u = dot(n2[...], wv[1, :, at]) + small[2:3, at]
        gate = 1 / (1 + jnp.exp(-u))
        ab[:, at] = (u * gate).astype(bf)
        ga = dot(cv[...], wv[2, at, :], 1, 1)
        du = ga * (gate * (1 + u * (1 - gate)))
        rv[2:3, at] = jnp.sum(du, axis=0, keepdims=True)
        ub[:, at] = du.astype(bf)
        rv[3:4, at] = jnp.sum(cv[:, at].astype(f32), axis=0, keepdims=True)

    over(D // wide, hidden)

    def up_back(n):
        at = chunk(n)
        dn[:, at] = dot(ub[...], wv[1, at, :], 1, 1)

    over(D // wide, up_back)

    def second(n):
        at = lines(n)
        z, r, d = x2[at, :], r2[at, :], dn[at, :]
        e = d * g2
        tilt = jnp.mean(e * z, axis=-1, keepdims=True)
        v = cv[at, :].astype(f32) + r * e - z * (r * r * r * tilt)
        rv[1:2, :] += jnp.sum(d * z * r, axis=0, keepdims=True)
        dn[at, :] = v
        eb[at, :] = v.astype(bf)

    over(T // rows, second)
    keep = pltpu.make_async_copy(dn, dx2, local.at[0])
    keep.start()

    def vec_z(i):
        return remote(rv, vz.at[i], vsend, vrecv, i, (s, lax.rem(f + i, F)))

    def vec_s(i):
        return remote(vp.at[0], vp.at[i], vsend, vrecv, F - 1 + i, (lax.rem(s + i, S), f))

    for i in range(1, F):
        vec_z(i).start()

    def head_out(i, to):
        return remote(dov.at[i], dm.at[s], dsend, drecv, i, (to, f))

    def heads(i, _):
        to = lax.rem(s + i, S)
        rows_of = pl.ds(pl.multiple_of(to * C, C), C)
        dov[i] = dot(wv[0, rows_of, :], eb[...], 1, 1).astype(bf)

        head_out(i, to).start()
        return 0

    lax.fori_loop(1, S, heads, 0)
    mine = pl.ds(pl.multiple_of(s * C, C), C)
    dov[0] = dot(wv[0, mine, :], eb[...], 1, 1).astype(bf)
    home = pltpu.make_async_copy(dov.at[0], dm.at[s], local.at[1])
    home.start()

    by_core(1, jnp.transpose(n2[...]))
    by_core(2, jnp.transpose(ab[...]))
    right = [eb, ub, cv]

    def pass_on(n):
        return remote(sb.at[n], rb.at[n], gsend, grecv, n, mate)

    for n in range(NW):

        def send_side(k, n=n):
            at = chunk(k)
            sb[n, :, at] = dot(lt[n, other], right[n][:, at]).astype(bf)

        over(D // wide, send_side)
        pass_on(n).start()

    part = rv[...]
    for i in range(1, F):
        vec_z(i).wait_recv()
        part = part + vz[i]
    vp[0] = part
    for i in range(1, S):
        vec_s(i).start()

    def top(n):
        at = chunk(n)
        y = x2[:, at] + dot(ab[...], wv[2, :, at]) + small[3:4, at]
        xv[:, at] = y.astype(bf)

    over(D // wide, top)
    done = pltpu.make_async_copy(xv, out, local.at[2])
    done.start()
    for n in range(NW):
        pass_on(n).wait_recv()

        def keep_side(k, n=n):
            at = chunk(k)
            both = dot(lt[n, c], right[n][:, at]) + rb[n, :, at].astype(f32)
            ob[n, :, at] = both.astype(bf)

        over(D // wide, keep_side)
    stores = []
    for i in range(P_):
        here = pl.ds(pl.multiple_of(flip_bits(p, i) * G, G), G)
        stores.append(pltpu.make_async_copy(ob.at[:, here], gi.at[i], wsem.at[i]))
        stores[-1].start()
    part = vp[0]
    for i in range(1, S):
        vec_s(i).wait_recv()
        part = part + vp[i]
    vec[...] = part
    for i in range(1, F):
        vec_z(i).wait_send()
    for i in range(1, S):
        vec_s(i).wait_send()
    for i in range(1, S):
        remote(dov.at[0], dm.at[lax.rem(s + S - i, S)], dsend, drecv, i, mate).wait_recv()
    for store in stores:
        store.wait()
    keep.wait()
    home.wait()
    done.wait()
    for i in range(1, S):
        head_out(i, lax.rem(s + i, S)).wait_send()
    for n in range(NW):
        pass_on(n).wait_send()


def middle_all(S, F, nh, mixed, x, ct, wm, small):
    T, D = x.shape
    C = nh * HD
    P_ = S // 2
    NW = wm.shape[0]
    G = D // S
    any_ = pl.BlockSpec(memory_space=pl.ANY)
    vm = pl.BlockSpec(memory_space=pltpu.VMEM)
    dma = pltpu.SemaphoreType.DMA
    shape = jax.ShapeDtypeStruct
    V = pltpu.VMEM
    return pl.pallas_call(
        functools.partial(middle_kernel, S, F, nh),
        out_shape=[
            shape((T, D), bf),
            shape((T, D), f32),
            shape((S, C, T), bf),
            shape((P_, NW, G, D), bf),
            shape((8, D), f32),
        ],
        in_specs=[any_, any_, any_, any_, vm],
        out_specs=[any_, any_, any_, any_, vm],
        scratch_shapes=[
            V((S, C, T), bf),
            V((NW, 2, P_ * G, T), bf),
            V((T, D), bf),
            V((T, D), bf),
            V((NW, D, D), bf),
            V((T, D), f32),
            V((T, D), bf),
            V((T, D), f32),
            V((T, D), bf),
            V((T, D), bf),
            V((T, D), bf),
            V((T, 1), f32),
            V((NW, P_ * G, D), bf),
            V((NW, P_ * G, D), bf),
            V((NW, P_ * G, D), bf),
            V((S, C, T), bf),
            V((8, D), f32),
            V((F, 8, D), f32),
            V((S, 8, D), f32),
            dma((3,)),
            dma((max(NW, P_),)),
            dma((S,)),
            dma((S,)),
            dma((NW,)),
            dma((NW,)),
            dma((S + F,)),
            dma((S + F,)),
        ],
        compiler_params=pltpu.CompilerParams(
            collective_id=5, has_side_effects=True, vmem_limit_bytes=64_000_000
        ),
        name="middle",
    )(mixed, x, ct, wm, small)


def backward_kernel(S, F, nh, dm, qt, kt, q, k, v, ot, lse, n1, x_all, w, sc, g1, gi, dx2,
                    o_proj, o_up, o_down, in_out, o_q, o_k, o_v, vec_out, gp, gr_, gj,
                    dmt, wt, dwt, fm, tm, nx, xx, rr, mb, own, bi, bp, rl, ga, gb, gz, qi, qo,
                    vi, vz, vp, gf, gs_, local, nsem, bload,
                    gsend, grecv, bsend, brecv, qsend, qrecv, vsend, vrecv):
    s, f, p, c = spots()
    P_ = S // 2
    T, D = x_all.shape[1], x_all.shape[2]
    C = nh * HD
    L = S * T
    BQ = 2 * T
    BK = min(512, BQ)
    NW, R = gi.shape[1], gi.shape[3]
    other = 1 - c
    mate = (p * 2 + other, f)
    todo = []

    def go(copy):
        copy.start()
        todo.append(copy)

    chips = [flip_bits(p, i) for i in range(P_)]
    zero = s - s

    def num(n):
        return zero + n

    def chip(i):
        return chips[i]

    deeps = [lax.rem(f + i, F) for i in range(F)]

    def deep(i):
        return deeps[i]

    def head(ref, h, at):
        return ref[h * HD : (h + 1) * HD, at]

    loads = [
        pltpu.make_async_copy(dm.at[b], dmt.at[:, b * T : (b + 1) * T], bload.at[b])
        for b in range(S)
    ]
    for load in loads:
        load.start()
    greet(S, F)

    order = list(range(P_ - 1, -1, -1))
    wt[...] = jnp.transpose(w[...])
    dwt[...] = jnp.zeros_like(dwt)
    gf[...] = jnp.zeros_like(gf)
    gs_[...] = jnp.zeros_like(gs_)
    for load in loads:
        load.wait()

    def slabs(body):
        def one(n, _):
            body(lax.div(n, F), lax.rem(n, F))
            return 0

        lax.fori_loop(0, NW * F, one, 0)

    square = P_ == 4
    ZG = 10 if square else 2 * P_
    FH, H_ = F // 2, T // 2

    def half_g(ref, half):
        return ref.at[:, pl.ds(num(half * FH), FH)]

    def direct_g(i, half):
        src, dst = half_g(gi.at[num(i)], half), half_g(gp.at[num(i)], half)
        if half == 2 - i:
            src = gj.at[num(half)]
        return remote(src, dst, gsend, grecv, num(2 + 2 * i + half), (chip(i) * 2 + c, f))

    def relay_g(i):
        src = half_g(gi.at[num(3)], i - 1)
        return remote(src, gr_.at[num(i - 1)], gsend, grecv, num(7 + i), (chip(i) * 2 + c, f))

    def join_g(i):
        half = 2 - i
        la = pltpu.make_async_copy(half_g(gi.at[num(i)], half), half_g(ga, 0), local.at[num(1)])
        la.start()
        relay_g(3 - i).wait_recv()
        lb = pltpu.make_async_copy(gr_.at[num(half)], half_g(gb, 0), local.at[num(2)])
        lb.start()
        la.wait()
        lb.wait()

        def add(z, _):
            for a in range(NW):
                w_ = num(a)
                ga[w_, z] = (ga[w_, z].astype(f32) + gb[w_, z].astype(f32)).astype(bf)
            return 0

        lax.fori_loop(0, FH, add, 0)
        st = pltpu.make_async_copy(half_g(ga, 0), gj.at[num(half)], local.at[num(1)])
        st.start()
        st.wait()
        direct_g(i, half).start()

    def out_g(i):
        return remote(gi.at[num(i)], gp.at[num(i)], gsend, grecv, num(P_ + i), (chip(i) * 2 + c, f))

    if square:
        relay_g(1).start()
        relay_g(2).start()
        direct_g(2, 1).start()
        direct_g(1, 0).start()
    else:
        for i in order[:-1]:
            out_g(i).start()

    rows = 64
    wide = 256 if D % 256 == 0 else D

    def over(i):
        return remote(mb, bi.at[i], bsend, brecv, i, mate)

    def inverse(slot):
        def one(n, _):
            a = pl.ds(pl.multiple_of(n * rows, rows), rows)
            z = xx[slot, a, :].astype(f32)
            rr[a, :] = lax.rsqrt(jnp.mean(z * z, axis=-1, keepdims=True) + eps_norm)
            return 0

        lax.fori_loop(0, T // rows, one, 0)

    def back_part(slot, a, dst):
        back = dot(tm[slot], wt[:, a])
        dst[:, a] = back.astype(bf)
        hat = xx[slot, :, a].astype(f32) * rr[...]
        gf[:, a] += jnp.sum(back * hat, axis=0, keepdims=True)

    def finish_back(slot, dst):
        inverse(slot)

        def column(n, _):
            back_part(slot, pl.ds(pl.multiple_of(n * wide, wide), wide), dst)
            return 0

        lax.fori_loop(0, D // wide, column, 0)

    def combine(i):
        def one(n, _):
            a = pl.ds(pl.multiple_of(n * rows, rows), rows)
            bi[i, a, :] = (bi[i, a, :].astype(f32) + own[a, :].astype(f32)).astype(bf)
            return 0

        lax.fori_loop(0, T // rows, one, 0)

    def direct_b(i, half):
        part = pl.ds(pl.multiple_of(num(half * H_), H_), H_)
        src, dst = bi.at[num(i), part], bp.at[num(i - 1), part]
        return remote(src, dst, bsend, brecv, num(2 + 2 * i + half), (chip(i) * 2 + c, f))

    def relay_b(i):
        part = pl.ds(pl.multiple_of(num((i - 1) * H_), H_), H_)
        src = bi.at[num(3), part]
        return remote(src, rl.at[num(i - 1)], bsend, brecv, num(7 + i), (chip(i) * 2 + c, f))

    def join_b(i):
        half = 2 - i
        direct_b(i, 1 - half).start()
        relay_b(3 - i).wait_recv()
        few = min(rows, H_)

        def add(n, _):
            here = pl.ds(pl.multiple_of(half * H_ + n * few, few), few)
            there = pl.ds(pl.multiple_of(n * few, few), few)
            both = bi[num(i), here, :].astype(f32) + rl[num(half), there, :].astype(f32)
            bi[num(i), here, :] = both.astype(bf)
            return 0

        lax.fori_loop(0, H_ // few, add, 0)
        direct_b(i, half).start()

    def out_b(i, t):
        return pltpu.make_async_remote_copy(
            src_ref=bi.at[i],
            dst_ref=bp.at[i - 1],
            send_sem=bsend.at[P_ + i],
            recv_sem=brecv.at[P_ + i],
            device_id=(t * 2 + c, f),
            device_id_type=MESH,
        )

    def deep_g(i):
        src = ga.at[:, deep(i)]
        return remote(src, gz.at[num(i)], gsend, grecv, num(ZG + i), (s, deep(i)))

    def plane_sums():
        la = pltpu.make_async_copy(gi.at[num(0)], ga, local.at[num(1)])
        la.start()
        la.wait()
        for i in order[1:-1] if square else order[:-1]:
            if square:
                direct_g(i, 0).wait_recv()
                direct_g(i, 1).wait_recv()
            else:
                out_g(i).wait_recv()
            lb = pltpu.make_async_copy(gp.at[num(i)], gb, local.at[num(2)])
            lb.start()
            lb.wait()

            def more(z, _):
                for a in range(NW):
                    w_ = num(a)
                    ga[w_, z] = (ga[w_, z].astype(f32) + gb[w_, z].astype(f32)).astype(bf)
                return 0

            lax.fori_loop(0, F, more, 0)
        for i in range(1, F):
            deep_g(i).start()

    def attention(do, delta, dqt, dk, dv):
        dqt[...] = jnp.zeros_like(dqt)
        dk[...] = jnp.zeros_like(dk)
        dv[...] = jnp.zeros_like(dv)

        def turn(b, _):
            at = pl.ds(pl.multiple_of(b * T, T), T)
            for h in range(nh):
                do[h, at, :] = jnp.transpose(head(dmt, h, at))
                prod = head(dmt, h, at).astype(f32) * head(ot, h, at).astype(f32)
                delta[h : h + 1, at] = jnp.sum(prod, axis=0, keepdims=True)
            return 0

        lax.fori_loop(0, S, turn, 0)

        def tile(q0, k0, masked):
            qa = pl.ds(q0, BK)
            ka = pl.ds(k0, BK)
            scores = [dot(k[h, ka, :], head(qt, h, qa)) for h in range(nh)]
            dps = [dot(v[h, ka, :], head(dmt, h, qa)) for h in range(nh)]
            for h in range(nh):
                e = jnp.exp(scores[h] - lse[h : h + 1, qa])
                if masked:
                    kp = lax.broadcasted_iota(jnp.int32, e.shape, 0)
                    qp = lax.broadcasted_iota(jnp.int32, e.shape, 1)
                    e = jnp.where(kp <= qp, e, 0.0)
                ds = (e * (dps[h] - delta[h : h + 1, qa])).astype(bf)
                dv[h, ka, :] += dot(e.astype(bf), do[h, qa, :])
                dk[h, ka, :] += dot(ds, q[h, qa, :])
                dqt[h * HD : (h + 1) * HD, qa] += dot(head(kt, h, ka), ds)

        r = BQ // BK

        def rect(qb, kb):
            def one(n, _):
                q0 = pl.multiple_of(qb * BQ + lax.div(n, r) * BK, BK)
                k0 = pl.multiple_of(kb * BQ + lax.rem(n, r) * BK, BK)
                tile(q0, k0, False)
                return 0

            lax.fori_loop(0, r * r, one, 0)

        def triangle(t):
            def one(n, _):
                at = pl.multiple_of(t * BQ + n * BK, BK)
                tile(at, at, True)

                def below(j, _):
                    tile(at, pl.multiple_of(t * BQ + j * BK, BK), False)
                    return 0

                lax.fori_loop(0, n, below, 0)
                return 0

            lax.fori_loop(0, r, one, 0)

        def fetch(t, slot):
            b = t * 2 + ((other, c)[slot])
            return (
                pltpu.make_async_copy(n1.at[b], nx.at[slot], nsem.at[2 * slot]),
                pltpu.make_async_copy(x_all.at[b], xx.at[slot], nsem.at[2 * slot + 1]),
            )

        def fetch_both(t):
            for slot in range(2):
                for copy in fetch(t, slot):
                    copy.start()

        def prepare(t, slot):
            half = (other, c)[slot]
            at = pl.ds(pl.multiple_of((t * 2 + half) * T, T), T)
            dqs = dqt[:, at].astype(bf)
            dqf = dqs.astype(f32)
            gs_[...] += jnp.sum(dqf * qt[:, at].astype(f32), axis=1, keepdims=True)
            fm[:C, :] = (dqf * sc[...]).astype(bf)
            for h in range(nh):
                fm[C + h * HD : C + (h + 1) * HD, :] = jnp.transpose(dk[h, at, :]).astype(bf)
                fm[2 * C + h * HD : 2 * C + (h + 1) * HD, :] = jnp.transpose(dv[h, at, :]).astype(bf)
            tm[slot] = jnp.transpose(fm[...])
            for copy in fetch(t, slot):
                copy.wait()

        def weight_part(slot, a):
            dwt[:, a] += dot(fm[...], nx[slot, :, a])

        def finish(t, slot, dst):
            prepare(t, slot)
            inverse(slot)

            def column(n, _):
                a = pl.ds(pl.multiple_of(n * wide, wide), wide)
                back_part(slot, a, dst)
                weight_part(slot, a)
                return 0

            lax.fori_loop(0, D // wide, column, 0)

        def finish_weights(t, slot):
            prepare(t, slot)

            def column(n, _):
                weight_part(slot, pl.ds(pl.multiple_of(n * wide, wide), wide))
                return 0

            lax.fori_loop(0, D // wide, column, 0)

        def flash(i, t):
            fetch_both(t)

            def pair(m, _):
                u = xor(p, m, P_)
                rect(jnp.maximum(t, u), jnp.minimum(t, u))
                return 0

            lax.fori_loop(0, i, pair, 0)
            triangle(t)

        def advance(i, t):
            @pl.when(i == 1)
            def _():
                plane_sums()

            flash(i, t)
            if square:

                @pl.when(i == 3)
                def _():
                    join_g(2)
                    join_g(1)

            @pl.when(i < P_ - 1)
            def _():
                over(i + 1).wait_send()

            finish(t, 0, mb)
            over(i).start()
            finish(t, 1, own)
            over(i).wait_recv()
            combine(i)
            if not square:
                out_b(i, t).start()
                return

            @pl.when(i == 3)
            def _():
                relay_b(1).start()
                relay_b(2).start()

            @pl.when(i == 2)
            def _():
                join_b(2)

            @pl.when(i == 1)
            def _():
                join_b(1)

        def stage(n, _):
            i = P_ - 1 - n
            advance(i, xor(p, i, P_))
            return 0

        lax.fori_loop(0, P_ - 1, stage, 0)
        flash(0, p)
        finish_weights(p, 0)
        finish_weights(p, 1)


    V = pltpu.VMEM
    pl.run_scoped(
        attention,
        V((nh, L, HD), bf),
        V((nh, L), f32),
        V((C, L), f32),
        V((nh, L, HD), f32),
        V((nh, L, HD), f32),
    )

    def closing(dw, up, qm, qs_, go_, vo):
        dw[...] = jnp.transpose(dwt[...])

        bunch = 8 // math.gcd(R, 8)

        def piece(n, _):
            part = dw[pl.ds(pl.multiple_of(n * (bunch * R), 8), bunch * R), :]
            for j in range(bunch):
                to = n * bunch + j
                qm[lax.div(to, F), lax.rem(to, F)] = part[j * R : (j + 1) * R].astype(bf)
            return 0

        lax.fori_loop(0, S * F // bunch, piece, 0)
        for i in range(1, F):
            go(remote(qm.at[:, deep(i)], qi.at[i], qsend, qrecv, i, (s, deep(i))))
        up_load = pltpu.make_async_copy(dx2, up, local.at[0])
        up_load.start()
        over(1).wait_send()
        finish_back(0, mb)
        over(0).start()
        finish_back(1, own)
        vi[0:1, :] = gf[...]
        vi[1:2, :] = jnp.zeros_like(gf)
        turned = jnp.transpose(jnp.broadcast_to(gs_[...], (C, 128)))
        vi[1:2, 0:C] = turned[0:1, :]
        for i in range(1, F):
            go(remote(vi, vz.at[i], vsend, vrecv, i, (s, deep(i))))
        x_load = pltpu.make_async_copy(x_all.at[s], xx.at[0], nsem.at[1])
        x_load.start()
        over(0).wait_recv()
        combine(0)
        total = vi[...]
        for i in range(1, F):
            remote(vi, vz.at[i], vsend, vrecv, i, mate).wait_recv()
            total = total + vz[i]
        vp[0] = total
        for i in range(1, S):
            go(remote(vp.at[0], vp.at[i], vsend, vrecv, F - 1 + i, (lax.rem(s + i, S), f)))
        for i in range(1, F):
            remote(qm.at[:, f], qi.at[i], qsend, qrecv, i, mate).wait_recv()

        def sum_q(n, _):
            part = qm[n, f].astype(f32)
            for i in range(1, F):
                part = part + qi[i, n].astype(f32)
            qs_[n] = part.astype(bf)
            return 0

        lax.fori_loop(0, S, sum_q, 0)
        keep = pltpu.make_async_copy(qs_.at[s], qo.at[s], local.at[1])
        keep.start()
        for i in range(1, S):
            to = lax.rem(s + i, S)
            go(remote(qs_.at[to], qo.at[s], qsend, qrecv, F - 1 + i, (to, f)))
        up_load.wait()
        x_load.wait()
        over(0).wait_send()
        used = (1, 2) if square else range(1, P_)
        for i in used:
            if square:
                direct_b(i, 0).wait_recv()
                direct_b(i, 1).wait_recv()
            else:
                out_b(i, chip(i)).wait_recv()

        def below(n, _):
            a = pl.ds(pl.multiple_of(n * rows, rows), rows)
            back = bi[0, a, :].astype(f32)
            for i in used:
                back = back + bp[i - 1, a, :].astype(f32)
            z = xx[0, a, :].astype(f32)
            r1 = lax.rsqrt(jnp.mean(z * z, axis=-1, keepdims=True) + eps_norm)
            e1 = back * g1[...]
            tilt = jnp.mean(e1 * z, axis=-1, keepdims=True)
            mb[a, :] = (up[a, :] + r1 * e1 - z * (r1 * r1 * r1 * tilt)).astype(bf)
            return 0

        lax.fori_loop(0, T // rows, below, 0)
        outs = [pltpu.make_async_copy(mb, in_out, local.at[0])]
        outs[0].start()
        for i in range(1, F):
            remote(ga.at[:, f], gz.at[i], gsend, grecv, ZG + i, mate).wait_recv()
        for a in range(NW):
            part = ga[a, f].astype(f32)
            for i in range(1, F):
                part = part + gz[i, a].astype(f32)
            go_[a] = part
        for a, ref in enumerate((o_proj, o_up, o_down)):
            outs.append(pltpu.make_async_copy(go_.at[a], ref, bload.at[a]))
            outs[-1].start()
        total = vp[0]
        for i in range(1, S):
            remote(vp.at[0], vp.at[i], vsend, vrecv, F - 1 + i, mate).wait_recv()
            total = total + vp[i]
        vo[...] = total
        outs.append(pltpu.make_async_copy(vo, vec_out, nsem.at[0]))
        outs[-1].start()
        for i in range(1, S):
            src = lax.rem(s + S - i, S)
            remote(qs_.at[0], qo.at[src], qsend, qrecv, F - 1 + i, mate).wait_recv()
        keep.wait()
        for a, ref in enumerate((o_q, o_k, o_v)):
            for src in range(S):
                part = qo[src, :, a * C : (a + 1) * C].astype(f32)
                go_[NW + a, :, src * C : (src + 1) * C] = part
            outs.append(pltpu.make_async_copy(go_.at[NW + a], ref, bload.at[NW + a]))
            outs[-1].start()
        for out in outs:
            out.wait()
        for copy in todo:
            copy.wait_send()
        for i in range(1, F):
            deep_g(i).wait_send()
        for i in used:
            if square:
                relay_g(i).wait_send()
                relay_b(i).wait_send()
                for half in range(2):
                    direct_g(i, half).wait_send()
                    direct_b(i, half).wait_send()
            else:
                out_g(i).wait_send()
                out_b(i, chip(i)).wait_send()

    pl.run_scoped(
        closing,
        V((D, 3 * C), f32),
        V((T, D), f32),
        V((S, F, R, 3 * C), bf),
        V((S, R, 3 * C), bf),
        V((NW + 3, R, D), f32),
        V((2, D), f32),
    )


def backward_all(S, F, nh, dm, qt, kt, q, k, v, ot, lse, n1, x_all, w, sc, g1, gi, dx2):
    T, D = x_all.shape[1], x_all.shape[2]
    C = nh * HD
    L = S * T
    P_ = S // 2
    NW, R = gi.shape[1], gi.shape[3]
    any_ = pl.BlockSpec(memory_space=pl.ANY)
    vm = pl.BlockSpec(memory_space=pltpu.VMEM)
    dma = pltpu.SemaphoreType.DMA
    shape = jax.ShapeDtypeStruct
    V = pltpu.VMEM
    return pl.pallas_call(
        functools.partial(backward_kernel, S, F, nh),
        out_shape=[
            shape((R, D), f32),
            shape((R, D), f32),
            shape((R, D), f32),
            shape((T, D), bf),
            shape((R, D), f32),
            shape((R, D), f32),
            shape((R, D), f32),
            shape((2, D), f32),
            shape((P_, NW, F, R, D), bf),
            shape((2, NW, F // 2, R, D), bf),
            shape((2, NW, F // 2, R, D), bf),
        ],
        in_specs=[any_] + [vm] * 7 + [any_, any_, vm, vm, vm, any_, any_],
        out_specs=[any_] * 11,
        scratch_shapes=[
            V((C, L), bf),
            V((3 * C, D), bf),
            V((3 * C, D), f32),
            V((3 * C, T), bf),
            V((2, T, 3 * C), bf),
            V((2, T, D), bf),
            V((2, T, D), bf),
            V((T, 1), f32),
            V((T, D), bf),
            V((T, D), bf),
            V((P_, T, D), bf),
            V((2 if P_ == 4 else P_ - 1, T, D), bf),
            V((2, T // 2, D), bf),
            V((NW, F, R, D), bf),
            V((NW, F, R, D), bf),
            V((F, NW, R, D), bf),
            V((F, S, R, 3 * C), bf),
            V((S, R, 3 * C), bf),
            V((2, D), f32),
            V((F, 2, D), f32),
            V((S, 2, D), f32),
            V((1, D), f32),
            V((C, 1), f32),
            dma((3,)),
            dma((4,)),
            dma((S,)),
            dma((10 + 2 * P_ + F,)),
            dma((10 + 2 * P_ + F,)),
            dma((max(2 * P_, 10),)),
            dma((max(2 * P_, 10),)),
            dma((S + F,)),
            dma((S + F,)),
            dma((S + F,)),
            dma((S + F,)),
        ],
        compiler_params=pltpu.CompilerParams(
            collective_id=4, has_side_effects=True, vmem_limit_bytes=66_000_000
        ),
        name="backward",
    )(dm, qt, kt, q, k, v, ot, lse, n1, x_all, w, sc, g1, gi, dx2)


def body(
    inputs,
    w_query,
    w_key,
    w_value,
    w_proj,
    w_up,
    w_down,
    gain_first,
    gain_second,
    bias_up,
    bias_down,
    query_scale,
    cotangent,
):
    groups = lax.axis_size("seq")
    rows_of = lax.axis_size("fsdp")
    nh = H // groups
    cols = nh * HD
    both = ("seq", "fsdp")
    tokens, width = inputs.shape[1], inputs.shape[2]
    length = tokens * groups
    shard = w_query.shape[0]
    x_low = inputs.reshape(tokens, width)
    small = jnp.stack([gain_first, gain_second, bias_up, bias_down], 0)
    small = jnp.pad(small.astype(bf), ((0, 12), (0, 128 - shard)))
    x_all, qkv_w, small, weights = gather_all(
        groups, rows_of, x_low, small, w_query, w_key, w_value, w_proj, w_up, w_down
    )
    qkv_w = qkv_w.reshape(width, 3 * cols)
    small = small[:, :, :4, :shard].transpose(2, 0, 1, 3).reshape(4, width).astype(f32)
    scale_dims = jax.nn.softplus(query_scale) * log_two_inverse / math.sqrt(HD)
    scale_cols = jnp.tile(scale_dims, nh)
    normed, qt, kt, q, k, v, ot, lse, mixed, weights = forward_all(
        groups, rows_of, nh, x_all, qkv_w, small[:1], scale_cols[:, None], weights
    )
    result, grad_middle, dm, pairs, vectors = middle_all(
        groups,
        rows_of,
        nh,
        mixed,
        x_low,
        cotangent.reshape(tokens, width),
        weights.reshape(3, width, width),
        small,
    )
    (
        grad_proj,
        grad_up,
        grad_down,
        grad_inputs,
        grad_query,
        grad_key,
        grad_value,
        late,
        *unused,
    ) = backward_all(
        groups,
        rows_of,
        nh,
        dm,
        qt,
        kt,
        q,
        k,
        v,
        ot,
        lse,
        normed,
        x_all,
        qkv_w,
        scale_cols[:, None],
        small[:1],
        pairs.reshape(groups // 2, 3, rows_of, shard, width),
        grad_middle,
    )
    at = (lax.axis_index("seq") * rows_of + lax.axis_index("fsdp")) * shard
    vectors = jnp.concatenate([late[:1], vectors[1:4]], 0)
    mine = lax.dynamic_slice_in_dim(vectors, at, shard, 1)
    scale_total = jnp.sum(late[1, :cols].reshape(nh, HD), axis=0) / scale_dims
    grad_scale = scale_total * jax.nn.sigmoid(query_scale) * log_two_inverse / math.sqrt(HD)
    return (
        result.reshape(inputs.shape),
        grad_inputs.reshape(inputs.shape),
        grad_query,
        grad_key,
        grad_value,
        grad_proj,
        grad_up,
        grad_down,
        mine[0],
        mine[1],
        mine[2],
        mine[3],
        grad_scale,
    )


def solution(mesh):
    return jax.shard_map(
        body,
        mesh=mesh,
        in_specs=(
            P("fsdp", "seq", None),
            P(("seq", "fsdp"), None),
            P(("seq", "fsdp"), None),
            P(("seq", "fsdp"), None),
            P(("seq", "fsdp"), None),
            P(("seq", "fsdp"), None),
            P(("seq", "fsdp"), None),
            P(("seq", "fsdp")),
            P(("seq", "fsdp")),
            P(("seq", "fsdp")),
            P(("seq", "fsdp")),
            P(),
            P("fsdp", "seq", None),
        ),
        out_specs=(
            P("fsdp", "seq", None),
            P("fsdp", "seq", None),
            P(("seq", "fsdp"), None),
            P(("seq", "fsdp"), None),
            P(("seq", "fsdp"), None),
            P(("seq", "fsdp"), None),
            P(("seq", "fsdp"), None),
            P(("seq", "fsdp"), None),
            P(("seq", "fsdp")),
            P(("seq", "fsdp")),
            P(("seq", "fsdp")),
            P(("seq", "fsdp")),
            P(),
        ),
        check_vma=False,
    )
```

```python
import functools
import math

import jax
import jax.numpy as jnp
from jax import lax
from jax.experimental import pallas as pl
from jax.experimental.pallas import tpu as pltpu
from jax.sharding import PartitionSpec as P

H = 16
HD = 80
eps_norm = 1e-06
log_two_inverse = 1.442695
bf = jnp.bfloat16
f32 = jnp.float32
NEG = -1e30


def dot(a,b,ca=1,cb=0):
    return lax.dot_general(a,b,(((ca,),(cb,)),((),())),preferred_element_type=f32)


MESH = pl.DeviceIdType.MESH


def spots():
    s, f = lax.axis_index("seq"), lax.axis_index("fsdp")
    return s, f, s // 2, lax.rem(s, 2)


def greet(S, F):
    s, f, _, _ = spots()
    barrier = pltpu.get_barrier_semaphore()
    for i in range(1, S):
        pl.semaphore_signal(barrier, inc=1, device_id=(lax.rem(s + i, S), f), device_id_type=MESH)
    for i in range(1, F):
        pl.semaphore_signal(barrier, inc=1, device_id=(s, lax.rem(f + i, F)), device_id_type=MESH)
    pl.semaphore_wait(barrier, S + F - 2)


def remote(src, dst, sends, recvs, n, to):
    return pltpu.make_async_remote_copy(
        src_ref=src,
        dst_ref=dst,
        send_sem=sends.at[n],
        recv_sem=recvs.at[n],
        device_id=to,
        device_id_type=MESH,
    )


def gather_kernel(S, F, x, sm, w_q, w_k, w_v, w_o, w_1, w_2, x_all, wq_all, sm_all, wm_all, xv, qv, sv, mv, local,
                  xs, xr, qs, qr, ss, sr, ms, mr):
    s, f, p, c = spots()
    P_ = S // 2
    other = 1 - c
    loads = [
        pltpu.make_async_copy(sm, sv, local.at[0]),
        pltpu.make_async_copy(x, xv, local.at[2]),
    ]
    for load in loads:
        load.start()
    greet(S, F)
    mate = (p * 2 + other, f)
    todo = []

    def go(copy):
        copy.start()
        todo.append(copy)

    def chip(i):
        return lax.rem(p + i, P_) * 2 + c

    def back(i):
        return lax.rem(p + P_ - i, P_) * 2 + c

    def near_chip(i):
        return flip_bits(p, i) * 2 + c

    H_ = x.shape[0] // 2

    def deep(i):
        return lax.rem(f + i, F)

    def behind(i):
        return lax.rem(f + F - i, F)

    loads[0].wait()
    keep0 = pltpu.make_async_copy(sv, sm_all.at[s, f], local.at[0])
    keep0.start()
    for i in range(1, F):
        go(remote(sv, sm_all.at[s, f], ss, sr, i, (s, deep(i))))
    C = qv.shape[2] // 3
    for n, w in enumerate((w_q, w_k, w_v)):
        for to in range(S):
            qv[to, :, n * C : (n + 1) * C] = w[:, to * C : (to + 1) * C].astype(bf)
    keep1 = pltpu.make_async_copy(qv.at[s], wq_all.at[s, f], local.at[1])
    keep1.start()
    for i in range(1, S):
        to = lax.rem(s + i, S)
        go(remote(qv.at[to], wq_all.at[s, f], qs, qr, i, (to, f)))
    loads[1].wait()
    keep2 = pltpu.make_async_copy(xv, x_all.at[s], local.at[2])
    keep2.start()
    if P_ == 4:
        for first in range(2):
            for i in (1, 2):
                half = first if i == 1 else 1 - first
                part = pl.ds(half * H_, H_)
                go(remote(xv.at[part], x_all.at[s, part], xs, xr, 2 * i + half, (near_chip(i), f)))
    else:
        for i in range(1, P_):
            go(remote(xv, x_all.at[s], xs, xr, i, (chip(i), f)))
    go(remote(xv, x_all.at[s], xs, xr, 0, mate))
    for n, w in enumerate((w_o, w_1, w_2)):
        mv[n] = w[...].astype(bf)
    keep3 = pltpu.make_async_copy(mv, wm_all.at[:, f], local.at[3])
    keep3.start()
    for i in range(1, F):
        go(remote(mv, wm_all.at[:, f], ms, mr, i, (s, deep(i))))
    for i in range(1, F):
        g = behind(i)
        remote(sv, sm_all.at[s, g], ss, sr, i, mate).wait_recv()
    keep0.wait()
    for i in range(1, S):
        go(remote(sm_all.at[s], sm_all.at[s], ss, sr, F - 1 + i, (lax.rem(s + i, S), f)))
    for i in range(1, S):
        remote(qv.at[0], wq_all.at[lax.rem(s + S - i, S), f], qs, qr, i, mate).wait_recv()
    keep1.wait()
    for i in range(1, F):
        go(remote(wq_all.at[:, f], wq_all.at[:, f], qs, qr, S - 1 + i, (s, deep(i))))
    for i in range(1, F):
        remote(mv, wm_all.at[:, behind(i)], ms, mr, i, mate).wait_recv()
    keep3.wait()
    if P_ == 4:
        for i in (1, 2):
            half = i - 1
            part = pl.ds(half * H_, H_)
            src = near_chip(i)
            remote(xv.at[part], x_all.at[src, part], xs, xr, 2 * i + half, mate).wait_recv()
            blk = x_all.at[src, part]
            go(remote(blk, blk, xs, xr, 6 + half, (near_chip(3 - i), f)))
        for i in (1, 2):
            half = 2 - i
            part = pl.ds(half * H_, H_)
            src = near_chip(i)
            remote(xv.at[part], x_all.at[src, part], xs, xr, 2 * i + half, mate).wait_recv()
            go(remote(x_all.at[src], x_all.at[src], xs, xr, 8 + i, mate))
    for i in range(1, P_ if P_ != 4 else 1):
        src = back(i)
        remote(xv, x_all.at[src], xs, xr, i, mate).wait_recv()
        go(remote(x_all.at[src], x_all.at[src], xs, xr, P_ - 1 + i, mate))
    for i in range(1, S):
        src = lax.rem(s + S - i, S)
        remote(sm_all.at[src], sm_all.at[src], ss, sr, F - 1 + i, mate).wait_recv()
    for i in range(1, F):
        g = behind(i)
        remote(wq_all.at[:, g], wq_all.at[:, g], qs, qr, S - 1 + i, mate).wait_recv()
    near = p * 2 + other
    remote(xv, x_all.at[near], xs, xr, 0, mate).wait_recv()
    if P_ == 4:
        for half in range(2):
            part = pl.ds(half * H_, H_)
            blk = x_all.at[near_chip(3), part]
            remote(blk, blk, xs, xr, 6 + half, mate).wait_recv()
            go(remote(blk, blk, xs, xr, 11 + half, mate))
        for i in (1, 2):
            blk = x_all.at[flip_bits(p, i) * 2 + other]
            remote(blk, blk, xs, xr, 8 + i, mate).wait_recv()
        for half in range(2):
            blk = x_all.at[flip_bits(p, 3) * 2 + other, pl.ds(half * H_, H_)]
            remote(blk, blk, xs, xr, 11 + half, mate).wait_recv()
    else:
        for i in range(1, P_):
            src = lax.rem(p + P_ - i, P_) * 2 + other
            remote(xv, x_all.at[src], xs, xr, P_ - 1 + i, mate).wait_recv()
    keep2.wait()
    for copy in todo:
        copy.wait_send()


def gather_all(S, F, x, sm, *weights):
    R, D = weights[0].shape
    C3 = 3 * D // S
    vm = pl.BlockSpec(memory_space=pltpu.VMEM)
    any_ = pl.BlockSpec(memory_space=pl.ANY)
    shapes = [
        (S,) + x.shape,
        (S, F, R, C3),
        (S, F) + sm.shape,
        (3, F, R, D),
    ]
    P_ = S // 2
    dma = pltpu.SemaphoreType.DMA
    counts = [max(2 * P_ - 1, 12), S + F - 1, F + S - 1, F]
    sems = []
    for n in counts:
        sems += [dma((n + 1,)), dma((n + 1,))]
    return pl.pallas_call(
        functools.partial(gather_kernel, S, F),
        out_shape=[
            jax.ShapeDtypeStruct(sh, bf) for sh in shapes
        ],
        in_specs=[any_] * 2 + [vm] * 6,
        out_specs=[any_] * 4,
        scratch_shapes=[
            pltpu.VMEM(x.shape, x.dtype),
            pltpu.VMEM((S, R, C3), bf),
            pltpu.VMEM(sm.shape, sm.dtype),
            pltpu.VMEM((3, R, D), bf),
            dma((4,)),
        ]
        + sems,
        compiler_params=pltpu.CompilerParams(collective_id=1, has_side_effects=True),
        name="gather",
    )(x, sm, *weights)


def xor(a, b, n):
    out, bit = 0, 1
    while bit < n:
        both = lax.rem(lax.div(a, bit), 2) + lax.rem(lax.div(b, bit), 2)
        out = out + bit * lax.rem(both, 2)
        bit *= 2
    return out


def flip_bits(p, i):
    out, bit = p, 1
    while bit <= i:
        if i & bit:
            out = out + bit - 2 * bit * lax.rem(lax.div(p, bit), 2)
        bit *= 2
    return out


def forward_kernel(S, F, nh, x_all, w, g1, sc, wz, n1, qt, kt, qn, kk, vn, ot, lse, mixed, wm,
                   wt, vt, xb, nb, wv, inx, outn, local, osend, orecv, wsend, wrecv):
    s, f, p, c = spots()
    P_ = S // 2
    T, D = x_all.shape[1], x_all.shape[2]
    C = nh * HD
    L = S * T
    BQ = 2 * T
    BK = min(512, BQ)
    other = 1 - c
    mate = (p * 2 + other, f)
    load = pltpu.make_async_copy(wz, wv, local.at[0])
    load.start()

    def fetch(b):
        return pltpu.make_async_copy(x_all.at[b], xb.at[lax.rem(b, 2)], inx.at[lax.rem(b, 2)])

    def store(b):
        return pltpu.make_async_copy(nb.at[lax.rem(b, 2)], n1.at[b], outn.at[lax.rem(b, 2)])

    fetch(0).start()
    greet(S, F)
    load.wait()
    keep = pltpu.make_async_copy(wv, wm.at[:, s], local.at[0])
    keep.start()

    zero = s - s
    chips = [flip_bits(p, i) for i in range(P_)]

    def num(n):
        return zero + n

    def spread(i):
        return remote(wv, wm.at[:, s], wsend, wrecv, i, (xor(p, i, P_) * 2 + c, f))

    def forward(i):
        src = xor(p, i, P_) * 2 + c
        n = (7 if P_ == 4 else P_) + i
        return remote(wm.at[:, src], wm.at[:, src], wsend, wrecv, n, mate)

    def part_of(src, half):
        return wm.at[:, src, pl.ds(num(half * (F // 2)), F // 2)]

    def direct(i, half):
        src = wv.at[:, pl.ds(half * (F // 2), F // 2)]
        to = (flip_bits(p, i) * 2 + c, f)
        return remote(src, part_of(s, half), wsend, wrecv, 2 * i + half, to)

    def arrived(i, half):
        blk = part_of(chips[i] * 2 + c, half)
        remote(blk, blk, wsend, wrecv, num(2 * i + half), mate).wait_recv()

    def relay(i):
        blk = part_of(flip_bits(p, i) * 2 + c, i - 1)
        return remote(blk, blk, wsend, wrecv, 5 + i, (flip_bits(p, 3 - i) * 2 + c, f))

    def relayed(half):
        blk = part_of(chips[3] * 2 + c, half)
        return remote(blk, blk, wsend, wrecv, num(6 + half), mate)

    def corner(half, core):
        blk = part_of(chips[3] * 2 + core, half)
        return remote(blk, blk, wsend, wrecv, num(10 + half), mate)

    square = P_ == 4
    if square:
        for first in range(2):
            for i in (1, 2):
                direct(i, first if i == 1 else 1 - first).start()
    else:
        for i in range(1, P_):
            spread(P_ - i).start()
    near = remote(wv, wm.at[:, s], wsend, wrecv, 0, mate)
    near.start()
    wt[...] = jnp.transpose(w[...])

    rows = 64

    def project(b, _):
        slot = lax.rem(b, 2)
        fetch(b).wait()

        @pl.when(b + 1 < S)
        def _():
            fetch(b + 1).start()

        @pl.when(b >= 2)
        def _():
            store(b - 2).wait()

        def norm(k, _):
            at = pl.ds(pl.multiple_of(k * rows, rows), rows)
            v = xb[slot, at, :].astype(f32)
            r = lax.rsqrt(jnp.mean(v * v, axis=-1, keepdims=True) + eps_norm)
            nb[slot, at, :] = (v * r * g1[...]).astype(bf)
            return 0

        lax.fori_loop(0, T // rows, norm, 0)
        store(b).start()
        cols = pl.ds(pl.multiple_of(b * T, T), T)
        res = dot(wt[...], nb[slot], 1, 1)
        qt[:, cols] = (res[:C] * sc[...]).astype(bf)
        kt[:, cols] = res[C : 2 * C].astype(bf)
        vt[:, cols] = res[2 * C :].astype(bf)
        for h in range(nh):
            part = slice(h * HD, (h + 1) * HD)
            qn[h, cols, :] = jnp.transpose(res[:C][part] * sc[part]).astype(bf)
            kk[h, cols, :] = jnp.transpose(res[C : 2 * C][part]).astype(bf)
            vn[h, cols, :] = jnp.transpose(res[2 * C :][part]).astype(bf)
        return 0

    lax.fori_loop(0, S, project, 0)
    if square:
        for i in (1, 2):
            arrived(i, i - 1)
            relay(i).start()
    store(S - 2).wait()
    store(S - 1).wait()

    r = BQ // BK

    def attend(t):
        first = pl.multiple_of(t * BQ, BQ)
        q = [qt[h * HD : (h + 1) * HD, pl.ds(first, BQ)] for h in range(nh)]

        def step(j, carry, diag=None):
            at = pl.ds(pl.multiple_of(j * BK, BK), BK)
            scores = [dot(kk[h, at, :], q[h]) for h in range(nh)]
            out = []
            for h in range(nh):
                m, l, acc = carry[h]
                sh = scores[h]
                if diag is not None:
                    kp = lax.broadcasted_iota(jnp.int32, sh.shape, 0) + diag * BK
                    qp = lax.broadcasted_iota(jnp.int32, sh.shape, 1)
                    sh = jnp.where(kp <= qp, sh, NEG)
                mn = jnp.maximum(m, jnp.max(sh, axis=0, keepdims=True))
                a = jnp.exp(m - mn)
                e = jnp.exp(sh - mn)
                l = l * a + jnp.sum(e, axis=0, keepdims=True)
                acc = acc * a + dot(vt[h * HD : (h + 1) * HD, at], e.astype(bf))
                out.append((mn, l, acc))
            return tuple(out)

        carry = tuple(
            (jnp.full((1, BQ), NEG, f32), jnp.zeros((1, BQ), f32), jnp.zeros((HD, BQ), f32))
            for _ in range(nh)
        )
        carry = lax.fori_loop(0, t * r, step, carry)
        for d in range(r):
            carry = step(t * r + d, carry, d)
        for h in range(nh):
            m, l, acc = carry[h]
            ot[h * HD : (h + 1) * HD, pl.ds(first, BQ)] = (acc / l).astype(bf)
            lse[h : h + 1, pl.ds(first, BQ)] = m + jnp.log(l)

    def to_owner(src, n, i, to):
        return pltpu.make_async_remote_copy(
            src_ref=src,
            dst_ref=mixed.at[s],
            send_sem=osend.at[n],
            recv_sem=orecv.at[2 * i + c],
            device_id=to,
            device_id_type=MESH,
        )

    def send(i, half):
        t = xor(p, i, P_)
        src = ot.at[:, pl.ds(pl.multiple_of(t * BQ + half * T, T), T)]
        return to_owner(src, 2 * i + half, i, (t * 2 + half, f))

    def turn(n, _):
        i = P_ - 1 - n
        attend(xor(p, i, P_))
        send(i, 0).start()
        send(i, 1).start()
        if not square:
            spread(i).wait_recv()
            forward(i).start()
            return 0

        @pl.when(i == 3)
        def _():
            arrived(2, 0)
            forward(num(2)).start()

        @pl.when(i == 2)
        def _():
            arrived(1, 1)
            forward(num(1)).start()

        @pl.when(i == 1)
        def _():
            for half in range(2):
                relayed(half).wait_recv()
                corner(half, c).start()

        return 0

    lax.fori_loop(0, P_ - 1, turn, 0)
    attend(p)
    mine = ot.at[:, pl.ds(pl.multiple_of(s * T, T), T)]
    theirs = ot.at[:, pl.ds(pl.multiple_of((p * 2 + other) * T, T), T)]
    last = to_owner(theirs, 0, 0, mate)
    last.start()
    own = pltpu.make_async_copy(mine, mixed.at[s], local.at[1])
    own.start()
    def from_source(i, core):
        return pltpu.make_async_remote_copy(
            src_ref=mine,
            dst_ref=mixed.at[flip_bits(p, i) * 2 + core],
            send_sem=osend.at[0],
            recv_sem=orecv.at[2 * i + core],
            device_id=mate,
            device_id_type=MESH,
        )

    for i in range(1, P_):
        for core in range(2):
            from_source(i, core).wait_recv()
    from_source(0, other).wait_recv()
    last.wait_send()
    own.wait()
    keep.wait()
    near.wait()
    if square:
        for i in (1, 2):
            forward(i).wait()
            relay(i).wait_send()
            for half in range(2):
                direct(i, half).wait_send()
        for half in range(2):
            corner(half, c).wait_send()
            corner(half, other).wait_recv()
    for i in range(1, P_):
        if not square:
            forward(i).wait()
            spread(i).wait_send()
        send(i, 0).wait_send()
        send(i, 1).wait_send()


def forward_all(S, F, nh, x_all, w, g1, sc, wz):
    T, D = x_all.shape[1], x_all.shape[2]
    C = nh * HD
    L = S * T
    P_ = S // 2
    any_ = pl.BlockSpec(memory_space=pl.ANY)
    vm = pl.BlockSpec(memory_space=pltpu.VMEM)
    dma = pltpu.SemaphoreType.DMA
    shape = jax.ShapeDtypeStruct
    NW, R = wz.shape[0], wz.shape[2]
    V = pltpu.VMEM
    return pl.pallas_call(
        functools.partial(forward_kernel, S, F, nh),
        out_shape=[
            shape((S, T, D), bf),
            shape((C, L), bf),
            shape((C, L), bf),
            shape((nh, L, HD), bf),
            shape((nh, L, HD), bf),
            shape((nh, L, HD), bf),
            shape((C, L), bf),
            shape((nh, L), f32),
            shape((S, C, T), bf),
            shape((NW, S, F, R, D), bf),
        ],
        in_specs=[any_, vm, vm, vm, any_],
        out_specs=[any_] + [vm] * 7 + [any_, any_],
        scratch_shapes=[
            V((3 * C, D), bf),
            V((C, L), bf),
            V((2, T, D), bf),
            V((2, T, D), bf),
            V((NW, F, R, D), bf),
            dma((2,)),
            dma((2,)),
            dma((2,)),
            dma((2 * P_,)),
            dma((2 * P_,)),
            dma((max(2 * P_, 12),)),
            dma((max(2 * P_, 12),)),
        ],
        compiler_params=pltpu.CompilerParams(
            collective_id=3, has_side_effects=True, vmem_limit_bytes=60 << 20
        ),
        name="forward",
    )(x_all, w, g1, sc, wz)


def middle_kernel(S, F, nh, mixed, x, ct, wm, small, out, dx2, dm, gi, vec,
                  mx, lt, xv, cv, wv, x2, n2, dn, ab, ub, eb, r2, sb, rb, ob, dov, et, rv, vz, vp, local, wsem,
                  dsend, drecv, gsend, grecv, vsend, vrecv):
    s, f, p, c = spots()
    P_ = S // 2
    T, D = x.shape
    C = nh * HD
    NW = wm.shape[0]
    G = D // S
    other = 1 - c
    mate = (p * 2 + other, f)
    wide = 256 if D % 256 == 0 else D
    rows = 64
    loads = [
        pltpu.make_async_copy(mixed, mx, local.at[0]),
        pltpu.make_async_copy(x, xv, local.at[1]),
        pltpu.make_async_copy(ct, cv, local.at[2]),
    ]
    loads += [pltpu.make_async_copy(wm.at[n], wv.at[n], wsem.at[n]) for n in range(NW)]
    for load in loads:
        load.start()
    greet(S, F)
    g2, b1, b2 = small[1:2, :], small[2:3, :], small[3:4, :]

    def by_core(n, tall):
        for t in range(P_):
            for core in range(2):
                at = (t * 2 + core) * G
                lt[n, core, t * G : (t + 1) * G, :] = tall[at : at + G]

    def chunk(n):
        return pl.ds(pl.multiple_of(n * wide, wide), wide)

    def over(n, body):
        def one(k, _):
            body(k)
            return 0

        lax.fori_loop(0, n, one, 0)

    def lines(n):
        return pl.ds(pl.multiple_of(n * rows, rows), rows)

    loads[0].wait()
    tall = mx[...].reshape(D, T)
    by_core(0, tall)
    ub[...] = jnp.transpose(tall)
    loads[1].wait()
    loads[2].wait()
    loads[3].wait()

    def attend_out(n):
        at = chunk(n)
        x2[:, at] = xv[:, at].astype(f32) + dot(ub[...], wv[0, :, at])

    over(D // wide, attend_out)

    def norm(n):
        at = lines(n)
        z = x2[at, :]
        r = lax.rsqrt(jnp.mean(z * z, axis=-1, keepdims=True) + eps_norm)
        r2[at, :] = r
        n2[at, :] = (z * r * g2).astype(bf)

    over(T // rows, norm)
    loads[4].wait()
    loads[5].wait()
    rv[...] = jnp.zeros_like(rv)

    def hidden(n):
        at = chunk(n)
        u = dot(n2[...], wv[1, :, at]) + small[2:3, at]
        gate = 1 / (1 + jnp.exp(-u))
        ab[:, at] = (u * gate).astype(bf)
        ga = dot(cv[...], wv[2, at, :], 1, 1)
        du = ga * (gate * (1 + u * (1 - gate)))
        rv[2:3, at] = jnp.sum(du, axis=0, keepdims=True)
        ub[:, at] = du.astype(bf)
        rv[3:4, at] = jnp.sum(cv[:, at].astype(f32), axis=0, keepdims=True)

    over(D // wide, hidden)

    def up_back(n):
        at = chunk(n)
        dn[:, at] = dot(ub[...], wv[1, at, :], 1, 1)

    over(D // wide, up_back)

    def second(n):
        at = lines(n)
        z, r, d = x2[at, :], r2[at, :], dn[at, :]
        e = d * g2
        tilt = jnp.mean(e * z, axis=-1, keepdims=True)
        v = cv[at, :].astype(f32) + r * e - z * (r * r * r * tilt)
        rv[1:2, :] += jnp.sum(d * z * r, axis=0, keepdims=True)
        dn[at, :] = v
        eb[at, :] = v.astype(bf)

    over(T // rows, second)
    keep = pltpu.make_async_copy(dn, dx2, local.at[0])
    keep.start()

    def vec_z(i):
        return remote(rv, vz.at[i], vsend, vrecv, i, (s, lax.rem(f + i, F)))

    def vec_s(i):
        return remote(vp.at[0], vp.at[i], vsend, vrecv, F - 1 + i, (lax.rem(s + i, S), f))

    for i in range(1, F):
        vec_z(i).start()

    def head_out(i, to):
        return remote(dov.at[i], dm.at[s], dsend, drecv, i, (to, f))

    et[...] = jnp.transpose(eb[...])

    def heads(i, _):
        to = lax.rem(s + i, S)
        rows_of = pl.ds(pl.multiple_of(to * C, C), C)
        dov[i] = dot(wv[0, rows_of, :], et[...]).astype(bf)

        head_out(i, to).start()
        return 0

    lax.fori_loop(1, S, heads, 0)
    mine = pl.ds(pl.multiple_of(s * C, C), C)
    dov[0] = dot(wv[0, mine, :], et[...]).astype(bf)
    home = pltpu.make_async_copy(dov.at[0], dm.at[s], local.at[1])
    home.start()

    by_core(1, jnp.transpose(n2[...]))
    by_core(2, jnp.transpose(ab[...]))
    right = [eb, ub, cv]

    def pass_on(n):
        return remote(sb.at[n], rb.at[n], gsend, grecv, n, mate)

    for n in range(NW):

        def send_side(k, n=n):
            at = chunk(k)
            sb[n, :, at] = dot(lt[n, other], right[n][:, at]).astype(bf)

        over(D // wide, send_side)
        pass_on(n).start()

    part = rv[...]
    for i in range(1, F):
        vec_z(i).wait_recv()
        part = part + vz[i]
    vp[0] = part
    for i in range(1, S):
        vec_s(i).start()

    def top(n):
        at = chunk(n)
        y = x2[:, at] + dot(ab[...], wv[2, :, at]) + small[3:4, at]
        xv[:, at] = y.astype(bf)

    over(D // wide, top)
    done = pltpu.make_async_copy(xv, out, local.at[2])
    done.start()
    for n in range(NW):
        pass_on(n).wait_recv()

        def keep_side(k, n=n):
            at = chunk(k)
            both = dot(lt[n, c], right[n][:, at]) + rb[n, :, at].astype(f32)
            ob[n, :, at] = both.astype(bf)

        over(D // wide, keep_side)
    stores = []
    for i in range(P_):
        here = pl.ds(pl.multiple_of(flip_bits(p, i) * G, G), G)
        stores.append(pltpu.make_async_copy(ob.at[:, here], gi.at[i], wsem.at[i]))
        stores[-1].start()
    part = vp[0]
    for i in range(1, S):
        vec_s(i).wait_recv()
        part = part + vp[i]
    vec[...] = part
    for i in range(1, F):
        vec_z(i).wait_send()
    for i in range(1, S):
        vec_s(i).wait_send()
    for i in range(1, S):
        remote(dov.at[0], dm.at[lax.rem(s + S - i, S)], dsend, drecv, i, mate).wait_recv()
    for store in stores:
        store.wait()
    keep.wait()
    home.wait()
    done.wait()
    for i in range(1, S):
        head_out(i, lax.rem(s + i, S)).wait_send()
    for n in range(NW):
        pass_on(n).wait_send()


def middle_all(S, F, nh, mixed, x, ct, wm, small):
    T, D = x.shape
    C = nh * HD
    P_ = S // 2
    NW = wm.shape[0]
    G = D // S
    any_ = pl.BlockSpec(memory_space=pl.ANY)
    vm = pl.BlockSpec(memory_space=pltpu.VMEM)
    dma = pltpu.SemaphoreType.DMA
    shape = jax.ShapeDtypeStruct
    V = pltpu.VMEM
    return pl.pallas_call(
        functools.partial(middle_kernel, S, F, nh),
        out_shape=[
            shape((T, D), bf),
            shape((T, D), f32),
            shape((S, C, T), bf),
            shape((P_, NW, G, D), bf),
            shape((8, D), f32),
        ],
        in_specs=[any_, any_, any_, any_, vm],
        out_specs=[any_, any_, any_, any_, vm],
        scratch_shapes=[
            V((S, C, T), bf),
            V((NW, 2, P_ * G, T), bf),
            V((T, D), bf),
            V((T, D), bf),
            V((NW, D, D), bf),
            V((T, D), f32),
            V((T, D), bf),
            V((T, D), f32),
            V((T, D), bf),
            V((T, D), bf),
            V((T, D), bf),
            V((T, 1), f32),
            V((NW, P_ * G, D), bf),
            V((NW, P_ * G, D), bf),
            V((NW, P_ * G, D), bf),
            V((S, C, T), bf),
            V((D, T), bf),
            V((8, D), f32),
            V((F, 8, D), f32),
            V((S, 8, D), f32),
            dma((3,)),
            dma((max(NW, P_),)),
            dma((S,)),
            dma((S,)),
            dma((NW,)),
            dma((NW,)),
            dma((S + F,)),
            dma((S + F,)),
        ],
        compiler_params=pltpu.CompilerParams(
            collective_id=5, has_side_effects=True, vmem_limit_bytes=64_000_000
        ),
        name="middle",
    )(mixed, x, ct, wm, small)


def backward_kernel(S, F, nh, dm, qt_in, kt_in, q_in, k_in, v_in, ot_in, lse, n1, x_all, w, sc, g1,
                    gi, dx2,
                    o_proj, o_up, o_down, in_out, o_q, o_k, o_v, vec_out, gp, gr_, gj,
                    qt, kt, q, k, v, ot, dmt, wt, dwt, fm, tm, nx, xx, rr, mb, own, bi, bp, rl, ga, gb, gz, qi, qo,
                    vi, vz, vp, gf, gs_, local, nsem, bload, early,
                    gsend, grecv, bsend, brecv, qsend, qrecv, vsend, vrecv):
    s, f, p, c = spots()
    P_ = S // 2
    T, D = x_all.shape[1], x_all.shape[2]
    C = nh * HD
    L = S * T
    BQ = 2 * T
    BK = min(512, BQ)
    NW, R = gi.shape[1], gi.shape[3]
    other = 1 - c
    mate = (p * 2 + other, f)
    todo = []

    def go(copy):
        copy.start()
        todo.append(copy)

    chips = [flip_bits(p, i) for i in range(P_)]
    zero = s - s

    def num(n):
        return zero + n

    def chip(i):
        return chips[i]

    deeps = [lax.rem(f + i, F) for i in range(F)]

    def deep(i):
        return deeps[i]

    def head(ref, h, at):
        return ref[h * HD : (h + 1) * HD, at]

    loads = [
        pltpu.make_async_copy(dm.at[b], dmt.at[:, b * T : (b + 1) * T], bload.at[b])
        for b in range(S)
    ]
    pairs_in = ((qt_in, qt), (kt_in, kt), (q_in, q), (k_in, k), (v_in, v), (ot_in, ot))
    loads += [
        pltpu.make_async_copy(src, dst, early.at[n]) for n, (src, dst) in enumerate(pairs_in)
    ]
    for load in loads:
        load.start()
    greet(S, F)

    order = list(range(P_ - 1, -1, -1))
    wt[...] = jnp.transpose(w[...])
    dwt[...] = jnp.zeros_like(dwt)
    gf[...] = jnp.zeros_like(gf)
    gs_[...] = jnp.zeros_like(gs_)

    def slabs(body):
        def one(n, _):
            body(lax.div(n, F), lax.rem(n, F))
            return 0

        lax.fori_loop(0, NW * F, one, 0)

    square = P_ == 4
    ZG = 10 if square else 2 * P_
    FH, H_ = F // 2, T // 2

    def half_g(ref, half):
        return ref.at[:, pl.ds(num(half * FH), FH)]

    def direct_g(i, half):
        src, dst = half_g(gi.at[num(i)], half), half_g(gp.at[num(i)], half)
        if half == 2 - i:
            src = gj.at[num(half)]
        return remote(src, dst, gsend, grecv, num(2 + 2 * i + half), (chip(i) * 2 + c, f))

    def relay_g(i):
        src = half_g(gi.at[num(3)], i - 1)
        return remote(src, gr_.at[num(i - 1)], gsend, grecv, num(7 + i), (chip(i) * 2 + c, f))

    def join_g(i):
        half = 2 - i
        la = pltpu.make_async_copy(half_g(gi.at[num(i)], half), half_g(ga, 0), local.at[num(1)])
        la.start()
        relay_g(3 - i).wait_recv()
        lb = pltpu.make_async_copy(gr_.at[num(half)], half_g(gb, 0), local.at[num(2)])
        lb.start()
        la.wait()
        lb.wait()

        def add(z, _):
            for a in range(NW):
                w_ = num(a)
                ga[w_, z] = (ga[w_, z].astype(f32) + gb[w_, z].astype(f32)).astype(bf)
            return 0

        lax.fori_loop(0, FH, add, 0)
        st = pltpu.make_async_copy(half_g(ga, 0), gj.at[num(half)], local.at[num(1)])
        st.start()
        st.wait()
        direct_g(i, half).start()

    def out_g(i):
        return remote(gi.at[num(i)], gp.at[num(i)], gsend, grecv, num(P_ + i), (chip(i) * 2 + c, f))

    if square:
        relay_g(1).start()
        relay_g(2).start()
        direct_g(2, 1).start()
        direct_g(1, 0).start()
    else:
        for i in order[:-1]:
            out_g(i).start()

    for load in loads:
        load.wait()

    rows = 64
    wide = 256 if D % 256 == 0 else D

    def over(i):
        return remote(mb, bi.at[i], bsend, brecv, i, mate)

    def inverse(slot):
        def one(n, _):
            a = pl.ds(pl.multiple_of(n * rows, rows), rows)
            z = xx[slot, a, :].astype(f32)
            rr[a, :] = lax.rsqrt(jnp.mean(z * z, axis=-1, keepdims=True) + eps_norm)
            return 0

        lax.fori_loop(0, T // rows, one, 0)

    def back_part(slot, a, dst):
        back = dot(tm[slot], wt[:, a])
        dst[:, a] = back.astype(bf)
        hat = xx[slot, :, a].astype(f32) * rr[...]
        gf[:, a] += jnp.sum(back * hat, axis=0, keepdims=True)

    def finish_back(slot, dst):
        inverse(slot)

        def column(n, _):
            back_part(slot, pl.ds(pl.multiple_of(n * wide, wide), wide), dst)
            return 0

        lax.fori_loop(0, D // wide, column, 0)

    def combine(i):
        def one(n, _):
            a = pl.ds(pl.multiple_of(n * rows, rows), rows)
            bi[i, a, :] = (bi[i, a, :].astype(f32) + own[a, :].astype(f32)).astype(bf)
            return 0

        lax.fori_loop(0, T // rows, one, 0)

    def direct_b(i, half):
        part = pl.ds(pl.multiple_of(num(half * H_), H_), H_)
        src, dst = bi.at[num(i), part], bp.at[num(i - 1), part]
        return remote(src, dst, bsend, brecv, num(2 + 2 * i + half), (chip(i) * 2 + c, f))

    def relay_b(i):
        part = pl.ds(pl.multiple_of(num((i - 1) * H_), H_), H_)
        src = bi.at[num(3), part]
        return remote(src, rl.at[num(i - 1)], bsend, brecv, num(7 + i), (chip(i) * 2 + c, f))

    def join_b(i):
        half = 2 - i
        direct_b(i, 1 - half).start()
        relay_b(3 - i).wait_recv()
        few = min(rows, H_)

        def add(n, _):
            here = pl.ds(pl.multiple_of(half * H_ + n * few, few), few)
            there = pl.ds(pl.multiple_of(n * few, few), few)
            both = bi[num(i), here, :].astype(f32) + rl[num(half), there, :].astype(f32)
            bi[num(i), here, :] = both.astype(bf)
            return 0

        lax.fori_loop(0, H_ // few, add, 0)
        direct_b(i, half).start()

    def out_b(i, t):
        return pltpu.make_async_remote_copy(
            src_ref=bi.at[i],
            dst_ref=bp.at[i - 1],
            send_sem=bsend.at[P_ + i],
            recv_sem=brecv.at[P_ + i],
            device_id=(t * 2 + c, f),
            device_id_type=MESH,
        )

    def deep_g(i):
        src = ga.at[:, deep(i)]
        return remote(src, gz.at[num(i)], gsend, grecv, num(ZG + i), (s, deep(i)))

    def plane_sums():
        la = pltpu.make_async_copy(gi.at[num(0)], ga, local.at[num(1)])
        la.start()
        la.wait()
        for i in order[1:-1] if square else order[:-1]:
            if square:
                direct_g(i, 0).wait_recv()
                direct_g(i, 1).wait_recv()
            else:
                out_g(i).wait_recv()
            lb = pltpu.make_async_copy(gp.at[num(i)], gb, local.at[num(2)])
            lb.start()
            lb.wait()

            def more(z, _):
                for a in range(NW):
                    w_ = num(a)
                    ga[w_, z] = (ga[w_, z].astype(f32) + gb[w_, z].astype(f32)).astype(bf)
                return 0

            lax.fori_loop(0, F, more, 0)
        for i in range(1, F):
            deep_g(i).start()

    def attention(do, delta, dqt, dk, dv):
        dqt[...] = jnp.zeros_like(dqt)
        dk[...] = jnp.zeros_like(dk)
        dv[...] = jnp.zeros_like(dv)

        def turn(b, _):
            at = pl.ds(pl.multiple_of(b * T, T), T)
            for h in range(nh):
                do[h, at, :] = jnp.transpose(head(dmt, h, at))
                prod = head(dmt, h, at).astype(f32) * head(ot, h, at).astype(f32)
                delta[h : h + 1, at] = jnp.sum(prod, axis=0, keepdims=True)
            return 0

        lax.fori_loop(0, S, turn, 0)

        def tile(q0, k0, masked):
            qa = pl.ds(q0, BK)
            ka = pl.ds(k0, BK)
            scores = [dot(k[h, ka, :], head(qt, h, qa)) for h in range(nh)]
            dps = [dot(v[h, ka, :], head(dmt, h, qa)) for h in range(nh)]
            for h in range(nh):
                e = jnp.exp(scores[h] - lse[h : h + 1, qa])
                if masked:
                    kp = lax.broadcasted_iota(jnp.int32, e.shape, 0)
                    qp = lax.broadcasted_iota(jnp.int32, e.shape, 1)
                    e = jnp.where(kp <= qp, e, 0.0)
                ds = (e * (dps[h] - delta[h : h + 1, qa])).astype(bf)
                dv[h, ka, :] += dot(e.astype(bf), do[h, qa, :])
                dk[h, ka, :] += dot(ds, q[h, qa, :])
                dqt[h * HD : (h + 1) * HD, qa] += dot(head(kt, h, ka), ds)

        r = BQ // BK

        def rect(qb, kb):
            def one(n, _):
                q0 = pl.multiple_of(qb * BQ + lax.div(n, r) * BK, BK)
                k0 = pl.multiple_of(kb * BQ + lax.rem(n, r) * BK, BK)
                tile(q0, k0, False)
                return 0

            lax.fori_loop(0, r * r, one, 0)

        def triangle(t):
            def one(n, _):
                at = pl.multiple_of(t * BQ + n * BK, BK)
                tile(at, at, True)

                def below(j, _):
                    tile(at, pl.multiple_of(t * BQ + j * BK, BK), False)
                    return 0

                lax.fori_loop(0, n, below, 0)
                return 0

            lax.fori_loop(0, r, one, 0)

        def fetch(t, slot):
            b = t * 2 + ((other, c)[slot])
            return (
                pltpu.make_async_copy(n1.at[b], nx.at[slot], nsem.at[2 * slot]),
                pltpu.make_async_copy(x_all.at[b], xx.at[slot], nsem.at[2 * slot + 1]),
            )

        def fetch_both(t):
            for slot in range(2):
                for copy in fetch(t, slot):
                    copy.start()

        def prepare(t, slot):
            half = (other, c)[slot]
            at = pl.ds(pl.multiple_of((t * 2 + half) * T, T), T)
            dqs = dqt[:, at].astype(bf)
            dqf = dqs.astype(f32)
            gs_[...] += jnp.sum(dqf * qt[:, at].astype(f32), axis=1, keepdims=True)
            fm[:C, :] = (dqf * sc[...]).astype(bf)
            for h in range(nh):
                fm[C + h * HD : C + (h + 1) * HD, :] = jnp.transpose(dk[h, at, :]).astype(bf)
                fm[2 * C + h * HD : 2 * C + (h + 1) * HD, :] = jnp.transpose(dv[h, at, :]).astype(bf)
            tm[slot] = jnp.transpose(fm[...])
            for copy in fetch(t, slot):
                copy.wait()

        def weight_part(slot, a):
            dwt[:, a] += dot(fm[...], nx[slot, :, a])

        def finish(t, slot, dst):
            prepare(t, slot)
            inverse(slot)

            def column(n, _):
                a = pl.ds(pl.multiple_of(n * wide, wide), wide)
                back_part(slot, a, dst)
                weight_part(slot, a)
                return 0

            lax.fori_loop(0, D // wide, column, 0)

        def finish_weights(t, slot):
            prepare(t, slot)

            def column(n, _):
                weight_part(slot, pl.ds(pl.multiple_of(n * wide, wide), wide))
                return 0

            lax.fori_loop(0, D // wide, column, 0)

        def flash(i, t):
            fetch_both(t)

            def pair(m, _):
                u = xor(p, m, P_)
                rect(jnp.maximum(t, u), jnp.minimum(t, u))
                return 0

            lax.fori_loop(0, i, pair, 0)
            triangle(t)

        def advance(i, t):
            @pl.when(i == 1)
            def _():
                plane_sums()

            flash(i, t)
            if square:

                @pl.when(i == 3)
                def _():
                    join_g(2)
                    join_g(1)

            @pl.when(i < P_ - 1)
            def _():
                over(i + 1).wait_send()

            finish(t, 0, mb)
            over(i).start()
            finish(t, 1, own)
            over(i).wait_recv()
            combine(i)
            if not square:
                out_b(i, t).start()
                return

            @pl.when(i == 3)
            def _():
                relay_b(1).start()
                relay_b(2).start()

            @pl.when(i == 2)
            def _():
                join_b(2)

            @pl.when(i == 1)
            def _():
                join_b(1)

        def stage(n, _):
            i = P_ - 1 - n
            advance(i, xor(p, i, P_))
            return 0

        lax.fori_loop(0, P_ - 1, stage, 0)
        flash(0, p)
        finish_weights(p, 0)
        finish_weights(p, 1)


    V = pltpu.VMEM
    pl.run_scoped(
        attention,
        V((nh, L, HD), bf),
        V((nh, L), f32),
        V((C, L), f32),
        V((nh, L, HD), f32),
        V((nh, L, HD), f32),
    )

    def closing(dw, up, qm, qs_, go_, vo):
        dw[...] = jnp.transpose(dwt[...])

        bunch = 8 // math.gcd(R, 8)

        def piece(n, _):
            part = dw[pl.ds(pl.multiple_of(n * (bunch * R), 8), bunch * R), :]
            for j in range(bunch):
                to = n * bunch + j
                qm[lax.div(to, F), lax.rem(to, F)] = part[j * R : (j + 1) * R].astype(bf)
            return 0

        lax.fori_loop(0, S * F // bunch, piece, 0)
        for i in range(1, F):
            go(remote(qm.at[:, deep(i)], qi.at[i], qsend, qrecv, i, (s, deep(i))))
        up_load = pltpu.make_async_copy(dx2, up, local.at[0])
        up_load.start()
        over(1).wait_send()
        finish_back(0, mb)
        over(0).start()
        finish_back(1, own)
        vi[0:1, :] = gf[...]
        vi[1:2, :] = jnp.zeros_like(gf)
        turned = jnp.transpose(jnp.broadcast_to(gs_[...], (C, 128)))
        vi[1:2, 0:C] = turned[0:1, :]
        for i in range(1, F):
            go(remote(vi, vz.at[i], vsend, vrecv, i, (s, deep(i))))
        x_load = pltpu.make_async_copy(x_all.at[s], xx.at[0], nsem.at[1])
        x_load.start()
        over(0).wait_recv()
        combine(0)
        total = vi[...]
        for i in range(1, F):
            remote(vi, vz.at[i], vsend, vrecv, i, mate).wait_recv()
            total = total + vz[i]
        vp[0] = total
        for i in range(1, S):
            go(remote(vp.at[0], vp.at[i], vsend, vrecv, F - 1 + i, (lax.rem(s + i, S), f)))
        for i in range(1, F):
            remote(qm.at[:, f], qi.at[i], qsend, qrecv, i, mate).wait_recv()

        def sum_q(n, _):
            part = qm[n, f].astype(f32)
            for i in range(1, F):
                part = part + qi[i, n].astype(f32)
            qs_[n] = part.astype(bf)
            return 0

        lax.fori_loop(0, S, sum_q, 0)
        keep = pltpu.make_async_copy(qs_.at[s], qo.at[s], local.at[1])
        keep.start()
        for i in range(1, S):
            to = lax.rem(s + i, S)
            go(remote(qs_.at[to], qo.at[s], qsend, qrecv, F - 1 + i, (to, f)))
        up_load.wait()
        x_load.wait()
        over(0).wait_send()
        used = (1, 2) if square else range(1, P_)
        for i in used:
            if square:
                direct_b(i, 0).wait_recv()
                direct_b(i, 1).wait_recv()
            else:
                out_b(i, chip(i)).wait_recv()

        def below(n, _):
            a = pl.ds(pl.multiple_of(n * rows, rows), rows)
            back = bi[0, a, :].astype(f32)
            for i in used:
                back = back + bp[i - 1, a, :].astype(f32)
            z = xx[0, a, :].astype(f32)
            r1 = lax.rsqrt(jnp.mean(z * z, axis=-1, keepdims=True) + eps_norm)
            e1 = back * g1[...]
            tilt = jnp.mean(e1 * z, axis=-1, keepdims=True)
            mb[a, :] = (up[a, :] + r1 * e1 - z * (r1 * r1 * r1 * tilt)).astype(bf)
            return 0

        lax.fori_loop(0, T // rows, below, 0)
        outs = [pltpu.make_async_copy(mb, in_out, local.at[0])]
        outs[0].start()
        for i in range(1, F):
            remote(ga.at[:, f], gz.at[i], gsend, grecv, ZG + i, mate).wait_recv()
        for a in range(NW):
            part = ga[a, f].astype(f32)
            for i in range(1, F):
                part = part + gz[i, a].astype(f32)
            go_[a] = part
        for a, ref in enumerate((o_proj, o_up, o_down)):
            outs.append(pltpu.make_async_copy(go_.at[a], ref, bload.at[a]))
            outs[-1].start()
        total = vp[0]
        for i in range(1, S):
            remote(vp.at[0], vp.at[i], vsend, vrecv, F - 1 + i, mate).wait_recv()
            total = total + vp[i]
        vo[...] = total
        outs.append(pltpu.make_async_copy(vo, vec_out, nsem.at[0]))
        outs[-1].start()
        for i in range(1, S):
            src = lax.rem(s + S - i, S)
            remote(qs_.at[0], qo.at[src], qsend, qrecv, F - 1 + i, mate).wait_recv()
        keep.wait()
        for a, ref in enumerate((o_q, o_k, o_v)):
            for src in range(S):
                part = qo[src, :, a * C : (a + 1) * C].astype(f32)
                go_[NW + a, :, src * C : (src + 1) * C] = part
            outs.append(pltpu.make_async_copy(go_.at[NW + a], ref, bload.at[NW + a]))
            outs[-1].start()
        for out in outs:
            out.wait()
        for copy in todo:
            copy.wait_send()
        for i in range(1, F):
            deep_g(i).wait_send()
        for i in used:
            if square:
                relay_g(i).wait_send()
                relay_b(i).wait_send()
                for half in range(2):
                    direct_g(i, half).wait_send()
                    direct_b(i, half).wait_send()
            else:
                out_g(i).wait_send()
                out_b(i, chip(i)).wait_send()

    pl.run_scoped(
        closing,
        V((D, 3 * C), f32),
        V((T, D), f32),
        V((S, F, R, 3 * C), bf),
        V((S, R, 3 * C), bf),
        V((NW + 3, R, D), f32),
        V((2, D), f32),
    )


def backward_all(S, F, nh, dm, qt, kt, q, k, v, ot, lse, n1, x_all, w, sc, g1, gi, dx2):
    T, D = x_all.shape[1], x_all.shape[2]
    C = nh * HD
    L = S * T
    P_ = S // 2
    NW, R = gi.shape[1], gi.shape[3]
    any_ = pl.BlockSpec(memory_space=pl.ANY)
    vm = pl.BlockSpec(memory_space=pltpu.VMEM)
    dma = pltpu.SemaphoreType.DMA
    shape = jax.ShapeDtypeStruct
    V = pltpu.VMEM
    return pl.pallas_call(
        functools.partial(backward_kernel, S, F, nh),
        out_shape=[
            shape((R, D), f32),
            shape((R, D), f32),
            shape((R, D), f32),
            shape((T, D), bf),
            shape((R, D), f32),
            shape((R, D), f32),
            shape((R, D), f32),
            shape((2, D), f32),
            shape((P_, NW, F, R, D), bf),
            shape((2, NW, F // 2, R, D), bf),
            shape((2, NW, F // 2, R, D), bf),
        ],
        in_specs=[any_] * 7 + [vm, any_, any_, vm, vm, vm, any_, any_],
        out_specs=[any_] * 11,
        scratch_shapes=[
            V((C, L), bf),
            V((C, L), bf),
            V((nh, L, HD), bf),
            V((nh, L, HD), bf),
            V((nh, L, HD), bf),
            V((C, L), bf),
            V((C, L), bf),
            V((3 * C, D), bf),
            V((3 * C, D), f32),
            V((3 * C, T), bf),
            V((2, T, 3 * C), bf),
            V((2, T, D), bf),
            V((2, T, D), bf),
            V((T, 1), f32),
            V((T, D), bf),
            V((T, D), bf),
            V((P_, T, D), bf),
            V((2 if P_ == 4 else P_ - 1, T, D), bf),
            V((2, T // 2, D), bf),
            V((NW, F, R, D), bf),
            V((NW, F, R, D), bf),
            V((F, NW, R, D), bf),
            V((F, S, R, 3 * C), bf),
            V((S, R, 3 * C), bf),
            V((2, D), f32),
            V((F, 2, D), f32),
            V((S, 2, D), f32),
            V((1, D), f32),
            V((C, 1), f32),
            dma((3,)),
            dma((4,)),
            dma((S,)),
            dma((6,)),
            dma((10 + 2 * P_ + F,)),
            dma((10 + 2 * P_ + F,)),
            dma((max(2 * P_, 10),)),
            dma((max(2 * P_, 10),)),
            dma((S + F,)),
            dma((S + F,)),
            dma((S + F,)),
            dma((S + F,)),
        ],
        compiler_params=pltpu.CompilerParams(
            collective_id=4, has_side_effects=True, vmem_limit_bytes=66_000_000
        ),
        name="backward",
    )(dm, qt, kt, q, k, v, ot, lse, n1, x_all, w, sc, g1, gi, dx2)


def body(
    inputs,
    w_query,
    w_key,
    w_value,
    w_proj,
    w_up,
    w_down,
    gain_first,
    gain_second,
    bias_up,
    bias_down,
    query_scale,
    cotangent,
):
    groups = lax.axis_size("seq")
    rows_of = lax.axis_size("fsdp")
    nh = H // groups
    cols = nh * HD
    both = ("seq", "fsdp")
    tokens, width = inputs.shape[1], inputs.shape[2]
    length = tokens * groups
    shard = w_query.shape[0]
    x_low = inputs.reshape(tokens, width)
    small = jnp.stack([gain_first, gain_second, bias_up, bias_down], 0)
    small = jnp.pad(small.astype(bf), ((0, 12), (0, 128 - shard)))
    x_all, qkv_w, small, weights = gather_all(
        groups, rows_of, x_low, small, w_query, w_key, w_value, w_proj, w_up, w_down
    )
    qkv_w = qkv_w.reshape(width, 3 * cols)
    small = small[:, :, :4, :shard].transpose(2, 0, 1, 3).reshape(4, width).astype(f32)
    scale_dims = jax.nn.softplus(query_scale) * log_two_inverse / math.sqrt(HD)
    scale_cols = jnp.tile(scale_dims, nh)
    normed, qt, kt, q, k, v, ot, lse, mixed, weights = forward_all(
        groups, rows_of, nh, x_all, qkv_w, small[:1], scale_cols[:, None], weights
    )
    result, grad_middle, dm, pairs, vectors = middle_all(
        groups,
        rows_of,
        nh,
        mixed,
        x_low,
        cotangent.reshape(tokens, width),
        weights.reshape(3, width, width),
        small,
    )
    (
        grad_proj,
        grad_up,
        grad_down,
        grad_inputs,
        grad_query,
        grad_key,
        grad_value,
        late,
        *unused,
    ) = backward_all(
        groups,
        rows_of,
        nh,
        dm,
        qt,
        kt,
        q,
        k,
        v,
        ot,
        lse,
        normed,
        x_all,
        qkv_w,
        scale_cols[:, None],
        small[:1],
        pairs.reshape(groups // 2, 3, rows_of, shard, width),
        grad_middle,
    )
    at = (lax.axis_index("seq") * rows_of + lax.axis_index("fsdp")) * shard
    vectors = jnp.concatenate([late[:1], vectors[1:4]], 0)
    mine = lax.dynamic_slice_in_dim(vectors, at, shard, 1)
    scale_total = jnp.sum(late[1, :cols].reshape(nh, HD), axis=0) / scale_dims
    grad_scale = scale_total * jax.nn.sigmoid(query_scale) * log_two_inverse / math.sqrt(HD)
    return (
        result.reshape(inputs.shape),
        grad_inputs.reshape(inputs.shape),
        grad_query,
        grad_key,
        grad_value,
        grad_proj,
        grad_up,
        grad_down,
        mine[0],
        mine[1],
        mine[2],
        mine[3],
        grad_scale,
    )


def solution(mesh):
    return jax.shard_map(
        body,
        mesh=mesh,
        in_specs=(
            P("fsdp", "seq", None),
            P(("seq", "fsdp"), None),
            P(("seq", "fsdp"), None),
            P(("seq", "fsdp"), None),
            P(("seq", "fsdp"), None),
            P(("seq", "fsdp"), None),
            P(("seq", "fsdp"), None),
            P(("seq", "fsdp")),
            P(("seq", "fsdp")),
            P(("seq", "fsdp")),
            P(("seq", "fsdp")),
            P(),
            P("fsdp", "seq", None),
        ),
        out_specs=(
            P("fsdp", "seq", None),
            P("fsdp", "seq", None),
            P(("seq", "fsdp"), None),
            P(("seq", "fsdp"), None),
            P(("seq", "fsdp"), None),
            P(("seq", "fsdp"), None),
            P(("seq", "fsdp"), None),
            P(("seq", "fsdp"), None),
            P(("seq", "fsdp")),
            P(("seq", "fsdp")),
            P(("seq", "fsdp")),
            P(("seq", "fsdp")),
            P(),
        ),
        check_vma=False,
    )
```

```python
import functools
import math

import jax
import jax.numpy as jnp
from jax import lax
from jax.experimental import pallas as pl
from jax.experimental.pallas import tpu as pltpu
from jax.sharding import PartitionSpec as P

H = 16
HD = 80
eps_norm = 1e-06
log_two_inverse = 1.442695
bf = jnp.bfloat16
f32 = jnp.float32
NEG = -1e30


def dot(a,b,ca=1,cb=0):
    return lax.dot_general(a,b,(((ca,),(cb,)),((),())),preferred_element_type=f32)


MESH = pl.DeviceIdType.MESH


def spots():
    s, f = lax.axis_index("seq"), lax.axis_index("fsdp")
    return s, f, s // 2, lax.rem(s, 2)


def greet(S, F):
    s, f, _, _ = spots()
    barrier = pltpu.get_barrier_semaphore()
    for i in range(1, S):
        pl.semaphore_signal(barrier, inc=1, device_id=(lax.rem(s + i, S), f), device_id_type=MESH)
    for i in range(1, F):
        pl.semaphore_signal(barrier, inc=1, device_id=(s, lax.rem(f + i, F)), device_id_type=MESH)
    pl.semaphore_wait(barrier, S + F - 2)


def remote(src, dst, sends, recvs, n, to):
    return pltpu.make_async_remote_copy(
        src_ref=src,
        dst_ref=dst,
        send_sem=sends.at[n],
        recv_sem=recvs.at[n],
        device_id=to,
        device_id_type=MESH,
    )


def gather_kernel(S, F, x, sm, w_q, w_k, w_v, w_o, w_1, w_2, x_all, wq_all, sm_all, wm_all, xv, qv, sv, mv, local,
                  xs, xr, qs, qr, ss, sr, ms, mr):
    s, f, p, c = spots()
    P_ = S // 2
    other = 1 - c
    loads = [
        pltpu.make_async_copy(sm, sv, local.at[0]),
        pltpu.make_async_copy(x, xv, local.at[2]),
    ]
    for load in loads:
        load.start()
    greet(S, F)
    mate = (p * 2 + other, f)
    todo = []

    def go(copy):
        copy.start()
        todo.append(copy)

    def chip(i):
        return lax.rem(p + i, P_) * 2 + c

    def back(i):
        return lax.rem(p + P_ - i, P_) * 2 + c

    def near_chip(i):
        return flip_bits(p, i) * 2 + c

    H_ = x.shape[0] // 2

    def deep(i):
        return lax.rem(f + i, F)

    def behind(i):
        return lax.rem(f + F - i, F)

    loads[0].wait()
    keep0 = pltpu.make_async_copy(sv, sm_all.at[s, f], local.at[0])
    keep0.start()
    for i in range(1, F):
        go(remote(sv, sm_all.at[s, f], ss, sr, i, (s, deep(i))))
    C = qv.shape[2] // 3
    for n, w in enumerate((w_q, w_k, w_v)):
        for to in range(S):
            qv[to, :, n * C : (n + 1) * C] = w[:, to * C : (to + 1) * C].astype(bf)
    keep1 = pltpu.make_async_copy(qv.at[s], wq_all.at[s, f], local.at[1])
    keep1.start()
    for i in range(1, S):
        to = lax.rem(s + i, S)
        go(remote(qv.at[to], wq_all.at[s, f], qs, qr, i, (to, f)))
    loads[1].wait()
    keep2 = pltpu.make_async_copy(xv, x_all.at[s], local.at[2])
    keep2.start()
    if P_ == 4:
        for first in range(2):
            for i in (1, 2):
                half = first if i == 1 else 1 - first
                part = pl.ds(half * H_, H_)
                go(remote(xv.at[part], x_all.at[s, part], xs, xr, 2 * i + half, (near_chip(i), f)))
    else:
        for i in range(1, P_):
            go(remote(xv, x_all.at[s], xs, xr, i, (chip(i), f)))
    go(remote(xv, x_all.at[s], xs, xr, 0, mate))
    for n, w in enumerate((w_o, w_1, w_2)):
        mv[n] = w[...].astype(bf)
    keep3 = pltpu.make_async_copy(mv, wm_all.at[:, f], local.at[3])
    keep3.start()
    for i in range(1, F):
        go(remote(mv, wm_all.at[:, f], ms, mr, i, (s, deep(i))))
    for i in range(1, F):
        g = behind(i)
        remote(sv, sm_all.at[s, g], ss, sr, i, mate).wait_recv()
    keep0.wait()
    for i in range(1, S):
        go(remote(sm_all.at[s], sm_all.at[s], ss, sr, F - 1 + i, (lax.rem(s + i, S), f)))
    for i in range(1, S):
        remote(qv.at[0], wq_all.at[lax.rem(s + S - i, S), f], qs, qr, i, mate).wait_recv()
    keep1.wait()
    for i in range(1, F):
        go(remote(wq_all.at[:, f], wq_all.at[:, f], qs, qr, S - 1 + i, (s, deep(i))))
    for i in range(1, F):
        remote(mv, wm_all.at[:, behind(i)], ms, mr, i, mate).wait_recv()
    keep3.wait()
    if P_ == 4:
        for i in (1, 2):
            half = i - 1
            part = pl.ds(half * H_, H_)
            src = near_chip(i)
            remote(xv.at[part], x_all.at[src, part], xs, xr, 2 * i + half, mate).wait_recv()
            blk = x_all.at[src, part]
            go(remote(blk, blk, xs, xr, 6 + half, (near_chip(3 - i), f)))
        for i in (1, 2):
            half = 2 - i
            part = pl.ds(half * H_, H_)
            src = near_chip(i)
            remote(xv.at[part], x_all.at[src, part], xs, xr, 2 * i + half, mate).wait_recv()
            go(remote(x_all.at[src], x_all.at[src], xs, xr, 8 + i, mate))
    for i in range(1, P_ if P_ != 4 else 1):
        src = back(i)
        remote(xv, x_all.at[src], xs, xr, i, mate).wait_recv()
        go(remote(x_all.at[src], x_all.at[src], xs, xr, P_ - 1 + i, mate))
    for i in range(1, S):
        src = lax.rem(s + S - i, S)
        remote(sm_all.at[src], sm_all.at[src], ss, sr, F - 1 + i, mate).wait_recv()
    for i in range(1, F):
        g = behind(i)
        remote(wq_all.at[:, g], wq_all.at[:, g], qs, qr, S - 1 + i, mate).wait_recv()
    near = p * 2 + other
    remote(xv, x_all.at[near], xs, xr, 0, mate).wait_recv()
    if P_ == 4:
        for half in range(2):
            part = pl.ds(half * H_, H_)
            blk = x_all.at[near_chip(3), part]
            remote(blk, blk, xs, xr, 6 + half, mate).wait_recv()
            go(remote(blk, blk, xs, xr, 11 + half, mate))
        for i in (1, 2):
            blk = x_all.at[flip_bits(p, i) * 2 + other]
            remote(blk, blk, xs, xr, 8 + i, mate).wait_recv()
        for half in range(2):
            blk = x_all.at[flip_bits(p, 3) * 2 + other, pl.ds(half * H_, H_)]
            remote(blk, blk, xs, xr, 11 + half, mate).wait_recv()
    else:
        for i in range(1, P_):
            src = lax.rem(p + P_ - i, P_) * 2 + other
            remote(xv, x_all.at[src], xs, xr, P_ - 1 + i, mate).wait_recv()
    keep2.wait()
    for copy in todo:
        copy.wait_send()


def gather_all(S, F, x, sm, *weights):
    R, D = weights[0].shape
    C3 = 3 * D // S
    vm = pl.BlockSpec(memory_space=pltpu.VMEM)
    any_ = pl.BlockSpec(memory_space=pl.ANY)
    shapes = [
        (S,) + x.shape,
        (S, F, R, C3),
        (S, F) + sm.shape,
        (3, F, R, D),
    ]
    P_ = S // 2
    dma = pltpu.SemaphoreType.DMA
    counts = [max(2 * P_ - 1, 12), S + F - 1, F + S - 1, F]
    sems = []
    for n in counts:
        sems += [dma((n + 1,)), dma((n + 1,))]
    return pl.pallas_call(
        functools.partial(gather_kernel, S, F),
        out_shape=[
            jax.ShapeDtypeStruct(sh, bf) for sh in shapes
        ],
        in_specs=[any_] * 2 + [vm] * 6,
        out_specs=[any_] * 4,
        scratch_shapes=[
            pltpu.VMEM(x.shape, x.dtype),
            pltpu.VMEM((S, R, C3), bf),
            pltpu.VMEM(sm.shape, sm.dtype),
            pltpu.VMEM((3, R, D), bf),
            dma((4,)),
        ]
        + sems,
        compiler_params=pltpu.CompilerParams(collective_id=1, has_side_effects=True),
        name="gather",
    )(x, sm, *weights)


def xor(a, b, n):
    out, bit = 0, 1
    while bit < n:
        both = lax.rem(lax.div(a, bit), 2) + lax.rem(lax.div(b, bit), 2)
        out = out + bit * lax.rem(both, 2)
        bit *= 2
    return out


def flip_bits(p, i):
    out, bit = p, 1
    while bit <= i:
        if i & bit:
            out = out + bit - 2 * bit * lax.rem(lax.div(p, bit), 2)
        bit *= 2
    return out


def forward_kernel(S, F, nh, x_all, w, g1, sc, wz, n1, qt_o, kt_o, qn_o, kk_o, vn_o, ot, lse,
                   mixed, wm, qt, kt, qn, kk, vn, wt, vt, xb, nb, wv, inx, outn, local, late, osend, orecv, wsend, wrecv):
    s, f, p, c = spots()
    P_ = S // 2
    T, D = x_all.shape[1], x_all.shape[2]
    C = nh * HD
    L = S * T
    BQ = 2 * T
    BK = min(512, BQ)
    other = 1 - c
    mate = (p * 2 + other, f)
    load = pltpu.make_async_copy(wz, wv, local.at[0])
    load.start()

    def fetch(b):
        return pltpu.make_async_copy(x_all.at[b], xb.at[lax.rem(b, 2)], inx.at[lax.rem(b, 2)])

    def store(b):
        return pltpu.make_async_copy(nb.at[lax.rem(b, 2)], n1.at[b], outn.at[lax.rem(b, 2)])

    fetch(0).start()
    greet(S, F)
    load.wait()
    keep = pltpu.make_async_copy(wv, wm.at[:, s], local.at[0])
    keep.start()

    zero = s - s
    chips = [flip_bits(p, i) for i in range(P_)]

    def num(n):
        return zero + n

    def spread(i):
        return remote(wv, wm.at[:, s], wsend, wrecv, i, (xor(p, i, P_) * 2 + c, f))

    def forward(i):
        src = xor(p, i, P_) * 2 + c
        n = (7 if P_ == 4 else P_) + i
        return remote(wm.at[:, src], wm.at[:, src], wsend, wrecv, n, mate)

    def part_of(src, half):
        return wm.at[:, src, pl.ds(num(half * (F // 2)), F // 2)]

    def direct(i, half):
        src = wv.at[:, pl.ds(half * (F // 2), F // 2)]
        to = (flip_bits(p, i) * 2 + c, f)
        return remote(src, part_of(s, half), wsend, wrecv, 2 * i + half, to)

    def arrived(i, half):
        blk = part_of(chips[i] * 2 + c, half)
        remote(blk, blk, wsend, wrecv, num(2 * i + half), mate).wait_recv()

    def relay(i):
        blk = part_of(flip_bits(p, i) * 2 + c, i - 1)
        return remote(blk, blk, wsend, wrecv, 5 + i, (flip_bits(p, 3 - i) * 2 + c, f))

    def relayed(half):
        blk = part_of(chips[3] * 2 + c, half)
        return remote(blk, blk, wsend, wrecv, num(6 + half), mate)

    def corner(half, core):
        blk = part_of(chips[3] * 2 + core, half)
        return remote(blk, blk, wsend, wrecv, num(10 + half), mate)

    square = P_ == 4
    if square:
        for first in range(2):
            for i in (1, 2):
                direct(i, first if i == 1 else 1 - first).start()
    else:
        for i in range(1, P_):
            spread(P_ - i).start()
    near = remote(wv, wm.at[:, s], wsend, wrecv, 0, mate)
    near.start()
    wt[...] = jnp.transpose(w[...])

    rows = 64

    def project(b, _):
        slot = lax.rem(b, 2)
        fetch(b).wait()

        @pl.when(b + 1 < S)
        def _():
            fetch(b + 1).start()

        @pl.when(b >= 2)
        def _():
            store(b - 2).wait()

        def norm(k, _):
            at = pl.ds(pl.multiple_of(k * rows, rows), rows)
            v = xb[slot, at, :].astype(f32)
            r = lax.rsqrt(jnp.mean(v * v, axis=-1, keepdims=True) + eps_norm)
            nb[slot, at, :] = (v * r * g1[...]).astype(bf)
            return 0

        lax.fori_loop(0, T // rows, norm, 0)
        store(b).start()
        cols = pl.ds(pl.multiple_of(b * T, T), T)
        res = dot(wt[...], nb[slot], 1, 1)
        qt[:, cols] = (res[:C] * sc[...]).astype(bf)
        kt[:, cols] = res[C : 2 * C].astype(bf)
        vt[:, cols] = res[2 * C :].astype(bf)
        for h in range(nh):
            part = slice(h * HD, (h + 1) * HD)
            qn[h, cols, :] = jnp.transpose(res[:C][part] * sc[part]).astype(bf)
            kk[h, cols, :] = jnp.transpose(res[C : 2 * C][part]).astype(bf)
            vn[h, cols, :] = jnp.transpose(res[2 * C :][part]).astype(bf)
        return 0

    lax.fori_loop(0, S, project, 0)
    if square:
        for i in (1, 2):
            arrived(i, i - 1)
            relay(i).start()
    store(S - 2).wait()
    store(S - 1).wait()
    kept = [
        pltpu.make_async_copy(src, dst, late.at[n])
        for n, (src, dst) in enumerate(
            ((qt, qt_o), (kt, kt_o), (qn, qn_o), (kk, kk_o), (vn, vn_o))
        )
    ]
    for copy in kept:
        copy.start()

    r = BQ // BK

    def attend(t):
        first = pl.multiple_of(t * BQ, BQ)
        q = [qt[h * HD : (h + 1) * HD, pl.ds(first, BQ)] for h in range(nh)]

        def step(j, carry, diag=None):
            at = pl.ds(pl.multiple_of(j * BK, BK), BK)
            scores = [dot(kk[h, at, :], q[h]) for h in range(nh)]
            out = []
            for h in range(nh):
                m, l, acc = carry[h]
                sh = scores[h]
                if diag is not None:
                    kp = lax.broadcasted_iota(jnp.int32, sh.shape, 0) + diag * BK
                    qp = lax.broadcasted_iota(jnp.int32, sh.shape, 1)
                    sh = jnp.where(kp <= qp, sh, NEG)
                mn = jnp.maximum(m, jnp.max(sh, axis=0, keepdims=True))
                a = jnp.exp(m - mn)
                e = jnp.exp(sh - mn)
                l = l * a + jnp.sum(e, axis=0, keepdims=True)
                acc = acc * a + dot(vt[h * HD : (h + 1) * HD, at], e.astype(bf))
                out.append((mn, l, acc))
            return tuple(out)

        carry = tuple(
            (jnp.full((1, BQ), NEG, f32), jnp.zeros((1, BQ), f32), jnp.zeros((HD, BQ), f32))
            for _ in range(nh)
        )
        carry = lax.fori_loop(0, t * r, step, carry)
        for d in range(r):
            carry = step(t * r + d, carry, d)
        for h in range(nh):
            m, l, acc = carry[h]
            ot[h * HD : (h + 1) * HD, pl.ds(first, BQ)] = (acc / l).astype(bf)
            lse[h : h + 1, pl.ds(first, BQ)] = m + jnp.log(l)

    def to_owner(src, n, i, to):
        return pltpu.make_async_remote_copy(
            src_ref=src,
            dst_ref=mixed.at[s],
            send_sem=osend.at[n],
            recv_sem=orecv.at[2 * i + c],
            device_id=to,
            device_id_type=MESH,
        )

    def send(i, half):
        t = xor(p, i, P_)
        src = ot.at[:, pl.ds(pl.multiple_of(t * BQ + half * T, T), T)]
        return to_owner(src, 2 * i + half, i, (t * 2 + half, f))

    def turn(n, _):
        i = P_ - 1 - n
        attend(xor(p, i, P_))
        send(i, 0).start()
        send(i, 1).start()
        if not square:
            spread(i).wait_recv()
            forward(i).start()
            return 0

        @pl.when(i == 3)
        def _():
            arrived(2, 0)
            forward(num(2)).start()

        @pl.when(i == 2)
        def _():
            arrived(1, 1)
            forward(num(1)).start()

        @pl.when(i == 1)
        def _():
            for half in range(2):
                relayed(half).wait_recv()
                corner(half, c).start()

        return 0

    lax.fori_loop(0, P_ - 1, turn, 0)
    attend(p)
    mine = ot.at[:, pl.ds(pl.multiple_of(s * T, T), T)]
    theirs = ot.at[:, pl.ds(pl.multiple_of((p * 2 + other) * T, T), T)]
    last = to_owner(theirs, 0, 0, mate)
    last.start()
    own = pltpu.make_async_copy(mine, mixed.at[s], local.at[1])
    own.start()
    def from_source(i, core):
        return pltpu.make_async_remote_copy(
            src_ref=mine,
            dst_ref=mixed.at[flip_bits(p, i) * 2 + core],
            send_sem=osend.at[0],
            recv_sem=orecv.at[2 * i + core],
            device_id=mate,
            device_id_type=MESH,
        )

    for i in range(1, P_):
        for core in range(2):
            from_source(i, core).wait_recv()
    from_source(0, other).wait_recv()
    last.wait_send()
    own.wait()
    keep.wait()
    for copy in kept:
        copy.wait()
    near.wait()
    if square:
        for i in (1, 2):
            forward(i).wait()
            relay(i).wait_send()
            for half in range(2):
                direct(i, half).wait_send()
        for half in range(2):
            corner(half, c).wait_send()
            corner(half, other).wait_recv()
    for i in range(1, P_):
        if not square:
            forward(i).wait()
            spread(i).wait_send()
        send(i, 0).wait_send()
        send(i, 1).wait_send()


def forward_all(S, F, nh, x_all, w, g1, sc, wz):
    T, D = x_all.shape[1], x_all.shape[2]
    C = nh * HD
    L = S * T
    P_ = S // 2
    any_ = pl.BlockSpec(memory_space=pl.ANY)
    vm = pl.BlockSpec(memory_space=pltpu.VMEM)
    dma = pltpu.SemaphoreType.DMA
    shape = jax.ShapeDtypeStruct
    NW, R = wz.shape[0], wz.shape[2]
    V = pltpu.VMEM
    return pl.pallas_call(
        functools.partial(forward_kernel, S, F, nh),
        out_shape=[
            shape((S, T, D), bf),
            shape((C, L), bf),
            shape((C, L), bf),
            shape((nh, L, HD), bf),
            shape((nh, L, HD), bf),
            shape((nh, L, HD), bf),
            shape((C, L), bf),
            shape((nh, L), f32),
            shape((S, C, T), bf),
            shape((NW, S, F, R, D), bf),
        ],
        in_specs=[any_, vm, vm, vm, any_],
        out_specs=[any_] * 6 + [vm] * 2 + [any_, any_],
        scratch_shapes=[
            V((C, L), bf),
            V((C, L), bf),
            V((nh, L, HD), bf),
            V((nh, L, HD), bf),
            V((nh, L, HD), bf),
            V((3 * C, D), bf),
            V((C, L), bf),
            V((2, T, D), bf),
            V((2, T, D), bf),
            V((NW, F, R, D), bf),
            dma((2,)),
            dma((2,)),
            dma((2,)),
            dma((5,)),
            dma((2 * P_,)),
            dma((2 * P_,)),
            dma((max(2 * P_, 12),)),
            dma((max(2 * P_, 12),)),
        ],
        compiler_params=pltpu.CompilerParams(
            collective_id=3, has_side_effects=True, vmem_limit_bytes=60 << 20
        ),
        name="forward",
    )(x_all, w, g1, sc, wz)


def middle_kernel(S, F, nh, mixed, x, ct, wm, small, out, dx2, dm, gi, vec,
                  mx, lt, xv, cv, wv, x2, n2, dn, ab, ub, eb, r2, sb, rb, ob, dov, et, rv, vz, vp, local, wsem,
                  dsend, drecv, gsend, grecv, vsend, vrecv):
    s, f, p, c = spots()
    P_ = S // 2
    T, D = x.shape
    C = nh * HD
    NW = wm.shape[0]
    G = D // S
    other = 1 - c
    mate = (p * 2 + other, f)
    wide = 256 if D % 256 == 0 else D
    rows = 64
    loads = [
        pltpu.make_async_copy(mixed, mx, local.at[0]),
        pltpu.make_async_copy(x, xv, local.at[1]),
        pltpu.make_async_copy(ct, cv, local.at[2]),
    ]
    loads += [pltpu.make_async_copy(wm.at[n], wv.at[n], wsem.at[n]) for n in range(NW)]
    for load in loads:
        load.start()
    greet(S, F)
    g2, b1, b2 = small[1:2, :], small[2:3, :], small[3:4, :]

    def by_core(n, tall):
        for t in range(P_):
            for core in range(2):
                at = (t * 2 + core) * G
                lt[n, core, t * G : (t + 1) * G, :] = tall[at : at + G]

    def chunk(n):
        return pl.ds(pl.multiple_of(n * wide, wide), wide)

    def over(n, body):
        def one(k, _):
            body(k)
            return 0

        lax.fori_loop(0, n, one, 0)

    def lines(n):
        return pl.ds(pl.multiple_of(n * rows, rows), rows)

    loads[0].wait()
    tall = mx[...].reshape(D, T)
    by_core(0, tall)
    ub[...] = jnp.transpose(tall)
    loads[1].wait()
    loads[2].wait()
    loads[3].wait()

    def attend_out(n):
        at = chunk(n)
        x2[:, at] = xv[:, at].astype(f32) + dot(ub[...], wv[0, :, at])

    over(D // wide, attend_out)

    def norm(n):
        at = lines(n)
        z = x2[at, :]
        r = lax.rsqrt(jnp.mean(z * z, axis=-1, keepdims=True) + eps_norm)
        r2[at, :] = r
        n2[at, :] = (z * r * g2).astype(bf)

    over(T // rows, norm)
    loads[4].wait()
    loads[5].wait()
    rv[...] = jnp.zeros_like(rv)

    def hidden(n):
        at = chunk(n)
        u = dot(n2[...], wv[1, :, at]) + small[2:3, at]
        gate = 1 / (1 + jnp.exp(-u))
        ab[:, at] = (u * gate).astype(bf)
        ga = dot(cv[...], wv[2, at, :], 1, 1)
        du = ga * (gate * (1 + u * (1 - gate)))
        rv[2:3, at] = jnp.sum(du, axis=0, keepdims=True)
        ub[:, at] = du.astype(bf)
        rv[3:4, at] = jnp.sum(cv[:, at].astype(f32), axis=0, keepdims=True)

    over(D // wide, hidden)

    def up_back(n):
        at = chunk(n)
        dn[:, at] = dot(ub[...], wv[1, at, :], 1, 1)

    over(D // wide, up_back)

    def second(n):
        at = lines(n)
        z, r, d = x2[at, :], r2[at, :], dn[at, :]
        e = d * g2
        tilt = jnp.mean(e * z, axis=-1, keepdims=True)
        v = cv[at, :].astype(f32) + r * e - z * (r * r * r * tilt)
        rv[1:2, :] += jnp.sum(d * z * r, axis=0, keepdims=True)
        dn[at, :] = v
        eb[at, :] = v.astype(bf)

    over(T // rows, second)
    keep = pltpu.make_async_copy(dn, dx2, local.at[0])
    keep.start()

    def vec_z(i):
        return remote(rv, vz.at[i], vsend, vrecv, i, (s, lax.rem(f + i, F)))

    def vec_s(i):
        return remote(vp.at[0], vp.at[i], vsend, vrecv, F - 1 + i, (lax.rem(s + i, S), f))

    for i in range(1, F):
        vec_z(i).start()

    def head_out(i, to):
        return remote(dov.at[i], dm.at[s], dsend, drecv, i, (to, f))

    et[...] = jnp.transpose(eb[...])

    def heads(i, _):
        to = lax.rem(s + i, S)
        rows_of = pl.ds(pl.multiple_of(to * C, C), C)
        dov[i] = dot(wv[0, rows_of, :], et[...]).astype(bf)

        head_out(i, to).start()
        return 0

    lax.fori_loop(1, S, heads, 0)
    mine = pl.ds(pl.multiple_of(s * C, C), C)
    dov[0] = dot(wv[0, mine, :], et[...]).astype(bf)
    home = pltpu.make_async_copy(dov.at[0], dm.at[s], local.at[1])
    home.start()

    by_core(1, jnp.transpose(n2[...]))
    by_core(2, jnp.transpose(ab[...]))
    right = [eb, ub, cv]

    def pass_on(n):
        return remote(sb.at[n], rb.at[n], gsend, grecv, n, mate)

    for n in range(NW):

        def send_side(k, n=n):
            at = chunk(k)
            sb[n, :, at] = dot(lt[n, other], right[n][:, at]).astype(bf)

        over(D // wide, send_side)
        pass_on(n).start()

    part = rv[...]
    for i in range(1, F):
        vec_z(i).wait_recv()
        part = part + vz[i]
    vp[0] = part
    for i in range(1, S):
        vec_s(i).start()

    def top(n):
        at = chunk(n)
        y = x2[:, at] + dot(ab[...], wv[2, :, at]) + small[3:4, at]
        xv[:, at] = y.astype(bf)

    over(D // wide, top)
    done = pltpu.make_async_copy(xv, out, local.at[2])
    done.start()
    for n in range(NW):
        pass_on(n).wait_recv()

        def keep_side(k, n=n):
            at = chunk(k)
            both = dot(lt[n, c], right[n][:, at]) + rb[n, :, at].astype(f32)
            ob[n, :, at] = both.astype(bf)

        over(D // wide, keep_side)
    stores = []
    for i in range(P_):
        here = pl.ds(pl.multiple_of(flip_bits(p, i) * G, G), G)
        stores.append(pltpu.make_async_copy(ob.at[:, here], gi.at[i], wsem.at[i]))
        stores[-1].start()
    part = vp[0]
    for i in range(1, S):
        vec_s(i).wait_recv()
        part = part + vp[i]
    vec[...] = part
    for i in range(1, F):
        vec_z(i).wait_send()
    for i in range(1, S):
        vec_s(i).wait_send()
    for i in range(1, S):
        remote(dov.at[0], dm.at[lax.rem(s + S - i, S)], dsend, drecv, i, mate).wait_recv()
    for store in stores:
        store.wait()
    keep.wait()
    home.wait()
    done.wait()
    for i in range(1, S):
        head_out(i, lax.rem(s + i, S)).wait_send()
    for n in range(NW):
        pass_on(n).wait_send()


def middle_all(S, F, nh, mixed, x, ct, wm, small):
    T, D = x.shape
    C = nh * HD
    P_ = S // 2
    NW = wm.shape[0]
    G = D // S
    any_ = pl.BlockSpec(memory_space=pl.ANY)
    vm = pl.BlockSpec(memory_space=pltpu.VMEM)
    dma = pltpu.SemaphoreType.DMA
    shape = jax.ShapeDtypeStruct
    V = pltpu.VMEM
    return pl.pallas_call(
        functools.partial(middle_kernel, S, F, nh),
        out_shape=[
            shape((T, D), bf),
            shape((T, D), f32),
            shape((S, C, T), bf),
            shape((P_, NW, G, D), bf),
            shape((8, D), f32),
        ],
        in_specs=[any_, any_, any_, any_, vm],
        out_specs=[any_, any_, any_, any_, vm],
        scratch_shapes=[
            V((S, C, T), bf),
            V((NW, 2, P_ * G, T), bf),
            V((T, D), bf),
            V((T, D), bf),
            V((NW, D, D), bf),
            V((T, D), f32),
            V((T, D), bf),
            V((T, D), f32),
            V((T, D), bf),
            V((T, D), bf),
            V((T, D), bf),
            V((T, 1), f32),
            V((NW, P_ * G, D), bf),
            V((NW, P_ * G, D), bf),
            V((NW, P_ * G, D), bf),
            V((S, C, T), bf),
            V((D, T), bf),
            V((8, D), f32),
            V((F, 8, D), f32),
            V((S, 8, D), f32),
            dma((3,)),
            dma((max(NW, P_),)),
            dma((S,)),
            dma((S,)),
            dma((NW,)),
            dma((NW,)),
            dma((S + F,)),
            dma((S + F,)),
        ],
        compiler_params=pltpu.CompilerParams(
            collective_id=5, has_side_effects=True, vmem_limit_bytes=64_000_000
        ),
        name="middle",
    )(mixed, x, ct, wm, small)


def backward_kernel(S, F, nh, dm, qt_in, kt_in, q_in, k_in, v_in, ot_in, lse, n1, x_all, w, sc, g1,
                    gi, dx2,
                    o_proj, o_up, o_down, in_out, o_q, o_k, o_v, vec_out, gp, gr_, gj,
                    qt, kt, q, k, v, ot, dmt, wt, dwt, fm, tm, nx, xx, rr, mb, own, bi, bp, rl, ga, gb, gz, qi, qo,
                    vi, vz, vp, gf, gs_, local, nsem, bload, early,
                    gsend, grecv, bsend, brecv, qsend, qrecv, vsend, vrecv):
    s, f, p, c = spots()
    P_ = S // 2
    T, D = x_all.shape[1], x_all.shape[2]
    C = nh * HD
    L = S * T
    BQ = 2 * T
    BK = min(512, BQ)
    NW, R = gi.shape[1], gi.shape[3]
    other = 1 - c
    mate = (p * 2 + other, f)
    todo = []

    def go(copy):
        copy.start()
        todo.append(copy)

    chips = [flip_bits(p, i) for i in range(P_)]
    zero = s - s

    def num(n):
        return zero + n

    def chip(i):
        return chips[i]

    deeps = [lax.rem(f + i, F) for i in range(F)]

    def deep(i):
        return deeps[i]

    def head(ref, h, at):
        return ref[h * HD : (h + 1) * HD, at]

    loads = [
        pltpu.make_async_copy(dm.at[b], dmt.at[:, b * T : (b + 1) * T], bload.at[b])
        for b in range(S)
    ]
    pairs_in = ((qt_in, qt), (kt_in, kt), (q_in, q), (k_in, k), (v_in, v), (ot_in, ot))
    loads += [
        pltpu.make_async_copy(src, dst, early.at[n]) for n, (src, dst) in enumerate(pairs_in)
    ]
    for load in loads:
        load.start()
    greet(S, F)

    order = list(range(P_ - 1, -1, -1))
    wt[...] = jnp.transpose(w[...])
    dwt[...] = jnp.zeros_like(dwt)
    gf[...] = jnp.zeros_like(gf)
    gs_[...] = jnp.zeros_like(gs_)

    def slabs(body):
        def one(n, _):
            body(lax.div(n, F), lax.rem(n, F))
            return 0

        lax.fori_loop(0, NW * F, one, 0)

    square = P_ == 4
    ZG = 10 if square else 2 * P_
    FH, H_ = F // 2, T // 2

    def half_g(ref, half):
        return ref.at[:, pl.ds(num(half * FH), FH)]

    def direct_g(i, half):
        src, dst = half_g(gi.at[num(i)], half), half_g(gp.at[num(i)], half)
        if half == 2 - i:
            src = gj.at[num(half)]
        return remote(src, dst, gsend, grecv, num(2 + 2 * i + half), (chip(i) * 2 + c, f))

    def relay_g(i):
        src = half_g(gi.at[num(3)], i - 1)
        return remote(src, gr_.at[num(i - 1)], gsend, grecv, num(7 + i), (chip(i) * 2 + c, f))

    def join_g(i):
        half = 2 - i
        la = pltpu.make_async_copy(half_g(gi.at[num(i)], half), half_g(ga, 0), local.at[num(1)])
        la.start()
        relay_g(3 - i).wait_recv()
        lb = pltpu.make_async_copy(gr_.at[num(half)], half_g(gb, 0), local.at[num(2)])
        lb.start()
        la.wait()
        lb.wait()

        def add(z, _):
            for a in range(NW):
                w_ = num(a)
                ga[w_, z] = (ga[w_, z].astype(f32) + gb[w_, z].astype(f32)).astype(bf)
            return 0

        lax.fori_loop(0, FH, add, 0)
        st = pltpu.make_async_copy(half_g(ga, 0), gj.at[num(half)], local.at[num(1)])
        st.start()
        st.wait()
        direct_g(i, half).start()

    def out_g(i):
        return remote(gi.at[num(i)], gp.at[num(i)], gsend, grecv, num(P_ + i), (chip(i) * 2 + c, f))

    if square:
        relay_g(1).start()
        relay_g(2).start()
        direct_g(2, 1).start()
        direct_g(1, 0).start()
    else:
        for i in order[:-1]:
            out_g(i).start()

    for load in loads:
        load.wait()

    rows = 64
    wide = 256 if D % 256 == 0 else D

    def over(i):
        return remote(mb, bi.at[i], bsend, brecv, i, mate)

    def inverse(slot):
        def one(n, _):
            a = pl.ds(pl.multiple_of(n * rows, rows), rows)
            z = xx[slot, a, :].astype(f32)
            rr[a, :] = lax.rsqrt(jnp.mean(z * z, axis=-1, keepdims=True) + eps_norm)
            return 0

        lax.fori_loop(0, T // rows, one, 0)

    def back_part(slot, a, dst):
        back = dot(tm[slot], wt[:, a])
        dst[:, a] = back.astype(bf)
        hat = xx[slot, :, a].astype(f32) * rr[...]
        gf[:, a] += jnp.sum(back * hat, axis=0, keepdims=True)

    def finish_back(slot, dst):
        inverse(slot)

        def column(n, _):
            back_part(slot, pl.ds(pl.multiple_of(n * wide, wide), wide), dst)
            return 0

        lax.fori_loop(0, D // wide, column, 0)

    def combine(i):
        def one(n, _):
            a = pl.ds(pl.multiple_of(n * rows, rows), rows)
            bi[i, a, :] = (bi[i, a, :].astype(f32) + own[a, :].astype(f32)).astype(bf)
            return 0

        lax.fori_loop(0, T // rows, one, 0)

    def direct_b(i, half):
        part = pl.ds(pl.multiple_of(num(half * H_), H_), H_)
        src, dst = bi.at[num(i), part], bp.at[num(i - 1), part]
        return remote(src, dst, bsend, brecv, num(2 + 2 * i + half), (chip(i) * 2 + c, f))

    def relay_b(i):
        part = pl.ds(pl.multiple_of(num((i - 1) * H_), H_), H_)
        src = bi.at[num(3), part]
        return remote(src, rl.at[num(i - 1)], bsend, brecv, num(7 + i), (chip(i) * 2 + c, f))

    def join_b(i):
        half = 2 - i
        direct_b(i, 1 - half).start()
        relay_b(3 - i).wait_recv()
        few = min(rows, H_)

        def add(n, _):
            here = pl.ds(pl.multiple_of(half * H_ + n * few, few), few)
            there = pl.ds(pl.multiple_of(n * few, few), few)
            both = bi[num(i), here, :].astype(f32) + rl[num(half), there, :].astype(f32)
            bi[num(i), here, :] = both.astype(bf)
            return 0

        lax.fori_loop(0, H_ // few, add, 0)
        direct_b(i, half).start()

    def out_b(i, t):
        return pltpu.make_async_remote_copy(
            src_ref=bi.at[i],
            dst_ref=bp.at[i - 1],
            send_sem=bsend.at[P_ + i],
            recv_sem=brecv.at[P_ + i],
            device_id=(t * 2 + c, f),
            device_id_type=MESH,
        )

    def deep_g(i):
        src = ga.at[:, deep(i)]
        return remote(src, gz.at[num(i)], gsend, grecv, num(ZG + i), (s, deep(i)))

    def plane_sums():
        la = pltpu.make_async_copy(gi.at[num(0)], ga, local.at[num(1)])
        la.start()
        la.wait()
        for i in order[1:-1] if square else order[:-1]:
            if square:
                direct_g(i, 0).wait_recv()
                direct_g(i, 1).wait_recv()
            else:
                out_g(i).wait_recv()
            lb = pltpu.make_async_copy(gp.at[num(i)], gb, local.at[num(2)])
            lb.start()
            lb.wait()

            def more(z, _):
                for a in range(NW):
                    w_ = num(a)
                    ga[w_, z] = (ga[w_, z].astype(f32) + gb[w_, z].astype(f32)).astype(bf)
                return 0

            lax.fori_loop(0, F, more, 0)
        for i in range(1, F):
            deep_g(i).start()

    def attention(do, delta, dqt, dk, dv):
        dqt[...] = jnp.zeros_like(dqt)
        dk[...] = jnp.zeros_like(dk)
        dv[...] = jnp.zeros_like(dv)

        def turn(b, _):
            at = pl.ds(pl.multiple_of(b * T, T), T)
            for h in range(nh):
                do[h, at, :] = jnp.transpose(head(dmt, h, at))
                prod = head(dmt, h, at).astype(f32) * head(ot, h, at).astype(f32)
                delta[h : h + 1, at] = jnp.sum(prod, axis=0, keepdims=True)
            return 0

        lax.fori_loop(0, S, turn, 0)

        def tile(q0, k0, masked):
            qa = pl.ds(q0, BK)
            ka = pl.ds(k0, BK)
            scores = [dot(k[h, ka, :], head(qt, h, qa)) for h in range(nh)]
            dps = [dot(v[h, ka, :], head(dmt, h, qa)) for h in range(nh)]
            for h in range(nh):
                e = jnp.exp(scores[h] - lse[h : h + 1, qa])
                if masked:
                    kp = lax.broadcasted_iota(jnp.int32, e.shape, 0)
                    qp = lax.broadcasted_iota(jnp.int32, e.shape, 1)
                    e = jnp.where(kp <= qp, e, 0.0)
                ds = (e * (dps[h] - delta[h : h + 1, qa])).astype(bf)
                dv[h, ka, :] += dot(e.astype(bf), do[h, qa, :])
                dk[h, ka, :] += dot(ds, q[h, qa, :])
                dqt[h * HD : (h + 1) * HD, qa] += dot(head(kt, h, ka), ds)

        r = BQ // BK

        def rect(qb, kb):
            def one(n, _):
                q0 = pl.multiple_of(qb * BQ + lax.div(n, r) * BK, BK)
                k0 = pl.multiple_of(kb * BQ + lax.rem(n, r) * BK, BK)
                tile(q0, k0, False)
                return 0

            lax.fori_loop(0, r * r, one, 0)

        def triangle(t):
            def one(n, _):
                at = pl.multiple_of(t * BQ + n * BK, BK)
                tile(at, at, True)

                def below(j, _):
                    tile(at, pl.multiple_of(t * BQ + j * BK, BK), False)
                    return 0

                lax.fori_loop(0, n, below, 0)
                return 0

            lax.fori_loop(0, r, one, 0)

        def fetch(t, slot):
            b = t * 2 + ((other, c)[slot])
            return (
                pltpu.make_async_copy(n1.at[b], nx.at[slot], nsem.at[2 * slot]),
                pltpu.make_async_copy(x_all.at[b], xx.at[slot], nsem.at[2 * slot + 1]),
            )

        def fetch_both(t):
            for slot in range(2):
                for copy in fetch(t, slot):
                    copy.start()

        def prepare(t, slot):
            half = (other, c)[slot]
            at = pl.ds(pl.multiple_of((t * 2 + half) * T, T), T)
            dqs = dqt[:, at].astype(bf)
            dqf = dqs.astype(f32)
            gs_[...] += jnp.sum(dqf * qt[:, at].astype(f32), axis=1, keepdims=True)
            fm[:C, :] = (dqf * sc[...]).astype(bf)
            for h in range(nh):
                fm[C + h * HD : C + (h + 1) * HD, :] = jnp.transpose(dk[h, at, :]).astype(bf)
                fm[2 * C + h * HD : 2 * C + (h + 1) * HD, :] = jnp.transpose(dv[h, at, :]).astype(bf)
            tm[slot] = jnp.transpose(fm[...])
            for copy in fetch(t, slot):
                copy.wait()

        def weight_part(slot, a):
            dwt[:, a] += dot(fm[...], nx[slot, :, a])

        def finish(t, slot, dst):
            prepare(t, slot)
            inverse(slot)

            def column(n, _):
                a = pl.ds(pl.multiple_of(n * wide, wide), wide)
                back_part(slot, a, dst)
                weight_part(slot, a)
                return 0

            lax.fori_loop(0, D // wide, column, 0)

        def finish_weights(t, slot):
            prepare(t, slot)

            def column(n, _):
                weight_part(slot, pl.ds(pl.multiple_of(n * wide, wide), wide))
                return 0

            lax.fori_loop(0, D // wide, column, 0)

        def flash(i, t):
            fetch_both(t)

            def pair(m, _):
                u = xor(p, m, P_)
                rect(jnp.maximum(t, u), jnp.minimum(t, u))
                return 0

            lax.fori_loop(0, i, pair, 0)
            triangle(t)

        def advance(i, t):
            @pl.when(i == 1)
            def _():
                plane_sums()

            flash(i, t)
            if square:

                @pl.when(i == 3)
                def _():
                    join_g(2)
                    join_g(1)

            @pl.when(i < P_ - 1)
            def _():
                over(i + 1).wait_send()

            finish(t, 0, mb)
            over(i).start()
            finish(t, 1, own)
            over(i).wait_recv()
            combine(i)
            if not square:
                out_b(i, t).start()
                return

            @pl.when(i == 3)
            def _():
                relay_b(1).start()
                relay_b(2).start()

            @pl.when(i == 2)
            def _():
                join_b(2)

            @pl.when(i == 1)
            def _():
                join_b(1)

        def stage(n, _):
            i = P_ - 1 - n
            advance(i, xor(p, i, P_))
            return 0

        lax.fori_loop(0, P_ - 1, stage, 0)
        flash(0, p)
        finish_weights(p, 0)
        finish_weights(p, 1)


    V = pltpu.VMEM
    pl.run_scoped(
        attention,
        V((nh, L, HD), bf),
        V((nh, L), f32),
        V((C, L), f32),
        V((nh, L, HD), f32),
        V((nh, L, HD), f32),
    )

    def closing(dw, up, qm, qs_, go_, vo):
        dw[...] = jnp.transpose(dwt[...])

        bunch = 8 // math.gcd(R, 8)

        def piece(n, _):
            part = dw[pl.ds(pl.multiple_of(n * (bunch * R), 8), bunch * R), :]
            for j in range(bunch):
                to = n * bunch + j
                qm[lax.div(to, F), lax.rem(to, F)] = part[j * R : (j + 1) * R].astype(bf)
            return 0

        lax.fori_loop(0, S * F // bunch, piece, 0)
        for i in range(1, F):
            go(remote(qm.at[:, deep(i)], qi.at[i], qsend, qrecv, i, (s, deep(i))))
        up_load = pltpu.make_async_copy(dx2, up, local.at[0])
        up_load.start()
        over(1).wait_send()
        finish_back(0, mb)
        over(0).start()
        finish_back(1, own)
        vi[0:1, :] = gf[...]
        vi[1:2, :] = jnp.zeros_like(gf)
        turned = jnp.transpose(jnp.broadcast_to(gs_[...], (C, 128)))
        vi[1:2, 0:C] = turned[0:1, :]
        for i in range(1, F):
            go(remote(vi, vz.at[i], vsend, vrecv, i, (s, deep(i))))
        x_load = pltpu.make_async_copy(x_all.at[s], xx.at[0], nsem.at[1])
        x_load.start()
        over(0).wait_recv()
        combine(0)
        total = vi[...]
        for i in range(1, F):
            remote(vi, vz.at[i], vsend, vrecv, i, mate).wait_recv()
            total = total + vz[i]
        vp[0] = total
        for i in range(1, S):
            go(remote(vp.at[0], vp.at[i], vsend, vrecv, F - 1 + i, (lax.rem(s + i, S), f)))
        for i in range(1, F):
            remote(qm.at[:, f], qi.at[i], qsend, qrecv, i, mate).wait_recv()

        def sum_q(n, _):
            part = qm[n, f].astype(f32)
            for i in range(1, F):
                part = part + qi[i, n].astype(f32)
            qs_[n] = part.astype(bf)
            return 0

        lax.fori_loop(0, S, sum_q, 0)
        keep = pltpu.make_async_copy(qs_.at[s], qo.at[s], local.at[1])
        keep.start()
        for i in range(1, S):
            to = lax.rem(s + i, S)
            go(remote(qs_.at[to], qo.at[s], qsend, qrecv, F - 1 + i, (to, f)))
        up_load.wait()
        x_load.wait()
        over(0).wait_send()
        used = (1, 2) if square else range(1, P_)
        for i in used:
            if square:
                direct_b(i, 0).wait_recv()
                direct_b(i, 1).wait_recv()
            else:
                out_b(i, chip(i)).wait_recv()

        def below(n, _):
            a = pl.ds(pl.multiple_of(n * rows, rows), rows)
            back = bi[0, a, :].astype(f32)
            for i in used:
                back = back + bp[i - 1, a, :].astype(f32)
            z = xx[0, a, :].astype(f32)
            r1 = lax.rsqrt(jnp.mean(z * z, axis=-1, keepdims=True) + eps_norm)
            e1 = back * g1[...]
            tilt = jnp.mean(e1 * z, axis=-1, keepdims=True)
            mb[a, :] = (up[a, :] + r1 * e1 - z * (r1 * r1 * r1 * tilt)).astype(bf)
            return 0

        lax.fori_loop(0, T // rows, below, 0)
        outs = [pltpu.make_async_copy(mb, in_out, local.at[0])]
        outs[0].start()
        for i in range(1, F):
            remote(ga.at[:, f], gz.at[i], gsend, grecv, ZG + i, mate).wait_recv()
        for a in range(NW):
            part = ga[a, f].astype(f32)
            for i in range(1, F):
                part = part + gz[i, a].astype(f32)
            go_[a] = part
        for a, ref in enumerate((o_proj, o_up, o_down)):
            outs.append(pltpu.make_async_copy(go_.at[a], ref, bload.at[a]))
            outs[-1].start()
        total = vp[0]
        for i in range(1, S):
            remote(vp.at[0], vp.at[i], vsend, vrecv, F - 1 + i, mate).wait_recv()
            total = total + vp[i]
        vo[...] = total
        outs.append(pltpu.make_async_copy(vo, vec_out, nsem.at[0]))
        outs[-1].start()
        for i in range(1, S):
            src = lax.rem(s + S - i, S)
            remote(qs_.at[0], qo.at[src], qsend, qrecv, F - 1 + i, mate).wait_recv()
        keep.wait()
        for a, ref in enumerate((o_q, o_k, o_v)):
            for src in range(S):
                part = qo[src, :, a * C : (a + 1) * C].astype(f32)
                go_[NW + a, :, src * C : (src + 1) * C] = part
            outs.append(pltpu.make_async_copy(go_.at[NW + a], ref, bload.at[NW + a]))
            outs[-1].start()
        for out in outs:
            out.wait()
        for copy in todo:
            copy.wait_send()
        for i in range(1, F):
            deep_g(i).wait_send()
        for i in used:
            if square:
                relay_g(i).wait_send()
                relay_b(i).wait_send()
                for half in range(2):
                    direct_g(i, half).wait_send()
                    direct_b(i, half).wait_send()
            else:
                out_g(i).wait_send()
                out_b(i, chip(i)).wait_send()

    pl.run_scoped(
        closing,
        V((D, 3 * C), f32),
        V((T, D), f32),
        V((S, F, R, 3 * C), bf),
        V((S, R, 3 * C), bf),
        V((NW + 3, R, D), f32),
        V((2, D), f32),
    )


def backward_all(S, F, nh, dm, qt, kt, q, k, v, ot, lse, n1, x_all, w, sc, g1, gi, dx2):
    T, D = x_all.shape[1], x_all.shape[2]
    C = nh * HD
    L = S * T
    P_ = S // 2
    NW, R = gi.shape[1], gi.shape[3]
    any_ = pl.BlockSpec(memory_space=pl.ANY)
    vm = pl.BlockSpec(memory_space=pltpu.VMEM)
    dma = pltpu.SemaphoreType.DMA
    shape = jax.ShapeDtypeStruct
    V = pltpu.VMEM
    return pl.pallas_call(
        functools.partial(backward_kernel, S, F, nh),
        out_shape=[
            shape((R, D), f32),
            shape((R, D), f32),
            shape((R, D), f32),
            shape((T, D), bf),
            shape((R, D), f32),
            shape((R, D), f32),
            shape((R, D), f32),
            shape((2, D), f32),
            shape((P_, NW, F, R, D), bf),
            shape((2, NW, F // 2, R, D), bf),
            shape((2, NW, F // 2, R, D), bf),
        ],
        in_specs=[any_] * 7 + [vm, any_, any_, vm, vm, vm, any_, any_],
        out_specs=[any_] * 11,
        scratch_shapes=[
            V((C, L), bf),
            V((C, L), bf),
            V((nh, L, HD), bf),
            V((nh, L, HD), bf),
            V((nh, L, HD), bf),
            V((C, L), bf),
            V((C, L), bf),
            V((3 * C, D), bf),
            V((3 * C, D), f32),
            V((3 * C, T), bf),
            V((2, T, 3 * C), bf),
            V((2, T, D), bf),
            V((2, T, D), bf),
            V((T, 1), f32),
            V((T, D), bf),
            V((T, D), bf),
            V((P_, T, D), bf),
            V((2 if P_ == 4 else P_ - 1, T, D), bf),
            V((2, T // 2, D), bf),
            V((NW, F, R, D), bf),
            V((NW, F, R, D), bf),
            V((F, NW, R, D), bf),
            V((F, S, R, 3 * C), bf),
            V((S, R, 3 * C), bf),
            V((2, D), f32),
            V((F, 2, D), f32),
            V((S, 2, D), f32),
            V((1, D), f32),
            V((C, 1), f32),
            dma((3,)),
            dma((4,)),
            dma((S,)),
            dma((6,)),
            dma((10 + 2 * P_ + F,)),
            dma((10 + 2 * P_ + F,)),
            dma((max(2 * P_, 10),)),
            dma((max(2 * P_, 10),)),
            dma((S + F,)),
            dma((S + F,)),
            dma((S + F,)),
            dma((S + F,)),
        ],
        compiler_params=pltpu.CompilerParams(
            collective_id=4, has_side_effects=True, vmem_limit_bytes=66_000_000
        ),
        name="backward",
    )(dm, qt, kt, q, k, v, ot, lse, n1, x_all, w, sc, g1, gi, dx2)


def body(
    inputs,
    w_query,
    w_key,
    w_value,
    w_proj,
    w_up,
    w_down,
    gain_first,
    gain_second,
    bias_up,
    bias_down,
    query_scale,
    cotangent,
):
    groups = lax.axis_size("seq")
    rows_of = lax.axis_size("fsdp")
    nh = H // groups
    cols = nh * HD
    both = ("seq", "fsdp")
    tokens, width = inputs.shape[1], inputs.shape[2]
    length = tokens * groups
    shard = w_query.shape[0]
    x_low = inputs.reshape(tokens, width)
    small = jnp.stack([gain_first, gain_second, bias_up, bias_down], 0)
    small = jnp.pad(small.astype(bf), ((0, 12), (0, 128 - shard)))
    x_all, qkv_w, small, weights = gather_all(
        groups, rows_of, x_low, small, w_query, w_key, w_value, w_proj, w_up, w_down
    )
    qkv_w = qkv_w.reshape(width, 3 * cols)
    small = small[:, :, :4, :shard].transpose(2, 0, 1, 3).reshape(4, width).astype(f32)
    scale_dims = jax.nn.softplus(query_scale) * log_two_inverse / math.sqrt(HD)
    scale_cols = jnp.tile(scale_dims, nh)
    normed, qt, kt, q, k, v, ot, lse, mixed, weights = forward_all(
        groups, rows_of, nh, x_all, qkv_w, small[:1], scale_cols[:, None], weights
    )
    result, grad_middle, dm, pairs, vectors = middle_all(
        groups,
        rows_of,
        nh,
        mixed,
        x_low,
        cotangent.reshape(tokens, width),
        weights.reshape(3, width, width),
        small,
    )
    (
        grad_proj,
        grad_up,
        grad_down,
        grad_inputs,
        grad_query,
        grad_key,
        grad_value,
        late,
        *unused,
    ) = backward_all(
        groups,
        rows_of,
        nh,
        dm,
        qt,
        kt,
        q,
        k,
        v,
        ot,
        lse,
        normed,
        x_all,
        qkv_w,
        scale_cols[:, None],
        small[:1],
        pairs.reshape(groups // 2, 3, rows_of, shard, width),
        grad_middle,
    )
    at = (lax.axis_index("seq") * rows_of + lax.axis_index("fsdp")) * shard
    vectors = jnp.concatenate([late[:1], vectors[1:4]], 0)
    mine = lax.dynamic_slice_in_dim(vectors, at, shard, 1)
    scale_total = jnp.sum(late[1, :cols].reshape(nh, HD), axis=0) / scale_dims
    grad_scale = scale_total * jax.nn.sigmoid(query_scale) * log_two_inverse / math.sqrt(HD)
    return (
        result.reshape(inputs.shape),
        grad_inputs.reshape(inputs.shape),
        grad_query,
        grad_key,
        grad_value,
        grad_proj,
        grad_up,
        grad_down,
        mine[0],
        mine[1],
        mine[2],
        mine[3],
        grad_scale,
    )


def solution(mesh):
    return jax.shard_map(
        body,
        mesh=mesh,
        in_specs=(
            P("fsdp", "seq", None),
            P(("seq", "fsdp"), None),
            P(("seq", "fsdp"), None),
            P(("seq", "fsdp"), None),
            P(("seq", "fsdp"), None),
            P(("seq", "fsdp"), None),
            P(("seq", "fsdp"), None),
            P(("seq", "fsdp")),
            P(("seq", "fsdp")),
            P(("seq", "fsdp")),
            P(("seq", "fsdp")),
            P(),
            P("fsdp", "seq", None),
        ),
        out_specs=(
            P("fsdp", "seq", None),
            P("fsdp", "seq", None),
            P(("seq", "fsdp"), None),
            P(("seq", "fsdp"), None),
            P(("seq", "fsdp"), None),
            P(("seq", "fsdp"), None),
            P(("seq", "fsdp"), None),
            P(("seq", "fsdp"), None),
            P(("seq", "fsdp")),
            P(("seq", "fsdp")),
            P(("seq", "fsdp")),
            P(("seq", "fsdp")),
            P(),
        ),
        check_vma=False,
    )
```
